128 devices in a mesh: tile: 32 (over x_lo, z, y), cond: 4 (over x_hi, core).
Axes of the slice: x: 4 (x_hi: 2, x_lo: 2; x = x_hi * 2 + x_lo), y: 4, z: 4, core: 2. Of those that a mesh axis runs over, the one named last changes fastest.
Arguments:
- theta: float32 [16384, 512], P(('tile', 'cond')), may hold values from -6 to 6
- target: int32 [16384, 512], P('tile'), may hold values 0 or 1
- kernel_real: float32 [8, 2, 65, 65], P('cond'), may hold values from -24 to 24
- kernel_imag: float32 [8, 2, 65, 65], P('cond'), may hold values from -24 to 24
- weights: int32 [8], replicated, may hold values from 1 to 4
- thresholds: float32 [8], P('cond'), may hold values from 0.5 to 1.5
Outputs:
- gradient: float32 [16384, 512], P(('tile', 'cond'))
The draws below stay inside these ranges and needn't reach their ends.
Inputs may be any that keep to these rules, and one draw needn't show every extreme that they name: Each pixel of the target is 0 or 1. Condition weights are small positive integers.
All inputs are finite; a program needn't handle non-finite values. No bound on the sum of `target` on one device may be relied on, other than what follows from the above.
Results may differ from the reference program's by a relative error of at most 0.00021.
Values sent between devices are 32-bit elements; how exact they have to be, the bound alone decides.
A program may use at most 64 MiB of HBM per device.

```python
import jax
import jax.numpy as jnp
from jax import lax

TP = 512
HALO = 32
KSUP = 65
KERNELS = 2
CONDS = 8
NX = 16384


def touch_ends(result, key, least, high):
    spot = [jax.random.randint(jax.random.fold_in(key, axis), (), 0, length) for axis, length in enumerate(result.shape)]
    main_axis = result.shape.index(max(result.shape))
    neighbour = spot[:main_axis] + [(spot[main_axis] + 1) % result.shape[main_axis]] + spot[main_axis + 1:]
    return result.at[tuple(spot)].set(least).at[tuple(neighbour)].set(high)


def level_of(stream_key, dims, pieces, low, high):
    loudness = 1.0
    for axis_at, parts in pieces:
        steps = jax.random.uniform(jax.random.fold_in(jax.random.fold_in(stream_key, 6), axis_at), (parts,), jnp.float32, low / len(pieces), high / len(pieces))
        loudness = loudness * jnp.repeat(jnp.exp(steps), dims[axis_at] // parts).reshape((-1,) + (1,) * (len(dims) - 1 - axis_at))
    return loudness


def gaussian(key, shape, deviation, most, pieces=(), kind=jnp.bfloat16):
    drawn = jax.random.normal(key, shape, jnp.float32) * deviation
    if len(pieces) > 0:
        drawn = level_of(key, shape, pieces, -0.22, 0.18) * drawn
    return jnp.clip(drawn, min=-most, max=most).astype(kind)


def setup_inputs(seed: int = 0) -> dict:
    splits = jax.random.split(jax.random.key(seed), 7)
    theta = gaussian(splits[0], (NX, TP), 1.0, 6.0, ((0, 128),), jnp.float32)
    target = touch_ends((jax.random.randint(splits[1], (NX, TP), 0, 2) < 1).astype(jnp.int32), jax.random.fold_in(splits[1], 1), 0, 1)
    kernel_real = gaussian(splits[2], (CONDS, KERNELS, KSUP, KSUP), 4.0, 24.0, ((0, 4),), jnp.float32)
    kernel_imag = gaussian(splits[3], (CONDS, KERNELS, KSUP, KSUP), 4.0, 24.0, ((0, 4),), jnp.float32)
    weights = touch_ends(jax.random.randint(splits[4], (CONDS,), 1, 5), jax.random.fold_in(splits[4], 1), 1, 4).astype(jnp.int32)
    thresholds = jnp.clip(0.5 + 1.0 * jax.random.uniform(splits[5], (CONDS,), jnp.float32) ** level_of(splits[5], (CONDS,), ((0, 4),), -0.2, 0.2), 0.5, 1.5)
    return dict(theta=theta, target=target, kernel_real=kernel_real, kernel_imag=kernel_imag, weights=weights, thresholds=thresholds)


mask_steep = 2.0
resist_steep = 4.0
band_weight = 1.0


def tile_gradient(extended, target_map, kern_real, kern_imag, cond_weights, cond_thresholds):
    size_full = TP + 2 * HALO
    freq_index = (jnp.arange(KSUP, dtype=jnp.int32) - KSUP // 2) % size_full
    padded = jnp.zeros((size_full, size_full), extended.dtype).at[:, HALO:HALO + TP].set(extended)
    spectrum = jnp.fft.fft2(padded)[freq_index][:, freq_index]
    kernels = lax.complex(kern_real, kern_imag)

    def place(values):
        empty = jnp.zeros((size_full, size_full), spectrum.dtype)
        return empty.at[freq_index[:, None], freq_index[None, :]].set(values)

    def amplitudes(cond_kernels):
        grids = jax.vmap(place)(cond_kernels * spectrum)
        return jnp.fft.ifft2(grids)[:, HALO:HALO + TP, HALO:HALO + TP]

    def intensity(cond_kernels):
        amp_field = amplitudes(cond_kernels)
        return jnp.sum(jnp.real(amp_field) ** 2 + jnp.imag(amp_field) ** 2, axis=0)

    intensities = lax.map(intensity, kernels)
    resist_maps = jax.nn.sigmoid(resist_steep * (intensities - cond_thresholds[:, None, None]))
    band_mean = jnp.sum(resist_maps, axis=0) / CONDS
    slopes = 2.0 * cond_weights[:, None, None] * (resist_maps - target_map) + (2.0 * band_weight / CONDS) * (resist_maps - band_mean)
    fields = 2.0 * slopes * resist_steep * resist_maps * (1.0 - resist_maps)

    def backward(item):
        cond_kernels, weight_field = item
        amp_field = amplitudes(cond_kernels)
        drive = weight_field * amp_field
        grids = jnp.zeros((KERNELS, size_full, size_full), amp_field.dtype).at[:, HALO:HALO + TP, HALO:HALO + TP].set(drive)
        back_spec = jnp.fft.fft2(grids)[:, freq_index][:, :, freq_index]
        return jnp.sum(jnp.conj(cond_kernels) * back_spec, axis=0)

    adjoint = jnp.sum(lax.map(backward, (kernels, fields)), axis=0)
    return jnp.real(jnp.fft.ifft2(place(adjoint)))[:, HALO:HALO + TP]


def reference(theta, target, kernel_real, kernel_imag, weights, thresholds):
    tile_count = NX // TP
    mask_flat = jnp.tanh(mask_steep * theta)
    mask_tiles = mask_flat.reshape(tile_count, TP, TP)
    zero_tile = jnp.zeros((1, TP, TP), mask_tiles.dtype)
    before = jnp.concatenate([zero_tile, mask_tiles[:-1]], axis=0)[:, TP - HALO:]
    after = jnp.concatenate([mask_tiles[1:], zero_tile], axis=0)[:, :HALO]
    extended = jnp.concatenate([before, mask_tiles, after], axis=1)
    target_tiles = target.astype(jnp.float32).reshape(tile_count, TP, TP)
    cond_weights = weights.astype(jnp.float32) / jnp.sum(weights).astype(jnp.float32)

    def one_tile(item):
        return tile_gradient(item[0], item[1], kernel_real, kernel_imag, cond_weights, thresholds)

    sensitivity = lax.map(one_tile, (extended, target_tiles))
    zero_rim = jnp.zeros((1, HALO, TP), sensitivity.dtype)
    from_left = jnp.concatenate([zero_rim, sensitivity[:-1, HALO + TP:]], axis=0)
    from_right = jnp.concatenate([sensitivity[1:, :HALO], zero_rim], axis=0)
    mask_gradient = sensitivity[:, HALO:HALO + TP]
    mask_gradient = mask_gradient + jnp.pad(from_left, ((0, 0), (0, TP - HALO), (0, 0)))
    mask_gradient = mask_gradient + jnp.pad(from_right, ((0, 0), (TP - HALO, 0), (0, 0)))
    return mask_gradient.reshape(NX, TP) * (mask_steep * (1.0 - mask_flat * mask_flat))
```

```python
import functools
import math

import jax
import jax.numpy as jnp
import ml_dtypes
import numpy as np
from jax import lax
from jax.experimental import pallas as pl
from jax.experimental.pallas import tpu as pltpu
from jax.sharding import PartitionSpec as P

TP = 512
HALO = 32
KSUP = 65
HALF = KSUP // 2
CONDS = 8
KERNELS = 2
SIZE = TP + 2 * HALO
ROWS = 128
GROUP = 4
LOCAL = CONDS // GROUP
UH = 40
UR = 2 * UH
VH = 64
VR = 2 * VH

MASK_STEEP = 2.0
RESIST_STEEP = 4.0
BAND_WEIGHT = 1.0

BF = jnp.bfloat16
F32 = jnp.float32
MESH = pl.DeviceIdType.MESH


def split(x):
    hi = x.astype(BF)
    return hi, (x - hi.astype(F32)).astype(BF)


def np_split(x):
    hi = x.astype(ml_dtypes.bfloat16)
    return hi, (x - hi.astype(np.float64)).astype(ml_dtypes.bfloat16)


def basis(positions, pitch):
    phase = (np.asarray(positions)[:, None] * np.arange(HALF + 1)[None, :]) % SIZE
    angles = phase * (2.0 * math.pi / SIZE)
    out = np.zeros((len(positions), 2 * pitch))
    out[:, : HALF + 1] = np.cos(angles)
    out[:, pitch : pitch + HALF + 1] = np.sin(angles)
    out[:, pitch] = 0.0
    return out


def parity(pitch, columns):
    out = np.zeros((2 * pitch, columns))
    out[0, HALF] = 1.0
    for j in range(1, HALF + 1):
        out[j, HALF + j] = 1.0
        out[j, HALF - j] = 1.0
        out[pitch + j, HALF + j] = 1.0
        out[pitch + j, HALF - j] = -1.0
    return out


def tables():
    bf = ml_dtypes.bfloat16
    cols = basis(np.arange(TP) + HALO, VH)
    hi, lo = np_split(cols)
    by = np.concatenate([hi, lo], axis=1)
    bt = np.concatenate([hi.T, hi.T, lo.T], axis=0)
    pack = []
    turned = []
    for c in range(GROUP):
        own = basis(np.arange(ROWS) + HALO + ROWS * c, UH)
        near = np.zeros_like(own)
        if c == 0:
            near[:HALO] = basis(np.arange(HALO) + HALO + TP, UH)
        if c == GROUP - 1:
            near[ROWS - HALO :] = basis(np.arange(HALO), UH)
        row = []
        column = []
        for table in (own, near):
            thi, tlo = np_split(table)
            row += [thi, tlo, thi, np.zeros((ROWS, 256 - 3 * UR), bf)]
            column.append(np.concatenate([thi.T, thi.T], axis=1))
            column.append(np.concatenate([tlo.T, np.zeros((UR, ROWS), bf)], axis=1))
        pack.append(np.concatenate(row, axis=1))
        turned.append(np.concatenate(column, axis=0))
    pv = parity(VH, VR).T.astype(bf)
    pv = np.concatenate([pv, pv], axis=0)
    pu = parity(UH, UR).astype(bf)
    pu = np.concatenate([pu, pu], axis=1)
    return by, bt, np.stack(pack), np.stack(turned), pv, pu


def dot(a, b):
    return jnp.dot(a, b, preferred_element_type=F32)


def kernel(
    tiles,
    theta_h, target_h, kr_h, ki_h, weights_s, thresholds_s, by_h, bt_h, pack_h, turned_h, pv_h, pu_h,
    out_h,
    theta_v, target_v, raw_v, by, bt, pack, turned, pv, pu,
    stack, zbuf, rown, rhalo, rin, rsum, aown, ain, anear, jbuf, amps, resists, band, grad_v,
    load_sem, zs_sem, zr_sem, rs_sem, rr_sem, hs_sem, hr_sem, as_sem, ar_sem, near_sem, out_sem,
):
    t = lax.axis_index("tile")
    c = lax.axis_index("cond")
    first = c == 0
    final = c == GROUP - 1
    has_prev = t > 0
    has_next = t < tiles - 1

    loads = []

    def load(src, dst):
        copy = pltpu.make_async_copy(src, dst, load_sem.at[len(loads)])
        copy.start()
        loads.append(copy)
        return copy

    load_kr = load(kr_h, raw_v.at[0])
    load_ki = load(ki_h, raw_v.at[1])
    load_pv = load(pv_h, pv)
    load_pu = load(pu_h, pu)
    load_theta = load(theta_h, theta_v)
    load_by = load(by_h, by)
    load_turned = load(turned_h.at[c], turned)
    load_pack = load(pack_h.at[c], pack)
    load_bt = load(bt_h, bt)
    load_target = load(target_h.at[pl.ds(pl.multiple_of(c * ROWS, ROWS), ROWS), :], target_v)

    def partner(mask):
        return (t, c ^ mask)

    barrier = pltpu.get_barrier_semaphore()

    def greet(device):
        pl.semaphore_signal(barrier, inc=1, device_id=device, device_id_type=MESH)

    for mask in range(1, GROUP):
        greet(partner(mask))
    for other in range(GROUP):
        @pl.when(has_next & (final | (other == 0)))
        def _(other=other):
            greet((t + 1, other))

        @pl.when(has_prev & (first | (other == GROUP - 1)))
        def _(other=other):
            greet((t - 1, other))

    stack[...] = jnp.zeros_like(stack)
    load_kr.wait()
    load_ki.wait()
    for ri in range(2):
        for l in range(LOCAL):
            for k in range(KERNELS):
                at = ((l * KERNELS + k) * 2 + ri) * UR
                stack[at : at + KSUP, 0:KSUP] = raw_v[ri, l, k]
    load_pv.wait()
    load_pu.wait()
    hi, lo = split(stack[...])
    folded = dot(jnp.concatenate([hi, lo], axis=1), pv[...])
    hi, lo = split(folded)
    for n in range(LOCAL * KERNELS * 2):
        rhs = jnp.concatenate([hi[n * UR : (n + 1) * UR], lo[n * UR : (n + 1) * UR]], axis=0)
        zbuf[0, n // 4, (n // 2) % 2, n % 2] = dot(pu[...], rhs)
    for l in range(LOCAL):
        zbuf[0, l, 0, 0, HALF + 2 : HALF + 3, :] = jnp.full((1, VR), thresholds_s[l], F32)

    load_theta.wait()
    load_by.wait()
    load_turned.wait()
    mask_rows = jnp.tanh(MASK_STEEP * theta_v[...])
    hi, lo = split(mask_rows)
    wide = dot(jnp.concatenate([hi, lo], axis=0), by[...])
    column = wide[:ROWS, :VR] + wide[:ROWS, VR:] + wide[ROWS:, :VR]
    hi, lo = split(column)
    both = dot(turned[...], jnp.concatenate([hi, lo], axis=0))
    rown[...] = both[:UR] + both[UR : 2 * UR]
    rhalo[...] = both[2 * UR : 3 * UR] + both[3 * UR :]

    across_next = jnp.where(final, GROUP, 1) * has_next.astype(jnp.int32)
    across_prev = jnp.where(first, GROUP, 1) * has_prev.astype(jnp.int32)
    pl.semaphore_wait(barrier, GROUP - 1 + across_next + across_prev)

    def remote(src, dst, send, recv, device):
        return pltpu.make_async_remote_copy(
            src_ref=src, dst_ref=dst, send_sem=send, recv_sem=recv, device_id=device, device_id_type=MESH
        )

    def halo_next(other):
        return remote(rhalo, rin.at[3], hs_sem.at[other], hr_sem.at[0], (t + 1, other))

    def halo_prev(other):
        return remote(rhalo, rin.at[4], hs_sem.at[other], hr_sem.at[1], (t - 1, other))

    def part(mask):
        return remote(rown, rin.at[mask - 1], rs_sem.at[mask - 1], rr_sem.at[mask - 1], partner(mask))

    def kernels_to(mask):
        return remote(zbuf.at[0], zbuf.at[mask], zs_sem.at[mask - 1], zr_sem.at[mask - 1], partner(mask))

    @pl.when(has_next & final)
    def _():
        for other in range(GROUP):
            halo_next(other).start()

    @pl.when(has_prev & first)
    def _():
        for other in range(GROUP):
            halo_prev(other).start()

    for mask in range(1, GROUP):
        part(mask).start()
    for mask in range(1, GROUP):
        kernels_to(mask).start()

    @pl.when(jnp.logical_not(has_prev))
    def _():
        rin[3] = jnp.zeros((UR, VR), F32)

    @pl.when(jnp.logical_not(has_next))
    def _():
        rin[4] = jnp.zeros((UR, VR), F32)

    @pl.when(has_prev)
    def _():
        halo_next(0).wait_recv()

    @pl.when(has_next)
    def _():
        halo_prev(0).wait_recv()

    for mask in range(1, GROUP):
        part(mask).wait_recv()

    lane = lax.broadcasted_iota(jnp.int32, (UH, VR), 1)
    low = lane < VH
    sign_v = jnp.where(low, 1.0, -1.0).astype(F32)

    def swap(x):
        return pltpu.roll(x, VH, 1)

    total = rown[...] + rin[0] + rin[1] + rin[2] + rin[3] + rin[4]
    total = total * (1.0 / (SIZE * SIZE))
    for h in range(2):
        here = total[h * UH : (h + 1) * UH]
        there = total[(1 - h) * UH : (2 - h) * UH]
        sign_u = 1.0 - 2.0 * h
        rsum[0, h] = here
        rsum[1, h] = sign_v * swap(here)
        rsum[2, h] = sign_u * there
        rsum[3, h] = (-sign_u) * sign_v * swap(there)

    def parts_of(s, l, k):
        out = []
        for ri in range(2):
            for h in range(2):
                z = zbuf[s, l, k, ri, h * UH : (h + 1) * UH, :]
                turn = swap(z)
                out.append(jnp.where(low, z, turn))
                out.append(jnp.where(low, turn, z))
        return out

    load_pack.wait()
    load_bt.wait()

    def forward(i, carry):
        s = i // LOCAL
        l = i % LOCAL

        @pl.when((l == 0) & (s > 0))
        def _():
            remote(zbuf.at[0], zbuf.at[s], zs_sem.at[s - 1], zr_sem.at[s - 1], (t, c ^ 1)).wait_recv()

        intensity = None
        for k in range(KERNELS):
            ee_r, eo_r, oe_r, oo_r, ee_i, eo_i, oe_i, oo_i = parts_of(s, l, k)
            real = []
            imag = []
            for h in range(2):
                r0, r1, r2, r3 = (rsum[n, h] for n in range(4))
                real.append(ee_r * r0 + eo_i * r1 + oe_i * r2 + oo_r * r3)
                imag.append(ee_i * r0 - eo_r * r1 - oe_r * r2 + oo_i * r3)
            grid = jnp.concatenate(
                [jnp.concatenate(real, axis=0), jnp.concatenate(imag, axis=0)], axis=1
            )
            hi, lo = split(grid)
            tall = dot(pack[:, : 3 * UR], jnp.concatenate([hi, hi, lo], axis=0))
            tall = jnp.concatenate([tall[:, :VR], tall[:, VR:]], axis=0)
            hi, lo = split(tall)
            amp = dot(jnp.concatenate([hi, lo, hi], axis=1), bt[...])
            amps[i, k] = amp
            power = amp[:ROWS] * amp[:ROWS] + amp[ROWS:] * amp[ROWS:]
            intensity = power if intensity is None else intensity + power
        level = zbuf[s, l, 0, 0, HALF + 2 : HALF + 3, 0:1]
        resist = jax.nn.sigmoid(RESIST_STEEP * (intensity - level))
        resists[i] = resist

        @pl.when(i == 0)
        def _():
            band[...] = resist

        @pl.when(i > 0)
        def _():
            band[...] += resist

        return carry

    lax.fori_loop(0, CONDS, forward, 0)

    load_target.wait()
    weight_sum = weights_s[0]
    for n in range(1, CONDS):
        weight_sum = weight_sum + weights_s[n]
    weight_sum = jnp.full((8, TP), weight_sum, jnp.int32).astype(F32)
    jbuf[...] = jnp.zeros_like(jbuf)

    def backward(i, carry):
        s = i // LOCAL
        l = i % LOCAL
        weight = jnp.full((8, TP), weights_s[(c ^ s) * LOCAL + l], jnp.int32).astype(F32) / weight_sum
        weight = weight[0:1]
        resist = resists[i]
        slope = 2.0 * weight * (resist - target_v[...].astype(F32)) + (2.0 * BAND_WEIGHT / CONDS) * (
            resist - band[...] * (1.0 / CONDS)
        )
        field = 2.0 * slope * RESIST_STEEP * resist * (1.0 - resist)
        field = jnp.concatenate([field, field], axis=0)
        for k in range(KERNELS):
            hi, lo = split(field * amps[i, k])
            wide = dot(jnp.concatenate([hi, lo], axis=0), by[...])
            drive = wide[: 2 * ROWS, :VR] + wide[: 2 * ROWS, VR:] + wide[2 * ROWS :, :VR]
            drive = jnp.concatenate([drive[:ROWS], drive[ROWS:]], axis=1)
            hi, lo = split(drive)
            back = dot(turned[: 2 * UR, :], jnp.concatenate([hi, lo], axis=0))
            back = back[:UR] + back[UR:]
            ee_r, eo_r, oe_r, oo_r, ee_i, eo_i, oe_i, oo_i = parts_of(s, l, k)
            for h in range(2):
                qr = back[h * UH : (h + 1) * UH, :VR]
                qi = back[h * UH : (h + 1) * UH, VR:]
                jbuf[0, h] += ee_r * qr + ee_i * qi
                jbuf[1, h] += eo_i * qr - eo_r * qi
                jbuf[2, h] += oe_i * qr - oe_r * qi
                jbuf[3, h] += oo_r * qr + oo_i * qi
        return carry

    lax.fori_loop(0, CONDS, backward, 0)

    for h in range(2):
        sign_u = 1.0 - 2.0 * h
        aown[h * UH : (h + 1) * UH, :] = (
            jbuf[0, h]
            + swap(sign_v * jbuf[1, h])
            - sign_u * jbuf[2, 1 - h]
            + swap(sign_u * sign_v * jbuf[3, 1 - h])
        )

    def adjoint_part(mask):
        return remote(aown, ain.at[mask - 1], as_sem.at[mask - 1], ar_sem.at[mask - 1], partner(mask))

    def adjoint_prev():
        return remote(aown, anear.at[c], as_sem.at[3], near_sem.at[c], (t - 1, GROUP - 1))

    def adjoint_next():
        return remote(aown, anear.at[c], as_sem.at[4], near_sem.at[c], (t + 1, 0))

    def adjoint_near(other):
        return remote(aown, anear.at[other], as_sem.at[3], near_sem.at[other], (t, c ^ 1))

    @pl.when(has_prev)
    def _():
        adjoint_prev().start()

    @pl.when(has_next)
    def _():
        adjoint_next().start()

    for mask in range(1, GROUP):
        adjoint_part(mask).start()

    near = (first & has_prev) | (final & has_next)

    @pl.when(jnp.logical_not(near))
    def _():
        anear[...] = jnp.zeros_like(anear)

    factor = grad_v
    factor[...] = (MASK_STEEP / (SIZE * SIZE)) * (1.0 - jnp.square(jnp.tanh(MASK_STEEP * theta_v[...])))

    for mask in range(1, GROUP):
        adjoint_part(mask).wait_recv()

    @pl.when(near)
    def _():
        for other in range(GROUP):
            adjoint_near(other).wait_recv()

    rows = []
    for value in (aown[...] + ain[0] + ain[1] + ain[2], anear[0] + anear[1] + anear[2] + anear[3]):
        hi, lo = split(value)
        rows += [hi, hi, lo, jnp.zeros((256 - 3 * UR, VR), BF)]
    tall = dot(pack[...], jnp.concatenate(rows, axis=0))
    hi, lo = split(tall)
    grad_v[...] = dot(jnp.concatenate([hi, lo, hi], axis=1), bt[...]) * factor[...]
    out = pltpu.make_async_copy(grad_v, out_h, out_sem)
    out.start()

    @pl.when(has_next & final)
    def _():
        for other in range(GROUP):
            halo_next(other).wait_send()

    @pl.when(has_prev & first)
    def _():
        for other in range(GROUP):
            halo_prev(other).wait_send()

    for mask in range(1, GROUP):
        part(mask).wait_send()
        kernels_to(mask).wait_send()
        adjoint_part(mask).wait_send()

    @pl.when(has_prev)
    def _():
        adjoint_prev().wait_send()

    @pl.when(has_next)
    def _():
        adjoint_next().wait_send()

    out.wait()


def shards(tiles, theta, target, kernel_real, kernel_imag, weights, thresholds):
    constants = tables()
    anywhere = pl.BlockSpec(memory_space=pl.ANY)
    scalars = pl.BlockSpec(memory_space=pltpu.SMEM)
    dma = pltpu.SemaphoreType.DMA
    local = (LOCAL, KERNELS)
    by, bt, pack, turned, pv, pu = constants
    call = pl.pallas_call(
        functools.partial(kernel, tiles),
        out_shape=jax.ShapeDtypeStruct((ROWS, TP), F32),
        in_specs=[anywhere] * 4 + [scalars] * 2 + [anywhere] * 6,
        out_specs=anywhere,
        scratch_shapes=[
            pltpu.VMEM((ROWS, TP), F32),
            pltpu.VMEM((ROWS, TP), jnp.int32),
            pltpu.VMEM((2,) + local + (KSUP, KSUP), F32),
            pltpu.VMEM(by.shape, BF),
            pltpu.VMEM(bt.shape, BF),
            pltpu.VMEM(pack.shape[1:], BF),
            pltpu.VMEM(turned.shape[1:], BF),
            pltpu.VMEM(pv.shape, BF),
            pltpu.VMEM(pu.shape, BF),
            pltpu.VMEM((LOCAL * KERNELS * 2 * UR, VR), F32),
            pltpu.VMEM((GROUP,) + local + (2, UR, VR), F32),
            pltpu.VMEM((UR, VR), F32),
            pltpu.VMEM((UR, VR), F32),
            pltpu.VMEM((5, UR, VR), F32),
            pltpu.VMEM((4, 2, UH, VR), F32),
            pltpu.VMEM((UR, VR), F32),
            pltpu.VMEM((3, UR, VR), F32),
            pltpu.VMEM((GROUP, UR, VR), F32),
            pltpu.VMEM((4, 2, UH, VR), F32),
            pltpu.VMEM((CONDS, KERNELS, 2 * ROWS, TP), F32),
            pltpu.VMEM((CONDS, ROWS, TP), F32),
            pltpu.VMEM((ROWS, TP), F32),
            pltpu.VMEM((ROWS, TP), F32),
            dma((10,)),
            dma((3,)),
            dma((3,)),
            dma((3,)),
            dma((3,)),
            dma((4,)),
            dma((2,)),
            dma((5,)),
            dma((3,)),
            dma((4,)),
            dma,
        ],
        compiler_params=pltpu.CompilerParams(collective_id=0, has_side_effects=True),
        name="window_gradient",
    )
    return call(theta, target, kernel_real, kernel_imag, weights, thresholds, *(jnp.asarray(x) for x in constants))


def solution(mesh):
    in_specs = (
        P(("tile", "cond"), None),
        P("tile", None),
        P("cond", None, None, None),
        P("cond", None, None, None),
        P(),
        P("cond"),
    )
    out_specs = P(("tile", "cond"), None)
    body = functools.partial(shards, mesh.shape["tile"])
    return jax.shard_map(body, mesh=mesh, in_specs=in_specs, out_specs=out_specs, check_vma=False)
```

```python
import functools
import math

import jax
import jax.numpy as jnp
import ml_dtypes
import numpy as np
from jax import lax
from jax.experimental import pallas as pl
from jax.experimental.pallas import tpu as pltpu
from jax.sharding import PartitionSpec as P

TP = 512
HALO = 32
KSUP = 65
HALF = KSUP // 2
CONDS = 8
KERNELS = 2
SIZE = TP + 2 * HALO
ROWS = 128
GROUP = 4
LOCAL = CONDS // GROUP
UH = 40
UR = 2 * UH
VH = 64
VR = 2 * VH

MASK_STEEP = 2.0
RESIST_STEEP = 4.0
BAND_WEIGHT = 1.0

BF = jnp.bfloat16
F32 = jnp.float32
MESH = pl.DeviceIdType.MESH


def split(x):
    hi = x.astype(BF)
    return hi, (x - hi.astype(F32)).astype(BF)


def np_split(x):
    hi = x.astype(ml_dtypes.bfloat16)
    return hi, (x - hi.astype(np.float64)).astype(ml_dtypes.bfloat16)


def basis(positions, pitch):
    phase = (np.asarray(positions)[:, None] * np.arange(HALF + 1)[None, :]) % SIZE
    angles = phase * (2.0 * math.pi / SIZE)
    out = np.zeros((len(positions), 2 * pitch))
    out[:, : HALF + 1] = np.cos(angles)
    out[:, pitch : pitch + HALF + 1] = np.sin(angles)
    out[:, pitch] = 0.0
    return out


def parity(pitch, columns):
    out = np.zeros((2 * pitch, columns))
    out[0, HALF] = 1.0
    for j in range(1, HALF + 1):
        out[j, HALF + j] = 1.0
        out[j, HALF - j] = 1.0
        out[pitch + j, HALF + j] = 1.0
        out[pitch + j, HALF - j] = -1.0
    return out


def tables():
    bf = ml_dtypes.bfloat16
    cols = basis(np.arange(TP) + HALO, VH)
    hi, lo = np_split(cols)
    by = np.concatenate([hi, lo], axis=1)
    bt = np.concatenate([hi.T, hi.T, lo.T], axis=0)
    pack = []
    turned = []
    for c in range(GROUP):
        own = basis(np.arange(ROWS) + HALO + ROWS * c, UH)
        near = np.zeros_like(own)
        if c == 0:
            near[:HALO] = basis(np.arange(HALO) + HALO + TP, UH)
        if c == GROUP - 1:
            near[ROWS - HALO :] = basis(np.arange(HALO), UH)
        row = []
        column = []
        for table in (own, near):
            thi, tlo = np_split(table)
            row += [thi, tlo, thi, np.zeros((ROWS, 256 - 3 * UR), bf)]
            column.append(np.concatenate([thi.T, thi.T], axis=1))
            column.append(np.concatenate([tlo.T, np.zeros((UR, ROWS), bf)], axis=1))
        pack.append(np.concatenate(row, axis=1))
        turned.append(np.concatenate(column, axis=0))
    pv = parity(VH, VR).T.astype(bf)
    pv = np.concatenate([pv, pv], axis=0)
    pu = parity(UH, UR).astype(bf)
    pu = np.concatenate([pu, pu], axis=1)
    return by, bt, np.stack(pack), np.stack(turned), pv, pu


def dot(a, b):
    return jnp.dot(a, b, preferred_element_type=F32)


def kernel(
    tiles,
    theta_h, target_h, kr_h, ki_h, weights_s, thresholds_s, by_h, bt_h, pack_h, turned_h, pv_h, pu_h,
    out_h,
    theta_v, target_v, raw_v, by, bt, pack, turned, pv, pu,
    stack, zbuf, rown, rhalo, rin, rsum, aown, ain, anear, jbuf, amps, resists, band, wanted, grad_v,
    load_sem, zs_sem, zr_sem, rs_sem, rr_sem, hs_sem, hr_sem, as_sem, ar_sem, near_sem, out_sem,
):
    t = lax.axis_index("tile")
    c = lax.axis_index("cond")
    first = c == 0
    final = c == GROUP - 1
    has_prev = t > 0
    has_next = t < tiles - 1

    loads = []

    def load(src, dst):
        copy = pltpu.make_async_copy(src, dst, load_sem.at[len(loads)])
        copy.start()
        loads.append(copy)
        return copy

    load_kr = load(kr_h, raw_v.at[0])
    load_ki = load(ki_h, raw_v.at[1])
    load_pv = load(pv_h, pv)
    load_pu = load(pu_h, pu)
    load_theta = load(theta_h, theta_v)
    load_by = load(by_h, by)
    load_turned = load(turned_h.at[c], turned)
    load_pack = load(pack_h.at[c], pack)
    load_bt = load(bt_h, bt)
    load_target = load(target_h.at[pl.ds(pl.multiple_of(c * ROWS, ROWS), ROWS), :], target_v)

    def partner(mask):
        return (t, c ^ mask)

    barrier = pltpu.get_barrier_semaphore()

    def greet(device):
        pl.semaphore_signal(barrier, inc=1, device_id=device, device_id_type=MESH)

    mirror = ((t + tiles // 2) % tiles, c ^ 2)
    for mask in range(1, GROUP):
        greet(partner(mask))
    greet(mirror)
    for other in range(GROUP):
        @pl.when(has_next & (final | (other == 0)))
        def _(other=other):
            greet((t + 1, other))

        @pl.when(has_prev & (first | (other == GROUP - 1)))
        def _(other=other):
            greet((t - 1, other))

    stack[...] = jnp.zeros_like(stack)
    load_kr.wait()
    load_ki.wait()
    for ri in range(2):
        for l in range(LOCAL):
            for k in range(KERNELS):
                at = ((l * KERNELS + k) * 2 + ri) * UR
                stack[at : at + KSUP, 0:KSUP] = raw_v[ri, l, :, k, :]
    load_pv.wait()
    load_pu.wait()
    hi, lo = split(stack[...])
    folded = dot(jnp.concatenate([hi, lo], axis=1), pv[...])
    hi, lo = split(folded)
    for n in range(LOCAL * KERNELS * 2):
        rhs = jnp.concatenate([hi[n * UR : (n + 1) * UR], lo[n * UR : (n + 1) * UR]], axis=0)
        zbuf[0, n // 4, (n // 2) % 2, n % 2] = dot(pu[...], rhs)
    for l in range(LOCAL):
        zbuf[0, l, 0, 0, HALF + 2 : HALF + 3, :] = jnp.full((1, VR), thresholds_s[l], F32)

    load_theta.wait()
    load_by.wait()
    load_turned.wait()
    mask_rows = jnp.tanh(MASK_STEEP * theta_v[...])
    hi, lo = split(mask_rows)
    wide = dot(jnp.concatenate([hi, lo], axis=0), by[...])
    column = wide[:ROWS, :VR] + wide[:ROWS, VR:] + wide[ROWS:, :VR]
    hi, lo = split(column)
    both = dot(turned[...], jnp.concatenate([hi, lo], axis=0))
    rown[...] = both[:UR] + both[UR : 2 * UR]
    rhalo[...] = both[2 * UR : 3 * UR] + both[3 * UR :]

    across_next = jnp.where(final, GROUP, 1) * has_next.astype(jnp.int32)
    across_prev = jnp.where(first, GROUP, 1) * has_prev.astype(jnp.int32)
    pl.semaphore_wait(barrier, GROUP + across_next + across_prev)

    def remote(src, dst, send, recv, device):
        return pltpu.make_async_remote_copy(
            src_ref=src, dst_ref=dst, send_sem=send, recv_sem=recv, device_id=device, device_id_type=MESH
        )

    def halo_next(other):
        return remote(rhalo, rin.at[3], hs_sem.at[other], hr_sem.at[0], (t + 1, other))

    def halo_prev(other):
        return remote(rhalo, rin.at[4], hs_sem.at[other], hr_sem.at[1], (t - 1, other))

    def part(mask):
        return remote(rown, rin.at[mask - 1], rs_sem.at[mask - 1], rr_sem.at[mask - 1], partner(mask))

    def kernels_to(mask):
        device = partner(1) if mask != 2 else mirror
        source = 2 if mask == 3 else 0
        return remote(zbuf.at[source], zbuf.at[mask], zs_sem.at[mask - 1], zr_sem.at[mask - 1], device)

    @pl.when(has_next & final)
    def _():
        for other in range(GROUP):
            halo_next(other).start()

    @pl.when(has_prev & first)
    def _():
        for other in range(GROUP):
            halo_prev(other).start()

    for mask in range(1, GROUP):
        part(mask).start()
    for mask in (2, 1):
        kernels_to(mask).start()

    @pl.when(jnp.logical_not(has_prev))
    def _():
        rin[3] = jnp.zeros((UR, VR), F32)

    @pl.when(jnp.logical_not(has_next))
    def _():
        rin[4] = jnp.zeros((UR, VR), F32)

    @pl.when(has_prev)
    def _():
        halo_next(0).wait_recv()

    @pl.when(has_next)
    def _():
        halo_prev(0).wait_recv()

    for mask in range(1, GROUP):
        part(mask).wait_recv()

    lane = lax.broadcasted_iota(jnp.int32, (UH, VR), 1)
    low = lane < VH
    sign_v = jnp.where(low, 1.0, -1.0).astype(F32)

    def swap(x):
        return pltpu.roll(x, VH, 1)

    total = rown[...] + rin[0] + rin[1] + rin[2] + rin[3] + rin[4]
    total = total * (1.0 / (SIZE * SIZE))
    for h in range(2):
        here = total[h * UH : (h + 1) * UH]
        there = total[(1 - h) * UH : (2 - h) * UH]
        sign_u = 1.0 - 2.0 * h
        rsum[0, h] = here
        rsum[1, h] = sign_v * swap(here)
        rsum[2, h] = sign_u * there
        rsum[3, h] = (-sign_u) * sign_v * swap(there)

    def parts_of(s, l, k):
        out = []
        for ri in range(2):
            for h in range(2):
                z = zbuf[s, l, k, ri, h * UH : (h + 1) * UH, :]
                turn = swap(z)
                out.append(jnp.where(low, z, turn))
                out.append(jnp.where(low, turn, z))
        return out

    load_pack.wait()
    load_bt.wait()

    each = [(l, k) for l in range(LOCAL) for k in range(KERNELS)]

    def forward(s, carry):
        @pl.when(s == 1)
        def _():
            kernels_to(1).wait_recv()

        @pl.when(s == 2)
        def _():
            kernels_to(2).wait_recv()
            kernels_to(3).start()

        @pl.when(s == 3)
        def _():
            kernels_to(3).wait_recv()

        grids = []
        for l, k in each:
            ee_r, eo_r, oe_r, oo_r, ee_i, eo_i, oe_i, oo_i = parts_of(s, l, k)
            real = []
            imag = []
            for h in range(2):
                r0, r1, r2, r3 = (rsum[n, h] for n in range(4))
                real.append(ee_r * r0 + eo_i * r1 + oe_i * r2 + oo_r * r3)
                imag.append(ee_i * r0 - eo_r * r1 - oe_r * r2 + oo_i * r3)
            grid = jnp.concatenate([jnp.concatenate(real, axis=0), jnp.concatenate(imag, axis=0)], axis=1)
            hi, lo = split(grid)
            grids.append(jnp.concatenate([hi, hi, lo], axis=0))
        lhs = []
        for grid in grids:
            tall = dot(pack[:, : 3 * UR], grid)
            tall = jnp.concatenate([tall[:, :VR], tall[:, VR:]], axis=0)
            hi, lo = split(tall)
            lhs.append(jnp.concatenate([hi, lo, hi], axis=1))
        amp = dot(jnp.concatenate(lhs, axis=0), bt[...])
        amps[s] = amp
        total = None
        for l in range(LOCAL):
            intensity = None
            for part in range(4):
                piece = amp[(l * 4 + part) * ROWS : (l * 4 + part + 1) * ROWS]
                intensity = piece * piece if part == 0 else intensity + piece * piece
            level = zbuf[s, l, 0, 0, HALF + 2 : HALF + 3, 0:1]
            resist = jax.nn.sigmoid(RESIST_STEEP * (intensity - level))
            resists[s, l] = resist
            total = resist if l == 0 else total + resist

        @pl.when(s == 0)
        def _():
            band[...] = total

        @pl.when(s > 0)
        def _():
            band[...] += total

        return carry

    lax.fori_loop(0, GROUP, forward, 0)

    load_target.wait()
    weight_sum = weights_s[0]
    for n in range(1, CONDS):
        weight_sum = weight_sum + weights_s[n]
    weight_sum = jnp.full((8, TP), weight_sum, jnp.int32).astype(F32)
    jbuf[...] = jnp.zeros_like(jbuf)
    wanted[...] = target_v[...].astype(F32)
    band[...] = band[...] * (4.0 * RESIST_STEEP * BAND_WEIGHT / CONDS / CONDS)

    def backward(s, carry):
        drives = []
        for l in range(LOCAL):
            weight = jnp.full((8, TP), weights_s[(c ^ s) * LOCAL + l], jnp.int32).astype(F32) / weight_sum
            pull = (4.0 * RESIST_STEEP) * weight[0:1]
            resist = resists[s, l]
            slope = (pull + 4.0 * RESIST_STEEP * BAND_WEIGHT / CONDS) * resist - (pull * wanted[...] + band[...])
            field = slope * (resist - resist * resist)
            for part in range(4):
                at = (l * 4 + part) * ROWS
                drives.append(field * amps[s, at : at + ROWS])
        hi, lo = split(jnp.concatenate(drives, axis=0))
        wide = dot(jnp.concatenate([hi, lo], axis=0), by[...])
        half = 8 * ROWS
        drive = wide[:half, :VR] + wide[:half, VR:] + wide[half:, :VR]
        sums = [[None, None] for _ in range(4)]
        for n, (l, k) in enumerate(each):
            pair = jnp.concatenate([drive[2 * n * ROWS : (2 * n + 1) * ROWS], drive[(2 * n + 1) * ROWS : (2 * n + 2) * ROWS]], axis=1)
            hi, lo = split(pair)
            back = dot(turned[: 2 * UR, :], jnp.concatenate([hi, lo], axis=0))
            back = back[:UR] + back[UR:]
            ee_r, eo_r, oe_r, oo_r, ee_i, eo_i, oe_i, oo_i = parts_of(s, l, k)
            for h in range(2):
                qr = back[h * UH : (h + 1) * UH, :VR]
                qi = back[h * UH : (h + 1) * UH, VR:]
                terms = (
                    ee_r * qr + ee_i * qi,
                    eo_i * qr - eo_r * qi,
                    oe_i * qr - oe_r * qi,
                    oo_r * qr + oo_i * qi,
                )
                for m, term in enumerate(terms):
                    sums[m][h] = term if n == 0 else sums[m][h] + term
        for m in range(4):
            for h in range(2):
                jbuf[m, h] += sums[m][h]
        return carry

    lax.fori_loop(0, GROUP, backward, 0)

    for h in range(2):
        sign_u = 1.0 - 2.0 * h
        aown[h * UH : (h + 1) * UH, :] = (
            jbuf[0, h]
            + swap(sign_v * jbuf[1, h])
            - sign_u * jbuf[2, 1 - h]
            + swap(sign_u * sign_v * jbuf[3, 1 - h])
        )

    def adjoint_part(mask):
        return remote(aown, ain.at[mask - 1], as_sem.at[mask - 1], ar_sem.at[mask - 1], partner(mask))

    def adjoint_prev():
        return remote(aown, anear.at[c], as_sem.at[3], near_sem.at[c], (t - 1, GROUP - 1))

    def adjoint_next():
        return remote(aown, anear.at[c], as_sem.at[4], near_sem.at[c], (t + 1, 0))

    def adjoint_near(other):
        return remote(aown, anear.at[other], as_sem.at[3], near_sem.at[other], (t, c ^ 1))

    @pl.when(has_prev)
    def _():
        adjoint_prev().start()

    @pl.when(has_next)
    def _():
        adjoint_next().start()

    for mask in range(1, GROUP):
        adjoint_part(mask).start()

    near = (first & has_prev) | (final & has_next)

    @pl.when(jnp.logical_not(near))
    def _():
        anear[...] = jnp.zeros_like(anear)

    factor = grad_v
    factor[...] = (MASK_STEEP / (SIZE * SIZE)) * (1.0 - jnp.square(jnp.tanh(MASK_STEEP * theta_v[...])))

    for mask in range(1, GROUP):
        adjoint_part(mask).wait_recv()

    @pl.when(near)
    def _():
        for other in range(GROUP):
            adjoint_near(other).wait_recv()

    rows = []
    for value in (aown[...] + ain[0] + ain[1] + ain[2], anear[0] + anear[1] + anear[2] + anear[3]):
        hi, lo = split(value)
        rows += [hi, hi, lo, jnp.zeros((256 - 3 * UR, VR), BF)]
    tall = dot(pack[...], jnp.concatenate(rows, axis=0))
    hi, lo = split(tall)
    grad_v[...] = dot(jnp.concatenate([hi, lo, hi], axis=1), bt[...]) * factor[...]
    out = pltpu.make_async_copy(grad_v, out_h, out_sem)
    out.start()

    @pl.when(has_next & final)
    def _():
        for other in range(GROUP):
            halo_next(other).wait_send()

    @pl.when(has_prev & first)
    def _():
        for other in range(GROUP):
            halo_prev(other).wait_send()

    for mask in range(1, GROUP):
        part(mask).wait_send()
        kernels_to(mask).wait_send()
        adjoint_part(mask).wait_send()

    @pl.when(has_prev)
    def _():
        adjoint_prev().wait_send()

    @pl.when(has_next)
    def _():
        adjoint_next().wait_send()

    out.wait()


def shards(tiles, theta, target, kernel_real, kernel_imag, weights, thresholds):
    constants = tables()
    anywhere = pl.BlockSpec(memory_space=pl.ANY)
    scalars = pl.BlockSpec(memory_space=pltpu.SMEM)
    dma = pltpu.SemaphoreType.DMA
    local = (LOCAL, KERNELS)
    by, bt, pack, turned, pv, pu = constants
    call = pl.pallas_call(
        functools.partial(kernel, tiles),
        out_shape=jax.ShapeDtypeStruct((ROWS, TP), F32),
        in_specs=[anywhere] * 4 + [scalars] * 2 + [anywhere] * 6,
        out_specs=anywhere,
        scratch_shapes=[
            pltpu.VMEM((ROWS, TP), F32),
            pltpu.VMEM((ROWS, TP), jnp.int32),
            pltpu.VMEM((2, LOCAL, KSUP, KERNELS, KSUP), F32),
            pltpu.VMEM(by.shape, BF),
            pltpu.VMEM(bt.shape, BF),
            pltpu.VMEM(pack.shape[1:], BF),
            pltpu.VMEM(turned.shape[1:], BF),
            pltpu.VMEM(pv.shape, BF),
            pltpu.VMEM(pu.shape, BF),
            pltpu.VMEM((LOCAL * KERNELS * 2 * UR, VR), F32),
            pltpu.VMEM((GROUP,) + local + (2, UR, VR), F32),
            pltpu.VMEM((UR, VR), F32),
            pltpu.VMEM((UR, VR), F32),
            pltpu.VMEM((5, UR, VR), F32),
            pltpu.VMEM((4, 2, UH, VR), F32),
            pltpu.VMEM((UR, VR), F32),
            pltpu.VMEM((3, UR, VR), F32),
            pltpu.VMEM((GROUP, UR, VR), F32),
            pltpu.VMEM((4, 2, UH, VR), F32),
            pltpu.VMEM((GROUP, LOCAL * KERNELS * 2 * ROWS, TP), F32),
            pltpu.VMEM((GROUP, LOCAL, ROWS, TP), F32),
            pltpu.VMEM((ROWS, TP), F32),
            pltpu.VMEM((ROWS, TP), F32),
            pltpu.VMEM((ROWS, TP), F32),
            dma((10,)),
            dma((3,)),
            dma((3,)),
            dma((3,)),
            dma((3,)),
            dma((4,)),
            dma((2,)),
            dma((5,)),
            dma((3,)),
            dma((4,)),
            dma,
        ],
        compiler_params=pltpu.CompilerParams(collective_id=0, has_side_effects=True),
        name="window_gradient",
    )
    kernel_real, kernel_imag = (jnp.swapaxes(x, 1, 2) for x in (kernel_real, kernel_imag))
    return call(theta, target, kernel_real, kernel_imag, weights, thresholds, *(jnp.asarray(x) for x in constants))


def solution(mesh):
    in_specs = (
        P(("tile", "cond"), None),
        P("tile", None),
        P("cond", None, None, None),
        P("cond", None, None, None),
        P(),
        P("cond"),
    )
    out_specs = P(("tile", "cond"), None)
    body = functools.partial(shards, mesh.shape["tile"])
    return jax.shard_map(body, mesh=mesh, in_specs=in_specs, out_specs=out_specs, check_vma=False)
```

```python
import functools
import math

import jax
import jax.numpy as jnp
import ml_dtypes
import numpy as np
from jax import lax
from jax.experimental import pallas as pl
from jax.experimental.pallas import tpu as pltpu
from jax.sharding import PartitionSpec as P

TP = 512
HALO = 32
KSUP = 65
HALF = KSUP // 2
CONDS = 8
KERNELS = 2
SIZE = TP + 2 * HALO
ROWS = 128
GROUP = 4
LOCAL = CONDS // GROUP
UH = 40
UR = 2 * UH
VR = 128
FLAT = 2 * HALF
DEPTH = LOCAL * KERNELS
EDGE = DEPTH * UR
SPARE = HALF + 1

MASK_STEEP = 2.0
RESIST_STEEP = 4.0
BAND_WEIGHT = 1.0

BF = jnp.bfloat16
F32 = jnp.float32
MESH = pl.DeviceIdType.MESH


def split(x):
    hi = x.astype(BF)
    return hi, (x - hi.astype(F32)).astype(BF)


def np_split(x):
    hi = x.astype(ml_dtypes.bfloat16)
    return hi, (x - hi.astype(np.float64)).astype(ml_dtypes.bfloat16)


def waves(positions):
    phase = (np.asarray(positions)[:, None] * np.arange(HALF + 1)[None, :]) % SIZE
    angles = phase * (2.0 * math.pi / SIZE)
    return np.cos(angles), np.sin(angles)


def row_basis(positions):
    cos, sin = waves(positions)
    out = np.zeros((len(positions), UR))
    out[:, : HALF + 1] = cos
    out[:, UH + 1 : UH + HALF + 1] = sin[:, 1:]
    return out


def column_basis(positions):
    cos, sin = waves(positions)
    out = np.zeros((len(positions), VR))
    out[:, :HALF] = cos[:, 1:]
    out[:, HALF:FLAT] = sin[:, 1:]
    out[:, FLAT] = 1.0
    return out


def parity_rows():
    out = np.zeros((UR, UR))
    out[0, HALF] = 1.0
    for j in range(1, HALF + 1):
        out[j, HALF + j] = out[j, HALF - j] = out[UH + j, HALF + j] = 1.0
        out[UH + j, HALF - j] = -1.0
    return out


def parity_columns():
    out = np.zeros((2 * VR, 2 * VR))
    for ri in range(2):
        out[ri * VR + HALF, VR + ri] = 1.0
        for j in range(1, HALF + 1):
            even = ri * FLAT + j - 1
            out[ri * VR + HALF + j, even] = out[ri * VR + HALF - j, even] = 1.0
            out[ri * VR + HALF + j, even + HALF] = 1.0
            out[ri * VR + HALF - j, even + HALF] = -1.0
    return out


def tables():
    bf = ml_dtypes.bfloat16
    cols = column_basis(np.arange(TP) + HALO)
    hi, lo = np_split(cols)
    by = np.concatenate([hi, lo], axis=1)
    bt = np.concatenate([hi.T, hi.T, lo.T], axis=0)
    pack = []
    turned = []
    for c in range(GROUP):
        own = row_basis(np.arange(ROWS) + HALO + ROWS * c)
        near = np.zeros_like(own)
        if c == 0:
            near[:HALO] = row_basis(np.arange(HALO) + HALO + TP)
        if c == GROUP - 1:
            near[ROWS - HALO :] = row_basis(np.arange(HALO))
        row = []
        column = []
        for table in (own, near):
            thi, tlo = np_split(table)
            row += [thi, tlo, thi, np.zeros((ROWS, 256 - 3 * UR), bf)]
            column.append(np.concatenate([thi.T, thi.T], axis=1))
            column.append(np.concatenate([tlo.T, np.zeros((UR, ROWS), bf)], axis=1))
        pack.append(np.concatenate(row, axis=1))
        turned.append(np.concatenate(column, axis=0))
    pv = parity_columns().astype(bf)
    pv = np.concatenate([pv, pv], axis=0)
    pu = parity_rows().astype(bf)
    pu = np.concatenate([pu, pu], axis=1)
    return by, bt, np.stack(pack), np.stack(turned), pv, pu


def dot(a, b):
    return jnp.dot(a, b, preferred_element_type=F32)


def kernel(
    tiles,
    theta_h, target_h, kr_h, ki_h, weights_s, thresholds_s, by_h, bt_h, pack_h, turned_h, pv_h, pu_h,
    out_h,
    theta_v, target_v, raw_v, by, bt, pack, turned, pv, pu,
    stack, zbuf, coef, rown, rhalo, rin, rsum, aown, ain, anear, jbuf, amps, resists, band, wanted, grad_v,
    load_sem, zs_sem, zr_sem, rs_sem, rr_sem, hs_sem, hr_sem, as_sem, ar_sem, near_sem, out_sem,
):
    t = lax.axis_index("tile")
    c = lax.axis_index("cond")
    first = c == 0
    final = c == GROUP - 1
    has_prev = t > 0
    has_next = t < tiles - 1

    loads = []

    def load(src, dst):
        copy = pltpu.make_async_copy(src, dst, load_sem.at[len(loads)])
        copy.start()
        loads.append(copy)
        return copy

    load_kr = load(kr_h, raw_v.at[0])
    load_ki = load(ki_h, raw_v.at[1])
    load_pv = load(pv_h, pv)
    load_pu = load(pu_h, pu)
    load_theta = load(theta_h, theta_v)
    load_by = load(by_h, by)
    load_turned = load(turned_h.at[c], turned)
    load_pack = load(pack_h.at[c], pack)
    load_bt = load(bt_h, bt)
    load_target = load(target_h.at[pl.ds(pl.multiple_of(c * ROWS, ROWS), ROWS), :], target_v)

    def partner(mask):
        return (t, c ^ mask)

    barrier = pltpu.get_barrier_semaphore()

    def greet(device):
        pl.semaphore_signal(barrier, inc=1, device_id=device, device_id_type=MESH)

    mirror = ((t + tiles // 2) % tiles, c ^ 2)
    for mask in range(1, GROUP):
        greet(partner(mask))
    greet(mirror)
    for other in range(GROUP):
        @pl.when(has_next & (final | (other == 0)))
        def _(other=other):
            greet((t + 1, other))

        @pl.when(has_prev & (first | (other == GROUP - 1)))
        def _(other=other):
            greet((t - 1, other))

    lane = lax.broadcasted_iota(jnp.int32, (UH, VR), 1)
    row = lax.broadcasted_iota(jnp.int32, (UH, VR), 0)
    tall_lane = lax.broadcasted_iota(jnp.int32, (UR, VR), 1)
    diagonal = tall_lane == lax.broadcasted_iota(jnp.int32, (UR, VR), 0)
    sign_v = jnp.where((lane >= HALF) & (lane < FLAT), -1.0, 1.0).astype(F32)

    def swap(x):
        out = jnp.where(lane < HALF, pltpu.roll(x, VR - HALF, 1), pltpu.roll(x, HALF, 1))
        return jnp.where(lane < FLAT, out, 0.0)

    def packed(x):
        out = jnp.where(lane < FLAT, x[:UH], pltpu.roll(x[UH:], FLAT, 1))
        flat = jnp.sum(jnp.where(diagonal, x[:, FLAT : FLAT + 1], 0.0), axis=0, keepdims=True)
        return jnp.where(row == SPARE, flat, out)

    def unpacked(x):
        flat = jnp.sum(jnp.where(diagonal, x[SPARE : SPARE + 1], 0.0), axis=1, keepdims=True)
        keep = (lane < FLAT) & (row < SPARE)
        out = []
        for h, value in enumerate((x, pltpu.roll(x, FLAT, 1))):
            out.append(jnp.where(lane == FLAT, flat[h * UH : (h + 1) * UH], jnp.where(keep, value, 0.0)))
        return out

    def unpack_kernels(s):
        edge = zbuf[s, EDGE:, :]
        for n in range(DEPTH):
            p = zbuf[s, n * UR : (n + 1) * UR, :]
            p32, p64, p96 = (pltpu.roll(p, shift, 1) for shift in (HALF, 2 * HALF, 3 * HALF))
            first_half = tall_lane < HALF
            for at, (a, b) in enumerate(((p, p32), (p96, p), (p64, p96), (p32, p64))):
                value = jnp.where(first_half, a, b)
                if at % 2 == 0:
                    flat = pltpu.roll(edge, FLAT - (2 * n + at // 2), 1)
                    value = jnp.where(tall_lane == FLAT, flat, value)
                coef[s, n, at] = value

    stack[...] = jnp.zeros_like(stack)
    load_kr.wait()
    load_ki.wait()
    for ri in range(2):
        for l in range(LOCAL):
            for k in range(KERNELS):
                at = (l * KERNELS + k) * UR
                stack[at : at + KSUP, ri * VR : ri * VR + KSUP] = raw_v[ri, l, :, k, :]
    load_pv.wait()
    load_pu.wait()
    hi, lo = split(stack[...])
    folded = dot(jnp.concatenate([hi, lo], axis=1), pv[...])
    hi, lo = split(folded)
    edge = None
    for n in range(DEPTH):
        rhs = jnp.concatenate([hi[n * UR : (n + 1) * UR], lo[n * UR : (n + 1) * UR]], axis=0)
        value = dot(pu[...], rhs)
        zbuf[0, n * UR : (n + 1) * UR, :] = value[:, :VR]
        value = value[:, VR:]
        edge = value if n == 0 else edge + pltpu.roll(value, 2 * n, 1)
    zbuf[0, EDGE:, :] = edge
    for l in range(LOCAL):
        zbuf[0, EDGE + SPARE + l : EDGE + SPARE + l + 1, :] = jnp.full((1, VR), thresholds_s[l], F32)

    load_theta.wait()
    load_by.wait()
    load_turned.wait()
    mask_rows = jnp.tanh(MASK_STEEP * theta_v[...])
    hi, lo = split(mask_rows)
    wide = dot(jnp.concatenate([hi, lo], axis=0), by[...])
    column = wide[:ROWS, :VR] + wide[:ROWS, VR:] + wide[ROWS:, :VR]
    hi, lo = split(column)
    both = dot(turned[...], jnp.concatenate([hi, lo], axis=0))
    rown[...] = packed(both[:UR] + both[UR : 2 * UR])
    rhalo[...] = packed(both[2 * UR : 3 * UR] + both[3 * UR :])

    across_next = jnp.where(final, GROUP, 1) * has_next.astype(jnp.int32)
    across_prev = jnp.where(first, GROUP, 1) * has_prev.astype(jnp.int32)
    pl.semaphore_wait(barrier, GROUP + across_next + across_prev)

    def remote(src, dst, send, recv, device):
        return pltpu.make_async_remote_copy(
            src_ref=src, dst_ref=dst, send_sem=send, recv_sem=recv, device_id=device, device_id_type=MESH
        )

    def halo_next(other):
        return remote(rhalo, rin.at[3], hs_sem.at[other], hr_sem.at[0], (t + 1, other))

    def halo_prev(other):
        return remote(rhalo, rin.at[4], hs_sem.at[other], hr_sem.at[1], (t - 1, other))

    def part(mask):
        return remote(rown, rin.at[mask - 1], rs_sem.at[mask - 1], rr_sem.at[mask - 1], partner(mask))

    def kernels_to(mask):
        device = partner(1) if mask != 2 else mirror
        source = 2 if mask == 3 else 0
        return remote(zbuf.at[source], zbuf.at[mask], zs_sem.at[mask - 1], zr_sem.at[mask - 1], device)

    @pl.when(has_next & final)
    def _():
        for other in range(GROUP):
            halo_next(other).start()

    @pl.when(has_prev & first)
    def _():
        for other in range(GROUP):
            halo_prev(other).start()

    for mask in range(1, GROUP):
        part(mask).start()
    for mask in (2, 1):
        kernels_to(mask).start()

    @pl.when(jnp.logical_not(has_prev))
    def _():
        rin[3] = jnp.zeros((UH, VR), F32)

    @pl.when(jnp.logical_not(has_next))
    def _():
        rin[4] = jnp.zeros((UH, VR), F32)

    unpack_kernels(0)
    kernels_to(1).wait_recv()
    unpack_kernels(1)

    @pl.when(has_prev)
    def _():
        halo_next(0).wait_recv()

    @pl.when(has_next)
    def _():
        halo_prev(0).wait_recv()

    for mask in range(1, GROUP):
        part(mask).wait_recv()

    total = rown[...] + rin[0] + rin[1] + rin[2] + rin[3] + rin[4]
    halves = unpacked(total * (1.0 / (SIZE * SIZE)))
    for h in range(2):
        sign_u = 1.0 - 2.0 * h
        rsum[0, h] = halves[h]
        rsum[1, h] = sign_v * swap(halves[h])
        rsum[2, h] = sign_u * halves[1 - h]
        rsum[3, h] = (-sign_u) * sign_v * swap(halves[1 - h])

    def parts_of(s, n):
        return [coef[s, n, 2 * ri + v, u * UH : (u + 1) * UH, :] for ri in range(2) for u in range(2) for v in range(2)]

    load_pack.wait()
    load_bt.wait()

    def forward(s, carry):
        @pl.when(s == 2)
        def _():
            kernels_to(2).wait_recv()
            kernels_to(3).start()
            unpack_kernels(2)

        @pl.when(s == 3)
        def _():
            kernels_to(3).wait_recv()
            unpack_kernels(3)

        grids = []
        for n in range(DEPTH):
            ee_r, eo_r, oe_r, oo_r, ee_i, eo_i, oe_i, oo_i = parts_of(s, n)
            real = []
            imag = []
            for h in range(2):
                r0, r1, r2, r3 = (rsum[m, h] for m in range(4))
                real.append(ee_r * r0 + eo_i * r1 + oe_i * r2 + oo_r * r3)
                imag.append(ee_i * r0 - eo_r * r1 - oe_r * r2 + oo_i * r3)
            grid = jnp.concatenate([jnp.concatenate(real, axis=0), jnp.concatenate(imag, axis=0)], axis=1)
            hi, lo = split(grid)
            grids.append(jnp.concatenate([hi, hi, lo], axis=0))
        lhs = []
        for grid in grids:
            tall = dot(pack[:, : 3 * UR], grid)
            tall = jnp.concatenate([tall[:, :VR], tall[:, VR:]], axis=0)
            hi, lo = split(tall)
            lhs.append(jnp.concatenate([hi, lo, hi], axis=1))
        amp = dot(jnp.concatenate(lhs, axis=0), bt[...])
        amps[s] = amp
        total = None
        for l in range(LOCAL):
            intensity = None
            for part in range(4):
                piece = amp[(l * 4 + part) * ROWS : (l * 4 + part + 1) * ROWS]
                intensity = piece * piece if part == 0 else intensity + piece * piece
            level = zbuf[s, EDGE + SPARE + l : EDGE + SPARE + l + 1, 0:1]
            resist = jax.nn.sigmoid(RESIST_STEEP * (intensity - level))
            resists[s, l] = resist
            total = resist if l == 0 else total + resist

        @pl.when(s == 0)
        def _():
            band[...] = total

        @pl.when(s > 0)
        def _():
            band[...] += total

        return carry

    lax.fori_loop(0, GROUP, forward, 0)

    load_target.wait()
    weight_sum = weights_s[0]
    for n in range(1, CONDS):
        weight_sum = weight_sum + weights_s[n]
    weight_sum = jnp.full((8, TP), weight_sum, jnp.int32).astype(F32)
    jbuf[...] = jnp.zeros_like(jbuf)
    wanted[...] = target_v[...].astype(F32)
    band[...] = band[...] * (4.0 * RESIST_STEEP * BAND_WEIGHT / CONDS / CONDS)

    def backward(s, carry):
        drives = []
        for l in range(LOCAL):
            weight = jnp.full((8, TP), weights_s[(c ^ s) * LOCAL + l], jnp.int32).astype(F32) / weight_sum
            pull = (4.0 * RESIST_STEEP) * weight[0:1]
            resist = resists[s, l]
            slope = (pull + 4.0 * RESIST_STEEP * BAND_WEIGHT / CONDS) * resist - (pull * wanted[...] + band[...])
            field = slope * (resist - resist * resist)
            for part in range(4):
                at = (l * 4 + part) * ROWS
                drives.append(field * amps[s, at : at + ROWS])
        hi, lo = split(jnp.concatenate(drives, axis=0))
        wide = dot(jnp.concatenate([hi, lo], axis=0), by[...])
        half = 8 * ROWS
        drive = wide[:half, :VR] + wide[:half, VR:] + wide[half:, :VR]
        sums = [[None, None] for _ in range(4)]
        for n in range(DEPTH):
            pair = jnp.concatenate([drive[2 * n * ROWS : (2 * n + 1) * ROWS], drive[(2 * n + 1) * ROWS : (2 * n + 2) * ROWS]], axis=1)
            hi, lo = split(pair)
            back = dot(turned[: 2 * UR, :], jnp.concatenate([hi, lo], axis=0))
            back = back[:UR] + back[UR:]
            ee_r, eo_r, oe_r, oo_r, ee_i, eo_i, oe_i, oo_i = parts_of(s, n)
            for h in range(2):
                qr = back[h * UH : (h + 1) * UH, :VR]
                qi = back[h * UH : (h + 1) * UH, VR:]
                terms = (
                    ee_r * qr + ee_i * qi,
                    eo_i * qr - eo_r * qi,
                    oe_i * qr - oe_r * qi,
                    oo_r * qr + oo_i * qi,
                )
                for m, term in enumerate(terms):
                    sums[m][h] = term if n == 0 else sums[m][h] + term
        for m in range(4):
            for h in range(2):
                jbuf[m, h] += sums[m][h]
        return carry

    lax.fori_loop(0, GROUP, backward, 0)

    halves = []
    for h in range(2):
        sign_u = 1.0 - 2.0 * h
        halves.append(
            jbuf[0, h]
            + swap(sign_v * jbuf[1, h])
            - sign_u * jbuf[2, 1 - h]
            + swap(sign_u * sign_v * jbuf[3, 1 - h])
        )
    aown[...] = packed(jnp.concatenate(halves, axis=0))

    def adjoint_part(mask):
        return remote(aown, ain.at[mask - 1], as_sem.at[mask - 1], ar_sem.at[mask - 1], partner(mask))

    def adjoint_prev():
        return remote(aown, anear.at[c], as_sem.at[3], near_sem.at[c], (t - 1, GROUP - 1))

    def adjoint_next():
        return remote(aown, anear.at[c], as_sem.at[4], near_sem.at[c], (t + 1, 0))

    def adjoint_near(other):
        return remote(aown, anear.at[other], as_sem.at[3], near_sem.at[other], (t, c ^ 1))

    @pl.when(has_prev)
    def _():
        adjoint_prev().start()

    @pl.when(has_next)
    def _():
        adjoint_next().start()

    for mask in range(1, GROUP):
        adjoint_part(mask).start()

    near = (first & has_prev) | (final & has_next)

    @pl.when(jnp.logical_not(near))
    def _():
        anear[...] = jnp.zeros_like(anear)

    factor = grad_v
    factor[...] = (MASK_STEEP / (SIZE * SIZE)) * (1.0 - jnp.square(jnp.tanh(MASK_STEEP * theta_v[...])))

    for mask in range(1, GROUP):
        adjoint_part(mask).wait_recv()

    @pl.when(near)
    def _():
        for other in range(GROUP):
            adjoint_near(other).wait_recv()

    rows = []
    for value in (aown[...] + ain[0] + ain[1] + ain[2], anear[0] + anear[1] + anear[2] + anear[3]):
        hi, lo = split(jnp.concatenate(unpacked(value), axis=0))
        rows += [hi, hi, lo, jnp.zeros((256 - 3 * UR, VR), BF)]
    tall = dot(pack[...], jnp.concatenate(rows, axis=0))
    hi, lo = split(tall)
    grad_v[...] = dot(jnp.concatenate([hi, lo, hi], axis=1), bt[...]) * factor[...]
    out = pltpu.make_async_copy(grad_v, out_h, out_sem)
    out.start()

    @pl.when(has_next & final)
    def _():
        for other in range(GROUP):
            halo_next(other).wait_send()

    @pl.when(has_prev & first)
    def _():
        for other in range(GROUP):
            halo_prev(other).wait_send()

    for mask in range(1, GROUP):
        part(mask).wait_send()
        kernels_to(mask).wait_send()
        adjoint_part(mask).wait_send()

    @pl.when(has_prev)
    def _():
        adjoint_prev().wait_send()

    @pl.when(has_next)
    def _():
        adjoint_next().wait_send()

    out.wait()


def shards(tiles, theta, target, kernel_real, kernel_imag, weights, thresholds):
    constants = tables()
    anywhere = pl.BlockSpec(memory_space=pl.ANY)
    scalars = pl.BlockSpec(memory_space=pltpu.SMEM)
    dma = pltpu.SemaphoreType.DMA
    by, bt, pack, turned, pv, pu = constants
    call = pl.pallas_call(
        functools.partial(kernel, tiles),
        out_shape=jax.ShapeDtypeStruct((ROWS, TP), F32),
        in_specs=[anywhere] * 4 + [scalars] * 2 + [anywhere] * 6,
        out_specs=anywhere,
        scratch_shapes=[
            pltpu.VMEM((ROWS, TP), F32),
            pltpu.VMEM((ROWS, TP), jnp.int32),
            pltpu.VMEM((2, LOCAL, KSUP, KERNELS, KSUP), F32),
            pltpu.VMEM(by.shape, BF),
            pltpu.VMEM(bt.shape, BF),
            pltpu.VMEM(pack.shape[1:], BF),
            pltpu.VMEM(turned.shape[1:], BF),
            pltpu.VMEM(pv.shape, BF),
            pltpu.VMEM(pu.shape, BF),
            pltpu.VMEM((DEPTH * UR, 2 * VR), F32),
            pltpu.VMEM((GROUP, EDGE + UR, VR), F32),
            pltpu.VMEM((GROUP, DEPTH, 4, UR, VR), F32),
            pltpu.VMEM((UH, VR), F32),
            pltpu.VMEM((UH, VR), F32),
            pltpu.VMEM((5, UH, VR), F32),
            pltpu.VMEM((4, 2, UH, VR), F32),
            pltpu.VMEM((UH, VR), F32),
            pltpu.VMEM((3, UH, VR), F32),
            pltpu.VMEM((GROUP, UH, VR), F32),
            pltpu.VMEM((4, 2, UH, VR), F32),
            pltpu.VMEM((GROUP, LOCAL * KERNELS * 2 * ROWS, TP), F32),
            pltpu.VMEM((GROUP, LOCAL, ROWS, TP), F32),
            pltpu.VMEM((ROWS, TP), F32),
            pltpu.VMEM((ROWS, TP), F32),
            pltpu.VMEM((ROWS, TP), F32),
            dma((10,)),
            dma((3,)),
            dma((3,)),
            dma((3,)),
            dma((3,)),
            dma((4,)),
            dma((2,)),
            dma((5,)),
            dma((3,)),
            dma((4,)),
            dma,
        ],
        compiler_params=pltpu.CompilerParams(collective_id=0, has_side_effects=True),
        name="window_gradient",
    )
    kernel_real, kernel_imag = (jnp.swapaxes(x, 1, 2) for x in (kernel_real, kernel_imag))
    return call(theta, target, kernel_real, kernel_imag, weights, thresholds, *(jnp.asarray(x) for x in constants))


def solution(mesh):
    in_specs = (
        P(("tile", "cond"), None),
        P("tile", None),
        P("cond", None, None, None),
        P("cond", None, None, None),
        P(),
        P("cond"),
    )
    out_specs = P(("tile", "cond"), None)
    body = functools.partial(shards, mesh.shape["tile"])
    return jax.shard_map(body, mesh=mesh, in_specs=in_specs, out_specs=out_specs, check_vma=False)
```

```python
import functools
import math

import jax
import jax.numpy as jnp
import ml_dtypes
import numpy as np
from jax import lax
from jax.experimental import pallas as pl
from jax.experimental.pallas import tpu as pltpu
from jax.sharding import PartitionSpec as P

TP = 512
HALO = 32
KSUP = 65
HALF = KSUP // 2
CONDS = 8
KERNELS = 2
SIZE = TP + 2 * HALO
ROWS = 128
GROUP = 4
LOCAL = CONDS // GROUP
UH = 40
UR = 2 * UH
VR = 128
FLAT = 2 * HALF
DEPTH = LOCAL * KERNELS
EDGE = DEPTH * UR
SPARE = HALF + 1

MASK_STEEP = 2.0
RESIST_STEEP = 4.0
BAND_WEIGHT = 1.0

BF = jnp.bfloat16
F32 = jnp.float32
MESH = pl.DeviceIdType.MESH


def split(x):
    hi = x.astype(BF)
    return hi, (x - hi.astype(F32)).astype(BF)


def np_split(x):
    hi = x.astype(ml_dtypes.bfloat16)
    return hi, (x - hi.astype(np.float64)).astype(ml_dtypes.bfloat16)


def waves(positions):
    phase = (np.asarray(positions)[:, None] * np.arange(HALF + 1)[None, :]) % SIZE
    angles = phase * (2.0 * math.pi / SIZE)
    return np.cos(angles), np.sin(angles)


def row_basis(positions):
    cos, sin = waves(positions)
    out = np.zeros((len(positions), UR))
    out[:, : HALF + 1] = cos
    out[:, UH + 1 : UH + HALF + 1] = sin[:, 1:]
    return out


def column_basis(positions):
    cos, sin = waves(positions)
    out = np.zeros((len(positions), VR))
    out[:, :HALF] = cos[:, 1:]
    out[:, HALF:FLAT] = sin[:, 1:]
    out[:, FLAT] = 1.0
    return out


def parity_rows():
    out = np.zeros((UR, UR))
    out[0, HALF] = 1.0
    for j in range(1, HALF + 1):
        out[j, HALF + j] = out[j, HALF - j] = out[UH + j, HALF + j] = 1.0
        out[UH + j, HALF - j] = -1.0
    return out


def parity_columns():
    out = np.zeros((2 * VR, 2 * VR))
    for ri in range(2):
        out[ri * VR + HALF, VR + ri] = 1.0
        for j in range(1, HALF + 1):
            even = ri * FLAT + j - 1
            out[ri * VR + HALF + j, even] = out[ri * VR + HALF - j, even] = 1.0
            out[ri * VR + HALF + j, even + HALF] = 1.0
            out[ri * VR + HALF - j, even + HALF] = -1.0
    return out


def tables():
    bf = ml_dtypes.bfloat16
    cols = column_basis(np.arange(TP) + HALO)
    hi, lo = np_split(cols)
    by = np.concatenate([hi, lo], axis=1)
    bt = np.concatenate([hi.T, hi.T, lo.T], axis=0)
    pack = []
    turned = []
    for c in range(GROUP):
        own = row_basis(np.arange(ROWS) + HALO + ROWS * c)
        near = np.zeros_like(own)
        if c == 0:
            near[:HALO] = row_basis(np.arange(HALO) + HALO + TP)
        if c == GROUP - 1:
            near[ROWS - HALO :] = row_basis(np.arange(HALO))
        row = []
        column = []
        for table in (own, near):
            thi, tlo = np_split(table)
            row += [thi, tlo, thi, np.zeros((ROWS, 256 - 3 * UR), bf)]
            column.append(np.concatenate([thi.T, thi.T], axis=1))
            column.append(np.concatenate([tlo.T, np.zeros((UR, ROWS), bf)], axis=1))
        pack.append(np.concatenate(row, axis=1))
        turned.append(np.concatenate(column, axis=0))
    pv = parity_columns().astype(bf)
    pv = np.concatenate([pv, pv], axis=0)
    pu = parity_rows().astype(bf)
    pu = np.concatenate([pu, pu], axis=1)
    return by, bt, np.stack(pack), np.stack(turned), pv, pu


def dot(a, b):
    return jnp.dot(a, b, preferred_element_type=F32)


def kernel(
    tiles,
    theta_h, target_h, kr_h, ki_h, weights_h, thresholds_h, by_h, bt_h, pack_h, turned_h, pv_h, pu_h,
    out_v,
    weights_s, thresholds_s, theta_v, target_v, raw_v, by, bt, pack, turned, pv, pu,
    stack, zbuf, coef, rown, rhalo, rin, rsum, aown, ain, anear, jbuf, amps, resists, band, wanted, factor,
    load_sem, zs_sem, zr_sem, rs_sem, rr_sem, hs_sem, hr_sem, as_sem, ar_sem, near_sem,
):
    t = lax.axis_index("tile")
    c = lax.axis_index("cond")
    first = c == 0
    final = c == GROUP - 1
    has_prev = t > 0
    has_next = t < tiles - 1

    loads = []

    def load(src, dst):
        copy = pltpu.make_async_copy(src, dst, load_sem.at[len(loads)])
        copy.start()
        loads.append(copy)
        return copy

    load_kr = load(kr_h, raw_v.at[0])
    load_ki = load(ki_h, raw_v.at[1])
    load_pv = load(pv_h, pv)
    load_pu = load(pu_h, pu)
    load_thresholds = load(thresholds_h, thresholds_s)
    load_theta = load(theta_h, theta_v)
    load_by = load(by_h, by)
    load_turned = load(turned_h.at[c], turned)
    load_pack = load(pack_h.at[c], pack)
    load_bt = load(bt_h, bt)
    load_weights = load(weights_h, weights_s)
    load_target = load(target_h.at[pl.ds(pl.multiple_of(c * ROWS, ROWS), ROWS), :], target_v)

    def partner(mask):
        return (t, c ^ mask)

    barrier = pltpu.get_barrier_semaphore()

    def greet(device):
        pl.semaphore_signal(barrier, inc=1, device_id=device, device_id_type=MESH)

    mirror = ((t + tiles // 2) % tiles, c ^ 2)
    for mask in range(1, GROUP):
        greet(partner(mask))
    greet(mirror)

    @pl.when(has_next)
    def _():
        greet((t + 1, 0))

    @pl.when(has_prev)
    def _():
        greet((t - 1, GROUP - 1))

    lane = lax.broadcasted_iota(jnp.int32, (UH, VR), 1)
    row = lax.broadcasted_iota(jnp.int32, (UH, VR), 0)
    tall_lane = lax.broadcasted_iota(jnp.int32, (UR, VR), 1)
    diagonal = tall_lane == lax.broadcasted_iota(jnp.int32, (UR, VR), 0)
    sign_v = jnp.where((lane >= HALF) & (lane < FLAT), -1.0, 1.0).astype(F32)

    def swap(x):
        out = jnp.where(lane < HALF, pltpu.roll(x, VR - HALF, 1), pltpu.roll(x, HALF, 1))
        return jnp.where(lane < FLAT, out, 0.0)

    def packed(x):
        out = jnp.where(lane < FLAT, x[:UH], pltpu.roll(x[UH:], FLAT, 1))
        flat = jnp.sum(jnp.where(diagonal, x[:, FLAT : FLAT + 1], 0.0), axis=0, keepdims=True)
        return jnp.where(row == SPARE, flat, out)

    def unpacked(x):
        flat = jnp.sum(jnp.where(diagonal, x[SPARE : SPARE + 1], 0.0), axis=1, keepdims=True)
        keep = (lane < FLAT) & (row < SPARE)
        out = []
        for h, value in enumerate((x, pltpu.roll(x, FLAT, 1))):
            out.append(jnp.where(lane == FLAT, flat[h * UH : (h + 1) * UH], jnp.where(keep, value, 0.0)))
        return out

    def unpack_kernels(s):
        edge = zbuf[s, EDGE:, :]
        for n in range(DEPTH):
            p = zbuf[s, n * UR : (n + 1) * UR, :]
            p32, p64, p96 = (pltpu.roll(p, shift, 1) for shift in (HALF, 2 * HALF, 3 * HALF))
            first_half = tall_lane < HALF
            for at, (a, b) in enumerate(((p, p32), (p96, p), (p64, p96), (p32, p64))):
                value = jnp.where(first_half, a, b)
                if at % 2 == 0:
                    flat = pltpu.roll(edge, FLAT - (2 * n + at // 2), 1)
                    value = jnp.where(tall_lane == FLAT, flat, value)
                coef[s, n, at] = value

    stack[...] = jnp.zeros_like(stack)
    load_kr.wait()
    load_ki.wait()
    for ri in range(2):
        for l in range(LOCAL):
            for k in range(KERNELS):
                at = (l * KERNELS + k) * UR
                stack[at : at + KSUP, ri * VR : ri * VR + KSUP] = raw_v[ri, l, :, k, :]
    load_pv.wait()
    load_pu.wait()
    hi, lo = split(stack[...])
    folded = dot(jnp.concatenate([hi, lo], axis=1), pv[...])
    hi, lo = split(folded)
    edge = None
    for n in range(DEPTH):
        rhs = jnp.concatenate([hi[n * UR : (n + 1) * UR], lo[n * UR : (n + 1) * UR]], axis=0)
        value = dot(pu[...], rhs)
        zbuf[0, n * UR : (n + 1) * UR, :] = value[:, :VR]
        value = value[:, VR:]
        edge = value if n == 0 else edge + pltpu.roll(value, 2 * n, 1)
    zbuf[0, EDGE:, :] = edge
    load_thresholds.wait()
    for l in range(LOCAL):
        zbuf[0, EDGE + SPARE + l : EDGE + SPARE + l + 1, :] = jnp.full((1, VR), thresholds_s[l], F32)

    load_theta.wait()
    load_by.wait()
    load_turned.wait()
    mask_rows = jnp.tanh(MASK_STEEP * theta_v[...])
    hi, lo = split(mask_rows)
    wide = dot(jnp.concatenate([hi, lo], axis=0), by[...])
    column = wide[:ROWS, :VR] + wide[:ROWS, VR:] + wide[ROWS:, :VR]
    hi, lo = split(column)
    both = dot(turned[...], jnp.concatenate([hi, lo], axis=0))
    rown[...] = packed(both[:UR] + both[UR : 2 * UR])
    rhalo[...] = packed(both[2 * UR : 3 * UR] + both[3 * UR :])

    edge_of = (has_next & final) | (has_prev & first)
    pl.semaphore_wait(barrier, jnp.where(edge_of, 2 * GROUP, GROUP))

    def remote(src, dst, send, recv, device):
        return pltpu.make_async_remote_copy(
            src_ref=src, dst_ref=dst, send_sem=send, recv_sem=recv, device_id=device, device_id_type=MESH
        )

    def halo_next(other):
        return remote(rhalo, rin.at[3], hs_sem.at[other], hr_sem.at[0], (t + 1, other))

    def halo_prev(other):
        return remote(rhalo, rin.at[4], hs_sem.at[other], hr_sem.at[1], (t - 1, other))

    def part(mask):
        return remote(rown, rin.at[mask - 1], rs_sem.at[mask - 1], rr_sem.at[mask - 1], partner(mask))

    def kernels_to(mask):
        device = partner(1) if mask != 2 else mirror
        source = 2 if mask == 3 else 0
        return remote(zbuf.at[source], zbuf.at[mask], zs_sem.at[mask - 1], zr_sem.at[mask - 1], device)

    @pl.when(has_next & final)
    def _():
        for other in range(GROUP):
            halo_next(other).start()

    @pl.when(has_prev & first)
    def _():
        for other in range(GROUP):
            halo_prev(other).start()

    for mask in range(1, GROUP):
        part(mask).start()
    for mask in (2, 1):
        kernels_to(mask).start()

    @pl.when(jnp.logical_not(has_prev))
    def _():
        rin[3] = jnp.zeros((UH, VR), F32)

    @pl.when(jnp.logical_not(has_next))
    def _():
        rin[4] = jnp.zeros((UH, VR), F32)

    unpack_kernels(0)
    kernels_to(1).wait_recv()
    unpack_kernels(1)

    @pl.when(has_prev)
    def _():
        halo_next(0).wait_recv()

    @pl.when(has_next)
    def _():
        halo_prev(0).wait_recv()

    for mask in range(1, GROUP):
        part(mask).wait_recv()

    total = rown[...] + rin[0] + rin[1] + rin[2] + rin[3] + rin[4]
    halves = unpacked(total * (1.0 / (SIZE * SIZE)))
    for h in range(2):
        sign_u = 1.0 - 2.0 * h
        rsum[0, h] = halves[h]
        rsum[1, h] = sign_v * swap(halves[h])
        rsum[2, h] = sign_u * halves[1 - h]
        rsum[3, h] = (-sign_u) * sign_v * swap(halves[1 - h])

    def parts_of(s, n):
        return [coef[s, n, 2 * ri + v, u * UH : (u + 1) * UH, :] for ri in range(2) for u in range(2) for v in range(2)]

    load_pack.wait()
    load_bt.wait()

    def forward(s, carry):
        @pl.when(s == 2)
        def _():
            kernels_to(2).wait_recv()
            kernels_to(3).start()
            unpack_kernels(2)

        @pl.when(s == 3)
        def _():
            kernels_to(3).wait_recv()
            unpack_kernels(3)

        grids = []
        for n in range(DEPTH):
            ee_r, eo_r, oe_r, oo_r, ee_i, eo_i, oe_i, oo_i = parts_of(s, n)
            real = []
            imag = []
            for h in range(2):
                r0, r1, r2, r3 = (rsum[m, h] for m in range(4))
                real.append(ee_r * r0 + eo_i * r1 + oe_i * r2 + oo_r * r3)
                imag.append(ee_i * r0 - eo_r * r1 - oe_r * r2 + oo_i * r3)
            grid = jnp.concatenate([jnp.concatenate(real, axis=0), jnp.concatenate(imag, axis=0)], axis=1)
            hi, lo = split(grid)
            grids.append(jnp.concatenate([hi, hi, lo], axis=0))
        lhs = []
        for grid in grids:
            tall = dot(pack[:, : 3 * UR], grid)
            tall = jnp.concatenate([tall[:, :VR], tall[:, VR:]], axis=0)
            hi, lo = split(tall)
            lhs.append(jnp.concatenate([hi, lo, hi], axis=1))
        amp = dot(jnp.concatenate(lhs, axis=0), bt[...])
        amps[s] = amp
        total = None
        for l in range(LOCAL):
            intensity = None
            for part in range(4):
                piece = amp[(l * 4 + part) * ROWS : (l * 4 + part + 1) * ROWS]
                intensity = piece * piece if part == 0 else intensity + piece * piece
            level = zbuf[s, EDGE + SPARE + l : EDGE + SPARE + l + 1, 0:1]
            resist = jax.nn.sigmoid(RESIST_STEEP * (intensity - level))
            resists[s, l] = resist
            total = resist if l == 0 else total + resist

        @pl.when(s == 0)
        def _():
            band[...] = total

        @pl.when(s > 0)
        def _():
            band[...] += total

        return carry

    lax.fori_loop(0, GROUP, forward, 0)

    load_target.wait()
    load_weights.wait()
    weight_sum = weights_s[0]
    for n in range(1, CONDS):
        weight_sum = weight_sum + weights_s[n]
    weight_sum = jnp.full((8, TP), weight_sum, jnp.int32).astype(F32)
    jbuf[...] = jnp.zeros_like(jbuf)
    wanted[...] = target_v[...].astype(F32)
    band[...] = band[...] * (4.0 * RESIST_STEEP * BAND_WEIGHT / CONDS / CONDS)

    def backward(s, carry):
        drives = []
        for l in range(LOCAL):
            weight = jnp.full((8, TP), weights_s[(c ^ s) * LOCAL + l], jnp.int32).astype(F32) / weight_sum
            pull = (4.0 * RESIST_STEEP) * weight[0:1]
            resist = resists[s, l]
            slope = (pull + 4.0 * RESIST_STEEP * BAND_WEIGHT / CONDS) * resist - (pull * wanted[...] + band[...])
            field = slope * (resist - resist * resist)
            for part in range(4):
                at = (l * 4 + part) * ROWS
                drives.append(field * amps[s, at : at + ROWS])
        hi, lo = split(jnp.concatenate(drives, axis=0))
        wide = dot(jnp.concatenate([hi, lo], axis=0), by[...])
        half = 8 * ROWS
        drive = wide[:half, :VR] + wide[:half, VR:] + wide[half:, :VR]
        sums = [[None, None] for _ in range(4)]
        for n in range(DEPTH):
            pair = jnp.concatenate([drive[2 * n * ROWS : (2 * n + 1) * ROWS], drive[(2 * n + 1) * ROWS : (2 * n + 2) * ROWS]], axis=1)
            hi, lo = split(pair)
            back = dot(turned[: 2 * UR, :], jnp.concatenate([hi, lo], axis=0))
            back = back[:UR] + back[UR:]
            ee_r, eo_r, oe_r, oo_r, ee_i, eo_i, oe_i, oo_i = parts_of(s, n)
            for h in range(2):
                qr = back[h * UH : (h + 1) * UH, :VR]
                qi = back[h * UH : (h + 1) * UH, VR:]
                terms = (
                    ee_r * qr + ee_i * qi,
                    eo_i * qr - eo_r * qi,
                    oe_i * qr - oe_r * qi,
                    oo_r * qr + oo_i * qi,
                )
                for m, term in enumerate(terms):
                    sums[m][h] = term if n == 0 else sums[m][h] + term
        for m in range(4):
            for h in range(2):
                jbuf[m, h] += sums[m][h]
        return carry

    lax.fori_loop(0, GROUP, backward, 0)

    halves = []
    for h in range(2):
        sign_u = 1.0 - 2.0 * h
        halves.append(
            jbuf[0, h]
            + swap(sign_v * jbuf[1, h])
            - sign_u * jbuf[2, 1 - h]
            + swap(sign_u * sign_v * jbuf[3, 1 - h])
        )
    aown[...] = packed(jnp.concatenate(halves, axis=0))

    def adjoint_part(mask):
        return remote(aown, ain.at[mask - 1], as_sem.at[mask - 1], ar_sem.at[mask - 1], partner(mask))

    def adjoint_prev():
        return remote(aown, anear.at[c], as_sem.at[3], near_sem.at[c], (t - 1, GROUP - 1))

    def adjoint_next():
        return remote(aown, anear.at[c], as_sem.at[4], near_sem.at[c], (t + 1, 0))

    def adjoint_near(other):
        return remote(aown, anear.at[other], as_sem.at[3], near_sem.at[other], (t, c ^ 1))

    @pl.when(has_prev)
    def _():
        adjoint_prev().start()

    @pl.when(has_next)
    def _():
        adjoint_next().start()

    for mask in range(1, GROUP):
        adjoint_part(mask).start()

    near = (first & has_prev) | (final & has_next)

    @pl.when(jnp.logical_not(near))
    def _():
        anear[...] = jnp.zeros_like(anear)

    factor[...] = (MASK_STEEP / (SIZE * SIZE)) * (1.0 - jnp.square(jnp.tanh(MASK_STEEP * theta_v[...])))

    for mask in range(1, GROUP):
        adjoint_part(mask).wait_recv()

    @pl.when(near)
    def _():
        for other in range(GROUP):
            adjoint_near(other).wait_recv()

    rows = []
    for value in (aown[...] + ain[0] + ain[1] + ain[2], anear[0] + anear[1] + anear[2] + anear[3]):
        hi, lo = split(jnp.concatenate(unpacked(value), axis=0))
        rows += [hi, hi, lo, jnp.zeros((256 - 3 * UR, VR), BF)]
    tall = dot(pack[...], jnp.concatenate(rows, axis=0))
    hi, lo = split(tall)
    out_v[...] = dot(jnp.concatenate([hi, lo, hi], axis=1), bt[...]) * factor[...]

    @pl.when(has_next & final)
    def _():
        for other in range(GROUP):
            halo_next(other).wait_send()

    @pl.when(has_prev & first)
    def _():
        for other in range(GROUP):
            halo_prev(other).wait_send()

    for mask in range(1, GROUP):
        part(mask).wait_send()
        kernels_to(mask).wait_send()
        adjoint_part(mask).wait_send()

    @pl.when(has_prev)
    def _():
        adjoint_prev().wait_send()

    @pl.when(has_next)
    def _():
        adjoint_next().wait_send()


def shards(tiles, theta, target, kernel_real, kernel_imag, weights, thresholds):
    constants = tables()
    dma = pltpu.SemaphoreType.DMA
    by, bt, pack, turned, pv, pu = constants
    call = pl.pallas_call(
        functools.partial(kernel, tiles),
        out_shape=jax.ShapeDtypeStruct((ROWS, TP), F32),
        in_specs=[pl.BlockSpec(memory_space=pltpu.HBM)] * 12,
        out_specs=pl.BlockSpec(memory_space=pltpu.VMEM),
        scratch_shapes=[
            pltpu.SMEM((CONDS,), jnp.int32),
            pltpu.SMEM((LOCAL,), F32),
            pltpu.VMEM((ROWS, TP), F32),
            pltpu.VMEM((ROWS, TP), jnp.int32),
            pltpu.VMEM((2, LOCAL, KSUP, KERNELS, KSUP), F32),
            pltpu.VMEM(by.shape, BF),
            pltpu.VMEM(bt.shape, BF),
            pltpu.VMEM(pack.shape[1:], BF),
            pltpu.VMEM(turned.shape[1:], BF),
            pltpu.VMEM(pv.shape, BF),
            pltpu.VMEM(pu.shape, BF),
            pltpu.VMEM((DEPTH * UR, 2 * VR), F32),
            pltpu.VMEM((GROUP, EDGE + UR, VR), F32),
            pltpu.VMEM((GROUP, DEPTH, 4, UR, VR), F32),
            pltpu.VMEM((UH, VR), F32),
            pltpu.VMEM((UH, VR), F32),
            pltpu.VMEM((5, UH, VR), F32),
            pltpu.VMEM((4, 2, UH, VR), F32),
            pltpu.VMEM((UH, VR), F32),
            pltpu.VMEM((3, UH, VR), F32),
            pltpu.VMEM((GROUP, UH, VR), F32),
            pltpu.VMEM((4, 2, UH, VR), F32),
            pltpu.VMEM((GROUP, LOCAL * KERNELS * 2 * ROWS, TP), F32),
            pltpu.VMEM((GROUP, LOCAL, ROWS, TP), F32),
            pltpu.VMEM((ROWS, TP), F32),
            pltpu.VMEM((ROWS, TP), F32),
            pltpu.VMEM((ROWS, TP), F32),
            dma((12,)),
            dma((3,)),
            dma((3,)),
            dma((3,)),
            dma((3,)),
            dma((4,)),
            dma((2,)),
            dma((5,)),
            dma((3,)),
            dma((4,)),
        ],
        compiler_params=pltpu.CompilerParams(collective_id=0, has_side_effects=True, vmem_limit_bytes=32 * 1024 * 1024),
        name="window_gradient",
    )
    kernel_real, kernel_imag = (jnp.swapaxes(x, 1, 2) for x in (kernel_real, kernel_imag))
    arrays = (theta, target, kernel_real, kernel_imag, weights, thresholds, *(jnp.asarray(x) for x in constants))
    return call(*(pltpu.with_memory_space_constraint(x, pltpu.HBM) for x in arrays))


def solution(mesh):
    in_specs = (
        P(("tile", "cond"), None),
        P("tile", None),
        P("cond", None, None, None),
        P("cond", None, None, None),
        P(),
        P("cond"),
    )
    out_specs = P(("tile", "cond"), None)
    body = functools.partial(shards, mesh.shape["tile"])
    return jax.shard_map(body, mesh=mesh, in_specs=in_specs, out_specs=out_specs, check_vma=False)
```

```python
import functools
import math

import jax
import jax.numpy as jnp
import ml_dtypes
import numpy as np
from jax import lax
from jax.experimental import pallas as pl
from jax.experimental.pallas import tpu as pltpu
from jax.sharding import PartitionSpec as P

TP = 512
HALO = 32
KSUP = 65
HALF = KSUP // 2
CONDS = 8
KERNELS = 2
SIZE = TP + 2 * HALO
ROWS = 128
GROUP = 4
LOCAL = CONDS // GROUP
UH = 40
UR = 2 * UH
VR = 128
FLAT = 2 * HALF
DEPTH = LOCAL * KERNELS
EDGE = DEPTH * UR
GRID = 128
SPARE = HALF + 1

MASK_STEEP = 2.0
RESIST_STEEP = 4.0
BAND_WEIGHT = 1.0

BF = jnp.bfloat16
F32 = jnp.float32
MESH = pl.DeviceIdType.MESH


def split(x):
    hi = x.astype(BF)
    return hi, (x - hi.astype(F32)).astype(BF)


def np_split(x):
    hi = x.astype(ml_dtypes.bfloat16)
    return hi, (x - hi.astype(np.float64)).astype(ml_dtypes.bfloat16)


def waves(positions):
    phase = np.fmod(np.asarray(positions, np.float64)[:, None] * np.arange(HALF + 1)[None, :], SIZE)
    angles = phase * (2.0 * math.pi / SIZE)
    return np.cos(angles), np.sin(angles)


def row_basis(positions):
    cos, sin = waves(positions)
    out = np.zeros((len(positions), UR))
    out[:, : HALF + 1] = cos
    out[:, UH + 1 : UH + HALF + 1] = sin[:, 1:]
    return out


def column_basis(positions):
    cos, sin = waves(positions)
    out = np.zeros((len(positions), VR))
    out[:, :HALF] = cos[:, 1:]
    out[:, HALF:FLAT] = sin[:, 1:]
    out[:, FLAT] = 1.0
    return out


def parity_rows():
    out = np.zeros((UR, UR))
    out[0, HALF] = 1.0
    for j in range(1, HALF + 1):
        out[j, HALF + j] = out[j, HALF - j] = out[UH + j, HALF + j] = 1.0
        out[UH + j, HALF - j] = -1.0
    return out


def parity_columns():
    out = np.zeros((2 * VR, 2 * VR))
    for ri in range(2):
        out[ri * VR + HALF, VR + ri] = 1.0
        for j in range(1, HALF + 1):
            even = ri * FLAT + j - 1
            out[ri * VR + HALF + j, even] = out[ri * VR + HALF - j, even] = 1.0
            out[ri * VR + HALF + j, even + HALF] = 1.0
            out[ri * VR + HALF - j, even + HALF] = -1.0
    return out


def tables():
    bf = ml_dtypes.bfloat16
    cols = column_basis(np.arange(TP) + HALO)
    hi, lo = np_split(cols)
    by = np.concatenate([hi, lo], axis=1)
    bt = np.concatenate([hi.T, hi.T, lo.T], axis=0)
    places = column_basis(np.arange(GRID) * (SIZE / GRID))
    hi, lo = np_split(places.T)
    zero = np.zeros_like(hi)
    sample = np.concatenate([np.concatenate([hi, lo], axis=1), np.concatenate([hi, zero], axis=1)], axis=0)
    hi, lo = np_split(places)
    gather = np.concatenate([np.concatenate([hi, lo], axis=1), np.concatenate([hi, zero], axis=1)], axis=0)
    phase = (np.arange(TP) + HALO) * (2.0 * math.pi / SIZE)
    place = np.arange(GRID) * (2.0 * math.pi / GRID)
    spread = np.ones((GRID, TP))
    for f in range(1, GRID // 2):
        spread += 2.0 * np.cos(f * (phase[None, :] - place[:, None]))
    spread += np.cos(GRID // 2 * place)[:, None] * np.cos(GRID // 2 * phase)[None, :]
    spread /= GRID
    last = np.sin(GRID // 2 * phase)
    hi, lo = np_split(spread)
    last_hi, last_lo = np_split(last)
    rest = np.zeros((VR, TP), bf)
    rest[HALF - 1], rest[FLAT - 1], rest[FLAT + HALF - 1] = last_hi, last_lo, last_hi
    fine = np.concatenate([hi, hi, lo, rest], axis=0)
    coarse = np.concatenate([hi.T, lo.T], axis=1)
    half_last = np.broadcast_to(0.5 * last, (8, TP)).astype(np.float32)
    pack = []
    turned = []
    for c in range(GROUP):
        own = row_basis(np.arange(ROWS) + HALO + ROWS * c)
        near = np.zeros_like(own)
        if c == 0:
            near[:HALO] = row_basis(np.arange(HALO) + HALO + TP)
        if c == GROUP - 1:
            near[ROWS - HALO :] = row_basis(np.arange(HALO))
        row = []
        column = []
        for table in (own, near):
            thi, tlo = np_split(table)
            row += [thi, tlo, thi, np.zeros((ROWS, 256 - 3 * UR), bf)]
            column.append(np.concatenate([thi.T, thi.T], axis=1))
            column.append(np.concatenate([tlo.T, np.zeros((UR, ROWS), bf)], axis=1))
        pack.append(np.concatenate(row, axis=1))
        turned.append(np.concatenate(column, axis=0))
    pv = parity_columns().astype(bf)
    pv = np.concatenate([pv, pv], axis=0)
    pu = parity_rows().astype(bf)
    pu = np.concatenate([pu, pu], axis=1)
    return by, bt, np.stack(pack), np.stack(turned), pv, pu, sample, gather, fine, coarse, half_last


def dot(a, b):
    return jnp.dot(a, b, preferred_element_type=F32)


def kernel(
    tiles,
    theta_h, target_h, kr_h, ki_h, weights_h, thresholds_h, by_h, bt_h, pack_h, turned_h, pv_h, pu_h,
    sample_h, gather_h, fine_h, coarse_h, half_last_h,
    out_v,
    weights_s, thresholds_s, theta_v, target_v, raw_v, by, bt, pack, turned, pv, pu,
    sample, gather, fine, coarse, half_last, stack, zbuf, coef, rown, rhalo, rin, rsum, aown, ain, anear, jbuf, amps, crossed, resists, band, wanted, factor,
    load_sem, zs_sem, zr_sem, rs_sem, rr_sem, hs_sem, hr_sem, as_sem, ar_sem, near_sem,
):
    t = lax.axis_index("tile")
    c = lax.axis_index("cond")
    first = c == 0
    final = c == GROUP - 1
    has_prev = t > 0
    has_next = t < tiles - 1

    loads = []

    def load(src, dst):
        copy = pltpu.make_async_copy(src, dst, load_sem.at[len(loads)])
        copy.start()
        loads.append(copy)
        return copy

    load_kr = load(kr_h, raw_v.at[0])
    load_ki = load(ki_h, raw_v.at[1])
    load_pv = load(pv_h, pv)
    load_pu = load(pu_h, pu)
    load_thresholds = load(thresholds_h, thresholds_s)
    load_theta = load(theta_h, theta_v)
    load_by = load(by_h, by)
    load_turned = load(turned_h.at[c], turned)
    load_pack = load(pack_h.at[c], pack)
    load_sample = load(sample_h, sample)
    load_fine = load(fine_h, fine)
    load_coarse = load(coarse_h, coarse)
    load_half = load(half_last_h, half_last)
    load_gather = load(gather_h, gather)
    load_bt = load(bt_h, bt)
    load_weights = load(weights_h, weights_s)
    load_target = load(target_h.at[pl.ds(pl.multiple_of(c * ROWS, ROWS), ROWS), :], target_v)

    def partner(mask):
        return (t, c ^ mask)

    barrier = pltpu.get_barrier_semaphore()

    def greet(device):
        pl.semaphore_signal(barrier, inc=1, device_id=device, device_id_type=MESH)

    mirror = ((t + tiles // 2) % tiles, c ^ 2)
    for mask in range(1, GROUP):
        greet(partner(mask))
    greet(mirror)

    @pl.when(has_next)
    def _():
        greet((t + 1, 0))

    @pl.when(has_prev)
    def _():
        greet((t - 1, GROUP - 1))

    lane = lax.broadcasted_iota(jnp.int32, (UH, VR), 1)
    row = lax.broadcasted_iota(jnp.int32, (UH, VR), 0)
    tall_lane = lax.broadcasted_iota(jnp.int32, (UR, VR), 1)
    diagonal = tall_lane == lax.broadcasted_iota(jnp.int32, (UR, VR), 0)
    sign_v = jnp.where((lane >= HALF) & (lane < FLAT), -1.0, 1.0).astype(F32)

    def swap(x):
        out = jnp.where(lane < HALF, pltpu.roll(x, VR - HALF, 1), pltpu.roll(x, HALF, 1))
        return jnp.where(lane < FLAT, out, 0.0)

    def packed(x):
        out = jnp.where(lane < FLAT, x[:UH], pltpu.roll(x[UH:], FLAT, 1))
        flat = jnp.sum(jnp.where(diagonal, x[:, FLAT : FLAT + 1], 0.0), axis=0, keepdims=True)
        return jnp.where(row == SPARE, flat, out)

    def unpacked(x):
        flat = jnp.sum(jnp.where(diagonal, x[SPARE : SPARE + 1], 0.0), axis=1, keepdims=True)
        keep = (lane < FLAT) & (row < SPARE)
        out = []
        for h, value in enumerate((x, pltpu.roll(x, FLAT, 1))):
            out.append(jnp.where(lane == FLAT, flat[h * UH : (h + 1) * UH], jnp.where(keep, value, 0.0)))
        return out

    def unpack_kernels(s):
        edge = zbuf[s, EDGE:, :]
        for n in range(DEPTH):
            p = zbuf[s, n * UR : (n + 1) * UR, :]
            p32, p64, p96 = (pltpu.roll(p, shift, 1) for shift in (HALF, 2 * HALF, 3 * HALF))
            first_half = tall_lane < HALF
            for at, (a, b) in enumerate(((p, p32), (p96, p), (p64, p96), (p32, p64))):
                value = jnp.where(first_half, a, b)
                if at % 2 == 0:
                    flat = pltpu.roll(edge, FLAT - (2 * n + at // 2), 1)
                    value = jnp.where(tall_lane == FLAT, flat, value)
                coef[s, n, at] = value

    stack[...] = jnp.zeros_like(stack)
    load_kr.wait()
    load_ki.wait()
    for ri in range(2):
        for l in range(LOCAL):
            for k in range(KERNELS):
                at = (l * KERNELS + k) * UR
                stack[at : at + KSUP, ri * VR : ri * VR + KSUP] = raw_v[ri, l, :, k, :]
    load_pv.wait()
    load_pu.wait()
    hi, lo = split(stack[...])
    folded = dot(jnp.concatenate([hi, lo], axis=1), pv[...])
    hi, lo = split(folded)
    edge = None
    for n in range(DEPTH):
        rhs = jnp.concatenate([hi[n * UR : (n + 1) * UR], lo[n * UR : (n + 1) * UR]], axis=0)
        value = dot(pu[...], rhs)
        zbuf[0, n * UR : (n + 1) * UR, :] = value[:, :VR]
        value = value[:, VR:]
        edge = value if n == 0 else edge + pltpu.roll(value, 2 * n, 1)
    zbuf[0, EDGE:, :] = edge
    load_thresholds.wait()
    for l in range(LOCAL):
        zbuf[0, EDGE + SPARE + l : EDGE + SPARE + l + 1, :] = jnp.full((1, VR), thresholds_s[l], F32)

    load_theta.wait()
    load_by.wait()
    load_turned.wait()
    mask_rows = jnp.tanh(MASK_STEEP * theta_v[...])
    hi, lo = split(mask_rows)
    wide = dot(jnp.concatenate([hi, lo], axis=0), by[...])
    column = wide[:ROWS, :VR] + wide[:ROWS, VR:] + wide[ROWS:, :VR]
    hi, lo = split(column)
    both = dot(turned[...], jnp.concatenate([hi, lo], axis=0))
    rown[...] = packed(both[:UR] + both[UR : 2 * UR])
    rhalo[...] = packed(both[2 * UR : 3 * UR] + both[3 * UR :])

    edge_of = (has_next & final) | (has_prev & first)
    pl.semaphore_wait(barrier, jnp.where(edge_of, 2 * GROUP, GROUP))

    def remote(src, dst, send, recv, device):
        return pltpu.make_async_remote_copy(
            src_ref=src, dst_ref=dst, send_sem=send, recv_sem=recv, device_id=device, device_id_type=MESH
        )

    def halo_next(other):
        return remote(rhalo, rin.at[3], hs_sem.at[other], hr_sem.at[0], (t + 1, other))

    def halo_prev(other):
        return remote(rhalo, rin.at[4], hs_sem.at[other], hr_sem.at[1], (t - 1, other))

    def part(mask):
        return remote(rown, rin.at[mask - 1], rs_sem.at[mask - 1], rr_sem.at[mask - 1], partner(mask))

    def kernels_to(mask):
        device = partner(1) if mask != 2 else mirror
        source = 2 if mask == 3 else 0
        return remote(zbuf.at[source], zbuf.at[mask], zs_sem.at[mask - 1], zr_sem.at[mask - 1], device)

    @pl.when(has_next & final)
    def _():
        for other in range(GROUP):
            halo_next(other).start()

    @pl.when(has_prev & first)
    def _():
        for other in range(GROUP):
            halo_prev(other).start()

    for mask in range(1, GROUP):
        part(mask).start()
    for mask in (2, 1):
        kernels_to(mask).start()

    @pl.when(jnp.logical_not(has_prev))
    def _():
        rin[3] = jnp.zeros((UH, VR), F32)

    @pl.when(jnp.logical_not(has_next))
    def _():
        rin[4] = jnp.zeros((UH, VR), F32)

    unpack_kernels(0)
    kernels_to(1).wait_recv()
    unpack_kernels(1)

    @pl.when(has_prev)
    def _():
        halo_next(0).wait_recv()

    @pl.when(has_next)
    def _():
        halo_prev(0).wait_recv()

    for mask in range(1, GROUP):
        part(mask).wait_recv()

    total = rown[...] + rin[0] + rin[1] + rin[2] + rin[3] + rin[4]
    halves = unpacked(total * (1.0 / (SIZE * SIZE)))
    for h in range(2):
        sign_u = 1.0 - 2.0 * h
        rsum[0, h] = halves[h]
        rsum[1, h] = sign_v * swap(halves[h])
        rsum[2, h] = sign_u * halves[1 - h]
        rsum[3, h] = (-sign_u) * sign_v * swap(halves[1 - h])

    def parts_of(s, n):
        return [coef[s, n, 2 * ri + v, u * UH : (u + 1) * UH, :] for ri in range(2) for u in range(2) for v in range(2)]

    load_pack.wait()
    load_sample.wait()
    load_fine.wait()
    pair_lane = lax.broadcasted_iota(jnp.int32, (2 * ROWS, VR), 1)
    block_lane = lax.broadcasted_iota(jnp.int32, (ROWS, VR), 1)

    def forward(s, carry):
        @pl.when(s == 2)
        def _():
            kernels_to(2).wait_recv()
            kernels_to(3).start()
            unpack_kernels(2)

        @pl.when(s == 3)
        def _():
            kernels_to(3).wait_recv()
            unpack_kernels(3)

        grids = []
        for n in range(DEPTH):
            ee_r, eo_r, oe_r, oo_r, ee_i, eo_i, oe_i, oo_i = parts_of(s, n)
            real = []
            imag = []
            for h in range(2):
                r0, r1, r2, r3 = (rsum[m, h] for m in range(4))
                real.append(ee_r * r0 + eo_i * r1 + oe_i * r2 + oo_r * r3)
                imag.append(ee_i * r0 - eo_r * r1 - oe_r * r2 + oo_i * r3)
            grid = jnp.concatenate([jnp.concatenate(real, axis=0), jnp.concatenate(imag, axis=0)], axis=1)
            hi, lo = split(grid)
            grids.append(jnp.concatenate([hi, hi, lo], axis=0))
        lhs = []
        cross = []
        for n, grid in enumerate(grids):
            tall = dot(pack[:, : 3 * UR], grid)
            tall = jnp.concatenate([tall[:, :VR], tall[:, VR:]], axis=0)
            other = jnp.where(pair_lane == HALF - 1, pltpu.roll(tall, VR - HALF, 1), 0.0)
            other = jnp.where(pair_lane == FLAT - 1, pltpu.roll(tall, HALF, 1), other)
            crossed[s, n * 2 * ROWS : (n + 1) * 2 * ROWS, :] = other
            other = tall * other
            cross.append(other[:ROWS] + other[ROWS:])
            hi, lo = split(tall)
            lhs.append(jnp.concatenate([hi, lo], axis=1))
        amp = dot(jnp.concatenate(lhs, axis=0), sample[...])
        amp = amp[:, :GRID] + amp[:, GRID:]
        amps[s] = amp
        lhs = []
        for l in range(LOCAL):
            sampled = None
            for part in range(4):
                piece = amp[(l * 4 + part) * ROWS : (l * 4 + part + 1) * ROWS]
                sampled = piece * piece if part == 0 else sampled + piece * piece
            hi, lo = split(sampled)
            edge = cross[2 * l] + cross[2 * l + 1]
            near = edge.astype(BF).astype(F32)
            edge = jnp.where(block_lane < FLAT, near, pltpu.roll(edge - near, FLAT, 1)).astype(BF)
            lhs.append(jnp.concatenate([hi, lo, hi, edge], axis=1))
        intensities = dot(jnp.concatenate(lhs, axis=0), fine[...])
        total = None
        for l in range(LOCAL):
            intensity = intensities[l * ROWS : (l + 1) * ROWS]
            level = zbuf[s, EDGE + SPARE + l : EDGE + SPARE + l + 1, 0:1]
            resist = jax.nn.sigmoid(RESIST_STEEP * (intensity - level))
            resists[s, l] = resist
            total = resist if l == 0 else total + resist

        @pl.when(s == 0)
        def _():
            band[...] = total

        @pl.when(s > 0)
        def _():
            band[...] += total

        return carry

    lax.fori_loop(0, GROUP, forward, 0)

    load_target.wait()
    load_weights.wait()
    weight_sum = weights_s[0]
    for n in range(1, CONDS):
        weight_sum = weight_sum + weights_s[n]
    weight_sum = jnp.full((8, TP), weight_sum, jnp.int32).astype(F32)
    jbuf[...] = jnp.zeros_like(jbuf)
    wanted[...] = target_v[...].astype(F32)
    band[...] = band[...] * (4.0 * RESIST_STEEP * BAND_WEIGHT / CONDS / CONDS)

    load_coarse.wait()
    load_half.wait()
    load_gather.wait()

    def backward(s, carry):
        fields = []
        lasts = []
        for l in range(LOCAL):
            weight = jnp.full((8, TP), weights_s[(c ^ s) * LOCAL + l], jnp.int32).astype(F32) / weight_sum
            pull = (4.0 * RESIST_STEEP) * weight[0:1]
            resist = resists[s, l]
            slope = (pull + 4.0 * RESIST_STEEP * BAND_WEIGHT / CONDS) * resist - (pull * wanted[...] + band[...])
            field = slope * (resist - resist * resist)
            lasts.append(jnp.sum(field * half_last[0:1, :], axis=1, keepdims=True))
            fields.append(field)
        hi, lo = split(jnp.concatenate(fields, axis=0))
        wide = dot(jnp.concatenate([hi, lo], axis=0), coarse[...])
        half = LOCAL * ROWS
        push = wide[:half, :GRID] + wide[:half, GRID:] + wide[half:, :GRID]
        drives = []
        for l in range(LOCAL):
            for part in range(4):
                at = (l * 4 + part) * ROWS
                drives.append(push[l * ROWS : (l + 1) * ROWS] * amps[s, at : at + ROWS])
        hi, lo = split(jnp.concatenate(drives, axis=0))
        drive = dot(jnp.concatenate([hi, lo], axis=1), gather[...])
        drive = drive[:, :VR] + drive[:, VR:]
        drives = []
        for part in range(8):
            at = part * ROWS
            drives.append(drive[at : at + ROWS] + lasts[part // 4] * crossed[s, at : at + ROWS])
        sums = [[None, None] for _ in range(4)]
        for n in range(DEPTH):
            pair = jnp.concatenate(drives[2 * n : 2 * n + 2], axis=1)
            hi, lo = split(pair)
            back = dot(turned[: 2 * UR, :], jnp.concatenate([hi, lo], axis=0))
            back = back[:UR] + back[UR:]
            ee_r, eo_r, oe_r, oo_r, ee_i, eo_i, oe_i, oo_i = parts_of(s, n)
            for h in range(2):
                qr = back[h * UH : (h + 1) * UH, :VR]
                qi = back[h * UH : (h + 1) * UH, VR:]
                terms = (
                    ee_r * qr + ee_i * qi,
                    eo_i * qr - eo_r * qi,
                    oe_i * qr - oe_r * qi,
                    oo_r * qr + oo_i * qi,
                )
                for m, term in enumerate(terms):
                    sums[m][h] = term if n == 0 else sums[m][h] + term
        for m in range(4):
            for h in range(2):
                jbuf[m, h] += sums[m][h]
        return carry

    lax.fori_loop(0, GROUP, backward, 0)

    halves = []
    for h in range(2):
        sign_u = 1.0 - 2.0 * h
        halves.append(
            jbuf[0, h]
            + swap(sign_v * jbuf[1, h])
            - sign_u * jbuf[2, 1 - h]
            + swap(sign_u * sign_v * jbuf[3, 1 - h])
        )
    aown[...] = packed(jnp.concatenate(halves, axis=0))

    def adjoint_part(mask):
        return remote(aown, ain.at[mask - 1], as_sem.at[mask - 1], ar_sem.at[mask - 1], partner(mask))

    def adjoint_prev():
        return remote(aown, anear.at[c], as_sem.at[3], near_sem.at[c], (t - 1, GROUP - 1))

    def adjoint_next():
        return remote(aown, anear.at[c], as_sem.at[4], near_sem.at[c], (t + 1, 0))

    def adjoint_near(other):
        return remote(aown, anear.at[other], as_sem.at[3], near_sem.at[other], (t, c ^ 1))

    @pl.when(has_prev)
    def _():
        adjoint_prev().start()

    @pl.when(has_next)
    def _():
        adjoint_next().start()

    for mask in range(1, GROUP):
        adjoint_part(mask).start()

    near = (first & has_prev) | (final & has_next)

    @pl.when(jnp.logical_not(near))
    def _():
        anear[...] = jnp.zeros_like(anear)

    factor[...] = (MASK_STEEP / (SIZE * SIZE)) * (1.0 - jnp.square(jnp.tanh(MASK_STEEP * theta_v[...])))

    for mask in range(1, GROUP):
        adjoint_part(mask).wait_recv()

    @pl.when(near)
    def _():
        for other in range(GROUP):
            adjoint_near(other).wait_recv()

    load_bt.wait()
    rows = []
    for value in (aown[...] + ain[0] + ain[1] + ain[2], anear[0] + anear[1] + anear[2] + anear[3]):
        hi, lo = split(jnp.concatenate(unpacked(value), axis=0))
        rows += [hi, hi, lo, jnp.zeros((256 - 3 * UR, VR), BF)]
    tall = dot(pack[...], jnp.concatenate(rows, axis=0))
    hi, lo = split(tall)
    out_v[...] = dot(jnp.concatenate([hi, lo, hi], axis=1), bt[...]) * factor[...]

    @pl.when(has_next & final)
    def _():
        for other in range(GROUP):
            halo_next(other).wait_send()

    @pl.when(has_prev & first)
    def _():
        for other in range(GROUP):
            halo_prev(other).wait_send()

    for mask in range(1, GROUP):
        part(mask).wait_send()
        kernels_to(mask).wait_send()
        adjoint_part(mask).wait_send()

    @pl.when(has_prev)
    def _():
        adjoint_prev().wait_send()

    @pl.when(has_next)
    def _():
        adjoint_next().wait_send()


def shards(tiles, theta, target, kernel_real, kernel_imag, weights, thresholds):
    constants = tables()
    dma = pltpu.SemaphoreType.DMA
    by, bt, pack, turned, pv, pu, sample, gather, fine, coarse, half_last = constants
    call = pl.pallas_call(
        functools.partial(kernel, tiles),
        out_shape=jax.ShapeDtypeStruct((ROWS, TP), F32),
        in_specs=[pl.BlockSpec(memory_space=pltpu.HBM)] * 17,
        out_specs=pl.BlockSpec(memory_space=pltpu.VMEM),
        scratch_shapes=[
            pltpu.SMEM((CONDS,), jnp.int32),
            pltpu.SMEM((LOCAL,), F32),
            pltpu.VMEM((ROWS, TP), F32),
            pltpu.VMEM((ROWS, TP), jnp.int32),
            pltpu.VMEM((2, LOCAL, KSUP, KERNELS, KSUP), F32),
            pltpu.VMEM(by.shape, BF),
            pltpu.VMEM(bt.shape, BF),
            pltpu.VMEM(pack.shape[1:], BF),
            pltpu.VMEM(turned.shape[1:], BF),
            pltpu.VMEM(pv.shape, BF),
            pltpu.VMEM(pu.shape, BF),
            pltpu.VMEM(sample.shape, BF),
            pltpu.VMEM(gather.shape, BF),
            pltpu.VMEM(fine.shape, BF),
            pltpu.VMEM(coarse.shape, BF),
            pltpu.VMEM(half_last.shape, F32),
            pltpu.VMEM((DEPTH * UR, 2 * VR), F32),
            pltpu.VMEM((GROUP, EDGE + UR, VR), F32),
            pltpu.VMEM((GROUP, DEPTH, 4, UR, VR), F32),
            pltpu.VMEM((UH, VR), F32),
            pltpu.VMEM((UH, VR), F32),
            pltpu.VMEM((5, UH, VR), F32),
            pltpu.VMEM((4, 2, UH, VR), F32),
            pltpu.VMEM((UH, VR), F32),
            pltpu.VMEM((3, UH, VR), F32),
            pltpu.VMEM((GROUP, UH, VR), F32),
            pltpu.VMEM((4, 2, UH, VR), F32),
            pltpu.VMEM((GROUP, LOCAL * KERNELS * 2 * ROWS, GRID), F32),
            pltpu.VMEM((GROUP, LOCAL * KERNELS * 2 * ROWS, VR), F32),
            pltpu.VMEM((GROUP, LOCAL, ROWS, TP), F32),
            pltpu.VMEM((ROWS, TP), F32),
            pltpu.VMEM((ROWS, TP), F32),
            pltpu.VMEM((ROWS, TP), F32),
            dma((17,)),
            dma((3,)),
            dma((3,)),
            dma((3,)),
            dma((3,)),
            dma((4,)),
            dma((2,)),
            dma((5,)),
            dma((3,)),
            dma((4,)),
        ],
        compiler_params=pltpu.CompilerParams(collective_id=0, has_side_effects=True, vmem_limit_bytes=32 * 1024 * 1024),
        name="window_gradient",
    )
    kernel_real, kernel_imag = (jnp.swapaxes(x, 1, 2) for x in (kernel_real, kernel_imag))
    arrays = (theta, target, kernel_real, kernel_imag, weights, thresholds, *(jnp.asarray(x) for x in constants))
    return call(*(pltpu.with_memory_space_constraint(x, pltpu.HBM) for x in arrays))


def solution(mesh):
    in_specs = (
        P(("tile", "cond"), None),
        P("tile", None),
        P("cond", None, None, None),
        P("cond", None, None, None),
        P(),
        P("cond"),
    )
    out_specs = P(("tile", "cond"), None)
    body = functools.partial(shards, mesh.shape["tile"])
    return jax.shard_map(body, mesh=mesh, in_specs=in_specs, out_specs=out_specs, check_vma=False)
```

```python
import functools
import math

import jax
import jax.numpy as jnp
import ml_dtypes
import numpy as np
from jax import lax
from jax.experimental import pallas as pl
from jax.experimental.pallas import tpu as pltpu
from jax.sharding import PartitionSpec as P

TP = 512
HALO = 32
KSUP = 65
HALF = KSUP // 2
CONDS = 8
KERNELS = 2
SIZE = TP + 2 * HALO
ROWS = 128
GROUP = 4
LOCAL = CONDS // GROUP
UH = 40
UR = 2 * UH
VR = 128
FLAT = 2 * HALF
DEPTH = LOCAL * KERNELS
EDGE = DEPTH * UR
GRID = 128
SPARE = HALF + 1

MASK_STEEP = 2.0
RESIST_STEEP = 4.0
BAND_WEIGHT = 1.0

BF = jnp.bfloat16
F32 = jnp.float32
MESH = pl.DeviceIdType.MESH


def split(x):
    hi = x.astype(BF)
    return hi, (x - hi.astype(F32)).astype(BF)


def np_split(x):
    hi = x.astype(ml_dtypes.bfloat16)
    return hi, (x - hi.astype(np.float64)).astype(ml_dtypes.bfloat16)


def waves(positions):
    phase = np.fmod(np.asarray(positions, np.float64)[:, None] * np.arange(HALF + 1)[None, :], SIZE)
    angles = phase * (2.0 * math.pi / SIZE)
    return np.cos(angles), np.sin(angles)


def row_basis(positions):
    cos, sin = waves(positions)
    out = np.zeros((len(positions), UR))
    out[:, : HALF + 1] = cos
    out[:, UH + 1 : UH + HALF + 1] = sin[:, 1:]
    return out


def column_basis(positions):
    cos, sin = waves(positions)
    out = np.zeros((len(positions), VR))
    out[:, :HALF] = cos[:, 1:]
    out[:, HALF:FLAT] = sin[:, 1:]
    out[:, FLAT] = 1.0
    return out


def parity_rows():
    out = np.zeros((UR, UR))
    out[0, HALF] = 1.0
    for j in range(1, HALF + 1):
        out[j, HALF + j] = out[j, HALF - j] = out[UH + j, HALF + j] = 1.0
        out[UH + j, HALF - j] = -1.0
    return out


def parity_columns():
    out = np.zeros((2 * VR, 2 * VR))
    for ri in range(2):
        out[ri * VR + HALF, VR + ri] = 1.0
        for j in range(1, HALF + 1):
            even = ri * FLAT + j - 1
            out[ri * VR + HALF + j, even] = out[ri * VR + HALF - j, even] = 1.0
            out[ri * VR + HALF + j, even + HALF] = 1.0
            out[ri * VR + HALF - j, even + HALF] = -1.0
    return out


def tables():
    bf = ml_dtypes.bfloat16
    cols = column_basis(np.arange(TP) + HALO)
    hi, lo = np_split(cols)
    by = np.concatenate([hi, lo], axis=1)
    bt = np.concatenate([hi.T, lo.T], axis=0)
    places = column_basis(np.arange(GRID) * (SIZE / GRID))
    hi, lo = np_split(places.T)
    zero = np.zeros_like(hi)
    sample = np.concatenate([np.concatenate([hi, lo], axis=1), np.concatenate([hi, zero], axis=1)], axis=0)
    hi, lo = np_split(places)
    gather = np.concatenate([np.concatenate([hi, lo], axis=1), np.concatenate([hi, zero], axis=1)], axis=0)
    phase = (np.arange(TP) + HALO) * (2.0 * math.pi / SIZE)
    place = np.arange(GRID) * (2.0 * math.pi / GRID)
    spread = np.ones((GRID, TP))
    for f in range(1, GRID // 2):
        spread += 2.0 * np.cos(f * (phase[None, :] - place[:, None]))
    spread += np.cos(GRID // 2 * place)[:, None] * np.cos(GRID // 2 * phase)[None, :]
    spread /= GRID
    last = np.sin(GRID // 2 * phase)
    hi, lo = np_split(spread)
    last_hi, last_lo = np_split(last)
    rest = np.zeros((VR, TP), bf)
    rest[HALF - 1], rest[FLAT - 1], rest[FLAT + HALF - 1] = last_hi, last_lo, last_hi
    fine = np.concatenate([hi, lo, rest], axis=0)
    coarse = np.concatenate([hi.T, lo.T], axis=1)
    half_last = np.broadcast_to(0.5 * last, (8, TP)).astype(np.float32)
    pack = []
    turned = []
    for c in range(GROUP):
        own = row_basis(np.arange(ROWS) + HALO + ROWS * c)
        near = np.zeros_like(own)
        if c == 0:
            near[:HALO] = row_basis(np.arange(HALO) + HALO + TP)
        if c == GROUP - 1:
            near[ROWS - HALO :] = row_basis(np.arange(HALO))
        row = []
        column = []
        for table in (own, near):
            thi, tlo = np_split(table)
            row += [thi, tlo, thi, np.zeros((ROWS, 256 - 3 * UR), bf)]
            column.append(np.concatenate([thi.T, thi.T], axis=1))
            column.append(np.concatenate([tlo.T, np.zeros((UR, ROWS), bf)], axis=1))
        pack.append(np.concatenate(row, axis=1))
        turned.append(np.concatenate(column, axis=0))
    pv = parity_columns().astype(bf)
    pu = parity_rows().astype(bf)
    pu = np.concatenate([pu, pu], axis=1)
    return by, bt, np.stack(pack), np.stack(turned), pv, pu, sample, gather, fine, coarse, half_last


def dot(a, b):
    return jnp.dot(a, b, preferred_element_type=F32)


def kernel(
    tiles,
    theta_h, target_h, kr_h, ki_h, weights_h, thresholds_h, by_h, bt_h, pack_h, turned_h, pv_h, pu_h,
    sample_h, gather_h, fine_h, coarse_h, half_last_h,
    out_v,
    weights_s, thresholds_s, theta_v, target_v, raw_v, by, bt, pack, turned, pv, pu,
    sample, gather, fine, coarse, half_last, stack, zbuf, coef, rown, rhalo, rin, rsum, aown, ain, anear, jbuf, amps, crossed, rows_v, edge_v, push_v, last_v, resists, band, wanted, factor,
    load_sem, zs_sem, zr_sem, rs_sem, rr_sem, hs_sem, hr_sem, as_sem, ar_sem, near_sem,
):
    t = lax.axis_index("tile")
    c = lax.axis_index("cond")
    first = c == 0
    final = c == GROUP - 1
    has_prev = t > 0
    has_next = t < tiles - 1

    loads = []

    def load(src, dst):
        copy = pltpu.make_async_copy(src, dst, load_sem.at[len(loads)])
        copy.start()
        loads.append(copy)
        return copy

    load_kr = load(kr_h, raw_v.at[0])
    load_ki = load(ki_h, raw_v.at[1])
    load_pv = [load(pv_h, pv.at[pl.ds(at, 2 * VR), :]) for at in (0, 2 * VR)]
    load_pu = load(pu_h, pu)
    load_thresholds = load(thresholds_h, thresholds_s)
    load_theta = load(theta_h, theta_v)
    load_by = load(by_h, by)
    load_turned = load(turned_h.at[c], turned)
    load_pack = load(pack_h.at[c], pack)
    load_sample = load(sample_h, sample)
    load_fine = [
        load(fine_h.at[pl.ds(0, GRID), :], fine.at[pl.ds(0, GRID), :]),
        load(fine_h, fine.at[pl.ds(GRID, 3 * GRID), :]),
    ]
    load_coarse = load(coarse_h, coarse)
    load_half = load(half_last_h, half_last)
    load_gather = load(gather_h, gather)
    load_bt = [
        load(bt_h.at[pl.ds(0, VR), :], bt.at[pl.ds(0, VR), :]),
        load(bt_h, bt.at[pl.ds(VR, 2 * VR), :]),
    ]
    load_weights = load(weights_h, weights_s)
    load_target = load(target_h.at[pl.ds(pl.multiple_of(c * ROWS, ROWS), ROWS), :], target_v)

    def partner(mask):
        return (t, c ^ mask)

    barrier = pltpu.get_barrier_semaphore()

    def greet(device):
        pl.semaphore_signal(barrier, inc=1, device_id=device, device_id_type=MESH)

    mirror = ((t + tiles // 2) % tiles, c ^ 2)
    for mask in range(1, GROUP):
        greet(partner(mask))
    greet(mirror)

    @pl.when(has_next)
    def _():
        greet((t + 1, 0))

    @pl.when(has_prev)
    def _():
        greet((t - 1, GROUP - 1))

    lane = lax.broadcasted_iota(jnp.int32, (UH, VR), 1)
    row = lax.broadcasted_iota(jnp.int32, (UH, VR), 0)
    tall_lane = lax.broadcasted_iota(jnp.int32, (UR, VR), 1)
    diagonal = tall_lane == lax.broadcasted_iota(jnp.int32, (UR, VR), 0)
    sign_v = jnp.where((lane >= HALF) & (lane < FLAT), -1.0, 1.0).astype(F32)

    def swap(x):
        out = jnp.where(lane < HALF, pltpu.roll(x, VR - HALF, 1), pltpu.roll(x, HALF, 1))
        return jnp.where(lane < FLAT, out, 0.0)

    def packed(x):
        out = jnp.where(lane < FLAT, x[:UH], pltpu.roll(x[UH:], FLAT, 1))
        flat = jnp.sum(jnp.where(diagonal, x[:, FLAT : FLAT + 1], 0.0), axis=0, keepdims=True)
        return jnp.where(row == SPARE, flat, out)

    def unpacked(x):
        flat = jnp.sum(jnp.where(diagonal, x[SPARE : SPARE + 1], 0.0), axis=1, keepdims=True)
        keep = (lane < FLAT) & (row < SPARE)
        out = []
        for h, value in enumerate((x, pltpu.roll(x, FLAT, 1))):
            out.append(jnp.where(lane == FLAT, flat[h * UH : (h + 1) * UH], jnp.where(keep, value, 0.0)))
        return out

    def unpack_kernels(s):
        edge = zbuf[s, EDGE:, :]
        for n in range(DEPTH):
            p = zbuf[s, n * UR : (n + 1) * UR, :]
            p32, p64, p96 = (pltpu.roll(p, shift, 1) for shift in (HALF, 2 * HALF, 3 * HALF))
            first_half = tall_lane < HALF
            for at, (a, b) in enumerate(((p, p32), (p96, p), (p64, p96), (p32, p64))):
                value = jnp.where(first_half, a, b)
                if at % 2 == 0:
                    flat = pltpu.roll(edge, FLAT - (2 * n + at // 2), 1)
                    value = jnp.where(tall_lane == FLAT, flat, value)
                coef[s, n, at] = value

    stack[...] = jnp.zeros_like(stack)
    load_kr.wait()
    load_ki.wait()
    for ri in range(2):
        for l in range(LOCAL):
            for k in range(KERNELS):
                at = (l * KERNELS + k) * UR
                stack[at : at + KSUP, ri * VR : ri * VR + KSUP] = raw_v[ri, l, :, k, :]
    for copy in load_pv:
        copy.wait()
    load_pu.wait()
    hi, lo = split(stack[...])
    folded = dot(jnp.concatenate([hi, lo], axis=1), pv[...])
    hi, lo = split(folded)
    edge = None
    for n in range(DEPTH):
        rhs = jnp.concatenate([hi[n * UR : (n + 1) * UR], lo[n * UR : (n + 1) * UR]], axis=0)
        value = dot(pu[...], rhs)
        zbuf[0, n * UR : (n + 1) * UR, :] = value[:, :VR]
        value = value[:, VR:]
        edge = value if n == 0 else edge + pltpu.roll(value, 2 * n, 1)
    zbuf[0, EDGE:, :] = edge
    load_thresholds.wait()
    for l in range(LOCAL):
        zbuf[0, EDGE + SPARE + l : EDGE + SPARE + l + 1, :] = jnp.full((1, VR), thresholds_s[l], F32)

    load_theta.wait()
    load_by.wait()
    load_turned.wait()
    mask_rows = jnp.tanh(MASK_STEEP * theta_v[...])
    hi, lo = split(mask_rows)
    wide = dot(jnp.concatenate([hi, lo], axis=0), by[...])
    column = wide[:ROWS, :VR] + wide[:ROWS, VR:] + wide[ROWS:, :VR]
    hi, lo = split(column)
    both = dot(turned[...], jnp.concatenate([hi, lo], axis=0))
    rown[...] = packed(both[:UR] + both[UR : 2 * UR])
    rhalo[...] = packed(both[2 * UR : 3 * UR] + both[3 * UR :])

    edge_of = (has_next & final) | (has_prev & first)
    pl.semaphore_wait(barrier, jnp.where(edge_of, 2 * GROUP, GROUP))

    def remote(src, dst, send, recv, device):
        return pltpu.make_async_remote_copy(
            src_ref=src, dst_ref=dst, send_sem=send, recv_sem=recv, device_id=device, device_id_type=MESH
        )

    def halo_next(other):
        return remote(rhalo, rin.at[3], hs_sem.at[other], hr_sem.at[0], (t + 1, other))

    def halo_prev(other):
        return remote(rhalo, rin.at[4], hs_sem.at[other], hr_sem.at[1], (t - 1, other))

    def part(mask):
        return remote(rown, rin.at[mask - 1], rs_sem.at[mask - 1], rr_sem.at[mask - 1], partner(mask))

    def kernels_to(mask):
        device = partner(1) if mask != 2 else mirror
        source = 2 if mask == 3 else 0
        return remote(zbuf.at[source], zbuf.at[mask], zs_sem.at[mask - 1], zr_sem.at[mask - 1], device)

    @pl.when(has_next & final)
    def _():
        for other in range(GROUP):
            halo_next(other).start()

    @pl.when(has_prev & first)
    def _():
        for other in range(GROUP):
            halo_prev(other).start()

    for mask in range(1, GROUP):
        part(mask).start()
    for mask in (2, 1):
        kernels_to(mask).start()

    @pl.when(jnp.logical_not(has_prev))
    def _():
        rin[3] = jnp.zeros((UH, VR), F32)

    @pl.when(jnp.logical_not(has_next))
    def _():
        rin[4] = jnp.zeros((UH, VR), F32)

    unpack_kernels(0)
    kernels_to(1).wait_recv()
    unpack_kernels(1)

    @pl.when(has_prev)
    def _():
        halo_next(0).wait_recv()

    @pl.when(has_next)
    def _():
        halo_prev(0).wait_recv()

    for mask in range(1, GROUP):
        part(mask).wait_recv()

    total = rown[...] + rin[0] + rin[1] + rin[2] + rin[3] + rin[4]
    halves = unpacked(total * (1.0 / (SIZE * SIZE)))
    for h in range(2):
        sign_u = 1.0 - 2.0 * h
        rsum[0, h] = halves[h]
        rsum[1, h] = sign_v * swap(halves[h])
        rsum[2, h] = sign_u * halves[1 - h]
        rsum[3, h] = (-sign_u) * sign_v * swap(halves[1 - h])

    def parts_of(s, n):
        return [coef[s, n, 2 * ri + v, u * UH : (u + 1) * UH, :] for ri in range(2) for u in range(2) for v in range(2)]

    load_pack.wait()
    load_sample.wait()
    for copy in load_fine:
        copy.wait()
    pair_lane = lax.broadcasted_iota(jnp.int32, (2 * ROWS, VR), 1)
    block_lane = lax.broadcasted_iota(jnp.int32, (ROWS, VR), 1)

    def grids_and_rows(s):
        cross = []
        grids = []
        for n in range(DEPTH):
            ee_r, eo_r, oe_r, oo_r, ee_i, eo_i, oe_i, oo_i = parts_of(s, n)
            real = []
            imag = []
            for h in range(2):
                r0, r1, r2, r3 = (rsum[m, h] for m in range(4))
                real.append(ee_r * r0 + eo_i * r1 + oe_i * r2 + oo_r * r3)
                imag.append(ee_i * r0 - eo_r * r1 - oe_r * r2 + oo_i * r3)
            grid = jnp.concatenate([jnp.concatenate(real, axis=0), jnp.concatenate(imag, axis=0)], axis=1)
            hi, lo = split(grid)
            grids.append(jnp.concatenate([hi, hi, lo], axis=0))
        for n, grid in enumerate(grids):
            tall = dot(pack[:, : 3 * UR], grid)
            tall = jnp.concatenate([tall[:, :VR], tall[:, VR:]], axis=0)
            other = jnp.where(pair_lane == HALF - 1, pltpu.roll(tall, VR - HALF, 1), 0.0)
            other = jnp.where(pair_lane == FLAT - 1, pltpu.roll(tall, HALF, 1), other)
            at = n * 2 * ROWS
            crossed[s, at : at + 2 * ROWS, :] = other
            other = tall * other
            cross.append(other[:ROWS] + other[ROWS:])
            hi, lo = split(tall)
            rows_v[s % 2, at : at + 2 * ROWS, :VR] = hi
            rows_v[s % 2, at : at + 2 * ROWS, VR:] = lo
        for l in range(LOCAL):
            edge = cross[2 * l] + cross[2 * l + 1]
            near = edge.astype(BF).astype(F32)
            edge = jnp.where(block_lane < FLAT, near, pltpu.roll(edge - near, FLAT, 1)).astype(BF)
            edge_v[s % 2, l * ROWS : (l + 1) * ROWS, :] = edge

    def resist_of(s):
        amp = dot(rows_v[s % 2], sample[...])
        amp = amp[:, :GRID] + amp[:, GRID:]
        amps[s] = amp
        lhs = []
        for l in range(LOCAL):
            sampled = None
            for part in range(4):
                piece = amp[(l * 4 + part) * ROWS : (l * 4 + part + 1) * ROWS]
                sampled = piece * piece if part == 0 else sampled + piece * piece
            hi, lo = split(sampled)
            lhs.append(jnp.concatenate([hi, lo, hi, edge_v[s % 2, l * ROWS : (l + 1) * ROWS, :]], axis=1))
        intensities = dot(jnp.concatenate(lhs, axis=0), fine[...])
        total = None
        for l in range(LOCAL):
            intensity = intensities[l * ROWS : (l + 1) * ROWS]
            level = zbuf[s, EDGE + SPARE + l : EDGE + SPARE + l + 1, 0:1]
            resist = jax.nn.sigmoid(RESIST_STEEP * (intensity - level))
            resists[s, l] = resist
            total = resist if l == 0 else total + resist
        if s == 0:
            band[...] = total
        else:
            band[...] += total

    grids_and_rows(0)
    kernels_to(2).wait_recv()
    kernels_to(3).start()
    unpack_kernels(2)
    resist_of(0)
    grids_and_rows(1)
    resist_of(1)
    grids_and_rows(2)
    kernels_to(3).wait_recv()
    unpack_kernels(3)
    resist_of(2)
    grids_and_rows(3)
    resist_of(3)

    load_target.wait()
    load_weights.wait()
    weight_sum = weights_s[0]
    for n in range(1, CONDS):
        weight_sum = weight_sum + weights_s[n]
    weight_sum = jnp.full((8, TP), weight_sum, jnp.int32).astype(F32)
    wanted[...] = target_v[...].astype(F32)
    band[...] = band[...] * (4.0 * RESIST_STEEP * BAND_WEIGHT / CONDS / CONDS)

    load_coarse.wait()
    load_half.wait()
    load_gather.wait()

    def push_of(s):
        fields = []
        for l in range(LOCAL):
            weight = jnp.full((8, TP), weights_s[(c ^ s) * LOCAL + l], jnp.int32).astype(F32) / weight_sum
            pull = (4.0 * RESIST_STEEP) * weight[0:1]
            resist = resists[s, l]
            slope = (pull + 4.0 * RESIST_STEEP * BAND_WEIGHT / CONDS) * resist - (pull * wanted[...] + band[...])
            field = slope * (resist - resist * resist)
            last = jnp.sum(field * half_last[0:1, :], axis=1, keepdims=True)
            last_v[s % 2, l * ROWS : (l + 1) * ROWS, :] = jnp.broadcast_to(last, (ROWS, VR))
            fields.append(field)
        hi, lo = split(jnp.concatenate(fields, axis=0))
        wide = dot(jnp.concatenate([hi, lo], axis=0), coarse[...])
        half = LOCAL * ROWS
        push_v[s % 2] = wide[:half, :GRID] + wide[:half, GRID:] + wide[half:, :GRID]

    def adjoint_of(s):
        drives = []
        for l in range(LOCAL):
            for part in range(4):
                at = (l * 4 + part) * ROWS
                drives.append(push_v[s % 2, l * ROWS : (l + 1) * ROWS, :] * amps[s, at : at + ROWS])
        hi, lo = split(jnp.concatenate(drives, axis=0))
        drive = dot(jnp.concatenate([hi, lo], axis=1), gather[...])
        drive = drive[:, :VR] + drive[:, VR:]
        drives = []
        for part in range(8):
            at = part * ROWS
            last = last_v[s % 2, part // 4 * ROWS : (part // 4 + 1) * ROWS, :]
            drives.append(drive[at : at + ROWS] + last * crossed[s, at : at + ROWS])
        sums = [[None, None] for _ in range(4)]
        for n in range(DEPTH):
            pair = jnp.concatenate(drives[2 * n : 2 * n + 2], axis=1)
            hi, lo = split(pair)
            back = dot(turned[: 2 * UR, :], jnp.concatenate([hi, lo], axis=0))
            back = back[:UR] + back[UR:]
            ee_r, eo_r, oe_r, oo_r, ee_i, eo_i, oe_i, oo_i = parts_of(s, n)
            for h in range(2):
                qr = back[h * UH : (h + 1) * UH, :VR]
                qi = back[h * UH : (h + 1) * UH, VR:]
                terms = (
                    ee_r * qr + ee_i * qi,
                    eo_i * qr - eo_r * qi,
                    oe_i * qr - oe_r * qi,
                    oo_r * qr + oo_i * qi,
                )
                for m, term in enumerate(terms):
                    sums[m][h] = term if n == 0 else sums[m][h] + term
        for m in range(4):
            for h in range(2):
                if s == 0:
                    jbuf[m, h] = sums[m][h]
                else:
                    jbuf[m, h] += sums[m][h]

    push_of(0)
    for s in range(1, GROUP):
        adjoint_of(s - 1)
        push_of(s)
    adjoint_of(GROUP - 1)

    halves = []
    for h in range(2):
        sign_u = 1.0 - 2.0 * h
        halves.append(
            jbuf[0, h]
            + swap(sign_v * jbuf[1, h])
            - sign_u * jbuf[2, 1 - h]
            + swap(sign_u * sign_v * jbuf[3, 1 - h])
        )
    aown[...] = packed(jnp.concatenate(halves, axis=0))

    def adjoint_part(mask):
        return remote(aown, ain.at[mask - 1], as_sem.at[mask - 1], ar_sem.at[mask - 1], partner(mask))

    def adjoint_prev():
        return remote(aown, anear.at[c], as_sem.at[3], near_sem.at[c], (t - 1, GROUP - 1))

    def adjoint_next():
        return remote(aown, anear.at[c], as_sem.at[4], near_sem.at[c], (t + 1, 0))

    def adjoint_near(other):
        return remote(aown, anear.at[other], as_sem.at[3], near_sem.at[other], (t, c ^ 1))

    @pl.when(has_prev)
    def _():
        adjoint_prev().start()

    @pl.when(has_next)
    def _():
        adjoint_next().start()

    for mask in range(1, GROUP):
        adjoint_part(mask).start()

    near = (first & has_prev) | (final & has_next)

    @pl.when(jnp.logical_not(near))
    def _():
        anear[...] = jnp.zeros_like(anear)

    factor[...] = (MASK_STEEP / (SIZE * SIZE)) * (1.0 - jnp.square(jnp.tanh(MASK_STEEP * theta_v[...])))

    for mask in range(1, GROUP):
        adjoint_part(mask).wait_recv()

    @pl.when(near)
    def _():
        for other in range(GROUP):
            adjoint_near(other).wait_recv()

    for copy in load_bt:
        copy.wait()
    rows = []
    for value in (aown[...] + ain[0] + ain[1] + ain[2], anear[0] + anear[1] + anear[2] + anear[3]):
        hi, lo = split(jnp.concatenate(unpacked(value), axis=0))
        rows += [hi, hi, lo, jnp.zeros((256 - 3 * UR, VR), BF)]
    tall = dot(pack[...], jnp.concatenate(rows, axis=0))
    hi, lo = split(tall)
    out_v[...] = dot(jnp.concatenate([hi, lo, hi], axis=1), bt[...]) * factor[...]

    @pl.when(has_next & final)
    def _():
        for other in range(GROUP):
            halo_next(other).wait_send()

    @pl.when(has_prev & first)
    def _():
        for other in range(GROUP):
            halo_prev(other).wait_send()

    for mask in range(1, GROUP):
        part(mask).wait_send()
        kernels_to(mask).wait_send()
        adjoint_part(mask).wait_send()

    @pl.when(has_prev)
    def _():
        adjoint_prev().wait_send()

    @pl.when(has_next)
    def _():
        adjoint_next().wait_send()


def shards(tiles, theta, target, kernel_real, kernel_imag, weights, thresholds):
    constants = tables()
    dma = pltpu.SemaphoreType.DMA
    by, bt, pack, turned, pv, pu, sample, gather, fine, coarse, half_last = constants
    call = pl.pallas_call(
        functools.partial(kernel, tiles),
        out_shape=jax.ShapeDtypeStruct((ROWS, TP), F32),
        in_specs=[pl.BlockSpec(memory_space=pltpu.HBM)] * 17,
        out_specs=pl.BlockSpec(memory_space=pltpu.VMEM),
        scratch_shapes=[
            pltpu.SMEM((CONDS,), jnp.int32),
            pltpu.SMEM((LOCAL,), F32),
            pltpu.VMEM((ROWS, TP), F32),
            pltpu.VMEM((ROWS, TP), jnp.int32),
            pltpu.VMEM((2, LOCAL, KSUP, KERNELS, KSUP), F32),
            pltpu.VMEM(by.shape, BF),
            pltpu.VMEM((3 * VR, TP), BF),
            pltpu.VMEM(pack.shape[1:], BF),
            pltpu.VMEM(turned.shape[1:], BF),
            pltpu.VMEM((4 * VR, 2 * VR), BF),
            pltpu.VMEM(pu.shape, BF),
            pltpu.VMEM(sample.shape, BF),
            pltpu.VMEM(gather.shape, BF),
            pltpu.VMEM((4 * GRID, TP), BF),
            pltpu.VMEM(coarse.shape, BF),
            pltpu.VMEM(half_last.shape, F32),
            pltpu.VMEM((DEPTH * UR, 2 * VR), F32),
            pltpu.VMEM((GROUP, EDGE + UR, VR), F32),
            pltpu.VMEM((GROUP, DEPTH, 4, UR, VR), F32),
            pltpu.VMEM((UH, VR), F32),
            pltpu.VMEM((UH, VR), F32),
            pltpu.VMEM((5, UH, VR), F32),
            pltpu.VMEM((4, 2, UH, VR), F32),
            pltpu.VMEM((UH, VR), F32),
            pltpu.VMEM((3, UH, VR), F32),
            pltpu.VMEM((GROUP, UH, VR), F32),
            pltpu.VMEM((4, 2, UH, VR), F32),
            pltpu.VMEM((GROUP, LOCAL * KERNELS * 2 * ROWS, GRID), F32),
            pltpu.VMEM((GROUP, LOCAL * KERNELS * 2 * ROWS, VR), F32),
            pltpu.VMEM((2, LOCAL * KERNELS * 2 * ROWS, 2 * VR), BF),
            pltpu.VMEM((2, LOCAL * ROWS, VR), BF),
            pltpu.VMEM((2, LOCAL * ROWS, GRID), F32),
            pltpu.VMEM((2, LOCAL * ROWS, VR), F32),
            pltpu.VMEM((GROUP, LOCAL, ROWS, TP), F32),
            pltpu.VMEM((ROWS, TP), F32),
            pltpu.VMEM((ROWS, TP), F32),
            pltpu.VMEM((ROWS, TP), F32),
            dma((20,)),
            dma((3,)),
            dma((3,)),
            dma((3,)),
            dma((3,)),
            dma((4,)),
            dma((2,)),
            dma((5,)),
            dma((3,)),
            dma((4,)),
        ],
        compiler_params=pltpu.CompilerParams(collective_id=0, has_side_effects=True, vmem_limit_bytes=32 * 1024 * 1024),
        name="window_gradient",
    )
    kernel_real, kernel_imag = (jnp.swapaxes(x, 1, 2) for x in (kernel_real, kernel_imag))
    arrays = (theta, target, kernel_real, kernel_imag, weights, thresholds, *(jnp.asarray(x) for x in constants))
    return call(*(pltpu.with_memory_space_constraint(x, pltpu.HBM) for x in arrays))


def solution(mesh):
    in_specs = (
        P(("tile", "cond"), None),
        P("tile", None),
        P("cond", None, None, None),
        P("cond", None, None, None),
        P(),
        P("cond"),
    )
    out_specs = P(("tile", "cond"), None)
    body = functools.partial(shards, mesh.shape["tile"])
    return jax.shard_map(body, mesh=mesh, in_specs=in_specs, out_specs=out_specs, check_vma=False)
```

```python
import functools
import math

import jax
import jax.numpy as jnp
import ml_dtypes
import numpy as np
from jax import lax
from jax.experimental import pallas as pl
from jax.experimental.pallas import tpu as pltpu
from jax.sharding import PartitionSpec as P

TP = 512
HALO = 32
KSUP = 65
HALF = KSUP // 2
CONDS = 8
KERNELS = 2
SIZE = TP + 2 * HALO
ROWS = 128
GROUP = 4
LOCAL = CONDS // GROUP
UH = 40
UR = 2 * UH
VR = 128
FLAT = 2 * HALF
DEPTH = LOCAL * KERNELS
USED = UH + HALF
EDGE = 2 * DEPTH
CHUNK = EDGE + DEPTH // 2 * USED
WIRE = EDGE + DEPTH * USED
GRID = 128
SPARE = HALF + 1

MASK_STEEP = 2.0
RESIST_STEEP = 4.0
BAND_WEIGHT = 1.0

BF = jnp.bfloat16
F32 = jnp.float32
MESH = pl.DeviceIdType.MESH


def split(x):
    hi = x.astype(BF)
    return hi, (x - hi.astype(F32)).astype(BF)


def np_split(x):
    hi = x.astype(ml_dtypes.bfloat16)
    return hi, (x - hi.astype(np.float64)).astype(ml_dtypes.bfloat16)


def waves(positions):
    phase = np.fmod(np.asarray(positions, np.float64)[:, None] * np.arange(HALF + 1)[None, :], SIZE)
    angles = phase * (2.0 * math.pi / SIZE)
    return np.cos(angles), np.sin(angles)


def row_basis(positions):
    cos, sin = waves(positions)
    out = np.zeros((len(positions), UR))
    out[:, :HALF] = cos[:, 1:]
    out[:, HALF] = 1.0
    out[:, UH:USED] = sin[:, 1:]
    return out


def column_basis(positions):
    cos, sin = waves(positions)
    out = np.zeros((len(positions), VR))
    out[:, :HALF] = cos[:, 1:]
    out[:, HALF:FLAT] = sin[:, 1:]
    out[:, FLAT] = 1.0
    return out


def parity_rows():
    out = np.zeros((UR, UR))
    out[HALF, HALF] = 1.0
    for j in range(1, HALF + 1):
        out[j - 1, HALF + j] = out[j - 1, HALF - j] = out[UH + j - 1, HALF + j] = 1.0
        out[UH + j - 1, HALF - j] = -1.0
    return out


def parity_columns():
    out = np.zeros((2 * VR, 2 * VR))
    for ri in range(2):
        out[ri * VR + HALF, VR + ri] = 1.0
        for j in range(1, HALF + 1):
            even = ri * FLAT + j - 1
            out[ri * VR + HALF + j, even] = out[ri * VR + HALF - j, even] = 1.0
            out[ri * VR + HALF + j, even + HALF] = 1.0
            out[ri * VR + HALF - j, even + HALF] = -1.0
    return out


def tables():
    bf = ml_dtypes.bfloat16
    cols = column_basis(np.arange(TP) + HALO)
    hi, lo = np_split(cols)
    by = np.concatenate([hi, lo], axis=1)
    bt = np.concatenate([hi.T, lo.T], axis=0)
    places = column_basis(np.arange(GRID) * (SIZE / GRID))
    hi, lo = np_split(places.T)
    zero = np.zeros_like(hi)
    sample = np.concatenate([np.concatenate([hi, lo], axis=1), np.concatenate([hi, zero], axis=1)], axis=0)
    hi, lo = np_split(places)
    gather = np.concatenate([np.concatenate([hi, lo], axis=1), np.concatenate([hi, zero], axis=1)], axis=0)
    phase = (np.arange(TP) + HALO) * (2.0 * math.pi / SIZE)
    place = np.arange(GRID) * (2.0 * math.pi / GRID)
    spread = np.ones((GRID, TP))
    for f in range(1, GRID // 2):
        spread += 2.0 * np.cos(f * (phase[None, :] - place[:, None]))
    spread += np.cos(GRID // 2 * place)[:, None] * np.cos(GRID // 2 * phase)[None, :]
    spread /= GRID
    last = np.sin(GRID // 2 * phase)
    hi, lo = np_split(spread)
    last_hi, last_lo = np_split(last)
    rest = np.zeros((VR, TP), bf)
    rest[HALF - 1], rest[FLAT - 1], rest[FLAT + HALF - 1] = last_hi, last_lo, last_hi
    fine = np.concatenate([hi, lo, rest], axis=0)
    coarse = np.concatenate([hi.T, lo.T], axis=1)
    half_last = np.broadcast_to(0.5 * last, (8, TP)).astype(np.float32)
    pack = []
    turned = []
    for c in range(GROUP):
        own = row_basis(np.arange(ROWS) + HALO + ROWS * c)
        near = np.zeros_like(own)
        if c == 0:
            near[:HALO] = row_basis(np.arange(HALO) + HALO + TP)
        if c == GROUP - 1:
            near[ROWS - HALO :] = row_basis(np.arange(HALO))
        row = []
        column = []
        for table in (own, near):
            thi, tlo = np_split(table)
            row += [thi, tlo, thi, np.zeros((ROWS, 256 - 3 * UR), bf)]
            column.append(np.concatenate([thi.T, thi.T], axis=1))
            column.append(np.concatenate([tlo.T, np.zeros((UR, ROWS), bf)], axis=1))
        pack.append(np.concatenate(row, axis=1))
        turned.append(np.concatenate(column, axis=0))
    pv = parity_columns().astype(bf)
    pu = parity_rows().astype(bf)
    pu = np.concatenate([pu, pu], axis=1)
    return by, bt, np.stack(pack), np.stack(turned), pv, pu, sample, gather, fine, coarse, half_last


def dot(a, b):
    return jnp.dot(a, b, preferred_element_type=F32)


def kernel(
    tiles,
    theta_h, target_h, kr_h, ki_h, weights_h, thresholds_h, by_h, bt_h, pack_h, turned_h, pv_h, pu_h,
    sample_h, gather_h, fine_h, coarse_h, half_last_h,
    out_v,
    weights_s, thresholds_s, theta_v, target_v, raw_v, by, bt, pack, turned, pv, pu,
    sample, gather, fine, coarse, half_last, stack, zbuf, coef, rown, rhalo, rin, rsum, aown, ain, anear, jbuf, amps, crossed, rows_v, edge_v, push_v, last_v, resists, band, wanted, factor,
    load_sem, zs_sem, zr_sem, rs_sem, rr_sem, hs_sem, hr_sem, as_sem, ar_sem, near_sem,
):
    t = lax.axis_index("tile")
    c = lax.axis_index("cond")
    first = c == 0
    final = c == GROUP - 1
    has_prev = t > 0
    has_next = t < tiles - 1

    loads = []

    def load(src, dst):
        copy = pltpu.make_async_copy(src, dst, load_sem.at[len(loads)])
        copy.start()
        loads.append(copy)
        return copy

    load_kr = load(kr_h, raw_v.at[0])
    load_ki = load(ki_h, raw_v.at[1])
    load_pv = [load(pv_h, pv.at[pl.ds(at, 2 * VR), :]) for at in (0, 2 * VR)]
    load_pu = load(pu_h, pu)
    load_thresholds = load(thresholds_h, thresholds_s)
    load_theta = load(theta_h, theta_v)
    load_by = load(by_h, by)
    load_turned = load(turned_h.at[c], turned)
    load_pack = load(pack_h.at[c], pack)
    load_sample = load(sample_h, sample)
    load_fine = [
        load(fine_h.at[pl.ds(0, GRID), :], fine.at[pl.ds(0, GRID), :]),
        load(fine_h, fine.at[pl.ds(GRID, 3 * GRID), :]),
    ]
    load_coarse = load(coarse_h, coarse)
    load_half = load(half_last_h, half_last)
    load_gather = load(gather_h, gather)
    load_bt = [
        load(bt_h.at[pl.ds(0, VR), :], bt.at[pl.ds(0, VR), :]),
        load(bt_h, bt.at[pl.ds(VR, 2 * VR), :]),
    ]
    load_weights = load(weights_h, weights_s)
    load_target = load(target_h.at[pl.ds(pl.multiple_of(c * ROWS, ROWS), ROWS), :], target_v)

    def partner(mask):
        return (t, c ^ mask)

    barrier = pltpu.get_barrier_semaphore()

    def greet(device):
        pl.semaphore_signal(barrier, inc=1, device_id=device, device_id_type=MESH)

    mirror = ((t + tiles // 2) % tiles, c ^ 2)
    for mask in range(1, GROUP):
        greet(partner(mask))
    greet(mirror)

    @pl.when(has_next)
    def _():
        greet((t + 1, 0))

    @pl.when(has_prev)
    def _():
        greet((t - 1, GROUP - 1))

    lane = lax.broadcasted_iota(jnp.int32, (UH, VR), 1)
    row = lax.broadcasted_iota(jnp.int32, (UH, VR), 0)
    tall_lane = lax.broadcasted_iota(jnp.int32, (UR, VR), 1)
    diagonal = tall_lane == lax.broadcasted_iota(jnp.int32, (UR, VR), 0)
    sign_v = jnp.where((lane >= HALF) & (lane < FLAT), -1.0, 1.0).astype(F32)

    def swap(x):
        out = jnp.where(lane < HALF, pltpu.roll(x, VR - HALF, 1), pltpu.roll(x, HALF, 1))
        return jnp.where(lane < FLAT, out, 0.0)

    def packed(x):
        out = jnp.where(lane < FLAT, x[:UH], pltpu.roll(x[UH:], FLAT, 1))
        flat = jnp.sum(jnp.where(diagonal, x[:, FLAT : FLAT + 1], 0.0), axis=0, keepdims=True)
        return jnp.where(row == SPARE, flat, out)

    def unpacked(x):
        flat = jnp.sum(jnp.where(diagonal, x[SPARE : SPARE + 1], 0.0), axis=1, keepdims=True)
        keep = (lane < FLAT) & (row < SPARE)
        out = []
        for h, value in enumerate((x, pltpu.roll(x, FLAT, 1))):
            out.append(jnp.where(lane == FLAT, flat[h * UH : (h + 1) * UH], jnp.where(keep, value, 0.0)))
        return out

    def unpack_kernels(s):
        used_lane, used_diagonal = tall_lane[:USED], diagonal[:USED]
        for n in range(DEPTH):
            p = zbuf[s, EDGE + n * USED : EDGE + (n + 1) * USED, :]
            p32, p64, p96 = (pltpu.roll(p, shift, 1) for shift in (HALF, 2 * HALF, 3 * HALF))
            for at, (a, b) in enumerate(((p, p32), (p96, p), (p64, p96), (p32, p64))):
                value = jnp.where(used_lane < HALF, a, b)
                if at % 2 == 0:
                    flat = zbuf[s, 2 * n + at // 2 : 2 * n + at // 2 + 1, :]
                    flat = jnp.sum(jnp.where(used_diagonal, flat, 0.0), axis=1, keepdims=True)
                    value = jnp.where(used_lane == FLAT, flat, value)
                coef[s, n, at, :USED] = value

    stack[...] = jnp.zeros_like(stack)
    load_kr.wait()
    load_ki.wait()
    for ri in range(2):
        for l in range(LOCAL):
            for k in range(KERNELS):
                at = (l * KERNELS + k) * UR
                stack[at : at + KSUP, ri * VR : ri * VR + KSUP] = raw_v[ri, l, :, k, :]
    for copy in load_pv:
        copy.wait()
    load_pu.wait()
    hi, lo = split(stack[...])
    folded = dot(jnp.concatenate([hi, lo], axis=1), pv[...])
    hi, lo = split(folded)
    coef[:, :, :, USED:, :] = jnp.zeros((GROUP, DEPTH, 4, UR - USED, VR), F32)
    load_thresholds.wait()
    for n in range(DEPTH):
        rhs = jnp.concatenate([hi[n * UR : (n + 1) * UR], lo[n * UR : (n + 1) * UR]], axis=0)
        value = dot(pu[...], rhs)
        zbuf[0, EDGE + n * USED : EDGE + (n + 1) * USED, :] = value[:USED, :VR]
        for ri in range(2):
            flat = jnp.sum(jnp.where(diagonal, value[:, VR + ri : VR + ri + 1], 0.0), axis=0, keepdims=True)
            if 2 * n + ri < LOCAL:
                flat = jnp.where(lane[:1] == VR - 1, thresholds_s[2 * n + ri], flat)
            zbuf[0, 2 * n + ri : 2 * n + ri + 1, :] = flat

    load_theta.wait()
    load_by.wait()
    load_turned.wait()
    mask_rows = jnp.tanh(MASK_STEEP * theta_v[...])
    hi, lo = split(mask_rows)
    wide = dot(jnp.concatenate([hi, lo], axis=0), by[...])
    column = wide[:ROWS, :VR] + wide[:ROWS, VR:] + wide[ROWS:, :VR]
    hi, lo = split(column)
    both = dot(turned[...], jnp.concatenate([hi, lo], axis=0))
    rown[...] = packed(both[:UR] + both[UR : 2 * UR])
    rhalo[...] = packed(both[2 * UR : 3 * UR] + both[3 * UR :])

    edge_of = (has_next & final) | (has_prev & first)
    pl.semaphore_wait(barrier, jnp.where(edge_of, 2 * GROUP, GROUP))

    def remote(src, dst, send, recv, device):
        return pltpu.make_async_remote_copy(
            src_ref=src, dst_ref=dst, send_sem=send, recv_sem=recv, device_id=device, device_id_type=MESH
        )

    def halo_next(other):
        return remote(rhalo, rin.at[3], hs_sem.at[other], hr_sem.at[0], (t + 1, other))

    def halo_prev(other):
        return remote(rhalo, rin.at[4], hs_sem.at[other], hr_sem.at[1], (t - 1, other))

    def part(mask):
        return remote(rown, rin.at[mask - 1], rs_sem.at[mask - 1], rr_sem.at[mask - 1], partner(mask))

    def kernels_to(mask, chunk):
        device = partner(1) if mask != 2 else mirror
        source = 2 if mask == 3 else 0
        rows = pl.ds(0, CHUNK) if chunk == 0 else pl.ds(CHUNK, WIRE - CHUNK)
        sem = 2 * (mask - 1) + chunk
        return remote(
            zbuf.at[source, rows, :], zbuf.at[mask, rows, :], zs_sem.at[sem], zr_sem.at[sem], device
        )

    @pl.when(has_next & final)
    def _():
        for other in range(GROUP):
            halo_next(other).start()

    @pl.when(has_prev & first)
    def _():
        for other in range(GROUP):
            halo_prev(other).start()

    for mask in range(1, GROUP):
        part(mask).start()
    for mask in (2, 1):
        for chunk in range(2):
            kernels_to(mask, chunk).start()

    @pl.when(jnp.logical_not(has_prev))
    def _():
        rin[3] = jnp.zeros((UH, VR), F32)

    @pl.when(jnp.logical_not(has_next))
    def _():
        rin[4] = jnp.zeros((UH, VR), F32)

    unpack_kernels(0)
    for chunk in range(2):
        kernels_to(1, chunk).wait_recv()
    unpack_kernels(1)

    @pl.when(has_prev)
    def _():
        halo_next(0).wait_recv()

    @pl.when(has_next)
    def _():
        halo_prev(0).wait_recv()

    for mask in range(1, GROUP):
        part(mask).wait_recv()

    total = rown[...] + rin[0] + rin[1] + rin[2] + rin[3] + rin[4]
    halves = unpacked(total * (1.0 / (SIZE * SIZE)))
    for h in range(2):
        sign_u = 1.0 - 2.0 * h
        rsum[0, h] = halves[h]
        rsum[1, h] = sign_v * swap(halves[h])
        rsum[2, h] = sign_u * halves[1 - h]
        rsum[3, h] = (-sign_u) * sign_v * swap(halves[1 - h])

    def parts_of(s, n):
        return [coef[s, n, 2 * ri + v, u * UH : (u + 1) * UH, :] for ri in range(2) for u in range(2) for v in range(2)]

    load_pack.wait()
    load_sample.wait()
    for copy in load_fine:
        copy.wait()
    pair_lane = lax.broadcasted_iota(jnp.int32, (2 * ROWS, VR), 1)
    block_lane = lax.broadcasted_iota(jnp.int32, (ROWS, VR), 1)

    def grids_and_rows(s):
        cross = []
        grids = []
        for n in range(DEPTH):
            ee_r, eo_r, oe_r, oo_r, ee_i, eo_i, oe_i, oo_i = parts_of(s, n)
            real = []
            imag = []
            for h in range(2):
                r0, r1, r2, r3 = (rsum[m, h] for m in range(4))
                real.append(ee_r * r0 + eo_i * r1 + oe_i * r2 + oo_r * r3)
                imag.append(ee_i * r0 - eo_r * r1 - oe_r * r2 + oo_i * r3)
            grid = jnp.concatenate([jnp.concatenate(real, axis=0), jnp.concatenate(imag, axis=0)], axis=1)
            hi, lo = split(grid)
            grids.append(jnp.concatenate([hi, hi, lo], axis=0))
        for n, grid in enumerate(grids):
            tall = dot(pack[:, : 3 * UR], grid)
            tall = jnp.concatenate([tall[:, :VR], tall[:, VR:]], axis=0)
            other = jnp.where(pair_lane == HALF - 1, pltpu.roll(tall, VR - HALF, 1), 0.0)
            other = jnp.where(pair_lane == FLAT - 1, pltpu.roll(tall, HALF, 1), other)
            at = n * 2 * ROWS
            crossed[s, at : at + 2 * ROWS, :] = other
            other = tall * other
            cross.append(other[:ROWS] + other[ROWS:])
            hi, lo = split(tall)
            rows_v[s % 2, at : at + 2 * ROWS, :VR] = hi
            rows_v[s % 2, at : at + 2 * ROWS, VR:] = lo
        for l in range(LOCAL):
            edge = cross[2 * l] + cross[2 * l + 1]
            near = edge.astype(BF).astype(F32)
            edge = jnp.where(block_lane < FLAT, near, pltpu.roll(edge - near, FLAT, 1)).astype(BF)
            edge_v[s % 2, l * ROWS : (l + 1) * ROWS, :] = edge

    def resist_of(s):
        amp = dot(rows_v[s % 2], sample[...])
        amp = amp[:, :GRID] + amp[:, GRID:]
        amps[s] = amp
        lhs = []
        for l in range(LOCAL):
            sampled = None
            for part in range(4):
                piece = amp[(l * 4 + part) * ROWS : (l * 4 + part + 1) * ROWS]
                sampled = piece * piece if part == 0 else sampled + piece * piece
            hi, lo = split(sampled)
            lhs.append(jnp.concatenate([hi, lo, hi, edge_v[s % 2, l * ROWS : (l + 1) * ROWS, :]], axis=1))
        intensities = dot(jnp.concatenate(lhs, axis=0), fine[...])
        total = None
        for l in range(LOCAL):
            intensity = intensities[l * ROWS : (l + 1) * ROWS]
            level = zbuf[s, l : l + 1, VR - 1 : VR]
            resist = jax.nn.sigmoid(RESIST_STEEP * (intensity - level))
            resists[s, l] = resist
            total = resist if l == 0 else total + resist
        if s == 0:
            band[...] = total
        else:
            band[...] += total

    grids_and_rows(0)
    kernels_to(2, 0).wait_recv()
    kernels_to(3, 0).start()
    resist_of(0)
    grids_and_rows(1)
    kernels_to(2, 1).wait_recv()
    kernels_to(3, 1).start()
    unpack_kernels(2)
    resist_of(1)
    grids_and_rows(2)
    for chunk in range(2):
        kernels_to(3, chunk).wait_recv()
    unpack_kernels(3)
    resist_of(2)
    grids_and_rows(3)
    resist_of(3)

    load_target.wait()
    load_weights.wait()
    weight_sum = weights_s[0]
    for n in range(1, CONDS):
        weight_sum = weight_sum + weights_s[n]
    weight_sum = jnp.full((8, TP), weight_sum, jnp.int32).astype(F32)
    wanted[...] = target_v[...].astype(F32)
    band[...] = band[...] * (4.0 * RESIST_STEEP * BAND_WEIGHT / CONDS / CONDS)

    load_coarse.wait()
    load_half.wait()
    load_gather.wait()

    def push_of(s):
        fields = []
        for l in range(LOCAL):
            weight = jnp.full((8, TP), weights_s[(c ^ s) * LOCAL + l], jnp.int32).astype(F32) / weight_sum
            pull = (4.0 * RESIST_STEEP) * weight[0:1]
            resist = resists[s, l]
            slope = (pull + 4.0 * RESIST_STEEP * BAND_WEIGHT / CONDS) * resist - (pull * wanted[...] + band[...])
            field = slope * (resist - resist * resist)
            last = jnp.sum(field * half_last[0:1, :], axis=1, keepdims=True)
            last_v[s % 2, l * ROWS : (l + 1) * ROWS, :] = jnp.broadcast_to(last, (ROWS, VR))
            fields.append(field)
        hi, lo = split(jnp.concatenate(fields, axis=0))
        wide = dot(jnp.concatenate([hi, lo], axis=0), coarse[...])
        half = LOCAL * ROWS
        push_v[s % 2] = wide[:half, :GRID] + wide[:half, GRID:] + wide[half:, :GRID]

    def adjoint_of(s):
        drives = []
        for l in range(LOCAL):
            for part in range(4):
                at = (l * 4 + part) * ROWS
                drives.append(push_v[s % 2, l * ROWS : (l + 1) * ROWS, :] * amps[s, at : at + ROWS])
        hi, lo = split(jnp.concatenate(drives, axis=0))
        drive = dot(jnp.concatenate([hi, lo], axis=1), gather[...])
        drive = drive[:, :VR] + drive[:, VR:]
        drives = []
        for part in range(8):
            at = part * ROWS
            last = last_v[s % 2, part // 4 * ROWS : (part // 4 + 1) * ROWS, :]
            drives.append(drive[at : at + ROWS] + last * crossed[s, at : at + ROWS])
        sums = [[None, None] for _ in range(4)]
        for n in range(DEPTH):
            pair = jnp.concatenate(drives[2 * n : 2 * n + 2], axis=1)
            hi, lo = split(pair)
            back = dot(turned[: 2 * UR, :], jnp.concatenate([hi, lo], axis=0))
            back = back[:UR] + back[UR:]
            ee_r, eo_r, oe_r, oo_r, ee_i, eo_i, oe_i, oo_i = parts_of(s, n)
            for h in range(2):
                qr = back[h * UH : (h + 1) * UH, :VR]
                qi = back[h * UH : (h + 1) * UH, VR:]
                terms = (
                    ee_r * qr + ee_i * qi,
                    eo_i * qr - eo_r * qi,
                    oe_i * qr - oe_r * qi,
                    oo_r * qr + oo_i * qi,
                )
                for m, term in enumerate(terms):
                    sums[m][h] = term if n == 0 else sums[m][h] + term
        for m in range(4):
            for h in range(2):
                if s == 0:
                    jbuf[m, h] = sums[m][h]
                else:
                    jbuf[m, h] += sums[m][h]

    push_of(0)
    for s in range(1, GROUP):
        adjoint_of(s - 1)
        push_of(s)
    adjoint_of(GROUP - 1)

    halves = []
    for h in range(2):
        sign_u = 1.0 - 2.0 * h
        halves.append(
            jbuf[0, h]
            + swap(sign_v * jbuf[1, h])
            - sign_u * jbuf[2, 1 - h]
            + swap(sign_u * sign_v * jbuf[3, 1 - h])
        )
    aown[...] = packed(jnp.concatenate(halves, axis=0))

    def adjoint_part(mask):
        return remote(aown, ain.at[mask - 1], as_sem.at[mask - 1], ar_sem.at[mask - 1], partner(mask))

    def adjoint_prev():
        return remote(aown, anear.at[c], as_sem.at[3], near_sem.at[c], (t - 1, GROUP - 1))

    def adjoint_next():
        return remote(aown, anear.at[c], as_sem.at[4], near_sem.at[c], (t + 1, 0))

    def adjoint_near(other):
        return remote(aown, anear.at[other], as_sem.at[3], near_sem.at[other], (t, c ^ 1))

    @pl.when(has_prev)
    def _():
        adjoint_prev().start()

    @pl.when(has_next)
    def _():
        adjoint_next().start()

    for mask in range(1, GROUP):
        adjoint_part(mask).start()

    near = (first & has_prev) | (final & has_next)

    @pl.when(jnp.logical_not(near))
    def _():
        anear[...] = jnp.zeros_like(anear)

    factor[...] = (MASK_STEEP / (SIZE * SIZE)) * (1.0 - jnp.square(jnp.tanh(MASK_STEEP * theta_v[...])))

    for mask in range(1, GROUP):
        adjoint_part(mask).wait_recv()

    @pl.when(near)
    def _():
        for other in range(GROUP):
            adjoint_near(other).wait_recv()

    for copy in load_bt:
        copy.wait()
    rows = []
    for value in (aown[...] + ain[0] + ain[1] + ain[2], anear[0] + anear[1] + anear[2] + anear[3]):
        hi, lo = split(jnp.concatenate(unpacked(value), axis=0))
        rows += [hi, hi, lo, jnp.zeros((256 - 3 * UR, VR), BF)]
    tall = dot(pack[...], jnp.concatenate(rows, axis=0))
    hi, lo = split(tall)
    out_v[...] = dot(jnp.concatenate([hi, lo, hi], axis=1), bt[...]) * factor[...]

    @pl.when(has_next & final)
    def _():
        for other in range(GROUP):
            halo_next(other).wait_send()

    @pl.when(has_prev & first)
    def _():
        for other in range(GROUP):
            halo_prev(other).wait_send()

    for mask in range(1, GROUP):
        part(mask).wait_send()
        for chunk in range(2):
            kernels_to(mask, chunk).wait_send()
        adjoint_part(mask).wait_send()

    @pl.when(has_prev)
    def _():
        adjoint_prev().wait_send()

    @pl.when(has_next)
    def _():
        adjoint_next().wait_send()


def shards(tiles, theta, target, kernel_real, kernel_imag, weights, thresholds):
    constants = tables()
    dma = pltpu.SemaphoreType.DMA
    by, bt, pack, turned, pv, pu, sample, gather, fine, coarse, half_last = constants
    call = pl.pallas_call(
        functools.partial(kernel, tiles),
        out_shape=jax.ShapeDtypeStruct((ROWS, TP), F32),
        in_specs=[pl.BlockSpec(memory_space=pltpu.HBM)] * 17,
        out_specs=pl.BlockSpec(memory_space=pltpu.VMEM),
        scratch_shapes=[
            pltpu.SMEM((CONDS,), jnp.int32),
            pltpu.SMEM((LOCAL,), F32),
            pltpu.VMEM((ROWS, TP), F32),
            pltpu.VMEM((ROWS, TP), jnp.int32),
            pltpu.VMEM((2, LOCAL, KSUP, KERNELS, KSUP), F32),
            pltpu.VMEM(by.shape, BF),
            pltpu.VMEM((3 * VR, TP), BF),
            pltpu.VMEM(pack.shape[1:], BF),
            pltpu.VMEM(turned.shape[1:], BF),
            pltpu.VMEM((4 * VR, 2 * VR), BF),
            pltpu.VMEM(pu.shape, BF),
            pltpu.VMEM(sample.shape, BF),
            pltpu.VMEM(gather.shape, BF),
            pltpu.VMEM((4 * GRID, TP), BF),
            pltpu.VMEM(coarse.shape, BF),
            pltpu.VMEM(half_last.shape, F32),
            pltpu.VMEM((DEPTH * UR, 2 * VR), F32),
            pltpu.VMEM((GROUP, WIRE, VR), F32),
            pltpu.VMEM((GROUP, DEPTH, 4, UR, VR), F32),
            pltpu.VMEM((UH, VR), F32),
            pltpu.VMEM((UH, VR), F32),
            pltpu.VMEM((5, UH, VR), F32),
            pltpu.VMEM((4, 2, UH, VR), F32),
            pltpu.VMEM((UH, VR), F32),
            pltpu.VMEM((3, UH, VR), F32),
            pltpu.VMEM((GROUP, UH, VR), F32),
            pltpu.VMEM((4, 2, UH, VR), F32),
            pltpu.VMEM((GROUP, LOCAL * KERNELS * 2 * ROWS, GRID), F32),
            pltpu.VMEM((GROUP, LOCAL * KERNELS * 2 * ROWS, VR), F32),
            pltpu.VMEM((2, LOCAL * KERNELS * 2 * ROWS, 2 * VR), BF),
            pltpu.VMEM((2, LOCAL * ROWS, VR), BF),
            pltpu.VMEM((2, LOCAL * ROWS, GRID), F32),
            pltpu.VMEM((2, LOCAL * ROWS, VR), F32),
            pltpu.VMEM((GROUP, LOCAL, ROWS, TP), F32),
            pltpu.VMEM((ROWS, TP), F32),
            pltpu.VMEM((ROWS, TP), F32),
            pltpu.VMEM((ROWS, TP), F32),
            dma((20,)),
            dma((6,)),
            dma((6,)),
            dma((3,)),
            dma((3,)),
            dma((4,)),
            dma((2,)),
            dma((5,)),
            dma((3,)),
            dma((4,)),
        ],
        compiler_params=pltpu.CompilerParams(collective_id=0, has_side_effects=True, vmem_limit_bytes=32 * 1024 * 1024),
        name="window_gradient",
    )
    kernel_real, kernel_imag = (jnp.swapaxes(x, 1, 2) for x in (kernel_real, kernel_imag))
    arrays = (theta, target, kernel_real, kernel_imag, weights, thresholds, *(jnp.asarray(x) for x in constants))
    return call(*(pltpu.with_memory_space_constraint(x, pltpu.HBM) for x in arrays))


def solution(mesh):
    in_specs = (
        P(("tile", "cond"), None),
        P("tile", None),
        P("cond", None, None, None),
        P("cond", None, None, None),
        P(),
        P("cond"),
    )
    out_specs = P(("tile", "cond"), None)
    body = functools.partial(shards, mesh.shape["tile"])
    return jax.shard_map(body, mesh=mesh, in_specs=in_specs, out_specs=out_specs, check_vma=False)
```

```python
import functools
import math

import jax
import jax.numpy as jnp
import ml_dtypes
import numpy as np
from jax import lax
from jax.experimental import pallas as pl
from jax.experimental.pallas import tpu as pltpu
from jax.sharding import PartitionSpec as P

TP = 512
HALO = 32
KSUP = 65
HALF = KSUP // 2
CONDS = 8
KERNELS = 2
SIZE = TP + 2 * HALO
ROWS = 128
GROUP = 4
LOCAL = CONDS // GROUP
UH = 40
UR = 2 * UH
VR = 128
FLAT = 2 * HALF
DEPTH = LOCAL * KERNELS
USED = UH + HALF
EDGE = 2 * DEPTH
CHUNK = EDGE + DEPTH // 2 * USED
WIRE = EDGE + DEPTH * USED
GRID = 128
SPARE = HALF + 1

MASK_STEEP = 2.0
RESIST_STEEP = 4.0
BAND_WEIGHT = 1.0

BF = jnp.bfloat16
F32 = jnp.float32
MESH = pl.DeviceIdType.MESH


def split(x):
    hi = x.astype(BF)
    return hi, (x - hi.astype(F32)).astype(BF)


def np_split(x):
    hi = x.astype(ml_dtypes.bfloat16)
    return hi, (x - hi.astype(np.float64)).astype(ml_dtypes.bfloat16)


def waves(positions):
    phase = np.fmod(np.asarray(positions, np.float64)[:, None] * np.arange(HALF + 1)[None, :], SIZE)
    angles = phase * (2.0 * math.pi / SIZE)
    return np.cos(angles), np.sin(angles)


def row_basis(positions):
    cos, sin = waves(positions)
    out = np.zeros((len(positions), UR))
    out[:, :HALF] = cos[:, 1:]
    out[:, HALF] = 1.0
    out[:, UH:USED] = sin[:, 1:]
    return out


def column_basis(positions):
    cos, sin = waves(positions)
    out = np.zeros((len(positions), VR))
    out[:, :HALF] = cos[:, 1:]
    out[:, HALF:FLAT] = sin[:, 1:]
    out[:, FLAT] = 1.0
    return out


def parity_rows():
    out = np.zeros((UR, UR))
    out[HALF, HALF] = 1.0
    for j in range(1, HALF + 1):
        out[j - 1, HALF + j] = out[j - 1, HALF - j] = out[UH + j - 1, HALF + j] = 1.0
        out[UH + j - 1, HALF - j] = -1.0
    return out


def parity_columns():
    out = np.zeros((2 * VR, 2 * VR))
    for ri in range(2):
        out[ri * VR + HALF, VR + ri] = 1.0
        for j in range(1, HALF + 1):
            even = ri * FLAT + j - 1
            out[ri * VR + HALF + j, even] = out[ri * VR + HALF - j, even] = 1.0
            out[ri * VR + HALF + j, even + HALF] = 1.0
            out[ri * VR + HALF - j, even + HALF] = -1.0
    return out


def tables():
    bf = ml_dtypes.bfloat16
    cols = column_basis(np.arange(TP) + HALO)
    hi, lo = np_split(cols)
    by = np.concatenate([hi, lo], axis=1)
    bt = np.concatenate([hi.T, lo.T], axis=0)
    places = column_basis(np.arange(GRID) * (SIZE / GRID))
    hi, lo = np_split(places[:, :FLAT])
    sample = np.zeros((3 * VR, 2 * GRID), bf)
    gather = np.zeros((4 * GRID, 2 * VR), bf)
    for ri in range(2):
        for block, part in enumerate((hi, hi, lo)):
            at = block * VR + ri * FLAT
            sample[at : at + FLAT, ri * GRID : (ri + 1) * GRID] = part.T
        gather[ri * GRID : (ri + 1) * GRID, ri * FLAT : (ri + 1) * FLAT] = hi
        gather[ri * GRID : (ri + 1) * GRID, VR + ri * FLAT : VR + (ri + 1) * FLAT] = lo
        gather[(2 + ri) * GRID : (3 + ri) * GRID, ri * FLAT : (ri + 1) * FLAT] = hi
    phase = (np.arange(TP) + HALO) * (2.0 * math.pi / SIZE)
    place = np.arange(GRID) * (2.0 * math.pi / GRID)
    spread = np.ones((GRID, TP))
    for f in range(1, GRID // 2):
        spread += 2.0 * np.cos(f * (phase[None, :] - place[:, None]))
    spread += np.cos(GRID // 2 * place)[:, None] * np.cos(GRID // 2 * phase)[None, :]
    spread /= GRID
    last = np.sin(GRID // 2 * phase)
    hi, lo = np_split(spread)
    last_hi, last_lo = np_split(last)
    rest = np.zeros((VR, TP), bf)
    for at in (0, FLAT):
        rest[at + HALF - 2], rest[at + HALF - 1], rest[at + FLAT - 1] = last_hi, last_hi, last_lo
    fine = np.concatenate([hi, lo, rest], axis=0)
    coarse = np.concatenate([hi.T, lo.T], axis=1)
    half_last = np.broadcast_to(0.5 * last, (8, TP)).astype(np.float32)
    pack = []
    turned = []
    for c in range(GROUP):
        own = row_basis(np.arange(ROWS) + HALO + ROWS * c)
        near = np.zeros_like(own)
        if c == 0:
            near[:HALO] = row_basis(np.arange(HALO) + HALO + TP)
        if c == GROUP - 1:
            near[ROWS - HALO :] = row_basis(np.arange(HALO))
        row = []
        column = []
        for table in (own, near):
            thi, tlo = np_split(table)
            row += [thi, tlo, thi, np.zeros((ROWS, 256 - 3 * UR), bf)]
            column.append(np.concatenate([thi.T, thi.T], axis=1))
            column.append(np.concatenate([tlo.T, np.zeros((UR, ROWS), bf)], axis=1))
        pack.append(np.concatenate(row, axis=1))
        turned.append(np.concatenate(column, axis=0))
    pv = parity_columns().astype(bf)
    pu = parity_rows().astype(bf)
    pu = np.concatenate([pu, pu], axis=1)
    return by, bt, np.stack(pack), np.stack(turned), pv, pu, sample, gather, fine, coarse, half_last


def dot(a, b):
    return jnp.dot(a, b, preferred_element_type=F32)


def kernel(
    tiles,
    theta_h, target_h, kr_h, ki_h, weights_h, thresholds_h, by_h, bt_h, pack_h, turned_h, pv_h, pu_h,
    sample_h, gather_h, fine_h, coarse_h, half_last_h,
    out_v,
    weights_s, thresholds_s, theta_v, target_v, raw_v, by, bt, pack, turned, pv, pu,
    sample, gather, fine, coarse, half_last, stack, zbuf, coef, ecoef, rown, rhalo, rin, rsum, erow, aown, ain, anear, jbuf, jflat, amps, crossed, rows_v, flat_v, edge_v, push_v, last_v, resists, band, wanted, factor,
    load_sem, zs_sem, zr_sem, rs_sem, rr_sem, hs_sem, hr_sem, as_sem, ar_sem, near_sem,
):
    t = lax.axis_index("tile")
    c = lax.axis_index("cond")
    first = c == 0
    final = c == GROUP - 1
    has_prev = t > 0
    has_next = t < tiles - 1

    loads = []

    def load(src, dst):
        copy = pltpu.make_async_copy(src, dst, load_sem.at[len(loads)])
        copy.start()
        loads.append(copy)
        return copy

    load_kr = load(kr_h, raw_v.at[0])
    load_ki = load(ki_h, raw_v.at[1])
    load_pv = [load(pv_h, pv.at[pl.ds(at, 2 * VR), :]) for at in (0, 2 * VR)]
    load_pu = load(pu_h, pu)
    load_thresholds = load(thresholds_h, thresholds_s)
    load_theta = load(theta_h, theta_v)
    load_by = load(by_h, by)
    load_turned = load(turned_h.at[c], turned)
    load_pack = load(pack_h.at[c], pack)
    load_sample = load(sample_h, sample)
    load_fine = [
        load(fine_h.at[pl.ds(0, GRID), :], fine.at[pl.ds(0, GRID), :]),
        load(fine_h, fine.at[pl.ds(GRID, 3 * GRID), :]),
    ]
    load_coarse = load(coarse_h, coarse)
    load_half = load(half_last_h, half_last)
    load_gather = load(gather_h, gather)
    load_bt = [
        load(bt_h.at[pl.ds(0, VR), :], bt.at[pl.ds(0, VR), :]),
        load(bt_h, bt.at[pl.ds(VR, 2 * VR), :]),
    ]
    load_weights = load(weights_h, weights_s)
    load_target = load(target_h.at[pl.ds(pl.multiple_of(c * ROWS, ROWS), ROWS), :], target_v)

    def partner(mask):
        return (t, c ^ mask)

    barrier = pltpu.get_barrier_semaphore()

    def greet(device):
        pl.semaphore_signal(barrier, inc=1, device_id=device, device_id_type=MESH)

    mirror = ((t + tiles // 2) % tiles, c ^ 2)
    for mask in range(1, GROUP):
        greet(partner(mask))
    greet(mirror)

    @pl.when(has_next)
    def _():
        greet((t + 1, 0))

    @pl.when(has_prev)
    def _():
        greet((t - 1, GROUP - 1))

    lane = lax.broadcasted_iota(jnp.int32, (UH, VR), 1)
    row = lax.broadcasted_iota(jnp.int32, (UH, VR), 0)
    tall_lane = lax.broadcasted_iota(jnp.int32, (UR, VR), 1)
    diagonal = tall_lane == lax.broadcasted_iota(jnp.int32, (UR, VR), 0)
    odd = lane % FLAT >= HALF
    sign_v = jnp.where(odd, -1.0, 1.0).astype(F32)
    sign_i = jnp.where(lane >= FLAT, -1.0, 1.0).astype(F32)
    edge_lane = lane[: 2 * DEPTH]
    edge_row = row[: 2 * DEPTH]

    def swap(x):
        return jnp.where(odd, pltpu.roll(x, HALF, 1), pltpu.roll(x, VR - HALF, 1))

    def turned_edge(x):
        out = jnp.where(edge_lane < UH, pltpu.roll(x, VR - UH, 1), -pltpu.roll(x, UH, 1))
        return jnp.where(edge_lane < UR, out, 0.0)

    def stacked(x):
        near = x.astype(BF).astype(F32)
        return jnp.concatenate([near, x - near], axis=0).astype(BF)

    def packed(x):
        out = jnp.where(lane < FLAT, x[:UH], pltpu.roll(x[UH:], FLAT, 1))
        flat = jnp.sum(jnp.where(diagonal, x[:, FLAT : FLAT + 1], 0.0), axis=0, keepdims=True)
        return jnp.where(row == SPARE, flat, out)

    def unpacked(x):
        flat = jnp.sum(jnp.where(diagonal, x[SPARE : SPARE + 1], 0.0), axis=1, keepdims=True)
        keep = (lane < FLAT) & (row < SPARE)
        out = []
        for h, value in enumerate((x, pltpu.roll(x, FLAT, 1))):
            out.append(jnp.where(lane == FLAT, flat[h * UH : (h + 1) * UH], jnp.where(keep, value, 0.0)))
        return out

    def unpack_kernels(s):
        for n in range(DEPTH):
            at = EDGE + n * USED
            even = zbuf[s, at : at + UH, :]
            uneven = zbuf[s, at + UH : at + USED, :]
            odd_rows = odd[: USED - UH]
            coef[s, n, 0] = jnp.where(odd, pltpu.roll(even, HALF, 1), even)
            coef[s, n, 1] = jnp.where(odd, pltpu.roll(even, FLAT, 1), pltpu.roll(even, HALF, 1))
            coef[s, n, 2, : USED - UH] = jnp.where(
                odd_rows, pltpu.roll(uneven, VR - HALF, 1), pltpu.roll(uneven, FLAT, 1)
            )
            coef[s, n, 3, : USED - UH] = jnp.where(odd_rows, uneven, pltpu.roll(uneven, VR - HALF, 1))
        flat = jnp.where(edge_lane < USED, zbuf[s, :EDGE, :], 0.0)
        other = jnp.where(edge_row % 2 == 0, pltpu.roll(flat, EDGE - 1, 0), -pltpu.roll(flat, 1, 0))
        ecoef[s, 0] = jnp.where(edge_lane < UH, flat, jnp.where(edge_lane < UR, pltpu.roll(flat, UH, 1), 0.0))
        ecoef[s, 1] = jnp.where(
            edge_lane < UH, pltpu.roll(other, VR - UH, 1), jnp.where(edge_lane < UR, other, 0.0)
        )

    stack[...] = jnp.zeros_like(stack)
    load_kr.wait()
    load_ki.wait()
    for ri in range(2):
        for l in range(LOCAL):
            for k in range(KERNELS):
                at = (l * KERNELS + k) * UR
                stack[at : at + KSUP, ri * VR : ri * VR + KSUP] = raw_v[ri, l, :, k, :]
    for copy in load_pv:
        copy.wait()
    load_pu.wait()
    hi, lo = split(stack[...])
    folded = dot(jnp.concatenate([hi, lo], axis=1), pv[...])
    hi, lo = split(folded)
    coef[:, :, 2:, USED - UH :, :] = jnp.zeros((GROUP, DEPTH, 2, UR - USED, VR), F32)
    load_thresholds.wait()
    for n in range(DEPTH):
        rhs = jnp.concatenate([hi[n * UR : (n + 1) * UR], lo[n * UR : (n + 1) * UR]], axis=0)
        value = dot(pu[...], rhs)
        zbuf[0, EDGE + n * USED : EDGE + (n + 1) * USED, :] = value[:USED, :VR]
        for ri in range(2):
            flat = jnp.sum(jnp.where(diagonal, value[:, VR + ri : VR + ri + 1], 0.0), axis=0, keepdims=True)
            if 2 * n + ri < LOCAL:
                flat = jnp.where(lane[:1] == VR - 1, thresholds_s[2 * n + ri], flat)
            zbuf[0, 2 * n + ri : 2 * n + ri + 1, :] = flat

    load_theta.wait()
    load_by.wait()
    load_turned.wait()
    mask_rows = jnp.tanh(MASK_STEEP * theta_v[...])
    hi, lo = split(mask_rows)
    wide = dot(jnp.concatenate([hi, lo], axis=0), by[...])
    column = wide[:ROWS, :VR] + wide[:ROWS, VR:] + wide[ROWS:, :VR]
    hi, lo = split(column)
    both = dot(turned[...], jnp.concatenate([hi, lo], axis=0))
    rown[...] = packed(both[:UR] + both[UR : 2 * UR])
    rhalo[...] = packed(both[2 * UR : 3 * UR] + both[3 * UR :])

    edge_of = (has_next & final) | (has_prev & first)
    pl.semaphore_wait(barrier, jnp.where(edge_of, 2 * GROUP, GROUP))

    def remote(src, dst, send, recv, device):
        return pltpu.make_async_remote_copy(
            src_ref=src, dst_ref=dst, send_sem=send, recv_sem=recv, device_id=device, device_id_type=MESH
        )

    def halo_next(other):
        return remote(rhalo, rin.at[3], hs_sem.at[other], hr_sem.at[0], (t + 1, other))

    def halo_prev(other):
        return remote(rhalo, rin.at[4], hs_sem.at[other], hr_sem.at[1], (t - 1, other))

    def part(mask):
        return remote(rown, rin.at[mask - 1], rs_sem.at[mask - 1], rr_sem.at[mask - 1], partner(mask))

    def kernels_to(mask, chunk):
        device = partner(1) if mask != 2 else mirror
        source = 2 if mask == 3 else 0
        rows = pl.ds(0, CHUNK) if chunk == 0 else pl.ds(CHUNK, WIRE - CHUNK)
        sem = 2 * (mask - 1) + chunk
        return remote(
            zbuf.at[source, rows, :], zbuf.at[mask, rows, :], zs_sem.at[sem], zr_sem.at[sem], device
        )

    @pl.when(has_next & final)
    def _():
        for other in range(GROUP):
            halo_next(other).start()

    @pl.when(has_prev & first)
    def _():
        for other in range(GROUP):
            halo_prev(other).start()

    for mask in range(1, GROUP):
        part(mask).start()
    for mask in (2, 1):
        for chunk in range(2):
            kernels_to(mask, chunk).start()

    @pl.when(jnp.logical_not(has_prev))
    def _():
        rin[3] = jnp.zeros((UH, VR), F32)

    @pl.when(jnp.logical_not(has_next))
    def _():
        rin[4] = jnp.zeros((UH, VR), F32)

    unpack_kernels(0)
    for chunk in range(2):
        kernels_to(1, chunk).wait_recv()
    unpack_kernels(1)
    for chunk in range(2):
        kernels_to(2, chunk).wait_recv()
        kernels_to(3, chunk).start()
    unpack_kernels(2)

    @pl.when(has_prev)
    def _():
        halo_next(0).wait_recv()

    @pl.when(has_next)
    def _():
        halo_prev(0).wait_recv()

    for mask in range(1, GROUP):
        part(mask).wait_recv()

    total = rown[...] + rin[0] + rin[1] + rin[2] + rin[3] + rin[4]
    total = total * (1.0 / (SIZE * SIZE))
    keep = row < SPARE
    turn = pltpu.roll(total, FLAT, 1)
    halves = [
        jnp.where(keep, jnp.where(lane < FLAT, total, turn), 0.0),
        jnp.where(keep, jnp.where(lane < FLAT, turn, total), 0.0),
    ]
    for h in range(2):
        sign_u = 1.0 - 2.0 * h
        rsum[0, h] = halves[h]
        rsum[1, h] = sign_i * sign_v * swap(halves[h])
        rsum[2, h] = sign_u * sign_i * halves[1 - h]
        rsum[3, h] = (-sign_u) * sign_v * swap(halves[1 - h])
    flat = jnp.where(edge_lane < UR, total[SPARE : SPARE + 1], 0.0)
    erow[0] = flat
    erow[1] = turned_edge(flat)

    load_pack.wait()
    load_sample.wait()
    for copy in load_fine:
        copy.wait()
    block_lane = lax.broadcasted_iota(jnp.int32, (ROWS, VR), 1)

    def grids_and_rows(s):
        grids = []
        for n in range(DEPTH):
            grid = []
            for h in range(2):
                terms = [coef[s, n, m] * rsum[m, h] for m in range(4)]
                grid.append((terms[0] + terms[1]) + (terms[2] + terms[3]))
            grids.append(jnp.concatenate(grid, axis=0))
        cross = [None] * LOCAL
        for l in range(LOCAL):
            hi, lo = split(jnp.concatenate(grids[KERNELS * l : KERNELS * (l + 1)], axis=1))
            tall = dot(pack[:, : 3 * UR], jnp.concatenate([hi, hi, lo], axis=0))
            for k in range(KERNELS):
                part = tall[:, k * VR : (k + 1) * VR]
                at = (l * KERNELS + k) * ROWS
                other = jnp.where(block_lane % FLAT == HALF - 1, pltpu.roll(part, VR - HALF, 1), 0.0)
                other = jnp.where(block_lane % FLAT == FLAT - 1, pltpu.roll(part, HALF, 1), other)
                crossed[s, at : at + ROWS, :] = other
                other = part * other
                cross[l] = other if k == 0 else cross[l] + other
                hi, lo = split(part)
                rows_v[s % 2, at : at + ROWS, :VR] = hi
                rows_v[s % 2, at : at + ROWS, VR:] = lo
        for l in range(LOCAL):
            near = cross[l].astype(BF).astype(F32)
            far = pltpu.roll(cross[l] - near, VR - 1, 1)
            edge_v[s % 2, l * ROWS : (l + 1) * ROWS, :] = jnp.where(block_lane % FLAT == HALF - 2, far, near).astype(BF)
        flat = stacked(ecoef[s, 0] * erow[0] + ecoef[s, 1] * erow[1])
        upper = dot(flat, turned[:VR, :ROWS])
        lower = dot(flat, turned[UR : UR + VR, :ROWS])
        flat_v[s % 2] = (upper[:EDGE] + upper[EDGE:] + lower[:EDGE]).T

    def resist_of(s):
        amp = dot(jnp.concatenate([rows_v[s % 2], rows_v[s % 2, :, :VR]], axis=1), sample[...])
        lhs = []
        for l in range(LOCAL):
            sampled = None
            for k in range(KERNELS):
                n = l * KERNELS + k
                for ri in range(2):
                    piece = amp[n * ROWS : (n + 1) * ROWS, ri * GRID : (ri + 1) * GRID]
                    piece = piece + flat_v[s % 2, :, 2 * n + ri : 2 * n + ri + 1]
                    amps[s, n * ROWS : (n + 1) * ROWS, ri * GRID : (ri + 1) * GRID] = piece
                    sampled = piece * piece if k + ri == 0 else sampled + piece * piece
            hi, lo = split(sampled)
            lhs.append(jnp.concatenate([hi, lo, hi, edge_v[s % 2, l * ROWS : (l + 1) * ROWS, :]], axis=1))
        intensities = dot(jnp.concatenate(lhs, axis=0), fine[...])
        total = None
        for l in range(LOCAL):
            intensity = intensities[l * ROWS : (l + 1) * ROWS]
            level = zbuf[s, l : l + 1, VR - 1 : VR]
            resist = jax.nn.sigmoid(RESIST_STEEP * (intensity - level))
            resists[s, l] = resist
            total = resist if l == 0 else total + resist
        if s == 0:
            band[...] = total
        else:
            band[...] += total

    grids_and_rows(0)
    resist_of(0)
    grids_and_rows(1)
    resist_of(1)
    grids_and_rows(2)
    for chunk in range(2):
        kernels_to(3, chunk).wait_recv()
    unpack_kernels(3)
    resist_of(2)
    grids_and_rows(3)
    resist_of(3)

    load_target.wait()
    load_weights.wait()
    weight_sum = weights_s[0]
    for n in range(1, CONDS):
        weight_sum = weight_sum + weights_s[n]
    weight_sum = jnp.full((8, TP), weight_sum, jnp.int32).astype(F32)
    wanted[...] = target_v[...].astype(F32)
    band[...] = band[...] * (4.0 * RESIST_STEEP * BAND_WEIGHT / CONDS / CONDS)

    load_coarse.wait()
    load_half.wait()
    load_gather.wait()

    def push_of(s):
        fields = []
        for l in range(LOCAL):
            weight = jnp.full((8, TP), weights_s[(c ^ s) * LOCAL + l], jnp.int32).astype(F32) / weight_sum
            pull = (4.0 * RESIST_STEEP) * weight[0:1]
            resist = resists[s, l]
            slope = (pull + 4.0 * RESIST_STEEP * BAND_WEIGHT / CONDS) * resist - (pull * wanted[...] + band[...])
            field = slope * (resist - resist * resist)
            last = jnp.sum(field * half_last[0:1, :], axis=1, keepdims=True)
            last_v[s % 2, l * ROWS : (l + 1) * ROWS, :] = jnp.broadcast_to(last, (ROWS, VR))
            fields.append(field)
        hi, lo = split(jnp.concatenate(fields, axis=0))
        wide = dot(jnp.concatenate([hi, lo], axis=0), coarse[...])
        half = LOCAL * ROWS
        push_v[s % 2] = wide[:half, :GRID] + wide[:half, GRID:] + wide[half:, :GRID]

    def adjoint_of(s):
        rows = []
        flat = jnp.zeros((ROWS, VR), F32)
        for n in range(DEPTH):
            push = push_v[s % 2, n // KERNELS * ROWS : (n // KERNELS + 1) * ROWS, :]
            drive = []
            for ri in range(2):
                piece = push * amps[s, n * ROWS : (n + 1) * ROWS, ri * GRID : (ri + 1) * GRID]
                flat = jnp.where(block_lane == 2 * n + ri, jnp.sum(piece, axis=1, keepdims=True), flat)
                drive.append(piece)
            hi, lo = split(jnp.concatenate(drive, axis=1))
            rows.append(jnp.concatenate([hi, lo], axis=1))
        drive = dot(jnp.concatenate(rows, axis=0), gather[...])
        drive = drive[:, :VR] + drive[:, VR:]
        sums = [[None, None] for _ in range(4)]
        for l in range(LOCAL):
            pair = []
            for n in (KERNELS * l, KERNELS * l + 1):
                last = last_v[s % 2, l * ROWS : (l + 1) * ROWS, :]
                pair.append(drive[n * ROWS : (n + 1) * ROWS] + last * crossed[s, n * ROWS : (n + 1) * ROWS, :])
            hi, lo = split(jnp.concatenate(pair, axis=1))
            back = dot(turned[: 2 * UR, :], jnp.concatenate([hi, lo], axis=0))
            back = back[:UR] + back[UR:]
            for k in range(KERNELS):
                for h in range(2):
                    value = back[h * UH : (h + 1) * UH, k * VR : (k + 1) * VR]
                    for m in range(4):
                        term = coef[s, l * KERNELS + k, m] * value
                        sums[m][h] = term if l + k == 0 else sums[m][h] + term
        for m in range(4):
            for h in range(2):
                if s == 0:
                    jbuf[m, h] = sums[m][h]
                else:
                    jbuf[m, h] += sums[m][h]
        wide = dot(stacked(flat.T[:EDGE]), pack[:, : 2 * VR])
        here = wide[:EDGE, :VR] + wide[EDGE:, :VR]
        upper = pltpu.roll(wide[:EDGE, :VR], VR - UR, 1)
        lower = pltpu.roll(wide[:EDGE, VR:], VR - UR, 1)
        here = here + jnp.where(edge_lane < VR - UR, upper, lower)
        term = ecoef[s, 0] * here - ecoef[s, 1] * turned_edge(here)
        if s == 0:
            jflat[...] = term
        else:
            jflat[...] += term

    push_of(0)
    for s in range(1, GROUP):
        adjoint_of(s - 1)
        push_of(s)
    adjoint_of(GROUP - 1)

    def folded_part(m, h):
        sign = 1.0 if m in (0, 3) else -1.0
        return jbuf[m, h] + sign * pltpu.roll(jbuf[m, h], FLAT, 1)

    halves = []
    for h in range(2):
        sign_u = 1.0 - 2.0 * h
        halves.append(
            folded_part(0, h)
            + swap(sign_v * folded_part(1, h))
            - sign_u * folded_part(2, 1 - h)
            + swap(sign_u * sign_v * folded_part(3, 1 - h))
        )
    value = jnp.where(lane < FLAT, halves[0], pltpu.roll(halves[1], FLAT, 1))
    aown[...] = jnp.where(row == SPARE, jnp.sum(jflat[...], axis=0, keepdims=True), value)

    def adjoint_part(mask):
        return remote(aown, ain.at[mask - 1], as_sem.at[mask - 1], ar_sem.at[mask - 1], partner(mask))

    def adjoint_prev():
        return remote(aown, anear.at[c], as_sem.at[3], near_sem.at[c], (t - 1, GROUP - 1))

    def adjoint_next():
        return remote(aown, anear.at[c], as_sem.at[4], near_sem.at[c], (t + 1, 0))

    def adjoint_near(other):
        return remote(aown, anear.at[other], as_sem.at[3], near_sem.at[other], (t, c ^ 1))

    @pl.when(has_prev)
    def _():
        adjoint_prev().start()

    @pl.when(has_next)
    def _():
        adjoint_next().start()

    for mask in range(1, GROUP):
        adjoint_part(mask).start()

    near = (first & has_prev) | (final & has_next)

    @pl.when(jnp.logical_not(near))
    def _():
        anear[...] = jnp.zeros_like(anear)

    factor[...] = (MASK_STEEP / (SIZE * SIZE)) * (1.0 - jnp.square(jnp.tanh(MASK_STEEP * theta_v[...])))

    for mask in range(1, GROUP):
        adjoint_part(mask).wait_recv()

    @pl.when(near)
    def _():
        for other in range(GROUP):
            adjoint_near(other).wait_recv()

    for copy in load_bt:
        copy.wait()
    rows = []
    for value in (aown[...] + ain[0] + ain[1] + ain[2], anear[0] + anear[1] + anear[2] + anear[3]):
        hi, lo = split(jnp.concatenate(unpacked(value), axis=0))
        rows += [hi, hi, lo, jnp.zeros((256 - 3 * UR, VR), BF)]
    tall = dot(pack[...], jnp.concatenate(rows, axis=0))
    hi, lo = split(tall)
    out_v[...] = dot(jnp.concatenate([hi, lo, hi], axis=1), bt[...]) * factor[...]

    @pl.when(has_next & final)
    def _():
        for other in range(GROUP):
            halo_next(other).wait_send()

    @pl.when(has_prev & first)
    def _():
        for other in range(GROUP):
            halo_prev(other).wait_send()

    for mask in range(1, GROUP):
        part(mask).wait_send()
        for chunk in range(2):
            kernels_to(mask, chunk).wait_send()
        adjoint_part(mask).wait_send()

    @pl.when(has_prev)
    def _():
        adjoint_prev().wait_send()

    @pl.when(has_next)
    def _():
        adjoint_next().wait_send()


def shards(tiles, theta, target, kernel_real, kernel_imag, weights, thresholds):
    constants = tables()
    dma = pltpu.SemaphoreType.DMA
    by, bt, pack, turned, pv, pu, sample, gather, fine, coarse, half_last = constants
    call = pl.pallas_call(
        functools.partial(kernel, tiles),
        out_shape=jax.ShapeDtypeStruct((ROWS, TP), F32),
        in_specs=[pl.BlockSpec(memory_space=pltpu.HBM)] * 17,
        out_specs=pl.BlockSpec(memory_space=pltpu.VMEM),
        scratch_shapes=[
            pltpu.SMEM((CONDS,), jnp.int32),
            pltpu.SMEM((LOCAL,), F32),
            pltpu.VMEM((ROWS, TP), F32),
            pltpu.VMEM((ROWS, TP), jnp.int32),
            pltpu.VMEM((2, LOCAL, KSUP, KERNELS, KSUP), F32),
            pltpu.VMEM(by.shape, BF),
            pltpu.VMEM((3 * VR, TP), BF),
            pltpu.VMEM(pack.shape[1:], BF),
            pltpu.VMEM(turned.shape[1:], BF),
            pltpu.VMEM((4 * VR, 2 * VR), BF),
            pltpu.VMEM(pu.shape, BF),
            pltpu.VMEM(sample.shape, BF),
            pltpu.VMEM(gather.shape, BF),
            pltpu.VMEM((4 * GRID, TP), BF),
            pltpu.VMEM(coarse.shape, BF),
            pltpu.VMEM(half_last.shape, F32),
            pltpu.VMEM((DEPTH * UR, 2 * VR), F32),
            pltpu.VMEM((GROUP, WIRE, VR), F32),
            pltpu.VMEM((GROUP, DEPTH, 4, UH, VR), F32),
            pltpu.VMEM((GROUP, 2, EDGE, VR), F32),
            pltpu.VMEM((UH, VR), F32),
            pltpu.VMEM((UH, VR), F32),
            pltpu.VMEM((5, UH, VR), F32),
            pltpu.VMEM((4, 2, UH, VR), F32),
            pltpu.VMEM((2, EDGE, VR), F32),
            pltpu.VMEM((UH, VR), F32),
            pltpu.VMEM((3, UH, VR), F32),
            pltpu.VMEM((GROUP, UH, VR), F32),
            pltpu.VMEM((4, 2, UH, VR), F32),
            pltpu.VMEM((EDGE, VR), F32),
            pltpu.VMEM((GROUP, DEPTH * ROWS, 2 * GRID), F32),
            pltpu.VMEM((GROUP, DEPTH * ROWS, VR), F32),
            pltpu.VMEM((2, DEPTH * ROWS, 2 * VR), BF),
            pltpu.VMEM((2, ROWS, EDGE), F32),
            pltpu.VMEM((2, LOCAL * ROWS, VR), BF),
            pltpu.VMEM((2, LOCAL * ROWS, GRID), F32),
            pltpu.VMEM((2, LOCAL * ROWS, VR), F32),
            pltpu.VMEM((GROUP, LOCAL, ROWS, TP), F32),
            pltpu.VMEM((ROWS, TP), F32),
            pltpu.VMEM((ROWS, TP), F32),
            pltpu.VMEM((ROWS, TP), F32),
            dma((20,)),
            dma((6,)),
            dma((6,)),
            dma((3,)),
            dma((3,)),
            dma((4,)),
            dma((2,)),
            dma((5,)),
            dma((3,)),
            dma((4,)),
        ],
        compiler_params=pltpu.CompilerParams(collective_id=0, has_side_effects=True, vmem_limit_bytes=32 * 1024 * 1024),
        name="window_gradient",
    )
    kernel_real, kernel_imag = (jnp.swapaxes(x, 1, 2) for x in (kernel_real, kernel_imag))
    arrays = (theta, target, kernel_real, kernel_imag, weights, thresholds, *(jnp.asarray(x) for x in constants))
    return call(*(pltpu.with_memory_space_constraint(x, pltpu.HBM) for x in arrays))


def solution(mesh):
    in_specs = (
        P(("tile", "cond"), None),
        P("tile", None),
        P("cond", None, None, None),
        P("cond", None, None, None),
        P(),
        P("cond"),
    )
    out_specs = P(("tile", "cond"), None)
    body = functools.partial(shards, mesh.shape["tile"])
    return jax.shard_map(body, mesh=mesh, in_specs=in_specs, out_specs=out_specs, check_vma=False)
```

```python
import functools
import math

import jax
import jax.numpy as jnp
import ml_dtypes
import numpy as np
from jax import lax
from jax.experimental import pallas as pl
from jax.experimental.pallas import tpu as pltpu
from jax.sharding import PartitionSpec as P

TP = 512
HALO = 32
KSUP = 65
HALF = KSUP // 2
CONDS = 8
KERNELS = 2
SIZE = TP + 2 * HALO
ROWS = 128
GROUP = 4
LOCAL = CONDS // GROUP
UH = 40
UR = 2 * UH
VR = 128
FLAT = 2 * HALF
DEPTH = LOCAL * KERNELS
USED = UH + HALF
EDGE = 2 * DEPTH
CHUNK = EDGE + DEPTH // 2 * USED
WIRE = EDGE + DEPTH * USED
SPAN = DEPTH * ROWS
GRID = 128
SPARE = HALF + 1

MASK_STEEP = 2.0
RESIST_STEEP = 4.0
BAND_WEIGHT = 1.0

BF = jnp.bfloat16
F32 = jnp.float32
MESH = pl.DeviceIdType.MESH


def split(x):
    hi = x.astype(BF)
    return hi, (x - hi.astype(F32)).astype(BF)


def np_split(x):
    hi = x.astype(ml_dtypes.bfloat16)
    return hi, (x - hi.astype(np.float64)).astype(ml_dtypes.bfloat16)


def waves(positions):
    phase = np.fmod(np.asarray(positions, np.float64)[:, None] * np.arange(HALF + 1)[None, :], SIZE)
    angles = phase * (2.0 * math.pi / SIZE)
    return np.cos(angles), np.sin(angles)


def row_basis(positions):
    cos, sin = waves(positions)
    out = np.zeros((len(positions), UR))
    out[:, :HALF] = cos[:, 1:]
    out[:, HALF] = 1.0
    out[:, UH:USED] = sin[:, 1:]
    return out


def column_basis(positions):
    cos, sin = waves(positions)
    out = np.zeros((len(positions), VR))
    out[:, :HALF] = cos[:, 1:]
    out[:, HALF:FLAT] = sin[:, 1:]
    out[:, FLAT] = 1.0
    return out


def parity_rows():
    out = np.zeros((UR, UR))
    out[HALF, HALF] = 1.0
    for j in range(1, HALF + 1):
        out[j - 1, HALF + j] = out[j - 1, HALF - j] = out[UH + j - 1, HALF + j] = 1.0
        out[UH + j - 1, HALF - j] = -1.0
    return out


def parity_columns():
    out = np.zeros((2 * VR, 2 * VR))
    for ri in range(2):
        out[ri * VR + HALF, VR + ri] = 1.0
        for j in range(1, HALF + 1):
            even = ri * FLAT + j - 1
            out[ri * VR + HALF + j, even] = out[ri * VR + HALF - j, even] = 1.0
            out[ri * VR + HALF + j, even + HALF] = 1.0
            out[ri * VR + HALF - j, even + HALF] = -1.0
    return out


def tables():
    bf = ml_dtypes.bfloat16
    cols = column_basis(np.arange(TP) + HALO)
    hi, lo = np_split(cols)
    by = np.concatenate([hi, lo], axis=1)
    bt = np.concatenate([hi.T, lo.T], axis=0)
    places = column_basis(np.arange(GRID) * (SIZE / GRID))
    hi, lo = np_split(places[:, :FLAT])
    sample = np.zeros((3 * VR, 2 * GRID), bf)
    gather = np.zeros((4 * GRID, 2 * VR), bf)
    for ri in range(2):
        for block, part in enumerate((hi, hi, lo)):
            at = block * VR + ri * FLAT
            sample[at : at + FLAT, ri * GRID : (ri + 1) * GRID] = part.T
        gather[ri * GRID : (ri + 1) * GRID, ri * FLAT : (ri + 1) * FLAT] = hi
        gather[ri * GRID : (ri + 1) * GRID, VR + ri * FLAT : VR + (ri + 1) * FLAT] = lo
        gather[(2 + ri) * GRID : (3 + ri) * GRID, ri * FLAT : (ri + 1) * FLAT] = hi
    phase = (np.arange(TP) + HALO) * (2.0 * math.pi / SIZE)
    place = np.arange(GRID) * (2.0 * math.pi / GRID)
    spread = np.ones((GRID, TP))
    for f in range(1, GRID // 2):
        spread += 2.0 * np.cos(f * (phase[None, :] - place[:, None]))
    spread += np.cos(GRID // 2 * place)[:, None] * np.cos(GRID // 2 * phase)[None, :]
    spread /= GRID
    last = np.sin(GRID // 2 * phase)
    hi, lo = np_split(spread)
    last_hi, last_lo = np_split(last)
    rest = np.zeros((VR, TP), bf)
    for at in (0, FLAT):
        rest[at + HALF - 2], rest[at + HALF - 1], rest[at + FLAT - 1] = last_hi, last_hi, last_lo
    fine = np.concatenate([hi, lo, rest], axis=0)
    coarse = np.concatenate([hi.T, lo.T], axis=1)
    half_last = np.broadcast_to(0.5 * last, (8, TP)).astype(np.float32)
    pack = []
    turned = []
    for c in range(GROUP):
        own = row_basis(np.arange(ROWS) + HALO + ROWS * c)
        near = np.zeros_like(own)
        if c == 0:
            near[:HALO] = row_basis(np.arange(HALO) + HALO + TP)
        if c == GROUP - 1:
            near[ROWS - HALO :] = row_basis(np.arange(HALO))
        row = []
        column = []
        for table in (own, near):
            thi, tlo = np_split(table)
            row += [thi, tlo, thi, np.zeros((ROWS, 256 - 3 * UR), bf)]
            column.append(np.concatenate([thi.T, thi.T], axis=1))
            column.append(np.concatenate([tlo.T, np.zeros((UR, ROWS), bf)], axis=1))
        pack.append(np.concatenate(row, axis=1))
        turned.append(np.concatenate(column, axis=0))
    pv = parity_columns().astype(bf)
    pu = parity_rows().astype(bf)
    pu = np.concatenate([pu, pu], axis=1)
    return by, bt, np.stack(pack), np.stack(turned), pv, pu, sample, gather, fine, coarse, half_last


def dot(a, b):
    return jnp.dot(a, b, preferred_element_type=F32)


def kernel(
    tiles,
    theta_h, target_h, kr_h, ki_h, weights_h, thresholds_h, by_h, bt_h, pack_h, turned_h, pv_h, pu_h,
    sample_h, gather_h, fine_h, coarse_h, half_last_h,
    out_v,
    weights_s, thresholds_s, theta_v, target_v, raw_v, by, bt, pack, turned, pv, pu,
    sample, gather, fine, coarse, half_last, stack, zbuf, coef, ecoef, rown, rhalo, rin, rsum, erow, aown, ain, anear, jbuf, jflat, amps, crossed, rows_v, flat_v, edge_v, push_v, last_v, resists, band, wanted, factor,
    load_sem, zs_sem, zr_sem, rs_sem, rr_sem, hs_sem, hr_sem, as_sem, ar_sem, near_sem,
):
    t = lax.axis_index("tile")
    c = lax.axis_index("cond")
    first = c == 0
    final = c == GROUP - 1
    has_prev = t > 0
    has_next = t < tiles - 1

    loads = []

    def load(src, dst):
        copy = pltpu.make_async_copy(src, dst, load_sem.at[len(loads)])
        copy.start()
        loads.append(copy)
        return copy

    load_kr = load(kr_h, raw_v.at[0])
    load_ki = load(ki_h, raw_v.at[1])
    load_pv = [load(pv_h, pv.at[pl.ds(at, 2 * VR), :]) for at in (0, 2 * VR)]
    load_pu = load(pu_h, pu)
    load_thresholds = load(thresholds_h, thresholds_s)
    load_theta = load(theta_h, theta_v)
    load_by = load(by_h, by)
    load_turned = load(turned_h.at[c], turned)
    load_pack = load(pack_h.at[c], pack)
    load_sample = load(sample_h, sample)
    load_fine = [
        load(fine_h.at[pl.ds(0, GRID), :], fine.at[pl.ds(0, GRID), :]),
        load(fine_h, fine.at[pl.ds(GRID, 3 * GRID), :]),
    ]
    load_coarse = load(coarse_h, coarse)
    load_half = load(half_last_h, half_last)
    load_gather = load(gather_h, gather)
    load_bt = [
        load(bt_h.at[pl.ds(0, VR), :], bt.at[pl.ds(0, VR), :]),
        load(bt_h, bt.at[pl.ds(VR, 2 * VR), :]),
    ]
    load_weights = load(weights_h, weights_s)
    load_target = load(target_h.at[pl.ds(pl.multiple_of(c * ROWS, ROWS), ROWS), :], target_v)

    def partner(mask):
        return (t, c ^ mask)

    barrier = pltpu.get_barrier_semaphore()

    def greet(device):
        pl.semaphore_signal(barrier, inc=1, device_id=device, device_id_type=MESH)

    mirror = ((t + tiles // 2) % tiles, c ^ 2)
    for mask in range(1, GROUP):
        greet(partner(mask))
    greet(mirror)

    @pl.when(has_next)
    def _():
        greet((t + 1, 0))

    @pl.when(has_prev)
    def _():
        greet((t - 1, GROUP - 1))

    lane = lax.broadcasted_iota(jnp.int32, (UH, VR), 1)
    row = lax.broadcasted_iota(jnp.int32, (UH, VR), 0)
    tall_lane = lax.broadcasted_iota(jnp.int32, (UR, VR), 1)
    diagonal = tall_lane == lax.broadcasted_iota(jnp.int32, (UR, VR), 0)
    odd = lane % FLAT >= HALF
    sign_v = jnp.where(odd, -1.0, 1.0).astype(F32)
    sign_i = jnp.where(lane >= FLAT, -1.0, 1.0).astype(F32)
    edge_lane = lane[: 2 * DEPTH]
    edge_row = row[: 2 * DEPTH]

    def swap(x):
        return jnp.where(odd, pltpu.roll(x, HALF, 1), pltpu.roll(x, VR - HALF, 1))

    def turned_edge(x):
        out = jnp.where(edge_lane < UH, pltpu.roll(x, VR - UH, 1), -pltpu.roll(x, UH, 1))
        return jnp.where(edge_lane < UR, out, 0.0)

    def stacked(x):
        near = x.astype(BF).astype(F32)
        return jnp.concatenate([near, x - near], axis=0).astype(BF)

    def packed(x):
        out = jnp.where(lane < FLAT, x[:UH], pltpu.roll(x[UH:], FLAT, 1))
        flat = jnp.sum(jnp.where(diagonal, x[:, FLAT : FLAT + 1], 0.0), axis=0, keepdims=True)
        return jnp.where(row == SPARE, flat, out)

    def unpacked(x):
        flat = jnp.sum(jnp.where(diagonal, x[SPARE : SPARE + 1], 0.0), axis=1, keepdims=True)
        keep = (lane < FLAT) & (row < SPARE)
        out = []
        for h, value in enumerate((x, pltpu.roll(x, FLAT, 1))):
            out.append(jnp.where(lane == FLAT, flat[h * UH : (h + 1) * UH], jnp.where(keep, value, 0.0)))
        return out

    def unpack_kernels(s):
        for n in range(DEPTH):
            at = EDGE + n * USED
            even = zbuf[s, at : at + UH, :]
            uneven = zbuf[s, at + UH : at + USED, :]
            odd_rows = odd[: USED - UH]
            coef[s, n, 0] = jnp.where(odd, pltpu.roll(even, HALF, 1), even)
            coef[s, n, 1] = jnp.where(odd, pltpu.roll(even, FLAT, 1), pltpu.roll(even, HALF, 1))
            coef[s, n, 2, : USED - UH] = jnp.where(
                odd_rows, pltpu.roll(uneven, VR - HALF, 1), pltpu.roll(uneven, FLAT, 1)
            )
            coef[s, n, 3, : USED - UH] = jnp.where(odd_rows, uneven, pltpu.roll(uneven, VR - HALF, 1))
        flat = jnp.where(edge_lane < USED, zbuf[s, :EDGE, :], 0.0)
        other = jnp.where(edge_row % 2 == 0, pltpu.roll(flat, EDGE - 1, 0), -pltpu.roll(flat, 1, 0))
        ecoef[s, 0] = jnp.where(edge_lane < UH, flat, jnp.where(edge_lane < UR, pltpu.roll(flat, UH, 1), 0.0))
        ecoef[s, 1] = jnp.where(
            edge_lane < UH, pltpu.roll(other, VR - UH, 1), jnp.where(edge_lane < UR, other, 0.0)
        )

    stack[...] = jnp.zeros_like(stack)
    load_kr.wait()
    load_ki.wait()
    for ri in range(2):
        for l in range(LOCAL):
            for k in range(KERNELS):
                at = (l * KERNELS + k) * UR
                stack[at : at + KSUP, ri * VR : ri * VR + KSUP] = raw_v[ri, l, :, k, :]
    for copy in load_pv:
        copy.wait()
    load_pu.wait()
    hi, lo = split(stack[...])
    folded = dot(jnp.concatenate([hi, lo], axis=1), pv[...])
    hi, lo = split(folded)
    coef[:, :, 2:, USED - UH :, :] = jnp.zeros((GROUP, DEPTH, 2, UR - USED, VR), F32)
    load_thresholds.wait()
    for n in range(DEPTH):
        rhs = jnp.concatenate([hi[n * UR : (n + 1) * UR], lo[n * UR : (n + 1) * UR]], axis=0)
        value = dot(pu[...], rhs)
        zbuf[0, EDGE + n * USED : EDGE + (n + 1) * USED, :] = value[:USED, :VR]
        for ri in range(2):
            flat = jnp.sum(jnp.where(diagonal, value[:, VR + ri : VR + ri + 1], 0.0), axis=0, keepdims=True)
            if 2 * n + ri < LOCAL:
                flat = jnp.where(lane[:1] == VR - 1, thresholds_s[2 * n + ri], flat)
            zbuf[0, 2 * n + ri : 2 * n + ri + 1, :] = flat

    load_theta.wait()
    load_by.wait()
    load_turned.wait()
    mask_rows = jnp.tanh(MASK_STEEP * theta_v[...])
    hi, lo = split(mask_rows)
    wide = dot(jnp.concatenate([hi, lo], axis=0), by[...])
    column = wide[:ROWS, :VR] + wide[:ROWS, VR:] + wide[ROWS:, :VR]
    hi, lo = split(column)
    both = dot(turned[...], jnp.concatenate([hi, lo], axis=0))
    rown[...] = packed(both[:UR] + both[UR : 2 * UR])
    rhalo[...] = packed(both[2 * UR : 3 * UR] + both[3 * UR :])

    edge_of = (has_next & final) | (has_prev & first)
    pl.semaphore_wait(barrier, jnp.where(edge_of, 2 * GROUP, GROUP))

    def remote(src, dst, send, recv, device):
        return pltpu.make_async_remote_copy(
            src_ref=src, dst_ref=dst, send_sem=send, recv_sem=recv, device_id=device, device_id_type=MESH
        )

    def halo_next(other):
        return remote(rhalo, rin.at[3], hs_sem.at[other], hr_sem.at[0], (t + 1, other))

    def halo_prev(other):
        return remote(rhalo, rin.at[4], hs_sem.at[other], hr_sem.at[1], (t - 1, other))

    def part(mask):
        return remote(rown, rin.at[mask - 1], rs_sem.at[mask - 1], rr_sem.at[mask - 1], partner(mask))

    def kernels_to(mask, chunk):
        device = partner(1) if mask != 2 else mirror
        source = 2 if mask == 3 else 0
        rows = pl.ds(0, CHUNK) if chunk == 0 else pl.ds(CHUNK, WIRE - CHUNK)
        sem = 2 * (mask - 1) + chunk
        return remote(
            zbuf.at[source, rows, :], zbuf.at[mask, rows, :], zs_sem.at[sem], zr_sem.at[sem], device
        )

    @pl.when(has_next & final)
    def _():
        for other in range(GROUP):
            halo_next(other).start()

    @pl.when(has_prev & first)
    def _():
        for other in range(GROUP):
            halo_prev(other).start()

    for mask in range(1, GROUP):
        part(mask).start()
    for mask in (2, 1):
        for chunk in range(2):
            kernels_to(mask, chunk).start()

    @pl.when(jnp.logical_not(has_prev))
    def _():
        rin[3] = jnp.zeros((UH, VR), F32)

    @pl.when(jnp.logical_not(has_next))
    def _():
        rin[4] = jnp.zeros((UH, VR), F32)

    unpack_kernels(0)
    for chunk in range(2):
        kernels_to(1, chunk).wait_recv()
    unpack_kernels(1)
    kernels_to(2, 0).wait_recv()
    kernels_to(3, 0).start()

    @pl.when(has_prev)
    def _():
        halo_next(0).wait_recv()

    @pl.when(has_next)
    def _():
        halo_prev(0).wait_recv()

    for mask in range(1, GROUP):
        part(mask).wait_recv()

    total = rown[...] + rin[0] + rin[1] + rin[2] + rin[3] + rin[4]
    total = total * (1.0 / (SIZE * SIZE))
    keep = row < SPARE
    turn = pltpu.roll(total, FLAT, 1)
    halves = [
        jnp.where(keep, jnp.where(lane < FLAT, total, turn), 0.0),
        jnp.where(keep, jnp.where(lane < FLAT, turn, total), 0.0),
    ]
    for h in range(2):
        sign_u = 1.0 - 2.0 * h
        rsum[0, h] = halves[h]
        rsum[1, h] = sign_i * sign_v * swap(halves[h])
        rsum[2, h] = sign_u * sign_i * halves[1 - h]
        rsum[3, h] = (-sign_u) * sign_v * swap(halves[1 - h])
    flat = jnp.where(edge_lane < UR, total[SPARE : SPARE + 1], 0.0)
    erow[0] = flat
    erow[1] = turned_edge(flat)

    load_pack.wait()
    load_sample.wait()
    for copy in load_fine:
        copy.wait()
    block_lane = lax.broadcasted_iota(jnp.int32, (ROWS, VR), 1)

    def grids_and_rows(s):
        grids = []
        for n in range(DEPTH):
            grid = []
            for h in range(2):
                terms = [coef[s, n, m] * rsum[m, h] for m in range(4)]
                grid.append((terms[0] + terms[1]) + (terms[2] + terms[3]))
            grids.append(jnp.concatenate(grid, axis=0))
        cross = [None] * LOCAL
        for l in range(LOCAL):
            hi, lo = split(jnp.concatenate(grids[KERNELS * l : KERNELS * (l + 1)], axis=1))
            tall = dot(pack[:, : 3 * UR], jnp.concatenate([hi, hi, lo], axis=0))
            for k in range(KERNELS):
                part = tall[:, k * VR : (k + 1) * VR]
                at = (l * KERNELS + k) * ROWS
                other = jnp.where(block_lane % FLAT == HALF - 1, pltpu.roll(part, VR - HALF, 1), 0.0)
                other = jnp.where(block_lane % FLAT == FLAT - 1, pltpu.roll(part, HALF, 1), other)
                crossed[s, at : at + ROWS, :] = other
                other = part * other
                cross[l] = other if k == 0 else cross[l] + other
                hi, lo = split(part)
                rows_v[s // 2, s % 2 * SPAN + at : s % 2 * SPAN + at + ROWS, :VR] = hi
                rows_v[s // 2, s % 2 * SPAN + at : s % 2 * SPAN + at + ROWS, VR:] = lo
        for l in range(LOCAL):
            near = cross[l].astype(BF).astype(F32)
            far = pltpu.roll(cross[l] - near, VR - 1, 1)
            edge_v[s, l * ROWS : (l + 1) * ROWS, :] = jnp.where(block_lane % FLAT == HALF - 2, far, near).astype(BF)
        flat = stacked(ecoef[s, 0] * erow[0] + ecoef[s, 1] * erow[1])
        upper = dot(flat, turned[:VR, :ROWS])
        lower = dot(flat, turned[UR : UR + VR, :ROWS])
        flat_v[s] = (upper[:EDGE] + upper[EDGE:] + lower[:EDGE]).T

    def resist_of(slots):
        held = slots[0] // 2
        amp = dot(jnp.concatenate([rows_v[held], rows_v[held, :, :VR]], axis=1), sample[...])
        lhs = []
        for s in slots:
            for l in range(LOCAL):
                sampled = None
                for k in range(KERNELS):
                    n = l * KERNELS + k
                    at = s % 2 * SPAN + n * ROWS
                    for ri in range(2):
                        piece = amp[at : at + ROWS, ri * GRID : (ri + 1) * GRID]
                        piece = piece + flat_v[s, :, 2 * n + ri : 2 * n + ri + 1]
                        amps[s, n * ROWS : (n + 1) * ROWS, ri * GRID : (ri + 1) * GRID] = piece
                        sampled = piece * piece if k + ri == 0 else sampled + piece * piece
                hi, lo = split(sampled)
                lhs.append(jnp.concatenate([hi, lo, hi, edge_v[s, l * ROWS : (l + 1) * ROWS, :]], axis=1))
        intensities = dot(jnp.concatenate(lhs, axis=0), fine[...])
        total = None
        for s in slots:
            for l in range(LOCAL):
                at = (s % 2 * LOCAL + l) * ROWS
                level = zbuf[s, l : l + 1, VR - 1 : VR]
                resist = jax.nn.sigmoid(RESIST_STEEP * (intensities[at : at + ROWS] - level))
                resists[s, l] = resist
                total = resist if total is None else total + resist
        if slots[0] == 0:
            band[...] = total
        else:
            band[...] += total

    grids_and_rows(0)
    grids_and_rows(1)
    kernels_to(2, 1).wait_recv()
    kernels_to(3, 1).start()
    unpack_kernels(2)
    resist_of((0, 1))
    grids_and_rows(2)
    for chunk in range(2):
        kernels_to(3, chunk).wait_recv()
    unpack_kernels(3)
    grids_and_rows(3)
    resist_of((2, 3))

    load_target.wait()
    load_weights.wait()
    weight_sum = weights_s[0]
    for n in range(1, CONDS):
        weight_sum = weight_sum + weights_s[n]
    weight_sum = jnp.full((8, TP), weight_sum, jnp.int32).astype(F32)
    wanted[...] = target_v[...].astype(F32)
    band[...] = band[...] * (4.0 * RESIST_STEEP * BAND_WEIGHT / CONDS / CONDS)

    load_coarse.wait()
    load_half.wait()
    load_gather.wait()

    def push_of(slots):
        fields = []
        for s in slots:
            for l in range(LOCAL):
                weight = jnp.full((8, TP), weights_s[(c ^ s) * LOCAL + l], jnp.int32).astype(F32) / weight_sum
                pull = (4.0 * RESIST_STEEP) * weight[0:1]
                resist = resists[s, l]
                slope = (pull + 4.0 * RESIST_STEEP * BAND_WEIGHT / CONDS) * resist - (pull * wanted[...] + band[...])
                field = slope * (resist - resist * resist)
                last = jnp.sum(field * half_last[0:1, :], axis=1, keepdims=True)
                last_v[s, l * ROWS : (l + 1) * ROWS, :] = jnp.broadcast_to(last, (ROWS, VR))
                fields.append(field)
        hi, lo = split(jnp.concatenate(fields, axis=0))
        wide = dot(jnp.concatenate([hi, lo], axis=0), coarse[...])
        half = 2 * LOCAL * ROWS
        push_v[slots[0] // 2] = wide[:half, :GRID] + wide[:half, GRID:] + wide[half:, :GRID]

    def adjoint_of(slots):
        rows = []
        flats = []
        for s in slots:
            flat = []
            for n in range(DEPTH):
                at = (s % 2 * LOCAL + n // KERNELS) * ROWS
                push = push_v[slots[0] // 2, at : at + ROWS, :]
                drive = []
                for ri in range(2):
                    piece = push * amps[s, n * ROWS : (n + 1) * ROWS, ri * GRID : (ri + 1) * GRID]
                    flat.append(jnp.where(block_lane == 2 * n + ri, jnp.sum(piece, axis=1, keepdims=True), 0.0))
                    drive.append(piece)
                hi, lo = split(jnp.concatenate(drive, axis=1))
                rows.append(jnp.concatenate([hi, lo], axis=1))
            while len(flat) > 1:
                flat = [flat[i] + flat[i + 1] for i in range(0, len(flat), 2)]
            flats.append(flat[0])
        drive = dot(jnp.concatenate(rows, axis=0), gather[...])
        drive = drive[:, :VR] + drive[:, VR:]
        sums = [[None, None] for _ in range(4)]
        for s in slots:
            for l in range(LOCAL):
                pair = []
                for n in (KERNELS * l, KERNELS * l + 1):
                    at = s % 2 * SPAN + n * ROWS
                    last = last_v[s, l * ROWS : (l + 1) * ROWS, :]
                    pair.append(drive[at : at + ROWS] + last * crossed[s, n * ROWS : (n + 1) * ROWS, :])
                hi, lo = split(jnp.concatenate(pair, axis=1))
                back = dot(turned[: 2 * UR, :], jnp.concatenate([hi, lo], axis=0))
                back = back[:UR] + back[UR:]
                for k in range(KERNELS):
                    for h in range(2):
                        value = back[h * UH : (h + 1) * UH, k * VR : (k + 1) * VR]
                        for m in range(4):
                            term = coef[s, l * KERNELS + k, m] * value
                            sums[m][h] = term if sums[m][h] is None else sums[m][h] + term
        total = None
        for s, flat in zip(slots, flats):
            wide = dot(stacked(flat.T[:EDGE]), pack[:, : 2 * VR])
            here = wide[:EDGE, :VR] + wide[EDGE:, :VR]
            upper = pltpu.roll(wide[:EDGE, :VR], VR - UR, 1)
            lower = pltpu.roll(wide[:EDGE, VR:], VR - UR, 1)
            here = here + jnp.where(edge_lane < VR - UR, upper, lower)
            term = ecoef[s, 0] * here - ecoef[s, 1] * turned_edge(here)
            total = term if total is None else total + term
        for m in range(4):
            for h in range(2):
                if slots[0] == 0:
                    jbuf[m, h] = sums[m][h]
                else:
                    jbuf[m, h] += sums[m][h]
        if slots[0] == 0:
            jflat[...] = total
        else:
            jflat[...] += total

    push_of((0, 1))
    adjoint_of((0, 1))
    push_of((2, 3))
    adjoint_of((2, 3))

    def folded_part(m, h):
        sign = 1.0 if m in (0, 3) else -1.0
        return jbuf[m, h] + sign * pltpu.roll(jbuf[m, h], FLAT, 1)

    halves = []
    for h in range(2):
        sign_u = 1.0 - 2.0 * h
        halves.append(
            folded_part(0, h)
            + swap(sign_v * folded_part(1, h))
            - sign_u * folded_part(2, 1 - h)
            + swap(sign_u * sign_v * folded_part(3, 1 - h))
        )
    value = jnp.where(lane < FLAT, halves[0], pltpu.roll(halves[1], FLAT, 1))
    aown[...] = jnp.where(row == SPARE, jnp.sum(jflat[...], axis=0, keepdims=True), value)

    def adjoint_part(mask):
        return remote(aown, ain.at[mask - 1], as_sem.at[mask - 1], ar_sem.at[mask - 1], partner(mask))

    def adjoint_prev():
        return remote(aown, anear.at[c], as_sem.at[3], near_sem.at[c], (t - 1, GROUP - 1))

    def adjoint_next():
        return remote(aown, anear.at[c], as_sem.at[4], near_sem.at[c], (t + 1, 0))

    def adjoint_near(other):
        return remote(aown, anear.at[other], as_sem.at[3], near_sem.at[other], (t, c ^ 1))

    @pl.when(has_prev)
    def _():
        adjoint_prev().start()

    @pl.when(has_next)
    def _():
        adjoint_next().start()

    for mask in range(1, GROUP):
        adjoint_part(mask).start()

    near = (first & has_prev) | (final & has_next)

    @pl.when(jnp.logical_not(near))
    def _():
        anear[...] = jnp.zeros_like(anear)

    factor[...] = (MASK_STEEP / (SIZE * SIZE)) * (1.0 - jnp.square(jnp.tanh(MASK_STEEP * theta_v[...])))

    for mask in range(1, GROUP):
        adjoint_part(mask).wait_recv()

    @pl.when(near)
    def _():
        for other in range(GROUP):
            adjoint_near(other).wait_recv()

    for copy in load_bt:
        copy.wait()
    rows = []
    for value in (aown[...] + ain[0] + ain[1] + ain[2], anear[0] + anear[1] + anear[2] + anear[3]):
        hi, lo = split(jnp.concatenate(unpacked(value), axis=0))
        rows += [hi, hi, lo, jnp.zeros((256 - 3 * UR, VR), BF)]
    tall = dot(pack[...], jnp.concatenate(rows, axis=0))
    hi, lo = split(tall)
    out_v[...] = dot(jnp.concatenate([hi, lo, hi], axis=1), bt[...]) * factor[...]

    @pl.when(has_next & final)
    def _():
        for other in range(GROUP):
            halo_next(other).wait_send()

    @pl.when(has_prev & first)
    def _():
        for other in range(GROUP):
            halo_prev(other).wait_send()

    for mask in range(1, GROUP):
        part(mask).wait_send()
        for chunk in range(2):
            kernels_to(mask, chunk).wait_send()
        adjoint_part(mask).wait_send()

    @pl.when(has_prev)
    def _():
        adjoint_prev().wait_send()

    @pl.when(has_next)
    def _():
        adjoint_next().wait_send()


def shards(tiles, theta, target, kernel_real, kernel_imag, weights, thresholds):
    constants = tables()
    dma = pltpu.SemaphoreType.DMA
    by, bt, pack, turned, pv, pu, sample, gather, fine, coarse, half_last = constants
    call = pl.pallas_call(
        functools.partial(kernel, tiles),
        out_shape=jax.ShapeDtypeStruct((ROWS, TP), F32),
        in_specs=[pl.BlockSpec(memory_space=pltpu.HBM)] * 17,
        out_specs=pl.BlockSpec(memory_space=pltpu.VMEM),
        scratch_shapes=[
            pltpu.SMEM((CONDS,), jnp.int32),
            pltpu.SMEM((LOCAL,), F32),
            pltpu.VMEM((ROWS, TP), F32),
            pltpu.VMEM((ROWS, TP), jnp.int32),
            pltpu.VMEM((2, LOCAL, KSUP, KERNELS, KSUP), F32),
            pltpu.VMEM(by.shape, BF),
            pltpu.VMEM((3 * VR, TP), BF),
            pltpu.VMEM(pack.shape[1:], BF),
            pltpu.VMEM(turned.shape[1:], BF),
            pltpu.VMEM((4 * VR, 2 * VR), BF),
            pltpu.VMEM(pu.shape, BF),
            pltpu.VMEM(sample.shape, BF),
            pltpu.VMEM(gather.shape, BF),
            pltpu.VMEM((4 * GRID, TP), BF),
            pltpu.VMEM(coarse.shape, BF),
            pltpu.VMEM(half_last.shape, F32),
            pltpu.VMEM((DEPTH * UR, 2 * VR), F32),
            pltpu.VMEM((GROUP, WIRE, VR), F32),
            pltpu.VMEM((GROUP, DEPTH, 4, UH, VR), F32),
            pltpu.VMEM((GROUP, 2, EDGE, VR), F32),
            pltpu.VMEM((UH, VR), F32),
            pltpu.VMEM((UH, VR), F32),
            pltpu.VMEM((5, UH, VR), F32),
            pltpu.VMEM((4, 2, UH, VR), F32),
            pltpu.VMEM((2, EDGE, VR), F32),
            pltpu.VMEM((UH, VR), F32),
            pltpu.VMEM((3, UH, VR), F32),
            pltpu.VMEM((GROUP, UH, VR), F32),
            pltpu.VMEM((4, 2, UH, VR), F32),
            pltpu.VMEM((EDGE, VR), F32),
            pltpu.VMEM((GROUP, DEPTH * ROWS, 2 * GRID), F32),
            pltpu.VMEM((GROUP, DEPTH * ROWS, VR), F32),
            pltpu.VMEM((2, 2 * SPAN, 2 * VR), BF),
            pltpu.VMEM((GROUP, ROWS, EDGE), F32),
            pltpu.VMEM((GROUP, LOCAL * ROWS, VR), BF),
            pltpu.VMEM((2, 2 * LOCAL * ROWS, GRID), F32),
            pltpu.VMEM((GROUP, LOCAL * ROWS, VR), F32),
            pltpu.VMEM((GROUP, LOCAL, ROWS, TP), F32),
            pltpu.VMEM((ROWS, TP), F32),
            pltpu.VMEM((ROWS, TP), F32),
            pltpu.VMEM((ROWS, TP), F32),
            dma((20,)),
            dma((6,)),
            dma((6,)),
            dma((3,)),
            dma((3,)),
            dma((4,)),
            dma((2,)),
            dma((5,)),
            dma((3,)),
            dma((4,)),
        ],
        compiler_params=pltpu.CompilerParams(collective_id=0, has_side_effects=True, vmem_limit_bytes=32 * 1024 * 1024),
        name="window_gradient",
    )
    kernel_real, kernel_imag = (jnp.swapaxes(x, 1, 2) for x in (kernel_real, kernel_imag))
    arrays = (theta, target, kernel_real, kernel_imag, weights, thresholds, *(jnp.asarray(x) for x in constants))
    return call(*(pltpu.with_memory_space_constraint(x, pltpu.HBM) for x in arrays))


def solution(mesh):
    in_specs = (
        P(("tile", "cond"), None),
        P("tile", None),
        P("cond", None, None, None),
        P("cond", None, None, None),
        P(),
        P("cond"),
    )
    out_specs = P(("tile", "cond"), None)
    body = functools.partial(shards, mesh.shape["tile"])
    return jax.shard_map(body, mesh=mesh, in_specs=in_specs, out_specs=out_specs, check_vma=False)
```

```python
import functools
import math

import jax
import jax.numpy as jnp
import ml_dtypes
import numpy as np
from jax import lax
from jax.experimental import pallas as pl
from jax.experimental.pallas import tpu as pltpu
from jax.sharding import PartitionSpec as P

TP = 512
HALO = 32
KSUP = 65
HALF = KSUP // 2
CONDS = 8
KERNELS = 2
SIZE = TP + 2 * HALO
ROWS = 128
GROUP = 4
LOCAL = CONDS // GROUP
UH = 40
UR = 2 * UH
VR = 128
FLAT = 2 * HALF
DEPTH = LOCAL * KERNELS
USED = UH + HALF
EDGE = 2 * DEPTH
CHUNK = EDGE + DEPTH // 2 * USED
WIRE = EDGE + DEPTH * USED
SPAN = DEPTH * ROWS
GRID = 128
SPARE = HALF + 1

MASK_STEEP = 2.0
RESIST_STEEP = 4.0
BAND_WEIGHT = 1.0

BF = jnp.bfloat16
F32 = jnp.float32
MESH = pl.DeviceIdType.MESH


def split(x):
    hi = x.astype(BF)
    return hi, (x - hi.astype(F32)).astype(BF)


def np_split(x):
    hi = x.astype(ml_dtypes.bfloat16)
    return hi, (x - hi.astype(np.float64)).astype(ml_dtypes.bfloat16)


def waves(positions):
    phase = np.fmod(np.asarray(positions, np.float64)[:, None] * np.arange(HALF + 1)[None, :], SIZE)
    angles = phase * (2.0 * math.pi / SIZE)
    return np.cos(angles), np.sin(angles)


def row_basis(positions):
    cos, sin = waves(positions)
    out = np.zeros((len(positions), UR))
    out[:, :HALF] = cos[:, 1:]
    out[:, HALF] = 1.0
    out[:, UH:USED] = sin[:, 1:]
    return out


def column_basis(positions):
    cos, sin = waves(positions)
    out = np.zeros((len(positions), VR))
    out[:, :HALF] = cos[:, 1:]
    out[:, HALF:FLAT] = sin[:, 1:]
    out[:, FLAT] = 1.0
    return out


def parity_rows():
    out = np.zeros((UR, UR))
    out[HALF, HALF] = 1.0
    for j in range(1, HALF + 1):
        out[j - 1, HALF + j] = out[j - 1, HALF - j] = out[UH + j - 1, HALF + j] = 1.0
        out[UH + j - 1, HALF - j] = -1.0
    return out


def parity_columns():
    out = np.zeros((2 * VR, 2 * VR))
    for ri in range(2):
        out[ri * VR + HALF, VR + ri] = 1.0
        for j in range(1, HALF + 1):
            even = ri * FLAT + j - 1
            out[ri * VR + HALF + j, even] = out[ri * VR + HALF - j, even] = 1.0
            out[ri * VR + HALF + j, even + HALF] = 1.0
            out[ri * VR + HALF - j, even + HALF] = -1.0
    return out


def tables():
    bf = ml_dtypes.bfloat16
    cols = column_basis(np.arange(TP) + HALO)
    hi, lo = np_split(cols)
    by = np.concatenate([hi, lo], axis=1)
    bt = np.concatenate([hi.T, lo.T], axis=0)
    places = column_basis(np.arange(GRID) * (SIZE / GRID))
    hi, lo = np_split(places[:, :FLAT])
    sample = np.zeros((3 * VR, 2 * GRID), bf)
    gather = np.zeros((4 * GRID, 2 * VR), bf)
    for ri in range(2):
        for block, part in enumerate((hi, hi, lo)):
            at = block * VR + ri * FLAT
            sample[at : at + FLAT, ri * GRID : (ri + 1) * GRID] = part.T
        gather[ri * GRID : (ri + 1) * GRID, ri * FLAT : (ri + 1) * FLAT] = hi
        gather[ri * GRID : (ri + 1) * GRID, VR + ri * FLAT : VR + (ri + 1) * FLAT] = lo
        gather[(2 + ri) * GRID : (3 + ri) * GRID, ri * FLAT : (ri + 1) * FLAT] = hi
    phase = (np.arange(TP) + HALO) * (2.0 * math.pi / SIZE)
    place = np.arange(GRID) * (2.0 * math.pi / GRID)
    spread = np.ones((GRID, TP))
    for f in range(1, GRID // 2):
        spread += 2.0 * np.cos(f * (phase[None, :] - place[:, None]))
    spread += np.cos(GRID // 2 * place)[:, None] * np.cos(GRID // 2 * phase)[None, :]
    spread /= GRID
    last = np.sin(GRID // 2 * phase)
    hi, lo = np_split(spread)
    last_hi, last_lo = np_split(last)
    rest = np.zeros((VR, TP), bf)
    for at in (0, FLAT):
        rest[at + HALF - 2], rest[at + HALF - 1], rest[at + FLAT - 1] = last_hi, last_hi, last_lo
    fine = np.concatenate([hi, lo, rest], axis=0)
    coarse = np.concatenate([hi.T, lo.T], axis=1)
    half_last = np.broadcast_to(0.5 * last, (8, TP)).astype(np.float32)
    pack = []
    turned = []
    for c in range(GROUP):
        own = row_basis(np.arange(ROWS) + HALO + ROWS * c)
        near = np.zeros_like(own)
        if c == 0:
            near[:HALO] = row_basis(np.arange(HALO) + HALO + TP)
        if c == GROUP - 1:
            near[ROWS - HALO :] = row_basis(np.arange(HALO))
        row = []
        column = []
        for table in (own, near):
            thi, tlo = np_split(table)
            row += [thi, tlo, thi, np.zeros((ROWS, 256 - 3 * UR), bf)]
            column.append(np.concatenate([thi.T, thi.T], axis=1))
            column.append(np.concatenate([tlo.T, np.zeros((UR, ROWS), bf)], axis=1))
        pack.append(np.concatenate(row, axis=1))
        turned.append(np.concatenate(column, axis=0))
    pv = parity_columns().astype(bf)
    pu = parity_rows().astype(bf)
    pu = np.concatenate([pu, pu], axis=1)
    return by, bt, np.stack(pack), np.stack(turned), pv, pu, sample, gather, fine, coarse, half_last


def dot(a, b):
    return jnp.dot(a, b, preferred_element_type=F32)


def kernel(
    tiles,
    theta_h, target_h, kr_h, ki_h, weights_h, thresholds_h, by_h, bt_h, pack_h, turned_h, pv_h, pu_h,
    sample_h, gather_h, fine_h, coarse_h, half_last_h,
    out_v,
    weights_s, thresholds_s, theta_v, target_v, raw_v, by, bt, pack, turned, pv, pu,
    sample, gather, fine, coarse, half_last, stack, zbuf, coef, ecoef, passed, rown, rhalo, rin, rsum, erow, aown, ain, anear, jbuf, jflat, amps, crossed, rows_v, flat_v, edge_v, push_v, last_v, resists, band, wanted, factor,
    load_sem, zs_sem, zr_sem, rs_sem, rr_sem, hs_sem, hr_sem, as_sem, ar_sem, near_sem, pass_sem,
):
    t = lax.axis_index("tile")
    c = lax.axis_index("cond")
    first = c == 0
    final = c == GROUP - 1
    has_prev = t > 0
    has_next = t < tiles - 1

    loads = []

    def load(src, dst):
        copy = pltpu.make_async_copy(src, dst, load_sem.at[len(loads)])
        copy.start()
        loads.append(copy)
        return copy

    load_kr = load(kr_h, raw_v.at[0])
    load_ki = load(ki_h, raw_v.at[1])
    load_pv = [load(pv_h, pv.at[pl.ds(at, 2 * VR), :]) for at in (0, 2 * VR)]
    load_pu = load(pu_h, pu)
    load_thresholds = load(thresholds_h, thresholds_s)
    load_theta = load(theta_h, theta_v)
    load_by = load(by_h, by)
    load_turned = load(turned_h.at[c], turned)
    load_pack = load(pack_h.at[c], pack)
    load_sample = load(sample_h, sample)
    load_fine = [
        load(fine_h.at[pl.ds(0, GRID), :], fine.at[pl.ds(0, GRID), :]),
        load(fine_h, fine.at[pl.ds(GRID, 3 * GRID), :]),
    ]
    load_coarse = load(coarse_h, coarse)
    load_half = load(half_last_h, half_last)
    load_gather = load(gather_h, gather)
    load_bt = [
        load(bt_h.at[pl.ds(0, VR), :], bt.at[pl.ds(0, VR), :]),
        load(bt_h, bt.at[pl.ds(VR, 2 * VR), :]),
    ]
    load_weights = load(weights_h, weights_s)
    load_target = load(target_h.at[pl.ds(pl.multiple_of(c * ROWS, ROWS), ROWS), :], target_v)

    def partner(mask):
        return (t, c ^ mask)

    barrier = pltpu.get_barrier_semaphore()

    def greet(device):
        pl.semaphore_signal(barrier, inc=1, device_id=device, device_id_type=MESH)

    mirror = ((t + tiles // 2) % tiles, c ^ 2)
    for mask in range(1, GROUP):
        greet(partner(mask))
    greet(mirror)

    bend = tiles // 2 - 1
    via = (tiles - 4, 1)
    at_bend = t == bend
    after_bend = (t == bend + 1) & first
    relays = (t == via[0]) & (c == via[1])

    @pl.when(has_next)
    def _():
        greet((jnp.where(at_bend, via[0], t + 1), jnp.where(at_bend, via[1], 0)))

    @pl.when(has_prev)
    def _():
        greet((t - 1, GROUP - 1))

    @pl.when(relays)
    def _():
        greet((bend + 1, 0))

    lane = lax.broadcasted_iota(jnp.int32, (UH, VR), 1)
    row = lax.broadcasted_iota(jnp.int32, (UH, VR), 0)
    tall_lane = lax.broadcasted_iota(jnp.int32, (UR, VR), 1)
    diagonal = tall_lane == lax.broadcasted_iota(jnp.int32, (UR, VR), 0)
    odd = lane % FLAT >= HALF
    sign_v = jnp.where(odd, -1.0, 1.0).astype(F32)
    sign_i = jnp.where(lane >= FLAT, -1.0, 1.0).astype(F32)
    edge_lane = lane[: 2 * DEPTH]
    edge_row = row[: 2 * DEPTH]

    def swap(x):
        return jnp.where(odd, pltpu.roll(x, HALF, 1), pltpu.roll(x, VR - HALF, 1))

    def turned_edge(x):
        out = jnp.where(edge_lane < UH, pltpu.roll(x, VR - UH, 1), -pltpu.roll(x, UH, 1))
        return jnp.where(edge_lane < UR, out, 0.0)

    def stacked(x):
        near = x.astype(BF).astype(F32)
        return jnp.concatenate([near, x - near], axis=0).astype(BF)

    def packed(x):
        out = jnp.where(lane < FLAT, x[:UH], pltpu.roll(x[UH:], FLAT, 1))
        flat = jnp.sum(jnp.where(diagonal, x[:, FLAT : FLAT + 1], 0.0), axis=0, keepdims=True)
        return jnp.where(row == SPARE, flat, out)

    def unpacked(x):
        flat = jnp.sum(jnp.where(diagonal, x[SPARE : SPARE + 1], 0.0), axis=1, keepdims=True)
        keep = (lane < FLAT) & (row < SPARE)
        out = []
        for h, value in enumerate((x, pltpu.roll(x, FLAT, 1))):
            out.append(jnp.where(lane == FLAT, flat[h * UH : (h + 1) * UH], jnp.where(keep, value, 0.0)))
        return out

    def unpack_kernels(s):
        for n in range(DEPTH):
            at = EDGE + n * USED
            even = zbuf[s, at : at + UH, :]
            uneven = zbuf[s, at + UH : at + USED, :]
            odd_rows = odd[: USED - UH]
            coef[s, n, 0] = jnp.where(odd, pltpu.roll(even, HALF, 1), even)
            coef[s, n, 1] = jnp.where(odd, pltpu.roll(even, FLAT, 1), pltpu.roll(even, HALF, 1))
            coef[s, n, 2, : USED - UH] = jnp.where(
                odd_rows, pltpu.roll(uneven, VR - HALF, 1), pltpu.roll(uneven, FLAT, 1)
            )
            coef[s, n, 3, : USED - UH] = jnp.where(odd_rows, uneven, pltpu.roll(uneven, VR - HALF, 1))
        flat = jnp.where(edge_lane < USED, zbuf[s, :EDGE, :], 0.0)
        other = jnp.where(edge_row % 2 == 0, pltpu.roll(flat, EDGE - 1, 0), -pltpu.roll(flat, 1, 0))
        ecoef[s, 0] = jnp.where(edge_lane < UH, flat, jnp.where(edge_lane < UR, pltpu.roll(flat, UH, 1), 0.0))
        ecoef[s, 1] = jnp.where(
            edge_lane < UH, pltpu.roll(other, VR - UH, 1), jnp.where(edge_lane < UR, other, 0.0)
        )

    stack[...] = jnp.zeros_like(stack)
    load_kr.wait()
    load_ki.wait()
    for ri in range(2):
        for l in range(LOCAL):
            for k in range(KERNELS):
                at = (l * KERNELS + k) * UR
                stack[at : at + KSUP, ri * VR : ri * VR + KSUP] = raw_v[ri, l, :, k, :]
    for copy in load_pv:
        copy.wait()
    load_pu.wait()
    hi, lo = split(stack[...])
    folded = dot(jnp.concatenate([hi, lo], axis=1), pv[...])
    hi, lo = split(folded)
    coef[:, :, 2:, USED - UH :, :] = jnp.zeros((GROUP, DEPTH, 2, UR - USED, VR), F32)
    load_thresholds.wait()
    for n in range(DEPTH):
        rhs = jnp.concatenate([hi[n * UR : (n + 1) * UR], lo[n * UR : (n + 1) * UR]], axis=0)
        value = dot(pu[...], rhs)
        zbuf[0, EDGE + n * USED : EDGE + (n + 1) * USED, :] = value[:USED, :VR]
        for ri in range(2):
            flat = jnp.sum(jnp.where(diagonal, value[:, VR + ri : VR + ri + 1], 0.0), axis=0, keepdims=True)
            if 2 * n + ri < LOCAL:
                flat = jnp.where(lane[:1] == VR - 1, thresholds_s[2 * n + ri], flat)
            zbuf[0, 2 * n + ri : 2 * n + ri + 1, :] = flat

    load_theta.wait()
    load_by.wait()
    load_turned.wait()
    mask_rows = jnp.tanh(MASK_STEEP * theta_v[...])
    hi, lo = split(mask_rows)
    wide = dot(jnp.concatenate([hi, lo], axis=0), by[...])
    column = wide[:ROWS, :VR] + wide[:ROWS, VR:] + wide[ROWS:, :VR]
    hi, lo = split(column)
    both = dot(turned[...], jnp.concatenate([hi, lo], axis=0))
    rown[...] = packed(both[:UR] + both[UR : 2 * UR])
    rhalo[...] = packed(both[2 * UR : 3 * UR] + both[3 * UR :])

    edge_of = (has_next & final) | (has_prev & first)
    waited = jnp.where(edge_of | relays, 2 * GROUP, GROUP)
    pl.semaphore_wait(barrier, jnp.where(after_bend, GROUP + 1, waited))

    def remote(src, dst, send, recv, device):
        return pltpu.make_async_remote_copy(
            src_ref=src, dst_ref=dst, send_sem=send, recv_sem=recv, device_id=device, device_id_type=MESH
        )

    def halo_next(other):
        return remote(rhalo, rin.at[3], hs_sem.at[other], hr_sem.at[0], (t + 1, other))

    def halo_prev(other):
        return remote(rhalo, rin.at[4], hs_sem.at[other], hr_sem.at[1], (t - 1, other))

    def halo_via():
        return remote(rhalo, passed, hs_sem.at[0], pass_sem, via)

    def halo_passed(other):
        return remote(passed, rin.at[4], hs_sem.at[other], hr_sem.at[1], (bend, other))

    def part(mask):
        return remote(rown, rin.at[mask - 1], rs_sem.at[mask - 1], rr_sem.at[mask - 1], partner(mask))

    def kernels_to(mask, chunk):
        device = partner(1) if mask != 2 else mirror
        source = 2 if mask == 3 else 0
        rows = pl.ds(0, CHUNK) if chunk == 0 else pl.ds(CHUNK, WIRE - CHUNK)
        sem = 2 * (mask - 1) + chunk
        return remote(
            zbuf.at[source, rows, :], zbuf.at[mask, rows, :], zs_sem.at[sem], zr_sem.at[sem], device
        )

    @pl.when(has_next & final)
    def _():
        for other in range(GROUP):
            halo_next(other).start()

    @pl.when(has_prev & first & jnp.logical_not(after_bend))
    def _():
        for other in range(GROUP):
            halo_prev(other).start()

    @pl.when(after_bend)
    def _():
        halo_via().start()

    for mask in range(1, GROUP):
        part(mask).start()
    for mask in (2, 1):
        for chunk in range(2):
            kernels_to(mask, chunk).start()

    @pl.when(relays)
    def _():
        halo_via().wait_recv()
        for other in range(GROUP):
            halo_passed(other).start()

    @pl.when(jnp.logical_not(has_prev))
    def _():
        rin[3] = jnp.zeros((UH, VR), F32)

    @pl.when(jnp.logical_not(has_next))
    def _():
        rin[4] = jnp.zeros((UH, VR), F32)

    unpack_kernels(0)
    for chunk in range(2):
        kernels_to(1, chunk).wait_recv()
    unpack_kernels(1)
    kernels_to(2, 0).wait_recv()
    kernels_to(3, 0).start()

    @pl.when(has_prev)
    def _():
        halo_next(0).wait_recv()

    @pl.when(has_next)
    def _():
        halo_prev(0).wait_recv()

    for mask in range(1, GROUP):
        part(mask).wait_recv()

    total = rown[...] + rin[0] + rin[1] + rin[2] + rin[3] + rin[4]
    total = total * (1.0 / (SIZE * SIZE))
    keep = row < SPARE
    turn = pltpu.roll(total, FLAT, 1)
    halves = [
        jnp.where(keep, jnp.where(lane < FLAT, total, turn), 0.0),
        jnp.where(keep, jnp.where(lane < FLAT, turn, total), 0.0),
    ]
    for h in range(2):
        sign_u = 1.0 - 2.0 * h
        rsum[0, h] = halves[h]
        rsum[1, h] = sign_i * sign_v * swap(halves[h])
        rsum[2, h] = sign_u * sign_i * halves[1 - h]
        rsum[3, h] = (-sign_u) * sign_v * swap(halves[1 - h])
    flat = jnp.where(edge_lane < UR, total[SPARE : SPARE + 1], 0.0)
    erow[0] = flat
    erow[1] = turned_edge(flat)

    load_pack.wait()
    load_sample.wait()
    for copy in load_fine:
        copy.wait()
    block_lane = lax.broadcasted_iota(jnp.int32, (ROWS, VR), 1)

    def grids_and_rows(s):
        grids = []
        for n in range(DEPTH):
            grid = []
            for h in range(2):
                terms = [coef[s, n, m] * rsum[m, h] for m in range(4)]
                grid.append((terms[0] + terms[1]) + (terms[2] + terms[3]))
            grids.append(jnp.concatenate(grid, axis=0))
        cross = [None] * LOCAL
        for l in range(LOCAL):
            hi, lo = split(jnp.concatenate(grids[KERNELS * l : KERNELS * (l + 1)], axis=1))
            tall = dot(pack[:, : 3 * UR], jnp.concatenate([hi, hi, lo], axis=0))
            for k in range(KERNELS):
                part = tall[:, k * VR : (k + 1) * VR]
                at = (l * KERNELS + k) * ROWS
                other = jnp.where(block_lane % FLAT == HALF - 1, pltpu.roll(part, VR - HALF, 1), 0.0)
                other = jnp.where(block_lane % FLAT == FLAT - 1, pltpu.roll(part, HALF, 1), other)
                crossed[s, at : at + ROWS, :] = other
                other = part * other
                cross[l] = other if k == 0 else cross[l] + other
                hi, lo = split(part)
                rows_v[s // 2, s % 2 * SPAN + at : s % 2 * SPAN + at + ROWS, :VR] = hi
                rows_v[s // 2, s % 2 * SPAN + at : s % 2 * SPAN + at + ROWS, VR:] = lo
        for l in range(LOCAL):
            near = cross[l].astype(BF).astype(F32)
            far = pltpu.roll(cross[l] - near, VR - 1, 1)
            edge_v[s, l * ROWS : (l + 1) * ROWS, :] = jnp.where(block_lane % FLAT == HALF - 2, far, near).astype(BF)
        flat = stacked(ecoef[s, 0] * erow[0] + ecoef[s, 1] * erow[1])
        upper = dot(flat, turned[:VR, :ROWS])
        lower = dot(flat, turned[UR : UR + VR, :ROWS])
        flat_v[s] = (upper[:EDGE] + upper[EDGE:] + lower[:EDGE]).T

    def resist_of(slots):
        held = slots[0] // 2
        amp = dot(jnp.concatenate([rows_v[held], rows_v[held, :, :VR]], axis=1), sample[...])
        lhs = []
        for s in slots:
            for l in range(LOCAL):
                sampled = None
                for k in range(KERNELS):
                    n = l * KERNELS + k
                    at = s % 2 * SPAN + n * ROWS
                    for ri in range(2):
                        piece = amp[at : at + ROWS, ri * GRID : (ri + 1) * GRID]
                        piece = piece + flat_v[s, :, 2 * n + ri : 2 * n + ri + 1]
                        amps[s, n * ROWS : (n + 1) * ROWS, ri * GRID : (ri + 1) * GRID] = piece
                        sampled = piece * piece if k + ri == 0 else sampled + piece * piece
                hi, lo = split(sampled)
                lhs.append(jnp.concatenate([hi, lo, hi, edge_v[s, l * ROWS : (l + 1) * ROWS, :]], axis=1))
        intensities = dot(jnp.concatenate(lhs, axis=0), fine[...])
        total = None
        for s in slots:
            for l in range(LOCAL):
                at = (s % 2 * LOCAL + l) * ROWS
                level = zbuf[s, l : l + 1, VR - 1 : VR]
                resist = jax.nn.sigmoid(RESIST_STEEP * (intensities[at : at + ROWS] - level))
                resists[s, l] = resist
                total = resist if total is None else total + resist
        if slots[0] == 0:
            band[...] = total
        else:
            band[...] += total

    grids_and_rows(0)
    grids_and_rows(1)
    kernels_to(2, 1).wait_recv()
    kernels_to(3, 1).start()
    unpack_kernels(2)
    resist_of((0, 1))
    grids_and_rows(2)
    for chunk in range(2):
        kernels_to(3, chunk).wait_recv()
    unpack_kernels(3)
    grids_and_rows(3)
    resist_of((2, 3))

    load_target.wait()
    load_weights.wait()
    weight_sum = weights_s[0]
    for n in range(1, CONDS):
        weight_sum = weight_sum + weights_s[n]
    weight_sum = jnp.full((8, TP), weight_sum, jnp.int32).astype(F32)
    wanted[...] = target_v[...].astype(F32)
    band[...] = band[...] * (4.0 * RESIST_STEEP * BAND_WEIGHT / CONDS / CONDS)

    load_coarse.wait()
    load_half.wait()
    load_gather.wait()

    def push_of(slots):
        fields = []
        for s in slots:
            for l in range(LOCAL):
                weight = jnp.full((8, TP), weights_s[(c ^ s) * LOCAL + l], jnp.int32).astype(F32) / weight_sum
                pull = (4.0 * RESIST_STEEP) * weight[0:1]
                resist = resists[s, l]
                slope = (pull + 4.0 * RESIST_STEEP * BAND_WEIGHT / CONDS) * resist - (pull * wanted[...] + band[...])
                field = slope * (resist - resist * resist)
                last = jnp.sum(field * half_last[0:1, :], axis=1, keepdims=True)
                last_v[s, l * ROWS : (l + 1) * ROWS, :] = jnp.broadcast_to(last, (ROWS, VR))
                fields.append(field)
        hi, lo = split(jnp.concatenate(fields, axis=0))
        wide = dot(jnp.concatenate([hi, lo], axis=0), coarse[...])
        half = 2 * LOCAL * ROWS
        push_v[slots[0] // 2] = wide[:half, :GRID] + wide[:half, GRID:] + wide[half:, :GRID]

    def adjoint_of(slots):
        rows = []
        flats = []
        for s in slots:
            flat = []
            for n in range(DEPTH):
                at = (s % 2 * LOCAL + n // KERNELS) * ROWS
                push = push_v[slots[0] // 2, at : at + ROWS, :]
                drive = []
                for ri in range(2):
                    piece = push * amps[s, n * ROWS : (n + 1) * ROWS, ri * GRID : (ri + 1) * GRID]
                    flat.append(jnp.where(block_lane == 2 * n + ri, jnp.sum(piece, axis=1, keepdims=True), 0.0))
                    drive.append(piece)
                hi, lo = split(jnp.concatenate(drive, axis=1))
                rows.append(jnp.concatenate([hi, lo], axis=1))
            while len(flat) > 1:
                flat = [flat[i] + flat[i + 1] for i in range(0, len(flat), 2)]
            flats.append(flat[0])
        drive = dot(jnp.concatenate(rows, axis=0), gather[...])
        drive = drive[:, :VR] + drive[:, VR:]
        sums = [[None, None] for _ in range(4)]
        for s in slots:
            for l in range(LOCAL):
                pair = []
                for n in (KERNELS * l, KERNELS * l + 1):
                    at = s % 2 * SPAN + n * ROWS
                    last = last_v[s, l * ROWS : (l + 1) * ROWS, :]
                    pair.append(drive[at : at + ROWS] + last * crossed[s, n * ROWS : (n + 1) * ROWS, :])
                hi, lo = split(jnp.concatenate(pair, axis=1))
                back = dot(turned[: 2 * UR, :], jnp.concatenate([hi, lo], axis=0))
                back = back[:UR] + back[UR:]
                for k in range(KERNELS):
                    for h in range(2):
                        value = back[h * UH : (h + 1) * UH, k * VR : (k + 1) * VR]
                        for m in range(4):
                            term = coef[s, l * KERNELS + k, m] * value
                            sums[m][h] = term if sums[m][h] is None else sums[m][h] + term
        total = None
        for s, flat in zip(slots, flats):
            wide = dot(stacked(flat.T[:EDGE]), pack[:, : 2 * VR])
            here = wide[:EDGE, :VR] + wide[EDGE:, :VR]
            upper = pltpu.roll(wide[:EDGE, :VR], VR - UR, 1)
            lower = pltpu.roll(wide[:EDGE, VR:], VR - UR, 1)
            here = here + jnp.where(edge_lane < VR - UR, upper, lower)
            term = ecoef[s, 0] * here - ecoef[s, 1] * turned_edge(here)
            total = term if total is None else total + term
        for m in range(4):
            for h in range(2):
                if slots[0] == 0:
                    jbuf[m, h] = sums[m][h]
                else:
                    jbuf[m, h] += sums[m][h]
        if slots[0] == 0:
            jflat[...] = total
        else:
            jflat[...] += total

    push_of((0, 1))
    adjoint_of((0, 1))
    push_of((2, 3))
    adjoint_of((2, 3))

    def folded_part(m, h):
        sign = 1.0 if m in (0, 3) else -1.0
        return jbuf[m, h] + sign * pltpu.roll(jbuf[m, h], FLAT, 1)

    halves = []
    for h in range(2):
        sign_u = 1.0 - 2.0 * h
        halves.append(
            folded_part(0, h)
            + swap(sign_v * folded_part(1, h))
            - sign_u * folded_part(2, 1 - h)
            + swap(sign_u * sign_v * folded_part(3, 1 - h))
        )
    value = jnp.where(lane < FLAT, halves[0], pltpu.roll(halves[1], FLAT, 1))
    aown[...] = jnp.where(row == SPARE, jnp.sum(jflat[...], axis=0, keepdims=True), value)

    def adjoint_part(mask):
        return remote(aown, ain.at[mask - 1], as_sem.at[mask - 1], ar_sem.at[mask - 1], partner(mask))

    def adjoint_prev():
        return remote(aown, anear.at[c], as_sem.at[3], near_sem.at[c], (t - 1, GROUP - 1))

    def adjoint_next():
        return remote(aown, anear.at[c], as_sem.at[4], near_sem.at[c], (t + 1, 0))

    def adjoint_near(other):
        return remote(aown, anear.at[other], as_sem.at[3], near_sem.at[other], (t, c ^ 1))

    @pl.when(has_prev)
    def _():
        adjoint_prev().start()

    @pl.when(has_next)
    def _():
        adjoint_next().start()

    for mask in range(1, GROUP):
        adjoint_part(mask).start()

    near = (first & has_prev) | (final & has_next)

    @pl.when(jnp.logical_not(near))
    def _():
        anear[...] = jnp.zeros_like(anear)

    factor[...] = (MASK_STEEP / (SIZE * SIZE)) * (1.0 - jnp.square(jnp.tanh(MASK_STEEP * theta_v[...])))

    for mask in range(1, GROUP):
        adjoint_part(mask).wait_recv()

    @pl.when(near)
    def _():
        for other in range(GROUP):
            adjoint_near(other).wait_recv()

    for copy in load_bt:
        copy.wait()
    rows = []
    for value in (aown[...] + ain[0] + ain[1] + ain[2], anear[0] + anear[1] + anear[2] + anear[3]):
        hi, lo = split(jnp.concatenate(unpacked(value), axis=0))
        rows += [hi, hi, lo, jnp.zeros((256 - 3 * UR, VR), BF)]
    tall = dot(pack[...], jnp.concatenate(rows, axis=0))
    hi, lo = split(tall)
    out_v[...] = dot(jnp.concatenate([hi, lo, hi], axis=1), bt[...]) * factor[...]

    @pl.when(has_next & final)
    def _():
        for other in range(GROUP):
            halo_next(other).wait_send()

    @pl.when(has_prev & first & jnp.logical_not(after_bend))
    def _():
        for other in range(GROUP):
            halo_prev(other).wait_send()

    @pl.when(after_bend)
    def _():
        halo_via().wait_send()

    @pl.when(relays)
    def _():
        for other in range(GROUP):
            halo_passed(other).wait_send()

    for mask in range(1, GROUP):
        part(mask).wait_send()
        for chunk in range(2):
            kernels_to(mask, chunk).wait_send()
        adjoint_part(mask).wait_send()

    @pl.when(has_prev)
    def _():
        adjoint_prev().wait_send()

    @pl.when(has_next)
    def _():
        adjoint_next().wait_send()


def shards(tiles, theta, target, kernel_real, kernel_imag, weights, thresholds):
    constants = tables()
    dma = pltpu.SemaphoreType.DMA
    by, bt, pack, turned, pv, pu, sample, gather, fine, coarse, half_last = constants
    call = pl.pallas_call(
        functools.partial(kernel, tiles),
        out_shape=jax.ShapeDtypeStruct((ROWS, TP), F32),
        in_specs=[pl.BlockSpec(memory_space=pltpu.HBM)] * 17,
        out_specs=pl.BlockSpec(memory_space=pltpu.VMEM),
        scratch_shapes=[
            pltpu.SMEM((CONDS,), jnp.int32),
            pltpu.SMEM((LOCAL,), F32),
            pltpu.VMEM((ROWS, TP), F32),
            pltpu.VMEM((ROWS, TP), jnp.int32),
            pltpu.VMEM((2, LOCAL, KSUP, KERNELS, KSUP), F32),
            pltpu.VMEM(by.shape, BF),
            pltpu.VMEM((3 * VR, TP), BF),
            pltpu.VMEM(pack.shape[1:], BF),
            pltpu.VMEM(turned.shape[1:], BF),
            pltpu.VMEM((4 * VR, 2 * VR), BF),
            pltpu.VMEM(pu.shape, BF),
            pltpu.VMEM(sample.shape, BF),
            pltpu.VMEM(gather.shape, BF),
            pltpu.VMEM((4 * GRID, TP), BF),
            pltpu.VMEM(coarse.shape, BF),
            pltpu.VMEM(half_last.shape, F32),
            pltpu.VMEM((DEPTH * UR, 2 * VR), F32),
            pltpu.VMEM((GROUP, WIRE, VR), F32),
            pltpu.VMEM((GROUP, DEPTH, 4, UH, VR), F32),
            pltpu.VMEM((GROUP, 2, EDGE, VR), F32),
            pltpu.VMEM((UH, VR), F32),
            pltpu.VMEM((UH, VR), F32),
            pltpu.VMEM((UH, VR), F32),
            pltpu.VMEM((5, UH, VR), F32),
            pltpu.VMEM((4, 2, UH, VR), F32),
            pltpu.VMEM((2, EDGE, VR), F32),
            pltpu.VMEM((UH, VR), F32),
            pltpu.VMEM((3, UH, VR), F32),
            pltpu.VMEM((GROUP, UH, VR), F32),
            pltpu.VMEM((4, 2, UH, VR), F32),
            pltpu.VMEM((EDGE, VR), F32),
            pltpu.VMEM((GROUP, DEPTH * ROWS, 2 * GRID), F32),
            pltpu.VMEM((GROUP, DEPTH * ROWS, VR), F32),
            pltpu.VMEM((2, 2 * SPAN, 2 * VR), BF),
            pltpu.VMEM((GROUP, ROWS, EDGE), F32),
            pltpu.VMEM((GROUP, LOCAL * ROWS, VR), BF),
            pltpu.VMEM((2, 2 * LOCAL * ROWS, GRID), F32),
            pltpu.VMEM((GROUP, LOCAL * ROWS, VR), F32),
            pltpu.VMEM((GROUP, LOCAL, ROWS, TP), F32),
            pltpu.VMEM((ROWS, TP), F32),
            pltpu.VMEM((ROWS, TP), F32),
            pltpu.VMEM((ROWS, TP), F32),
            dma((20,)),
            dma((6,)),
            dma((6,)),
            dma((3,)),
            dma((3,)),
            dma((4,)),
            dma((2,)),
            dma((5,)),
            dma((3,)),
            dma((4,)),
            dma,
        ],
        compiler_params=pltpu.CompilerParams(collective_id=0, has_side_effects=True, vmem_limit_bytes=32 * 1024 * 1024),
        name="window_gradient",
    )
    kernel_real, kernel_imag = (jnp.swapaxes(x, 1, 2) for x in (kernel_real, kernel_imag))
    arrays = (theta, target, kernel_real, kernel_imag, weights, thresholds, *(jnp.asarray(x) for x in constants))
    return call(*(pltpu.with_memory_space_constraint(x, pltpu.HBM) for x in arrays))


def solution(mesh):
    in_specs = (
        P(("tile", "cond"), None),
        P("tile", None),
        P("cond", None, None, None),
        P("cond", None, None, None),
        P(),
        P("cond"),
    )
    out_specs = P(("tile", "cond"), None)
    body = functools.partial(shards, mesh.shape["tile"])
    return jax.shard_map(body, mesh=mesh, in_specs=in_specs, out_specs=out_specs, check_vma=False)
```

```python
import functools
import math

import jax
import jax.numpy as jnp
import ml_dtypes
import numpy as np
from jax import lax
from jax.experimental import pallas as pl
from jax.experimental.pallas import tpu as pltpu
from jax.sharding import PartitionSpec as P

TP = 512
HALO = 32
KSUP = 65
HALF = KSUP // 2
CONDS = 8
KERNELS = 2
SIZE = TP + 2 * HALO
ROWS = 128
GROUP = 4
LOCAL = CONDS // GROUP
UH = 40
UR = 2 * UH
VR = 128
FLAT = 2 * HALF
DEPTH = LOCAL * KERNELS
USED = UH + HALF
EDGE = 2 * DEPTH
CHUNK = EDGE + DEPTH // 2 * USED
WIRE = EDGE + DEPTH * USED
SPAN = DEPTH * ROWS
GRID = 128
SPARE = HALF + 1

MASK_STEEP = 2.0
RESIST_STEEP = 4.0
BAND_WEIGHT = 1.0

BF = jnp.bfloat16
F32 = jnp.float32
MESH = pl.DeviceIdType.MESH


def split(x):
    hi = x.astype(BF)
    return hi, (x - hi.astype(F32)).astype(BF)


def np_split(x):
    hi = x.astype(ml_dtypes.bfloat16)
    return hi, (x - hi.astype(np.float64)).astype(ml_dtypes.bfloat16)


def waves(positions):
    phase = np.fmod(np.asarray(positions, np.float64)[:, None] * np.arange(HALF + 1)[None, :], SIZE)
    angles = phase * (2.0 * math.pi / SIZE)
    return np.cos(angles), np.sin(angles)


def row_basis(positions):
    cos, sin = waves(positions)
    out = np.zeros((len(positions), UR))
    out[:, :HALF] = cos[:, 1:]
    out[:, HALF] = 1.0
    out[:, UH:USED] = sin[:, 1:]
    return out


def column_basis(positions):
    cos, sin = waves(positions)
    out = np.zeros((len(positions), VR))
    out[:, :HALF] = cos[:, 1:]
    out[:, HALF:FLAT] = sin[:, 1:]
    out[:, FLAT] = 1.0
    return out


def parity_rows():
    out = np.zeros((UR, UR))
    out[HALF, HALF] = 1.0
    for j in range(1, HALF + 1):
        out[j - 1, HALF + j] = out[j - 1, HALF - j] = out[UH + j - 1, HALF + j] = 1.0
        out[UH + j - 1, HALF - j] = -1.0
    return out


def parity_columns():
    out = np.zeros((2 * VR, 2 * VR))
    for ri in range(2):
        out[ri * VR + HALF, VR + ri] = 1.0
        for j in range(1, HALF + 1):
            even = ri * FLAT + j - 1
            out[ri * VR + HALF + j, even] = out[ri * VR + HALF - j, even] = 1.0
            out[ri * VR + HALF + j, even + HALF] = 1.0
            out[ri * VR + HALF - j, even + HALF] = -1.0
    return out


def tables():
    bf = ml_dtypes.bfloat16
    cols = column_basis(np.arange(TP) + HALO)
    hi, lo = np_split(cols)
    by = np.concatenate([hi, lo], axis=1)
    bt = np.concatenate([hi.T, lo.T], axis=0)
    places = column_basis(np.arange(GRID) * (SIZE / GRID))
    hi, lo = np_split(places[:, :FLAT])
    sample = np.zeros((3 * VR, 2 * GRID), bf)
    gather = np.zeros((4 * GRID, 2 * VR), bf)
    for ri in range(2):
        for block, part in enumerate((hi, hi, lo)):
            at = block * VR + ri * FLAT
            sample[at : at + FLAT, ri * GRID : (ri + 1) * GRID] = part.T
        gather[ri * GRID : (ri + 1) * GRID, ri * FLAT : (ri + 1) * FLAT] = hi
        gather[ri * GRID : (ri + 1) * GRID, VR + ri * FLAT : VR + (ri + 1) * FLAT] = lo
        gather[(2 + ri) * GRID : (3 + ri) * GRID, ri * FLAT : (ri + 1) * FLAT] = hi
    phase = (np.arange(TP) + HALO) * (2.0 * math.pi / SIZE)
    place = np.arange(GRID) * (2.0 * math.pi / GRID)
    spread = np.ones((GRID, TP))
    for f in range(1, GRID // 2):
        spread += 2.0 * np.cos(f * (phase[None, :] - place[:, None]))
    spread += np.cos(GRID // 2 * place)[:, None] * np.cos(GRID // 2 * phase)[None, :]
    spread /= GRID
    last = np.sin(GRID // 2 * phase)
    hi, lo = np_split(spread)
    last_hi, last_lo = np_split(last)
    rest = np.zeros((VR, TP), bf)
    for at in (0, FLAT):
        rest[at + HALF - 2], rest[at + HALF - 1], rest[at + FLAT - 1] = last_hi, last_hi, last_lo
    fine = np.concatenate([hi, lo, rest], axis=0)
    coarse = np.concatenate([hi.T, lo.T], axis=1)
    half_last = np.broadcast_to(0.5 * last, (8, TP)).astype(np.float32)
    pack = []
    turned = []
    for c in range(GROUP):
        own = row_basis(np.arange(ROWS) + HALO + ROWS * c)
        near = np.zeros_like(own)
        if c == 0:
            near[:HALO] = row_basis(np.arange(HALO) + HALO + TP)
        if c == GROUP - 1:
            near[ROWS - HALO :] = row_basis(np.arange(HALO))
        row = []
        column = []
        for table in (own, near):
            thi, tlo = np_split(table)
            row += [thi, tlo, thi, np.zeros((ROWS, 256 - 3 * UR), bf)]
            column.append(np.concatenate([thi.T, thi.T], axis=1))
            column.append(np.concatenate([tlo.T, np.zeros((UR, ROWS), bf)], axis=1))
        pack.append(np.concatenate(row, axis=1))
        turned.append(np.concatenate(column, axis=0))
    pv = parity_columns().astype(bf)
    pu = parity_rows().astype(bf)
    pu = np.concatenate([pu, pu], axis=1)
    return by, bt, np.stack(pack), np.stack(turned), pv, pu, sample, gather, fine, coarse, half_last


def dot(a, b):
    return jnp.dot(a, b, preferred_element_type=F32)


def kernel(
    tiles,
    theta_h, target_h, kr_h, ki_h, weights_h, thresholds_h, by_h, bt_h, pack_h, turned_h, pv_h, pu_h,
    sample_h, gather_h, fine_h, coarse_h, half_last_h,
    out_v,
    weights_s, thresholds_s, theta_v, target_v, raw_v, by, bt, pack, turned, pv, pu,
    sample, gather, fine, coarse, half_last, stack, zbuf, coef, ecoef, passed, rown, rhalo, rin, rsum, erow, aown, ain, anear, jbuf, jflat, amps, crossed, rows_v, flat_v, edge_v, push_v, last_v, resists, band, wanted, factor,
    load_sem, zs_sem, zr_sem, rs_sem, rr_sem, hs_sem, hr_sem, as_sem, ar_sem, near_sem, pass_sem,
):
    t = lax.axis_index("tile")
    c = lax.axis_index("cond")
    first = c == 0
    final = c == GROUP - 1
    has_prev = t > 0
    has_next = t < tiles - 1

    loads = []

    def load(src, dst):
        copy = pltpu.make_async_copy(src, dst, load_sem.at[len(loads)])
        copy.start()
        loads.append(copy)
        return copy

    load_kr = load(kr_h, raw_v.at[0])
    load_ki = load(ki_h, raw_v.at[1])
    load_pv = [load(pv_h, pv.at[pl.ds(at, 2 * VR), :]) for at in (0, 2 * VR)]
    load_pu = load(pu_h, pu)
    load_thresholds = load(thresholds_h, thresholds_s)
    load_theta = load(theta_h, theta_v)
    load_by = load(by_h, by)
    load_turned = load(turned_h.at[c], turned)
    load_pack = load(pack_h.at[c], pack)
    load_sample = load(sample_h, sample)
    load_fine = [
        load(fine_h.at[pl.ds(0, GRID), :], fine.at[pl.ds(0, GRID), :]),
        load(fine_h, fine.at[pl.ds(GRID, 3 * GRID), :]),
    ]
    load_coarse = load(coarse_h, coarse)
    load_half = load(half_last_h, half_last)
    load_gather = load(gather_h, gather)
    load_bt = [
        load(bt_h.at[pl.ds(0, VR), :], bt.at[pl.ds(0, VR), :]),
        load(bt_h, bt.at[pl.ds(VR, 2 * VR), :]),
    ]
    load_weights = load(weights_h, weights_s)
    load_target = load(target_h.at[pl.ds(pl.multiple_of(c * ROWS, ROWS), ROWS), :], target_v)

    def partner(mask):
        return (t, c ^ mask)

    barrier = pltpu.get_barrier_semaphore()

    def greet(device):
        pl.semaphore_signal(barrier, inc=1, device_id=device, device_id_type=MESH)

    mirror = ((t + tiles // 2) % tiles, c ^ 2)
    for mask in range(1, GROUP):
        greet(partner(mask))
    greet(mirror)

    bend = tiles // 2 - 1
    between = bend - 3
    at_bend = t == bend
    after_bend = (t == bend + 1) & first
    relays = (t == between) & jnp.logical_not(first | final)

    @pl.when(has_next)
    def _():
        greet((jnp.where(at_bend, between, t + 1), jnp.where(at_bend, 1 + c // 2, 0)))

    @pl.when(has_prev)
    def _():
        greet((t - 1, GROUP - 1))

    @pl.when(relays)
    def _():
        greet((bend + 1, 0))

    lane = lax.broadcasted_iota(jnp.int32, (UH, VR), 1)
    row = lax.broadcasted_iota(jnp.int32, (UH, VR), 0)
    tall_lane = lax.broadcasted_iota(jnp.int32, (UR, VR), 1)
    diagonal = tall_lane == lax.broadcasted_iota(jnp.int32, (UR, VR), 0)
    odd = lane % FLAT >= HALF
    sign_v = jnp.where(odd, -1.0, 1.0).astype(F32)
    sign_i = jnp.where(lane >= FLAT, -1.0, 1.0).astype(F32)
    edge_lane = lane[: 2 * DEPTH]
    edge_row = row[: 2 * DEPTH]

    def swap(x):
        return jnp.where(odd, pltpu.roll(x, HALF, 1), pltpu.roll(x, VR - HALF, 1))

    def turned_edge(x):
        out = jnp.where(edge_lane < UH, pltpu.roll(x, VR - UH, 1), -pltpu.roll(x, UH, 1))
        return jnp.where(edge_lane < UR, out, 0.0)

    def stacked(x):
        near = x.astype(BF).astype(F32)
        return jnp.concatenate([near, x - near], axis=0).astype(BF)

    def packed(x):
        out = jnp.where(lane < FLAT, x[:UH], pltpu.roll(x[UH:], FLAT, 1))
        flat = jnp.sum(jnp.where(diagonal, x[:, FLAT : FLAT + 1], 0.0), axis=0, keepdims=True)
        return jnp.where(row == SPARE, flat, out)

    def unpacked(x):
        flat = jnp.sum(jnp.where(diagonal, x[SPARE : SPARE + 1], 0.0), axis=1, keepdims=True)
        keep = (lane < FLAT) & (row < SPARE)
        out = []
        for h, value in enumerate((x, pltpu.roll(x, FLAT, 1))):
            out.append(jnp.where(lane == FLAT, flat[h * UH : (h + 1) * UH], jnp.where(keep, value, 0.0)))
        return out

    def unpack_kernels(s):
        for n in range(DEPTH):
            at = EDGE + n * USED
            even = zbuf[s, at : at + UH, :]
            uneven = zbuf[s, at + UH : at + USED, :]
            odd_rows = odd[: USED - UH]
            coef[s, n, 0] = jnp.where(odd, pltpu.roll(even, HALF, 1), even)
            coef[s, n, 1] = jnp.where(odd, pltpu.roll(even, FLAT, 1), pltpu.roll(even, HALF, 1))
            coef[s, n, 2, : USED - UH] = jnp.where(
                odd_rows, pltpu.roll(uneven, VR - HALF, 1), pltpu.roll(uneven, FLAT, 1)
            )
            coef[s, n, 3, : USED - UH] = jnp.where(odd_rows, uneven, pltpu.roll(uneven, VR - HALF, 1))
        flat = jnp.where(edge_lane < USED, zbuf[s, :EDGE, :], 0.0)
        other = jnp.where(edge_row % 2 == 0, pltpu.roll(flat, EDGE - 1, 0), -pltpu.roll(flat, 1, 0))
        ecoef[s, 0] = jnp.where(edge_lane < UH, flat, jnp.where(edge_lane < UR, pltpu.roll(flat, UH, 1), 0.0))
        ecoef[s, 1] = jnp.where(
            edge_lane < UH, pltpu.roll(other, VR - UH, 1), jnp.where(edge_lane < UR, other, 0.0)
        )

    stack[...] = jnp.zeros_like(stack)
    load_kr.wait()
    load_ki.wait()
    for ri in range(2):
        for l in range(LOCAL):
            for k in range(KERNELS):
                at = (l * KERNELS + k) * UR
                stack[at : at + KSUP, ri * VR : ri * VR + KSUP] = raw_v[ri, l, :, k, :]
    for copy in load_pv:
        copy.wait()
    load_pu.wait()
    hi, lo = split(stack[...])
    folded = dot(jnp.concatenate([hi, lo], axis=1), pv[...])
    hi, lo = split(folded)
    coef[:, :, 2:, USED - UH :, :] = jnp.zeros((GROUP, DEPTH, 2, UR - USED, VR), F32)
    load_thresholds.wait()
    for n in range(DEPTH):
        rhs = jnp.concatenate([hi[n * UR : (n + 1) * UR], lo[n * UR : (n + 1) * UR]], axis=0)
        value = dot(pu[...], rhs)
        zbuf[0, EDGE + n * USED : EDGE + (n + 1) * USED, :] = value[:USED, :VR]
        for ri in range(2):
            flat = jnp.sum(jnp.where(diagonal, value[:, VR + ri : VR + ri + 1], 0.0), axis=0, keepdims=True)
            if 2 * n + ri < LOCAL:
                flat = jnp.where(lane[:1] == VR - 1, thresholds_s[2 * n + ri], flat)
            zbuf[0, 2 * n + ri : 2 * n + ri + 1, :] = flat

    load_theta.wait()
    load_by.wait()
    load_turned.wait()
    mask_rows = jnp.tanh(MASK_STEEP * theta_v[...])
    hi, lo = split(mask_rows)
    wide = dot(jnp.concatenate([hi, lo], axis=0), by[...])
    column = wide[:ROWS, :VR] + wide[:ROWS, VR:] + wide[ROWS:, :VR]
    hi, lo = split(column)
    both = dot(turned[...], jnp.concatenate([hi, lo], axis=0))
    rown[...] = packed(both[:UR] + both[UR : 2 * UR])
    rhalo[...] = packed(both[2 * UR : 3 * UR] + both[3 * UR :])

    edge_of = (has_next & final) | (has_prev & first)
    waited = jnp.where(edge_of, 2 * GROUP, GROUP)
    pl.semaphore_wait(barrier, jnp.where(after_bend | relays, GROUP + 2, waited))

    def remote(src, dst, send, recv, device):
        return pltpu.make_async_remote_copy(
            src_ref=src, dst_ref=dst, send_sem=send, recv_sem=recv, device_id=device, device_id_type=MESH
        )

    def halo_next(other):
        return remote(rhalo, rin.at[3], hs_sem.at[other], hr_sem.at[0], (t + 1, other))

    def halo_prev(other):
        return remote(rhalo, rin.at[4], hs_sem.at[other], hr_sem.at[1], (t - 1, other))

    def halo_via(side):
        return remote(rhalo, passed, hs_sem.at[side], pass_sem, (between, 1 + side))

    def halo_passed(core):
        return remote(passed, rin.at[4], hs_sem.at[core], hr_sem.at[1], (bend, 2 * (c - 1) + core))

    def part(mask):
        return remote(rown, rin.at[mask - 1], rs_sem.at[mask - 1], rr_sem.at[mask - 1], partner(mask))

    def kernels_to(mask, chunk):
        device = partner(1) if mask != 2 else mirror
        source = 2 if mask == 3 else 0
        rows = pl.ds(0, CHUNK) if chunk == 0 else pl.ds(CHUNK, WIRE - CHUNK)
        sem = 2 * (mask - 1) + chunk
        return remote(
            zbuf.at[source, rows, :], zbuf.at[mask, rows, :], zs_sem.at[sem], zr_sem.at[sem], device
        )

    @pl.when(has_next & final)
    def _():
        for other in range(GROUP):
            halo_next(other).start()

    @pl.when(has_prev & first & jnp.logical_not(after_bend))
    def _():
        for other in range(GROUP):
            halo_prev(other).start()

    @pl.when(after_bend)
    def _():
        for side in range(2):
            halo_via(side).start()

    for mask in range(1, GROUP):
        part(mask).start()
    for mask in (2, 1):
        for chunk in range(2):
            kernels_to(mask, chunk).start()

    @pl.when(relays)
    def _():
        halo_via(0).wait_recv()
        for core in range(2):
            halo_passed(core).start()

    @pl.when(jnp.logical_not(has_prev))
    def _():
        rin[3] = jnp.zeros((UH, VR), F32)

    @pl.when(jnp.logical_not(has_next))
    def _():
        rin[4] = jnp.zeros((UH, VR), F32)

    unpack_kernels(0)
    for chunk in range(2):
        kernels_to(1, chunk).wait_recv()
    unpack_kernels(1)

    @pl.when(has_prev)
    def _():
        halo_next(0).wait_recv()

    @pl.when(has_next)
    def _():
        halo_prev(0).wait_recv()

    for mask in range(1, GROUP):
        part(mask).wait_recv()

    total = rown[...] + rin[0] + rin[1] + rin[2] + rin[3] + rin[4]
    total = total * (1.0 / (SIZE * SIZE))
    keep = row < SPARE
    turn = pltpu.roll(total, FLAT, 1)
    halves = [
        jnp.where(keep, jnp.where(lane < FLAT, total, turn), 0.0),
        jnp.where(keep, jnp.where(lane < FLAT, turn, total), 0.0),
    ]
    for h in range(2):
        sign_u = 1.0 - 2.0 * h
        rsum[0, h] = halves[h]
        rsum[1, h] = sign_i * sign_v * swap(halves[h])
        rsum[2, h] = sign_u * sign_i * halves[1 - h]
        rsum[3, h] = (-sign_u) * sign_v * swap(halves[1 - h])
    flat = jnp.where(edge_lane < UR, total[SPARE : SPARE + 1], 0.0)
    erow[0] = flat
    erow[1] = turned_edge(flat)

    load_pack.wait()
    load_sample.wait()
    for copy in load_fine:
        copy.wait()
    block_lane = lax.broadcasted_iota(jnp.int32, (ROWS, VR), 1)

    def grids_and_rows(s):
        grids = []
        for n in range(DEPTH):
            grid = []
            for h in range(2):
                terms = [coef[s, n, m] * rsum[m, h] for m in range(4)]
                grid.append((terms[0] + terms[1]) + (terms[2] + terms[3]))
            grids.append(jnp.concatenate(grid, axis=0))
        cross = [None] * LOCAL
        for l in range(LOCAL):
            hi, lo = split(jnp.concatenate(grids[KERNELS * l : KERNELS * (l + 1)], axis=1))
            tall = dot(pack[:, : 3 * UR], jnp.concatenate([hi, hi, lo], axis=0))
            for k in range(KERNELS):
                part = tall[:, k * VR : (k + 1) * VR]
                at = (l * KERNELS + k) * ROWS
                other = jnp.where(block_lane % FLAT == HALF - 1, pltpu.roll(part, VR - HALF, 1), 0.0)
                other = jnp.where(block_lane % FLAT == FLAT - 1, pltpu.roll(part, HALF, 1), other)
                crossed[s, at : at + ROWS, :] = other
                other = part * other
                cross[l] = other if k == 0 else cross[l] + other
                hi, lo = split(part)
                rows_v[s // 2, s % 2 * SPAN + at : s % 2 * SPAN + at + ROWS, :VR] = hi
                rows_v[s // 2, s % 2 * SPAN + at : s % 2 * SPAN + at + ROWS, VR:] = lo
        for l in range(LOCAL):
            near = cross[l].astype(BF).astype(F32)
            far = pltpu.roll(cross[l] - near, VR - 1, 1)
            edge_v[s, l * ROWS : (l + 1) * ROWS, :] = jnp.where(block_lane % FLAT == HALF - 2, far, near).astype(BF)
        flat = stacked(ecoef[s, 0] * erow[0] + ecoef[s, 1] * erow[1])
        upper = dot(flat, turned[:VR, :ROWS])
        lower = dot(flat, turned[UR : UR + VR, :ROWS])
        flat_v[s] = (upper[:EDGE] + upper[EDGE:] + lower[:EDGE]).T

    def resist_of(slots):
        held = slots[0] // 2
        amp = dot(jnp.concatenate([rows_v[held], rows_v[held, :, :VR]], axis=1), sample[...])
        lhs = []
        for s in slots:
            for l in range(LOCAL):
                sampled = None
                for k in range(KERNELS):
                    n = l * KERNELS + k
                    at = s % 2 * SPAN + n * ROWS
                    for ri in range(2):
                        piece = amp[at : at + ROWS, ri * GRID : (ri + 1) * GRID]
                        piece = piece + flat_v[s, :, 2 * n + ri : 2 * n + ri + 1]
                        amps[s, n * ROWS : (n + 1) * ROWS, ri * GRID : (ri + 1) * GRID] = piece
                        sampled = piece * piece if k + ri == 0 else sampled + piece * piece
                hi, lo = split(sampled)
                lhs.append(jnp.concatenate([hi, lo, hi, edge_v[s, l * ROWS : (l + 1) * ROWS, :]], axis=1))
        intensities = dot(jnp.concatenate(lhs, axis=0), fine[...])
        total = None
        for s in slots:
            for l in range(LOCAL):
                at = (s % 2 * LOCAL + l) * ROWS
                level = zbuf[s, l : l + 1, VR - 1 : VR]
                resist = jax.nn.sigmoid(RESIST_STEEP * (intensities[at : at + ROWS] - level))
                resists[s, l] = resist
                total = resist if total is None else total + resist
        if slots[0] == 0:
            band[...] = total
        else:
            band[...] += total

    grids_and_rows(0)
    grids_and_rows(1)
    kernels_to(2, 0).wait_recv()
    kernels_to(3, 0).start()
    resist_of((0, 1))
    kernels_to(2, 1).wait_recv()
    kernels_to(3, 1).start()
    unpack_kernels(2)
    grids_and_rows(2)
    for chunk in range(2):
        kernels_to(3, chunk).wait_recv()
    unpack_kernels(3)
    grids_and_rows(3)
    resist_of((2, 3))

    load_target.wait()
    load_weights.wait()
    weight_sum = weights_s[0]
    for n in range(1, CONDS):
        weight_sum = weight_sum + weights_s[n]
    weight_sum = jnp.full((8, TP), weight_sum, jnp.int32).astype(F32)
    wanted[...] = target_v[...].astype(F32)
    band[...] = band[...] * (4.0 * RESIST_STEEP * BAND_WEIGHT / CONDS / CONDS)

    load_coarse.wait()
    load_half.wait()
    load_gather.wait()

    def push_of(slots):
        fields = []
        for s in slots:
            for l in range(LOCAL):
                weight = jnp.full((8, TP), weights_s[(c ^ s) * LOCAL + l], jnp.int32).astype(F32) / weight_sum
                pull = (4.0 * RESIST_STEEP) * weight[0:1]
                resist = resists[s, l]
                slope = (pull + 4.0 * RESIST_STEEP * BAND_WEIGHT / CONDS) * resist - (pull * wanted[...] + band[...])
                field = slope * (resist - resist * resist)
                last = jnp.sum(field * half_last[0:1, :], axis=1, keepdims=True)
                last_v[s, l * ROWS : (l + 1) * ROWS, :] = jnp.broadcast_to(last, (ROWS, VR))
                fields.append(field)
        hi, lo = split(jnp.concatenate(fields, axis=0))
        wide = dot(jnp.concatenate([hi, lo], axis=0), coarse[...])
        half = 2 * LOCAL * ROWS
        push_v[slots[0] // 2] = wide[:half, :GRID] + wide[:half, GRID:] + wide[half:, :GRID]

    def adjoint_of(slots):
        rows = []
        flats = []
        for s in slots:
            flat = []
            for n in range(DEPTH):
                at = (s % 2 * LOCAL + n // KERNELS) * ROWS
                push = push_v[slots[0] // 2, at : at + ROWS, :]
                drive = []
                for ri in range(2):
                    piece = push * amps[s, n * ROWS : (n + 1) * ROWS, ri * GRID : (ri + 1) * GRID]
                    flat.append(jnp.where(block_lane == 2 * n + ri, jnp.sum(piece, axis=1, keepdims=True), 0.0))
                    drive.append(piece)
                hi, lo = split(jnp.concatenate(drive, axis=1))
                rows.append(jnp.concatenate([hi, lo], axis=1))
            while len(flat) > 1:
                flat = [flat[i] + flat[i + 1] for i in range(0, len(flat), 2)]
            flats.append(flat[0])
        drive = dot(jnp.concatenate(rows, axis=0), gather[...])
        drive = drive[:, :VR] + drive[:, VR:]
        sums = [[None, None] for _ in range(4)]
        for s in slots:
            for l in range(LOCAL):
                pair = []
                for n in (KERNELS * l, KERNELS * l + 1):
                    at = s % 2 * SPAN + n * ROWS
                    last = last_v[s, l * ROWS : (l + 1) * ROWS, :]
                    pair.append(drive[at : at + ROWS] + last * crossed[s, n * ROWS : (n + 1) * ROWS, :])
                hi, lo = split(jnp.concatenate(pair, axis=1))
                back = dot(turned[: 2 * UR, :], jnp.concatenate([hi, lo], axis=0))
                back = back[:UR] + back[UR:]
                for k in range(KERNELS):
                    for h in range(2):
                        value = back[h * UH : (h + 1) * UH, k * VR : (k + 1) * VR]
                        for m in range(4):
                            term = coef[s, l * KERNELS + k, m] * value
                            sums[m][h] = term if sums[m][h] is None else sums[m][h] + term
        total = None
        for s, flat in zip(slots, flats):
            wide = dot(stacked(flat.T[:EDGE]), pack[:, : 2 * VR])
            here = wide[:EDGE, :VR] + wide[EDGE:, :VR]
            upper = pltpu.roll(wide[:EDGE, :VR], VR - UR, 1)
            lower = pltpu.roll(wide[:EDGE, VR:], VR - UR, 1)
            here = here + jnp.where(edge_lane < VR - UR, upper, lower)
            term = ecoef[s, 0] * here - ecoef[s, 1] * turned_edge(here)
            total = term if total is None else total + term
        for m in range(4):
            for h in range(2):
                if slots[0] == 0:
                    jbuf[m, h] = sums[m][h]
                else:
                    jbuf[m, h] += sums[m][h]
        if slots[0] == 0:
            jflat[...] = total
        else:
            jflat[...] += total

    push_of((0, 1))
    adjoint_of((0, 1))
    push_of((2, 3))
    adjoint_of((2, 3))

    def folded_part(m, h):
        sign = 1.0 if m in (0, 3) else -1.0
        return jbuf[m, h] + sign * pltpu.roll(jbuf[m, h], FLAT, 1)

    halves = []
    for h in range(2):
        sign_u = 1.0 - 2.0 * h
        halves.append(
            folded_part(0, h)
            + swap(sign_v * folded_part(1, h))
            - sign_u * folded_part(2, 1 - h)
            + swap(sign_u * sign_v * folded_part(3, 1 - h))
        )
    value = jnp.where(lane < FLAT, halves[0], pltpu.roll(halves[1], FLAT, 1))
    aown[...] = jnp.where(row == SPARE, jnp.sum(jflat[...], axis=0, keepdims=True), value)

    def adjoint_part(mask):
        return remote(aown, ain.at[mask - 1], as_sem.at[mask - 1], ar_sem.at[mask - 1], partner(mask))

    def adjoint_prev():
        return remote(aown, anear.at[c], as_sem.at[3], near_sem.at[c], (t - 1, GROUP - 1))

    def adjoint_next():
        return remote(aown, anear.at[c], as_sem.at[4], near_sem.at[c], (t + 1, 0))

    def adjoint_near(other):
        return remote(aown, anear.at[other], as_sem.at[3], near_sem.at[other], (t, c ^ 1))

    @pl.when(has_prev)
    def _():
        adjoint_prev().start()

    @pl.when(has_next)
    def _():
        adjoint_next().start()

    for mask in range(1, GROUP):
        adjoint_part(mask).start()

    near = (first & has_prev) | (final & has_next)

    factor[...] = (MASK_STEEP / (SIZE * SIZE)) * (1.0 - jnp.square(jnp.tanh(MASK_STEEP * theta_v[...])))
    for copy in load_bt:
        copy.wait()

    for mask in range(1, GROUP):
        adjoint_part(mask).wait_recv()

    def sensitivity(value, rows, columns):
        hi, lo = split(jnp.concatenate(unpacked(value), axis=0))
        value = jnp.concatenate([hi, hi, lo, jnp.zeros((256 - 3 * UR, VR), BF)], axis=0)
        hi, lo = split(dot(pack[rows, columns], value))
        return dot(jnp.concatenate([hi, lo, hi], axis=1), bt[...])

    out_v[...] = sensitivity(aown[...] + ain[0] + ain[1] + ain[2], slice(None), slice(0, 256)) * factor[...]

    @pl.when(near)
    def _():
        for other in range(GROUP):
            adjoint_near(other).wait_recv()
        edge = pl.ds(pl.multiple_of(jnp.where(first, 0, ROWS - HALO), HALO), HALO)
        value = anear[0] + anear[1] + anear[2] + anear[3]
        out_v[edge, :] += sensitivity(value, edge, slice(256, 512)) * factor[edge, :]

    @pl.when(has_next & final)
    def _():
        for other in range(GROUP):
            halo_next(other).wait_send()

    @pl.when(has_prev & first & jnp.logical_not(after_bend))
    def _():
        for other in range(GROUP):
            halo_prev(other).wait_send()

    @pl.when(after_bend)
    def _():
        for side in range(2):
            halo_via(side).wait_send()

    @pl.when(relays)
    def _():
        for core in range(2):
            halo_passed(core).wait_send()

    for mask in range(1, GROUP):
        part(mask).wait_send()
        for chunk in range(2):
            kernels_to(mask, chunk).wait_send()
        adjoint_part(mask).wait_send()

    @pl.when(has_prev)
    def _():
        adjoint_prev().wait_send()

    @pl.when(has_next)
    def _():
        adjoint_next().wait_send()


def shards(tiles, theta, target, kernel_real, kernel_imag, weights, thresholds):
    constants = tables()
    dma = pltpu.SemaphoreType.DMA
    by, bt, pack, turned, pv, pu, sample, gather, fine, coarse, half_last = constants
    call = pl.pallas_call(
        functools.partial(kernel, tiles),
        out_shape=jax.ShapeDtypeStruct((ROWS, TP), F32),
        in_specs=[pl.BlockSpec(memory_space=pltpu.HBM)] * 17,
        out_specs=pl.BlockSpec(memory_space=pltpu.VMEM),
        scratch_shapes=[
            pltpu.SMEM((CONDS,), jnp.int32),
            pltpu.SMEM((LOCAL,), F32),
            pltpu.VMEM((ROWS, TP), F32),
            pltpu.VMEM((ROWS, TP), jnp.int32),
            pltpu.VMEM((2, LOCAL, KSUP, KERNELS, KSUP), F32),
            pltpu.VMEM(by.shape, BF),
            pltpu.VMEM((3 * VR, TP), BF),
            pltpu.VMEM(pack.shape[1:], BF),
            pltpu.VMEM(turned.shape[1:], BF),
            pltpu.VMEM((4 * VR, 2 * VR), BF),
            pltpu.VMEM(pu.shape, BF),
            pltpu.VMEM(sample.shape, BF),
            pltpu.VMEM(gather.shape, BF),
            pltpu.VMEM((4 * GRID, TP), BF),
            pltpu.VMEM(coarse.shape, BF),
            pltpu.VMEM(half_last.shape, F32),
            pltpu.VMEM((DEPTH * UR, 2 * VR), F32),
            pltpu.VMEM((GROUP, WIRE, VR), F32),
            pltpu.VMEM((GROUP, DEPTH, 4, UH, VR), F32),
            pltpu.VMEM((GROUP, 2, EDGE, VR), F32),
            pltpu.VMEM((UH, VR), F32),
            pltpu.VMEM((UH, VR), F32),
            pltpu.VMEM((UH, VR), F32),
            pltpu.VMEM((5, UH, VR), F32),
            pltpu.VMEM((4, 2, UH, VR), F32),
            pltpu.VMEM((2, EDGE, VR), F32),
            pltpu.VMEM((UH, VR), F32),
            pltpu.VMEM((3, UH, VR), F32),
            pltpu.VMEM((GROUP, UH, VR), F32),
            pltpu.VMEM((4, 2, UH, VR), F32),
            pltpu.VMEM((EDGE, VR), F32),
            pltpu.VMEM((GROUP, DEPTH * ROWS, 2 * GRID), F32),
            pltpu.VMEM((GROUP, DEPTH * ROWS, VR), F32),
            pltpu.VMEM((2, 2 * SPAN, 2 * VR), BF),
            pltpu.VMEM((GROUP, ROWS, EDGE), F32),
            pltpu.VMEM((GROUP, LOCAL * ROWS, VR), BF),
            pltpu.VMEM((2, 2 * LOCAL * ROWS, GRID), F32),
            pltpu.VMEM((GROUP, LOCAL * ROWS, VR), F32),
            pltpu.VMEM((GROUP, LOCAL, ROWS, TP), F32),
            pltpu.VMEM((ROWS, TP), F32),
            pltpu.VMEM((ROWS, TP), F32),
            pltpu.VMEM((ROWS, TP), F32),
            dma((20,)),
            dma((6,)),
            dma((6,)),
            dma((3,)),
            dma((3,)),
            dma((4,)),
            dma((2,)),
            dma((5,)),
            dma((3,)),
            dma((4,)),
            dma,
        ],
        compiler_params=pltpu.CompilerParams(collective_id=0, has_side_effects=True, vmem_limit_bytes=32 * 1024 * 1024),
        name="window_gradient",
    )
    kernel_real, kernel_imag = (jnp.swapaxes(x, 1, 2) for x in (kernel_real, kernel_imag))
    arrays = (theta, target, kernel_real, kernel_imag, weights, thresholds, *(jnp.asarray(x) for x in constants))
    return call(*(pltpu.with_memory_space_constraint(x, pltpu.HBM) for x in arrays))


def solution(mesh):
    in_specs = (
        P(("tile", "cond"), None),
        P("tile", None),
        P("cond", None, None, None),
        P("cond", None, None, None),
        P(),
        P("cond"),
    )
    out_specs = P(("tile", "cond"), None)
    body = functools.partial(shards, mesh.shape["tile"])
    return jax.shard_map(body, mesh=mesh, in_specs=in_specs, out_specs=out_specs, check_vma=False)
```

```python
import functools
import math

import jax
import jax.numpy as jnp
import ml_dtypes
import numpy as np
from jax import lax
from jax.experimental import pallas as pl
from jax.experimental.pallas import tpu as pltpu
from jax.sharding import PartitionSpec as P

TP = 512
HALO = 32
KSUP = 65
HALF = KSUP // 2
CONDS = 8
KERNELS = 2
SIZE = TP + 2 * HALO
ROWS = 128
GROUP = 4
LOCAL = CONDS // GROUP
UH = 40
UR = 2 * UH
VR = 128
FLAT = 2 * HALF
DEPTH = LOCAL * KERNELS
USED = UH + HALF
EDGE = 2 * DEPTH
CHUNK = EDGE + DEPTH // 2 * USED
WIRE = EDGE + DEPTH * USED
SPAN = DEPTH * ROWS
GRID = 128
SPARE = HALF + 1

MASK_STEEP = 2.0
RESIST_STEEP = 4.0
BAND_WEIGHT = 1.0

BF = jnp.bfloat16
F32 = jnp.float32
MESH = pl.DeviceIdType.MESH


def split(x):
    hi = x.astype(BF)
    return hi, (x - hi.astype(F32)).astype(BF)


def np_split(x):
    hi = x.astype(ml_dtypes.bfloat16)
    return hi, (x - hi.astype(np.float64)).astype(ml_dtypes.bfloat16)


def waves(positions):
    phase = np.fmod(np.asarray(positions, np.float64)[:, None] * np.arange(HALF + 1)[None, :], SIZE)
    angles = phase * (2.0 * math.pi / SIZE)
    return np.cos(angles), np.sin(angles)


def row_basis(positions):
    cos, sin = waves(positions)
    out = np.zeros((len(positions), UR))
    out[:, :HALF] = cos[:, 1:]
    out[:, HALF] = 1.0
    out[:, UH:USED] = sin[:, 1:]
    return out


def column_basis(positions):
    cos, sin = waves(positions)
    out = np.zeros((len(positions), VR))
    out[:, :HALF] = cos[:, 1:]
    out[:, HALF:FLAT] = sin[:, 1:]
    out[:, FLAT] = 1.0
    return out


def parity_rows():
    out = np.zeros((UR, UR))
    out[HALF, HALF] = 1.0
    for j in range(1, HALF + 1):
        out[j - 1, HALF + j] = out[j - 1, HALF - j] = out[UH + j - 1, HALF + j] = 1.0
        out[UH + j - 1, HALF - j] = -1.0
    return out


def parity_columns():
    out = np.zeros((2 * VR, 2 * VR))
    for ri in range(2):
        out[ri * VR + HALF, VR + ri] = 1.0
        for j in range(1, HALF + 1):
            even = ri * FLAT + j - 1
            out[ri * VR + HALF + j, even] = out[ri * VR + HALF - j, even] = 1.0
            out[ri * VR + HALF + j, even + HALF] = 1.0
            out[ri * VR + HALF - j, even + HALF] = -1.0
    return out


def tables():
    bf = ml_dtypes.bfloat16
    cols = column_basis(np.arange(TP) + HALO)
    hi, lo = np_split(cols)
    by = np.concatenate([hi, lo], axis=1)
    bt = np.concatenate([hi.T, lo.T], axis=0)
    places = column_basis(np.arange(GRID) * (SIZE / GRID))
    hi, lo = np_split(places[:, :FLAT])
    sample = np.zeros((3 * VR, 2 * GRID), bf)
    gather = np.zeros((4 * GRID, 2 * VR), bf)
    for ri in range(2):
        for block, part in enumerate((hi, hi, lo)):
            at = block * VR + ri * FLAT
            sample[at : at + FLAT, ri * GRID : (ri + 1) * GRID] = part.T
        gather[ri * GRID : (ri + 1) * GRID, ri * FLAT : (ri + 1) * FLAT] = hi
        gather[ri * GRID : (ri + 1) * GRID, VR + ri * FLAT : VR + (ri + 1) * FLAT] = lo
        gather[(2 + ri) * GRID : (3 + ri) * GRID, ri * FLAT : (ri + 1) * FLAT] = hi
    phase = (np.arange(TP) + HALO) * (2.0 * math.pi / SIZE)
    place = np.arange(GRID) * (2.0 * math.pi / GRID)
    spread = np.ones((GRID, TP))
    for f in range(1, GRID // 2):
        spread += 2.0 * np.cos(f * (phase[None, :] - place[:, None]))
    spread += np.cos(GRID // 2 * place)[:, None] * np.cos(GRID // 2 * phase)[None, :]
    spread /= GRID
    last = np.sin(GRID // 2 * phase)
    hi, lo = np_split(spread)
    last_hi, last_lo = np_split(last)
    rest = np.zeros((VR, TP), bf)
    for at in (0, FLAT):
        rest[at + HALF - 2], rest[at + HALF - 1], rest[at + FLAT - 1] = last_hi, last_hi, last_lo
    fine = np.concatenate([hi, lo, rest], axis=0)
    coarse = np.concatenate([hi.T, lo.T], axis=1)
    half_last = np.broadcast_to(0.5 * last, (8, TP)).astype(np.float32)
    pack = []
    turned = []
    for c in range(GROUP):
        own = row_basis(np.arange(ROWS) + HALO + ROWS * c)
        near = np.zeros_like(own)
        if c == 0:
            near[:HALO] = row_basis(np.arange(HALO) + HALO + TP)
        if c == GROUP - 1:
            near[ROWS - HALO :] = row_basis(np.arange(HALO))
        row = []
        column = []
        for table in (own, near):
            thi, tlo = np_split(table)
            row += [thi, tlo, thi, np.zeros((ROWS, 256 - 3 * UR), bf)]
            column.append(np.concatenate([thi.T, thi.T], axis=1))
            column.append(np.concatenate([tlo.T, np.zeros((UR, ROWS), bf)], axis=1))
        pack.append(np.concatenate(row, axis=1))
        turned.append(np.concatenate(column, axis=0))
    pv = parity_columns().astype(bf)
    pu = parity_rows().astype(bf)
    pu = np.concatenate([pu, pu], axis=1)
    return by, bt, np.stack(pack), np.stack(turned), pv, pu, sample, gather, fine, coarse, half_last


def dot(a, b):
    return jnp.dot(a, b, preferred_element_type=F32)


def kernel(
    tiles,
    theta_h, target_h, kr_h, ki_h, weights_h, thresholds_h, by_h, bt_h, pack_h, turned_h, pv_h, pu_h,
    sample_h, gather_h, fine_h, coarse_h, half_last_h,
    out_v,
    weights_s, thresholds_s, theta_v, target_v, raw_v, by, bt, pack, turned, pv, pu,
    sample, gather, fine, coarse, half_last, stack, zbuf, coef, ecoef, passed, rown, rhalo, rin, rsum, erow, aown, ain, anear, jbuf, jflat, amps, crossed, rows_v, flat_v, edge_v, push_v, last_v, resists, band, wanted, factor,
    load_sem, zs_sem, zr_sem, rs_sem, rr_sem, hs_sem, hr_sem, as_sem, ar_sem, near_sem, pass_sem,
):
    t = lax.axis_index("tile")
    c = lax.axis_index("cond")
    first = c == 0
    final = c == GROUP - 1
    has_prev = t > 0
    has_next = t < tiles - 1

    loads = []

    def load(src, dst):
        copy = pltpu.make_async_copy(src, dst, load_sem.at[len(loads)])
        copy.start()
        loads.append(copy)
        return copy

    load_kr = load(kr_h, raw_v.at[0])
    load_ki = load(ki_h, raw_v.at[1])
    load_pv = [load(pv_h, pv.at[pl.ds(at, 2 * VR), :]) for at in (0, 2 * VR)]
    load_pu = load(pu_h, pu)
    load_thresholds = load(thresholds_h, thresholds_s)
    load_theta = load(theta_h, theta_v)
    load_by = load(by_h, by)
    load_turned = load(turned_h.at[c], turned)
    load_pack = load(pack_h.at[c], pack)
    load_sample = load(sample_h, sample)
    load_fine = [
        load(fine_h.at[pl.ds(0, GRID), :], fine.at[pl.ds(0, GRID), :]),
        load(fine_h, fine.at[pl.ds(GRID, 3 * GRID), :]),
    ]
    load_coarse = load(coarse_h, coarse)
    load_half = load(half_last_h, half_last)
    load_gather = load(gather_h, gather)
    load_bt = [
        load(bt_h.at[pl.ds(0, VR), :], bt.at[pl.ds(0, VR), :]),
        load(bt_h, bt.at[pl.ds(VR, 2 * VR), :]),
    ]
    load_weights = load(weights_h, weights_s)
    load_target = load(target_h.at[pl.ds(pl.multiple_of(c * ROWS, ROWS), ROWS), :], target_v)

    def partner(mask):
        return (t, c ^ mask)

    barrier = pltpu.get_barrier_semaphore()

    def greet(device):
        pl.semaphore_signal(barrier, inc=1, device_id=device, device_id_type=MESH)

    mirror = ((t + tiles // 2) % tiles, c ^ 2)
    for mask in range(1, GROUP):
        greet(partner(mask))
    greet(mirror)

    bend = tiles // 2 - 1
    between = bend - 3
    at_bend = t == bend
    after_bend = (t == bend + 1) & first
    relays = (t == between) & jnp.logical_not(first | final)

    @pl.when(has_next)
    def _():
        greet((jnp.where(at_bend, between, t + 1), jnp.where(at_bend, 1 + c // 2, 0)))

    @pl.when(has_prev)
    def _():
        greet((t - 1, GROUP - 1))

    @pl.when(relays)
    def _():
        greet((bend + 1, 0))

    lane = lax.broadcasted_iota(jnp.int32, (UH, VR), 1)
    row = lax.broadcasted_iota(jnp.int32, (UH, VR), 0)
    tall_lane = lax.broadcasted_iota(jnp.int32, (UR, VR), 1)
    diagonal = tall_lane == lax.broadcasted_iota(jnp.int32, (UR, VR), 0)
    odd = lane % FLAT >= HALF
    sign_v = jnp.where(odd, -1.0, 1.0).astype(F32)
    sign_i = jnp.where(lane >= FLAT, -1.0, 1.0).astype(F32)
    edge_lane = lane[: 2 * DEPTH]
    edge_row = row[: 2 * DEPTH]

    def swap(x):
        return jnp.where(odd, pltpu.roll(x, HALF, 1), pltpu.roll(x, VR - HALF, 1))

    def turned_edge(x):
        out = jnp.where(edge_lane < UH, pltpu.roll(x, VR - UH, 1), -pltpu.roll(x, UH, 1))
        return jnp.where(edge_lane < UR, out, 0.0)

    def stacked(x):
        near = x.astype(BF).astype(F32)
        return jnp.concatenate([near, x - near], axis=0).astype(BF)

    def packed(x):
        out = jnp.where(lane < FLAT, x[:UH], pltpu.roll(x[UH:], FLAT, 1))
        flat = jnp.sum(jnp.where(diagonal, x[:, FLAT : FLAT + 1], 0.0), axis=0, keepdims=True)
        return jnp.where(row == SPARE, flat, out)

    def unpacked(x):
        flat = jnp.sum(jnp.where(diagonal, x[SPARE : SPARE + 1], 0.0), axis=1, keepdims=True)
        keep = (lane < FLAT) & (row < SPARE)
        out = []
        for h, value in enumerate((x, pltpu.roll(x, FLAT, 1))):
            out.append(jnp.where(lane == FLAT, flat[h * UH : (h + 1) * UH], jnp.where(keep, value, 0.0)))
        return out

    def unpack_kernels(s):
        for n in range(DEPTH):
            at = EDGE + n * USED
            even = zbuf[s, at : at + UH, :]
            uneven = zbuf[s, at + UH : at + USED, :]
            odd_rows = odd[: USED - UH]
            coef[s, n, 0] = jnp.where(odd, pltpu.roll(even, HALF, 1), even)
            coef[s, n, 1] = jnp.where(odd, pltpu.roll(even, FLAT, 1), pltpu.roll(even, HALF, 1))
            coef[s, n, 2, : USED - UH] = jnp.where(
                odd_rows, pltpu.roll(uneven, VR - HALF, 1), pltpu.roll(uneven, FLAT, 1)
            )
            coef[s, n, 3, : USED - UH] = jnp.where(odd_rows, uneven, pltpu.roll(uneven, VR - HALF, 1))
        flat = jnp.where(edge_lane < USED, zbuf[s, :EDGE, :], 0.0)
        other = jnp.where(edge_row % 2 == 0, pltpu.roll(flat, EDGE - 1, 0), -pltpu.roll(flat, 1, 0))
        ecoef[s, 0] = jnp.where(edge_lane < UH, flat, jnp.where(edge_lane < UR, pltpu.roll(flat, UH, 1), 0.0))
        ecoef[s, 1] = jnp.where(
            edge_lane < UH, pltpu.roll(other, VR - UH, 1), jnp.where(edge_lane < UR, other, 0.0)
        )

    stack[...] = jnp.zeros_like(stack)
    load_kr.wait()
    load_ki.wait()
    for ri in range(2):
        for l in range(LOCAL):
            for k in range(KERNELS):
                at = (l * KERNELS + k) * UR
                stack[at : at + KSUP, ri * VR : ri * VR + KSUP] = raw_v[ri, l, :, k, :]
    for copy in load_pv:
        copy.wait()
    load_pu.wait()
    hi, lo = split(stack[...])
    folded = dot(jnp.concatenate([hi, lo], axis=1), pv[...])
    hi, lo = split(folded)
    coef[:, :, 2:, USED - UH :, :] = jnp.zeros((GROUP, DEPTH, 2, UR - USED, VR), F32)
    load_thresholds.wait()
    for n in range(DEPTH):
        rhs = jnp.concatenate([hi[n * UR : (n + 1) * UR], lo[n * UR : (n + 1) * UR]], axis=0)
        value = dot(pu[...], rhs)
        zbuf[0, EDGE + n * USED : EDGE + (n + 1) * USED, :] = value[:USED, :VR]
        for ri in range(2):
            flat = jnp.sum(jnp.where(diagonal, value[:, VR + ri : VR + ri + 1], 0.0), axis=0, keepdims=True)
            if 2 * n + ri < LOCAL:
                flat = jnp.where(lane[:1] == VR - 1, thresholds_s[2 * n + ri], flat)
            zbuf[0, 2 * n + ri : 2 * n + ri + 1, :] = flat

    load_theta.wait()
    load_by.wait()
    load_turned.wait()
    mask_rows = jnp.tanh(MASK_STEEP * theta_v[...])
    hi, lo = split(mask_rows)
    wide = dot(jnp.concatenate([hi, lo], axis=0), by[...])
    column = wide[:ROWS, :VR] + wide[:ROWS, VR:] + wide[ROWS:, :VR]
    hi, lo = split(column)
    both = dot(turned[...], jnp.concatenate([hi, lo], axis=0))
    rown[...] = packed(both[:UR] + both[UR : 2 * UR])
    rhalo[...] = packed(both[2 * UR : 3 * UR] + both[3 * UR :])

    edge_of = (has_next & final) | (has_prev & first)
    waited = jnp.where(edge_of, 2 * GROUP, GROUP)
    pl.semaphore_wait(barrier, jnp.where(after_bend | relays, GROUP + 2, waited))

    def remote(src, dst, send, recv, device):
        return pltpu.make_async_remote_copy(
            src_ref=src, dst_ref=dst, send_sem=send, recv_sem=recv, device_id=device, device_id_type=MESH
        )

    def halo_next(other):
        return remote(rhalo, rin.at[3], hs_sem.at[other], hr_sem.at[0], (t + 1, other))

    def halo_prev(other):
        return remote(rhalo, rin.at[4], hs_sem.at[other], hr_sem.at[1], (t - 1, other))

    def halo_via(side):
        return remote(rhalo, passed, hs_sem.at[side], pass_sem, (between, 1 + side))

    def halo_passed(core):
        return remote(passed, rin.at[4], hs_sem.at[core], hr_sem.at[1], (bend, 2 * (c - 1) + core))

    def part(mask):
        return remote(rown, rin.at[mask - 1], rs_sem.at[mask - 1], rr_sem.at[mask - 1], partner(mask))

    def kernels_to(mask, chunk):
        device = partner(1) if mask != 2 else mirror
        source = 2 if mask == 3 else 0
        rows = pl.ds(0, CHUNK) if chunk == 0 else pl.ds(CHUNK, WIRE - CHUNK)
        sem = 2 * (mask - 1) + chunk
        return remote(
            zbuf.at[source, rows, :], zbuf.at[mask, rows, :], zs_sem.at[sem], zr_sem.at[sem], device
        )

    @pl.when(has_next & final)
    def _():
        for other in range(GROUP):
            halo_next(other).start()

    @pl.when(has_prev & first & jnp.logical_not(after_bend))
    def _():
        for other in range(GROUP):
            halo_prev(other).start()

    @pl.when(after_bend)
    def _():
        for side in range(2):
            halo_via(side).start()

    for mask in range(1, GROUP):
        part(mask).start()
    for mask in (2, 1):
        for chunk in range(2):
            kernels_to(mask, chunk).start()

    @pl.when(relays)
    def _():
        halo_via(0).wait_recv()
        for core in range(2):
            halo_passed(core).start()

    @pl.when(jnp.logical_not(has_prev))
    def _():
        rin[3] = jnp.zeros((UH, VR), F32)

    @pl.when(jnp.logical_not(has_next))
    def _():
        rin[4] = jnp.zeros((UH, VR), F32)

    unpack_kernels(0)
    for chunk in range(2):
        kernels_to(1, chunk).wait_recv()
    unpack_kernels(1)

    @pl.when(has_prev)
    def _():
        halo_next(0).wait_recv()

    @pl.when(has_next)
    def _():
        halo_prev(0).wait_recv()

    for mask in range(1, GROUP):
        part(mask).wait_recv()

    total = rown[...] + rin[0] + rin[1] + rin[2] + rin[3] + rin[4]
    total = total * (1.0 / (SIZE * SIZE))
    keep = row < SPARE
    turn = pltpu.roll(total, FLAT, 1)
    halves = [
        jnp.where(keep, jnp.where(lane < FLAT, total, turn), 0.0),
        jnp.where(keep, jnp.where(lane < FLAT, turn, total), 0.0),
    ]
    for h in range(2):
        sign_u = 1.0 - 2.0 * h
        rsum[0, h] = halves[h]
        rsum[1, h] = sign_i * sign_v * swap(halves[h])
        rsum[2, h] = sign_u * sign_i * halves[1 - h]
        rsum[3, h] = (-sign_u) * sign_v * swap(halves[1 - h])
    flat = jnp.where(edge_lane < UR, total[SPARE : SPARE + 1], 0.0)
    erow[0] = flat
    erow[1] = turned_edge(flat)

    load_pack.wait()
    load_sample.wait()
    for copy in load_fine:
        copy.wait()
    block_lane = lax.broadcasted_iota(jnp.int32, (ROWS, VR), 1)

    def grids_and_rows(s):
        grids = []
        for n in range(DEPTH):
            grid = []
            for h in range(2):
                terms = [coef[s, n, m] * rsum[m, h] for m in range(4)]
                grid.append((terms[0] + terms[1]) + (terms[2] + terms[3]))
            grids.append(jnp.concatenate(grid, axis=0))
        cross = [None] * LOCAL
        for l in range(LOCAL):
            hi, lo = split(jnp.concatenate(grids[KERNELS * l : KERNELS * (l + 1)], axis=1))
            tall = dot(pack[:, : 3 * UR], jnp.concatenate([hi, hi, lo], axis=0))
            for k in range(KERNELS):
                part = tall[:, k * VR : (k + 1) * VR]
                at = (l * KERNELS + k) * ROWS
                other = jnp.where(block_lane % FLAT == HALF - 1, pltpu.roll(part, VR - HALF, 1), 0.0)
                other = jnp.where(block_lane % FLAT == FLAT - 1, pltpu.roll(part, HALF, 1), other)
                crossed[s, at : at + ROWS, :] = other
                other = part * other
                cross[l] = other if k == 0 else cross[l] + other
                hi, lo = split(part)
                rows_v[s // 2, s % 2 * SPAN + at : s % 2 * SPAN + at + ROWS, :VR] = hi
                rows_v[s // 2, s % 2 * SPAN + at : s % 2 * SPAN + at + ROWS, VR:] = lo
        for l in range(LOCAL):
            near = cross[l].astype(BF).astype(F32)
            far = pltpu.roll(cross[l] - near, VR - 1, 1)
            edge_v[s, l * ROWS : (l + 1) * ROWS, :] = jnp.where(block_lane % FLAT == HALF - 2, far, near).astype(BF)
        flat = stacked(ecoef[s, 0] * erow[0] + ecoef[s, 1] * erow[1])
        upper = dot(flat, turned[:VR, :ROWS])
        lower = dot(flat, turned[UR : UR + VR, :ROWS])
        flat_v[s] = (upper[:EDGE] + upper[EDGE:] + lower[:EDGE]).T

    def resist_of(slots):
        held = slots[0] // 2
        amp = dot(jnp.concatenate([rows_v[held], rows_v[held, :, :VR]], axis=1), sample[...])
        lhs = []
        for s in slots:
            for l in range(LOCAL):
                sampled = None
                for k in range(KERNELS):
                    n = l * KERNELS + k
                    at = s % 2 * SPAN + n * ROWS
                    for ri in range(2):
                        piece = amp[at : at + ROWS, ri * GRID : (ri + 1) * GRID]
                        piece = piece + flat_v[s, :, 2 * n + ri : 2 * n + ri + 1]
                        amps[s, n * ROWS : (n + 1) * ROWS, ri * GRID : (ri + 1) * GRID] = piece
                        sampled = piece * piece if k + ri == 0 else sampled + piece * piece
                hi, lo = split(sampled)
                lhs.append(jnp.concatenate([hi, lo, hi, edge_v[s, l * ROWS : (l + 1) * ROWS, :]], axis=1))
        intensities = dot(jnp.concatenate(lhs, axis=0), fine[...])
        total = None
        for s in slots:
            for l in range(LOCAL):
                at = (s % 2 * LOCAL + l) * ROWS
                level = zbuf[s, l : l + 1, VR - 1 : VR]
                resist = jax.nn.sigmoid(RESIST_STEEP * (intensities[at : at + ROWS] - level))
                resists[s, l] = resist
                total = resist if total is None else total + resist
        if slots[0] == 0:
            band[...] = total
        else:
            band[...] += total

    grids_and_rows(0)
    kernels_to(2, 0).wait_recv()
    kernels_to(3, 0).start()
    grids_and_rows(1)
    kernels_to(2, 1).wait_recv()
    kernels_to(3, 1).start()
    unpack_kernels(2)
    resist_of((0, 1))
    grids_and_rows(2)
    for chunk in range(2):
        kernels_to(3, chunk).wait_recv()
    unpack_kernels(3)
    grids_and_rows(3)
    resist_of((2, 3))

    load_target.wait()
    load_weights.wait()
    weight_sum = weights_s[0]
    for n in range(1, CONDS):
        weight_sum = weight_sum + weights_s[n]
    weight_sum = jnp.full((8, TP), weight_sum, jnp.int32).astype(F32)
    wanted[...] = target_v[...].astype(F32)
    band[...] = band[...] * (4.0 * RESIST_STEEP * BAND_WEIGHT / CONDS / CONDS)

    load_coarse.wait()
    load_half.wait()
    load_gather.wait()

    def push_of(slots):
        fields = []
        for s in slots:
            for l in range(LOCAL):
                weight = jnp.full((8, TP), weights_s[(c ^ s) * LOCAL + l], jnp.int32).astype(F32) / weight_sum
                pull = (4.0 * RESIST_STEEP) * weight[0:1]
                resist = resists[s, l]
                slope = (pull + 4.0 * RESIST_STEEP * BAND_WEIGHT / CONDS) * resist - (pull * wanted[...] + band[...])
                field = slope * (resist - resist * resist)
                last = jnp.sum(field * half_last[0:1, :], axis=1, keepdims=True)
                last_v[s, l * ROWS : (l + 1) * ROWS, :] = jnp.broadcast_to(last, (ROWS, VR))
                fields.append(field)
        hi, lo = split(jnp.concatenate(fields, axis=0))
        wide = dot(jnp.concatenate([hi, lo], axis=0), coarse[...])
        half = 2 * LOCAL * ROWS
        push_v[slots[0] // 2] = wide[:half, :GRID] + wide[:half, GRID:] + wide[half:, :GRID]

    def adjoint_of(slots):
        rows = []
        flats = []
        for s in slots:
            flat = []
            for n in range(DEPTH):
                at = (s % 2 * LOCAL + n // KERNELS) * ROWS
                push = push_v[slots[0] // 2, at : at + ROWS, :]
                drive = []
                for ri in range(2):
                    piece = push * amps[s, n * ROWS : (n + 1) * ROWS, ri * GRID : (ri + 1) * GRID]
                    flat.append(jnp.where(block_lane == 2 * n + ri, jnp.sum(piece, axis=1, keepdims=True), 0.0))
                    drive.append(piece)
                hi, lo = split(jnp.concatenate(drive, axis=1))
                rows.append(jnp.concatenate([hi, lo], axis=1))
            while len(flat) > 1:
                flat = [flat[i] + flat[i + 1] for i in range(0, len(flat), 2)]
            flats.append(flat[0])
        drive = dot(jnp.concatenate(rows, axis=0), gather[...])
        drive = drive[:, :VR] + drive[:, VR:]
        sums = [[None, None] for _ in range(4)]
        for s in slots:
            for l in range(LOCAL):
                pair = []
                for n in (KERNELS * l, KERNELS * l + 1):
                    at = s % 2 * SPAN + n * ROWS
                    last = last_v[s, l * ROWS : (l + 1) * ROWS, :]
                    pair.append(drive[at : at + ROWS] + last * crossed[s, n * ROWS : (n + 1) * ROWS, :])
                hi, lo = split(jnp.concatenate(pair, axis=1))
                back = dot(turned[: 2 * UR, :], jnp.concatenate([hi, lo], axis=0))
                back = back[:UR] + back[UR:]
                for k in range(KERNELS):
                    for h in range(2):
                        value = back[h * UH : (h + 1) * UH, k * VR : (k + 1) * VR]
                        for m in range(4):
                            term = coef[s, l * KERNELS + k, m] * value
                            sums[m][h] = term if sums[m][h] is None else sums[m][h] + term
        total = None
        for s, flat in zip(slots, flats):
            wide = dot(stacked(flat.T[:EDGE]), pack[:, : 2 * VR])
            here = wide[:EDGE, :VR] + wide[EDGE:, :VR]
            upper = pltpu.roll(wide[:EDGE, :VR], VR - UR, 1)
            lower = pltpu.roll(wide[:EDGE, VR:], VR - UR, 1)
            here = here + jnp.where(edge_lane < VR - UR, upper, lower)
            term = ecoef[s, 0] * here - ecoef[s, 1] * turned_edge(here)
            total = term if total is None else total + term
        for m in range(4):
            for h in range(2):
                if slots[0] == 0:
                    jbuf[m, h] = sums[m][h]
                else:
                    jbuf[m, h] += sums[m][h]
        if slots[0] == 0:
            jflat[...] = total
        else:
            jflat[...] += total

    push_of((0, 1))
    adjoint_of((0, 1))
    push_of((2, 3))
    adjoint_of((2, 3))

    def folded_part(m, h):
        sign = 1.0 if m in (0, 3) else -1.0
        return jbuf[m, h] + sign * pltpu.roll(jbuf[m, h], FLAT, 1)

    halves = []
    for h in range(2):
        sign_u = 1.0 - 2.0 * h
        halves.append(
            folded_part(0, h)
            + swap(sign_v * folded_part(1, h))
            - sign_u * folded_part(2, 1 - h)
            + swap(sign_u * sign_v * folded_part(3, 1 - h))
        )
    value = jnp.where(lane < FLAT, halves[0], pltpu.roll(halves[1], FLAT, 1))
    aown[...] = jnp.where(row == SPARE, jnp.sum(jflat[...], axis=0, keepdims=True), value)

    def adjoint_part(mask):
        return remote(aown, ain.at[mask - 1], as_sem.at[mask - 1], ar_sem.at[mask - 1], partner(mask))

    def adjoint_prev():
        return remote(aown, anear.at[c], as_sem.at[3], near_sem.at[c], (t - 1, GROUP - 1))

    def adjoint_next():
        return remote(aown, anear.at[c], as_sem.at[4], near_sem.at[c], (t + 1, 0))

    def adjoint_near(other):
        return remote(aown, anear.at[other], as_sem.at[3], near_sem.at[other], (t, c ^ 1))

    @pl.when(has_prev)
    def _():
        adjoint_prev().start()

    @pl.when(has_next)
    def _():
        adjoint_next().start()

    for mask in range(1, GROUP):
        adjoint_part(mask).start()

    near = (first & has_prev) | (final & has_next)

    factor[...] = (MASK_STEEP / (SIZE * SIZE)) * (1.0 - jnp.square(jnp.tanh(MASK_STEEP * theta_v[...])))
    for copy in load_bt:
        copy.wait()

    for mask in range(1, GROUP):
        adjoint_part(mask).wait_recv()

    def sensitivity(value, rows, columns):
        hi, lo = split(jnp.concatenate(unpacked(value), axis=0))
        value = jnp.concatenate([hi, hi, lo, jnp.zeros((256 - 3 * UR, VR), BF)], axis=0)
        hi, lo = split(dot(pack[rows, columns], value))
        return dot(jnp.concatenate([hi, lo, hi], axis=1), bt[...])

    out_v[...] = sensitivity(aown[...] + ain[0] + ain[1] + ain[2], slice(None), slice(0, 256)) * factor[...]

    @pl.when(near)
    def _():
        for other in range(GROUP):
            adjoint_near(other).wait_recv()
        edge = pl.ds(pl.multiple_of(jnp.where(first, 0, ROWS - HALO), HALO), HALO)
        value = anear[0] + anear[1] + anear[2] + anear[3]
        out_v[edge, :] += sensitivity(value, edge, slice(256, 512)) * factor[edge, :]

    @pl.when(has_next & final)
    def _():
        for other in range(GROUP):
            halo_next(other).wait_send()

    @pl.when(has_prev & first & jnp.logical_not(after_bend))
    def _():
        for other in range(GROUP):
            halo_prev(other).wait_send()

    @pl.when(after_bend)
    def _():
        for side in range(2):
            halo_via(side).wait_send()

    @pl.when(relays)
    def _():
        for core in range(2):
            halo_passed(core).wait_send()

    for mask in range(1, GROUP):
        part(mask).wait_send()
        for chunk in range(2):
            kernels_to(mask, chunk).wait_send()
        adjoint_part(mask).wait_send()

    @pl.when(has_prev)
    def _():
        adjoint_prev().wait_send()

    @pl.when(has_next)
    def _():
        adjoint_next().wait_send()


def shards(tiles, theta, target, kernel_real, kernel_imag, weights, thresholds):
    constants = tables()
    dma = pltpu.SemaphoreType.DMA
    by, bt, pack, turned, pv, pu, sample, gather, fine, coarse, half_last = constants
    call = pl.pallas_call(
        functools.partial(kernel, tiles),
        out_shape=jax.ShapeDtypeStruct((ROWS, TP), F32),
        in_specs=[pl.BlockSpec(memory_space=pltpu.HBM)] * 17,
        out_specs=pl.BlockSpec(memory_space=pltpu.VMEM),
        scratch_shapes=[
            pltpu.SMEM((CONDS,), jnp.int32),
            pltpu.SMEM((LOCAL,), F32),
            pltpu.VMEM((ROWS, TP), F32),
            pltpu.VMEM((ROWS, TP), jnp.int32),
            pltpu.VMEM((2, LOCAL, KSUP, KERNELS, KSUP), F32),
            pltpu.VMEM(by.shape, BF),
            pltpu.VMEM((3 * VR, TP), BF),
            pltpu.VMEM(pack.shape[1:], BF),
            pltpu.VMEM(turned.shape[1:], BF),
            pltpu.VMEM((4 * VR, 2 * VR), BF),
            pltpu.VMEM(pu.shape, BF),
            pltpu.VMEM(sample.shape, BF),
            pltpu.VMEM(gather.shape, BF),
            pltpu.VMEM((4 * GRID, TP), BF),
            pltpu.VMEM(coarse.shape, BF),
            pltpu.VMEM(half_last.shape, F32),
            pltpu.VMEM((DEPTH * UR, 2 * VR), F32),
            pltpu.VMEM((GROUP, WIRE, VR), F32),
            pltpu.VMEM((GROUP, DEPTH, 4, UH, VR), F32),
            pltpu.VMEM((GROUP, 2, EDGE, VR), F32),
            pltpu.VMEM((UH, VR), F32),
            pltpu.VMEM((UH, VR), F32),
            pltpu.VMEM((UH, VR), F32),
            pltpu.VMEM((5, UH, VR), F32),
            pltpu.VMEM((4, 2, UH, VR), F32),
            pltpu.VMEM((2, EDGE, VR), F32),
            pltpu.VMEM((UH, VR), F32),
            pltpu.VMEM((3, UH, VR), F32),
            pltpu.VMEM((GROUP, UH, VR), F32),
            pltpu.VMEM((4, 2, UH, VR), F32),
            pltpu.VMEM((EDGE, VR), F32),
            pltpu.VMEM((GROUP, DEPTH * ROWS, 2 * GRID), F32),
            pltpu.VMEM((GROUP, DEPTH * ROWS, VR), F32),
            pltpu.VMEM((2, 2 * SPAN, 2 * VR), BF),
            pltpu.VMEM((GROUP, ROWS, EDGE), F32),
            pltpu.VMEM((GROUP, LOCAL * ROWS, VR), BF),
            pltpu.VMEM((2, 2 * LOCAL * ROWS, GRID), F32),
            pltpu.VMEM((GROUP, LOCAL * ROWS, VR), F32),
            pltpu.VMEM((GROUP, LOCAL, ROWS, TP), F32),
            pltpu.VMEM((ROWS, TP), F32),
            pltpu.VMEM((ROWS, TP), F32),
            pltpu.VMEM((ROWS, TP), F32),
            dma((20,)),
            dma((6,)),
            dma((6,)),
            dma((3,)),
            dma((3,)),
            dma((4,)),
            dma((2,)),
            dma((5,)),
            dma((3,)),
            dma((4,)),
            dma,
        ],
        compiler_params=pltpu.CompilerParams(collective_id=0, has_side_effects=True, vmem_limit_bytes=32 * 1024 * 1024),
        name="window_gradient",
    )
    kernel_real, kernel_imag = (jnp.swapaxes(x, 1, 2) for x in (kernel_real, kernel_imag))
    arrays = (theta, target, kernel_real, kernel_imag, weights, thresholds, *(jnp.asarray(x) for x in constants))
    return call(*(pltpu.with_memory_space_constraint(x, pltpu.HBM) for x in arrays))


def solution(mesh):
    in_specs = (
        P(("tile", "cond"), None),
        P("tile", None),
        P("cond", None, None, None),
        P("cond", None, None, None),
        P(),
        P("cond"),
    )
    out_specs = P(("tile", "cond"), None)
    body = functools.partial(shards, mesh.shape["tile"])
    return jax.shard_map(body, mesh=mesh, in_specs=in_specs, out_specs=out_specs, check_vma=False)
```

```python
import functools
import math

import jax
import jax.numpy as jnp
import ml_dtypes
import numpy as np
from jax import lax
from jax.experimental import pallas as pl
from jax.experimental.pallas import tpu as pltpu
from jax.sharding import PartitionSpec as P

TP = 512
HALO = 32
KSUP = 65
HALF = KSUP // 2
CONDS = 8
KERNELS = 2
SIZE = TP + 2 * HALO
ROWS = 128
GROUP = 4
LOCAL = CONDS // GROUP
UH = 40
UR = 2 * UH
VR = 128
FLAT = 2 * HALF
DEPTH = LOCAL * KERNELS
USED = UH + HALF
EDGE = 2 * DEPTH
CHUNK = EDGE + DEPTH // 2 * USED
WIRE = EDGE + DEPTH * USED
SPAN = DEPTH * ROWS
GRID = 128
SPARE = HALF + 1

MASK_STEEP = 2.0
RESIST_STEEP = 4.0
BAND_WEIGHT = 1.0

BF = jnp.bfloat16
F32 = jnp.float32
MESH = pl.DeviceIdType.MESH


def split(x):
    hi = x.astype(BF)
    return hi, (x - hi.astype(F32)).astype(BF)


def np_split(x):
    hi = x.astype(ml_dtypes.bfloat16)
    return hi, (x - hi.astype(np.float64)).astype(ml_dtypes.bfloat16)


def waves(positions):
    phase = np.fmod(np.asarray(positions, np.float64)[:, None] * np.arange(HALF + 1)[None, :], SIZE)
    angles = phase * (2.0 * math.pi / SIZE)
    return np.cos(angles), np.sin(angles)


def row_basis(positions):
    cos, sin = waves(positions)
    out = np.zeros((len(positions), UR))
    out[:, :HALF] = cos[:, 1:]
    out[:, HALF] = 1.0
    out[:, UH:USED] = sin[:, 1:]
    return out


def column_basis(positions):
    cos, sin = waves(positions)
    out = np.zeros((len(positions), VR))
    out[:, :HALF] = cos[:, 1:]
    out[:, HALF:FLAT] = sin[:, 1:]
    out[:, FLAT] = 1.0
    return out


def parity_rows():
    out = np.zeros((UR, UR))
    out[HALF, HALF] = 1.0
    for j in range(1, HALF + 1):
        out[j - 1, HALF + j] = out[j - 1, HALF - j] = out[UH + j - 1, HALF + j] = 1.0
        out[UH + j - 1, HALF - j] = -1.0
    return out


def parity_columns():
    out = np.zeros((2 * VR, 2 * VR))
    for ri in range(2):
        out[ri * VR + HALF, VR + ri] = 1.0
        for j in range(1, HALF + 1):
            even = ri * FLAT + j - 1
            out[ri * VR + HALF + j, even] = out[ri * VR + HALF - j, even] = 1.0
            out[ri * VR + HALF + j, even + HALF] = 1.0
            out[ri * VR + HALF - j, even + HALF] = -1.0
    return out


def tables():
    bf = ml_dtypes.bfloat16
    cols = column_basis(np.arange(TP) + HALO)
    hi, lo = np_split(cols)
    by = np.concatenate([hi, lo], axis=1)
    bt = np.concatenate([hi.T, lo.T], axis=0)
    places = column_basis(np.arange(GRID) * (SIZE / GRID))
    hi, lo = np_split(places[:, :FLAT])
    sample = np.zeros((3 * VR, 2 * GRID), bf)
    gather = np.zeros((4 * GRID, 2 * VR), bf)
    for ri in range(2):
        for block, part in enumerate((hi, hi, lo)):
            at = block * VR + ri * FLAT
            sample[at : at + FLAT, ri * GRID : (ri + 1) * GRID] = part.T
        gather[ri * GRID : (ri + 1) * GRID, ri * FLAT : (ri + 1) * FLAT] = hi
        gather[ri * GRID : (ri + 1) * GRID, VR + ri * FLAT : VR + (ri + 1) * FLAT] = lo
        gather[(2 + ri) * GRID : (3 + ri) * GRID, ri * FLAT : (ri + 1) * FLAT] = hi
    phase = (np.arange(TP) + HALO) * (2.0 * math.pi / SIZE)
    place = np.arange(GRID) * (2.0 * math.pi / GRID)
    spread = np.ones((GRID, TP))
    for f in range(1, GRID // 2):
        spread += 2.0 * np.cos(f * (phase[None, :] - place[:, None]))
    spread += np.cos(GRID // 2 * place)[:, None] * np.cos(GRID // 2 * phase)[None, :]
    spread /= GRID
    last = np.sin(GRID // 2 * phase)
    hi, lo = np_split(spread)
    last_hi, last_lo = np_split(last)
    rest = np.zeros((VR, TP), bf)
    for at in (0, FLAT):
        rest[at + HALF - 2], rest[at + HALF - 1], rest[at + FLAT - 1] = last_hi, last_hi, last_lo
    fine = np.concatenate([hi, lo, rest], axis=0)
    coarse = np.concatenate([hi.T, lo.T], axis=1)
    half_last = np.broadcast_to(0.5 * last, (8, TP)).astype(np.float32)
    pack = []
    turned = []
    for c in range(GROUP):
        own = row_basis(np.arange(ROWS) + HALO + ROWS * c)
        near = np.zeros_like(own)
        if c == 0:
            near[:HALO] = row_basis(np.arange(HALO) + HALO + TP)
        if c == GROUP - 1:
            near[ROWS - HALO :] = row_basis(np.arange(HALO))
        row = []
        column = []
        for table in (own, near):
            thi, tlo = np_split(table)
            row += [thi, tlo, thi, np.zeros((ROWS, 256 - 3 * UR), bf)]
            column.append(np.concatenate([thi.T, thi.T], axis=1))
            column.append(np.concatenate([tlo.T, np.zeros((UR, ROWS), bf)], axis=1))
        pack.append(np.concatenate(row, axis=1))
        turned.append(np.concatenate(column, axis=0))
    pv = parity_columns().astype(bf)
    pu = parity_rows().astype(bf)
    pu = np.concatenate([pu, pu], axis=1)
    return by, bt, np.stack(pack), np.stack(turned), pv, pu, sample, gather, fine, coarse, half_last


def dot(a, b):
    return jnp.dot(a, b, preferred_element_type=F32)


def kernel(
    tiles,
    theta_h, target_h, kr_h, ki_h, weights_h, thresholds_h, by_h, bt_h, pack_h, turned_h, pv_h, pu_h,
    sample_h, gather_h, fine_h, coarse_h, half_last_h,
    out_v,
    weights_s, thresholds_s, theta_v, target_v, raw_v, by, bt, pack, turned, pv, pu,
    sample, gather, fine, coarse, half_last, stack, zbuf, coef, ecoef, passed, rown, rhalo, rin, rsum, erow, aown, ain, anear, jbuf, jflat, amps, crossed, rows_v, flat_v, edge_v, push_v, last_v, resists, band, wanted, factor,
    load_sem, zs_sem, zr_sem, rs_sem, rr_sem, hs_sem, hr_sem, as_sem, ar_sem, near_sem, pass_sem,
):
    t = lax.axis_index("tile")
    c = lax.axis_index("cond")
    first = c == 0
    final = c == GROUP - 1
    has_prev = t > 0
    has_next = t < tiles - 1

    loads = []

    def load(src, dst):
        copy = pltpu.make_async_copy(src, dst, load_sem.at[len(loads)])
        copy.start()
        loads.append(copy)
        return copy

    load_kr = load(kr_h, raw_v.at[0])
    load_ki = load(ki_h, raw_v.at[1])
    load_pv = [load(pv_h, pv.at[pl.ds(at, 2 * VR), :]) for at in (0, 2 * VR)]
    load_pu = load(pu_h, pu)
    load_thresholds = load(thresholds_h, thresholds_s)
    load_theta = load(theta_h, theta_v)
    load_by = load(by_h, by)
    load_turned = load(turned_h.at[c], turned)
    load_pack = load(pack_h.at[c], pack)
    load_sample = load(sample_h, sample)
    load_fine = [
        load(fine_h.at[pl.ds(0, GRID), :], fine.at[pl.ds(0, GRID), :]),
        load(fine_h, fine.at[pl.ds(GRID, 3 * GRID), :]),
    ]
    load_coarse = load(coarse_h, coarse)
    load_half = load(half_last_h, half_last)
    load_gather = load(gather_h, gather)
    load_bt = [
        load(bt_h.at[pl.ds(0, VR), :], bt.at[pl.ds(0, VR), :]),
        load(bt_h, bt.at[pl.ds(VR, 2 * VR), :]),
    ]
    load_weights = load(weights_h, weights_s)
    load_target = load(target_h.at[pl.ds(pl.multiple_of(c * ROWS, ROWS), ROWS), :], target_v)

    def partner(mask):
        return (t, c ^ mask)

    barrier = pltpu.get_barrier_semaphore()

    def greet(device):
        pl.semaphore_signal(barrier, inc=1, device_id=device, device_id_type=MESH)

    mirror = ((t + tiles // 2) % tiles, c ^ 2)
    for mask in range(1, GROUP):
        greet(partner(mask))
    greet(mirror)

    bend = tiles // 2 - 1
    between = bend - 12
    at_bend = t == bend
    after_bend = (t == bend + 1) & first
    relays = (t == between) & jnp.logical_not(first | final)

    @pl.when(has_next)
    def _():
        greet((jnp.where(at_bend, between, t + 1), jnp.where(at_bend, 1 + c // 2, 0)))

    @pl.when(has_prev)
    def _():
        greet((t - 1, GROUP - 1))

    @pl.when(relays)
    def _():
        greet((bend + 1, 0))

    lane = lax.broadcasted_iota(jnp.int32, (UH, VR), 1)
    row = lax.broadcasted_iota(jnp.int32, (UH, VR), 0)
    tall_lane = lax.broadcasted_iota(jnp.int32, (UR, VR), 1)
    diagonal = tall_lane == lax.broadcasted_iota(jnp.int32, (UR, VR), 0)
    odd = lane % FLAT >= HALF
    sign_v = jnp.where(odd, -1.0, 1.0).astype(F32)
    sign_i = jnp.where(lane >= FLAT, -1.0, 1.0).astype(F32)
    edge_lane = lane[: 2 * DEPTH]
    edge_row = row[: 2 * DEPTH]

    def swap(x):
        return jnp.where(odd, pltpu.roll(x, HALF, 1), pltpu.roll(x, VR - HALF, 1))

    def turned_edge(x):
        out = jnp.where(edge_lane < UH, pltpu.roll(x, VR - UH, 1), -pltpu.roll(x, UH, 1))
        return jnp.where(edge_lane < UR, out, 0.0)

    def stacked(x):
        near = x.astype(BF).astype(F32)
        return jnp.concatenate([near, x - near], axis=0).astype(BF)

    def packed(x):
        out = jnp.where(lane < FLAT, x[:UH], pltpu.roll(x[UH:], FLAT, 1))
        flat = jnp.sum(jnp.where(diagonal, x[:, FLAT : FLAT + 1], 0.0), axis=0, keepdims=True)
        return jnp.where(row == SPARE, flat, out)

    def unpacked(x):
        flat = jnp.sum(jnp.where(diagonal, x[SPARE : SPARE + 1], 0.0), axis=1, keepdims=True)
        keep = (lane < FLAT) & (row < SPARE)
        out = []
        for h, value in enumerate((x, pltpu.roll(x, FLAT, 1))):
            out.append(jnp.where(lane == FLAT, flat[h * UH : (h + 1) * UH], jnp.where(keep, value, 0.0)))
        return out

    def unpack_kernels(s):
        for n in range(DEPTH):
            at = EDGE + n * USED
            even = zbuf[s, at : at + UH, :]
            uneven = zbuf[s, at + UH : at + USED, :]
            odd_rows = odd[: USED - UH]
            coef[s, n, 0] = jnp.where(odd, pltpu.roll(even, HALF, 1), even)
            coef[s, n, 1] = jnp.where(odd, pltpu.roll(even, FLAT, 1), pltpu.roll(even, HALF, 1))
            coef[s, n, 2, : USED - UH] = jnp.where(
                odd_rows, pltpu.roll(uneven, VR - HALF, 1), pltpu.roll(uneven, FLAT, 1)
            )
            coef[s, n, 3, : USED - UH] = jnp.where(odd_rows, uneven, pltpu.roll(uneven, VR - HALF, 1))
        flat = jnp.where(edge_lane < USED, zbuf[s, :EDGE, :], 0.0)
        other = jnp.where(edge_row % 2 == 0, pltpu.roll(flat, EDGE - 1, 0), -pltpu.roll(flat, 1, 0))
        ecoef[s, 0] = jnp.where(edge_lane < UH, flat, jnp.where(edge_lane < UR, pltpu.roll(flat, UH, 1), 0.0))
        ecoef[s, 1] = jnp.where(
            edge_lane < UH, pltpu.roll(other, VR - UH, 1), jnp.where(edge_lane < UR, other, 0.0)
        )

    stack[...] = jnp.zeros_like(stack)
    load_kr.wait()
    load_ki.wait()
    for ri in range(2):
        for l in range(LOCAL):
            for k in range(KERNELS):
                at = (l * KERNELS + k) * UR
                stack[at : at + KSUP, ri * VR : ri * VR + KSUP] = raw_v[ri, l, :, k, :]
    for copy in load_pv:
        copy.wait()
    load_pu.wait()
    hi, lo = split(stack[...])
    folded = dot(jnp.concatenate([hi, lo], axis=1), pv[...])
    hi, lo = split(folded)
    coef[:, :, 2:, USED - UH :, :] = jnp.zeros((GROUP, DEPTH, 2, UR - USED, VR), F32)
    load_thresholds.wait()
    for n in range(DEPTH):
        rhs = jnp.concatenate([hi[n * UR : (n + 1) * UR], lo[n * UR : (n + 1) * UR]], axis=0)
        value = dot(pu[...], rhs)
        zbuf[0, EDGE + n * USED : EDGE + (n + 1) * USED, :] = value[:USED, :VR]
        for ri in range(2):
            flat = jnp.sum(jnp.where(diagonal, value[:, VR + ri : VR + ri + 1], 0.0), axis=0, keepdims=True)
            if 2 * n + ri < LOCAL:
                flat = jnp.where(lane[:1] == VR - 1, thresholds_s[2 * n + ri], flat)
            zbuf[0, 2 * n + ri : 2 * n + ri + 1, :] = flat

    load_theta.wait()
    load_by.wait()
    load_turned.wait()
    mask_rows = jnp.tanh(MASK_STEEP * theta_v[...])
    hi, lo = split(mask_rows)
    wide = dot(jnp.concatenate([hi, lo], axis=0), by[...])
    column = wide[:ROWS, :VR] + wide[:ROWS, VR:] + wide[ROWS:, :VR]
    hi, lo = split(column)
    both = dot(turned[...], jnp.concatenate([hi, lo], axis=0))
    rown[...] = packed(both[:UR] + both[UR : 2 * UR])
    rhalo[...] = packed(both[2 * UR : 3 * UR] + both[3 * UR :])

    edge_of = (has_next & final) | (has_prev & first)
    waited = jnp.where(edge_of, 2 * GROUP, GROUP)
    pl.semaphore_wait(barrier, jnp.where(after_bend | relays, GROUP + 2, waited))

    def remote(src, dst, send, recv, device):
        return pltpu.make_async_remote_copy(
            src_ref=src, dst_ref=dst, send_sem=send, recv_sem=recv, device_id=device, device_id_type=MESH
        )

    def halo_next(other):
        return remote(rhalo, rin.at[3], hs_sem.at[other], hr_sem.at[0], (t + 1, other))

    def halo_prev(other):
        return remote(rhalo, rin.at[4], hs_sem.at[other], hr_sem.at[1], (t - 1, other))

    def halo_via(side):
        return remote(rhalo, passed, hs_sem.at[side], pass_sem, (between, 1 + side))

    def halo_passed(core):
        return remote(passed, rin.at[4], hs_sem.at[core], hr_sem.at[1], (bend, 2 * (c - 1) + core))

    def part(mask):
        return remote(rown, rin.at[mask - 1], rs_sem.at[mask - 1], rr_sem.at[mask - 1], partner(mask))

    def kernels_to(mask, chunk):
        device = partner(1) if mask != 2 else mirror
        source = 2 if mask == 3 else 0
        rows = pl.ds(0, CHUNK) if chunk == 0 else pl.ds(CHUNK, WIRE - CHUNK)
        sem = 2 * (mask - 1) + chunk
        return remote(
            zbuf.at[source, rows, :], zbuf.at[mask, rows, :], zs_sem.at[sem], zr_sem.at[sem], device
        )

    @pl.when(has_next & final)
    def _():
        for other in range(GROUP):
            halo_next(other).start()

    @pl.when(has_prev & first & jnp.logical_not(after_bend))
    def _():
        for other in range(GROUP):
            halo_prev(other).start()

    @pl.when(after_bend)
    def _():
        for side in range(2):
            halo_via(side).start()

    for mask in range(1, GROUP):
        part(mask).start()
    for mask in (2, 1):
        for chunk in range(2):
            kernels_to(mask, chunk).start()

    @pl.when(relays)
    def _():
        halo_via(0).wait_recv()
        for core in range(2):
            halo_passed(core).start()

    @pl.when(jnp.logical_not(has_prev))
    def _():
        rin[3] = jnp.zeros((UH, VR), F32)

    @pl.when(jnp.logical_not(has_next))
    def _():
        rin[4] = jnp.zeros((UH, VR), F32)

    unpack_kernels(0)
    for chunk in range(2):
        kernels_to(1, chunk).wait_recv()
    unpack_kernels(1)

    @pl.when(has_prev)
    def _():
        halo_next(0).wait_recv()

    @pl.when(has_next)
    def _():
        halo_prev(0).wait_recv()

    for mask in range(1, GROUP):
        part(mask).wait_recv()

    total = rown[...] + rin[0] + rin[1] + rin[2] + rin[3] + rin[4]
    total = total * (1.0 / (SIZE * SIZE))
    keep = row < SPARE
    turn = pltpu.roll(total, FLAT, 1)
    halves = [
        jnp.where(keep, jnp.where(lane < FLAT, total, turn), 0.0),
        jnp.where(keep, jnp.where(lane < FLAT, turn, total), 0.0),
    ]
    for h in range(2):
        sign_u = 1.0 - 2.0 * h
        rsum[0, h] = halves[h]
        rsum[1, h] = sign_i * sign_v * swap(halves[h])
        rsum[2, h] = sign_u * sign_i * halves[1 - h]
        rsum[3, h] = (-sign_u) * sign_v * swap(halves[1 - h])
    flat = jnp.where(edge_lane < UR, total[SPARE : SPARE + 1], 0.0)
    erow[0] = flat
    erow[1] = turned_edge(flat)

    load_pack.wait()
    load_sample.wait()
    for copy in load_fine:
        copy.wait()
    block_lane = lax.broadcasted_iota(jnp.int32, (ROWS, VR), 1)

    def grids_and_rows(s):
        grids = []
        for n in range(DEPTH):
            grid = []
            for h in range(2):
                terms = [coef[s, n, m] * rsum[m, h] for m in range(4)]
                grid.append((terms[0] + terms[1]) + (terms[2] + terms[3]))
            grids.append(jnp.concatenate(grid, axis=0))
        cross = [None] * LOCAL
        for l in range(LOCAL):
            hi, lo = split(jnp.concatenate(grids[KERNELS * l : KERNELS * (l + 1)], axis=1))
            tall = dot(pack[:, : 3 * UR], jnp.concatenate([hi, hi, lo], axis=0))
            for k in range(KERNELS):
                part = tall[:, k * VR : (k + 1) * VR]
                at = (l * KERNELS + k) * ROWS
                other = jnp.where(block_lane % FLAT == HALF - 1, pltpu.roll(part, VR - HALF, 1), 0.0)
                other = jnp.where(block_lane % FLAT == FLAT - 1, pltpu.roll(part, HALF, 1), other)
                crossed[s, at : at + ROWS, :] = other
                other = part * other
                cross[l] = other if k == 0 else cross[l] + other
                hi, lo = split(part)
                rows_v[s // 2, s % 2 * SPAN + at : s % 2 * SPAN + at + ROWS, :VR] = hi
                rows_v[s // 2, s % 2 * SPAN + at : s % 2 * SPAN + at + ROWS, VR:] = lo
        for l in range(LOCAL):
            near = cross[l].astype(BF).astype(F32)
            far = pltpu.roll(cross[l] - near, VR - 1, 1)
            edge_v[s, l * ROWS : (l + 1) * ROWS, :] = jnp.where(block_lane % FLAT == HALF - 2, far, near).astype(BF)
        flat = stacked(ecoef[s, 0] * erow[0] + ecoef[s, 1] * erow[1])
        upper = dot(flat, turned[:VR, :ROWS])
        lower = dot(flat, turned[UR : UR + VR, :ROWS])
        flat_v[s] = (upper[:EDGE] + upper[EDGE:] + lower[:EDGE]).T

    def resist_of(slots):
        held = slots[0] // 2
        amp = dot(jnp.concatenate([rows_v[held], rows_v[held, :, :VR]], axis=1), sample[...])
        lhs = []
        for s in slots:
            for l in range(LOCAL):
                sampled = None
                for k in range(KERNELS):
                    n = l * KERNELS + k
                    at = s % 2 * SPAN + n * ROWS
                    for ri in range(2):
                        piece = amp[at : at + ROWS, ri * GRID : (ri + 1) * GRID]
                        piece = piece + flat_v[s, :, 2 * n + ri : 2 * n + ri + 1]
                        amps[s, n * ROWS : (n + 1) * ROWS, ri * GRID : (ri + 1) * GRID] = piece
                        sampled = piece * piece if k + ri == 0 else sampled + piece * piece
                hi, lo = split(sampled)
                lhs.append(jnp.concatenate([hi, lo, hi, edge_v[s, l * ROWS : (l + 1) * ROWS, :]], axis=1))
        intensities = dot(jnp.concatenate(lhs, axis=0), fine[...])
        total = None
        for s in slots:
            for l in range(LOCAL):
                at = (s % 2 * LOCAL + l) * ROWS
                level = zbuf[s, l : l + 1, VR - 1 : VR]
                resist = jax.nn.sigmoid(RESIST_STEEP * (intensities[at : at + ROWS] - level))
                resists[s, l] = resist
                total = resist if total is None else total + resist
        if slots[0] == 0:
            band[...] = total
        else:
            band[...] += total

    grids_and_rows(0)
    kernels_to(2, 0).wait_recv()
    kernels_to(3, 0).start()
    grids_and_rows(1)
    kernels_to(2, 1).wait_recv()
    kernels_to(3, 1).start()
    unpack_kernels(2)
    resist_of((0, 1))
    grids_and_rows(2)
    for chunk in range(2):
        kernels_to(3, chunk).wait_recv()
    unpack_kernels(3)
    grids_and_rows(3)
    resist_of((2, 3))

    load_target.wait()
    load_weights.wait()
    weight_sum = weights_s[0]
    for n in range(1, CONDS):
        weight_sum = weight_sum + weights_s[n]
    weight_sum = jnp.full((8, TP), weight_sum, jnp.int32).astype(F32)
    wanted[...] = target_v[...].astype(F32)
    band[...] = band[...] * (4.0 * RESIST_STEEP * BAND_WEIGHT / CONDS / CONDS)

    load_coarse.wait()
    load_half.wait()
    load_gather.wait()

    def push_of(slots):
        fields = []
        for s in slots:
            for l in range(LOCAL):
                weight = jnp.full((8, TP), weights_s[(c ^ s) * LOCAL + l], jnp.int32).astype(F32) / weight_sum
                pull = (4.0 * RESIST_STEEP) * weight[0:1]
                resist = resists[s, l]
                slope = (pull + 4.0 * RESIST_STEEP * BAND_WEIGHT / CONDS) * resist - (pull * wanted[...] + band[...])
                field = slope * (resist - resist * resist)
                last = jnp.sum(field * half_last[0:1, :], axis=1, keepdims=True)
                last_v[s, l * ROWS : (l + 1) * ROWS, :] = jnp.broadcast_to(last, (ROWS, VR))
                fields.append(field)
        hi, lo = split(jnp.concatenate(fields, axis=0))
        wide = dot(jnp.concatenate([hi, lo], axis=0), coarse[...])
        half = 2 * LOCAL * ROWS
        push_v[slots[0] // 2] = wide[:half, :GRID] + wide[:half, GRID:] + wide[half:, :GRID]

    def adjoint_of(slots):
        rows = []
        flats = []
        for s in slots:
            flat = []
            for n in range(DEPTH):
                at = (s % 2 * LOCAL + n // KERNELS) * ROWS
                push = push_v[slots[0] // 2, at : at + ROWS, :]
                drive = []
                for ri in range(2):
                    piece = push * amps[s, n * ROWS : (n + 1) * ROWS, ri * GRID : (ri + 1) * GRID]
                    flat.append(jnp.where(block_lane == 2 * n + ri, jnp.sum(piece, axis=1, keepdims=True), 0.0))
                    drive.append(piece)
                hi, lo = split(jnp.concatenate(drive, axis=1))
                rows.append(jnp.concatenate([hi, lo], axis=1))
            while len(flat) > 1:
                flat = [flat[i] + flat[i + 1] for i in range(0, len(flat), 2)]
            flats.append(flat[0])
        drive = dot(jnp.concatenate(rows, axis=0), gather[...])
        drive = drive[:, :VR] + drive[:, VR:]
        sums = [[None, None] for _ in range(4)]
        for s in slots:
            for l in range(LOCAL):
                pair = []
                for n in (KERNELS * l, KERNELS * l + 1):
                    at = s % 2 * SPAN + n * ROWS
                    last = last_v[s, l * ROWS : (l + 1) * ROWS, :]
                    pair.append(drive[at : at + ROWS] + last * crossed[s, n * ROWS : (n + 1) * ROWS, :])
                hi, lo = split(jnp.concatenate(pair, axis=1))
                back = dot(turned[: 2 * UR, :], jnp.concatenate([hi, lo], axis=0))
                back = back[:UR] + back[UR:]
                for k in range(KERNELS):
                    for h in range(2):
                        value = back[h * UH : (h + 1) * UH, k * VR : (k + 1) * VR]
                        for m in range(4):
                            term = coef[s, l * KERNELS + k, m] * value
                            sums[m][h] = term if sums[m][h] is None else sums[m][h] + term
        total = None
        for s, flat in zip(slots, flats):
            wide = dot(stacked(flat.T[:EDGE]), pack[:, : 2 * VR])
            here = wide[:EDGE, :VR] + wide[EDGE:, :VR]
            upper = pltpu.roll(wide[:EDGE, :VR], VR - UR, 1)
            lower = pltpu.roll(wide[:EDGE, VR:], VR - UR, 1)
            here = here + jnp.where(edge_lane < VR - UR, upper, lower)
            term = ecoef[s, 0] * here - ecoef[s, 1] * turned_edge(here)
            total = term if total is None else total + term
        for m in range(4):
            for h in range(2):
                if slots[0] == 0:
                    jbuf[m, h] = sums[m][h]
                else:
                    jbuf[m, h] += sums[m][h]
        if slots[0] == 0:
            jflat[...] = total
        else:
            jflat[...] += total

    push_of((0, 1))
    adjoint_of((0, 1))
    push_of((2, 3))
    adjoint_of((2, 3))

    def folded_part(m, h):
        sign = 1.0 if m in (0, 3) else -1.0
        return jbuf[m, h] + sign * pltpu.roll(jbuf[m, h], FLAT, 1)

    halves = []
    for h in range(2):
        sign_u = 1.0 - 2.0 * h
        halves.append(
            folded_part(0, h)
            + swap(sign_v * folded_part(1, h))
            - sign_u * folded_part(2, 1 - h)
            + swap(sign_u * sign_v * folded_part(3, 1 - h))
        )
    value = jnp.where(lane < FLAT, halves[0], pltpu.roll(halves[1], FLAT, 1))
    aown[...] = jnp.where(row == SPARE, jnp.sum(jflat[...], axis=0, keepdims=True), value)

    def adjoint_part(mask):
        return remote(aown, ain.at[mask - 1], as_sem.at[mask - 1], ar_sem.at[mask - 1], partner(mask))

    def adjoint_prev():
        return remote(aown, anear.at[c], as_sem.at[3], near_sem.at[c], (t - 1, GROUP - 1))

    def adjoint_next():
        return remote(aown, anear.at[c], as_sem.at[4], near_sem.at[c], (t + 1, 0))

    def adjoint_near(other):
        return remote(aown, anear.at[other], as_sem.at[3], near_sem.at[other], (t, c ^ 1))

    @pl.when(has_prev)
    def _():
        adjoint_prev().start()

    @pl.when(has_next)
    def _():
        adjoint_next().start()

    for mask in range(1, GROUP):
        adjoint_part(mask).start()

    near = (first & has_prev) | (final & has_next)

    factor[...] = (MASK_STEEP / (SIZE * SIZE)) * (1.0 - jnp.square(jnp.tanh(MASK_STEEP * theta_v[...])))
    for copy in load_bt:
        copy.wait()

    for mask in range(1, GROUP):
        adjoint_part(mask).wait_recv()

    def sensitivity(value, rows, columns):
        hi, lo = split(jnp.concatenate(unpacked(value), axis=0))
        value = jnp.concatenate([hi, hi, lo, jnp.zeros((256 - 3 * UR, VR), BF)], axis=0)
        hi, lo = split(dot(pack[rows, columns], value))
        return dot(jnp.concatenate([hi, lo, hi], axis=1), bt[...])

    out_v[...] = sensitivity(aown[...] + ain[0] + ain[1] + ain[2], slice(None), slice(0, 256)) * factor[...]

    @pl.when(near)
    def _():
        for other in range(GROUP):
            adjoint_near(other).wait_recv()
        edge = pl.ds(pl.multiple_of(jnp.where(first, 0, ROWS - HALO), HALO), HALO)
        value = anear[0] + anear[1] + anear[2] + anear[3]
        out_v[edge, :] += sensitivity(value, edge, slice(256, 512)) * factor[edge, :]

    @pl.when(has_next & final)
    def _():
        for other in range(GROUP):
            halo_next(other).wait_send()

    @pl.when(has_prev & first & jnp.logical_not(after_bend))
    def _():
        for other in range(GROUP):
            halo_prev(other).wait_send()

    @pl.when(after_bend)
    def _():
        for side in range(2):
            halo_via(side).wait_send()

    @pl.when(relays)
    def _():
        for core in range(2):
            halo_passed(core).wait_send()

    for mask in range(1, GROUP):
        part(mask).wait_send()
        for chunk in range(2):
            kernels_to(mask, chunk).wait_send()
        adjoint_part(mask).wait_send()

    @pl.when(has_prev)
    def _():
        adjoint_prev().wait_send()

    @pl.when(has_next)
    def _():
        adjoint_next().wait_send()


def shards(tiles, theta, target, kernel_real, kernel_imag, weights, thresholds):
    constants = tables()
    dma = pltpu.SemaphoreType.DMA
    by, bt, pack, turned, pv, pu, sample, gather, fine, coarse, half_last = constants
    call = pl.pallas_call(
        functools.partial(kernel, tiles),
        out_shape=jax.ShapeDtypeStruct((ROWS, TP), F32),
        in_specs=[pl.BlockSpec(memory_space=pltpu.HBM)] * 17,
        out_specs=pl.BlockSpec(memory_space=pltpu.VMEM),
        scratch_shapes=[
            pltpu.SMEM((CONDS,), jnp.int32),
            pltpu.SMEM((LOCAL,), F32),
            pltpu.VMEM((ROWS, TP), F32),
            pltpu.VMEM((ROWS, TP), jnp.int32),
            pltpu.VMEM((2, LOCAL, KSUP, KERNELS, KSUP), F32),
            pltpu.VMEM(by.shape, BF),
            pltpu.VMEM((3 * VR, TP), BF),
            pltpu.VMEM(pack.shape[1:], BF),
            pltpu.VMEM(turned.shape[1:], BF),
            pltpu.VMEM((4 * VR, 2 * VR), BF),
            pltpu.VMEM(pu.shape, BF),
            pltpu.VMEM(sample.shape, BF),
            pltpu.VMEM(gather.shape, BF),
            pltpu.VMEM((4 * GRID, TP), BF),
            pltpu.VMEM(coarse.shape, BF),
            pltpu.VMEM(half_last.shape, F32),
            pltpu.VMEM((DEPTH * UR, 2 * VR), F32),
            pltpu.VMEM((GROUP, WIRE, VR), F32),
            pltpu.VMEM((GROUP, DEPTH, 4, UH, VR), F32),
            pltpu.VMEM((GROUP, 2, EDGE, VR), F32),
            pltpu.VMEM((UH, VR), F32),
            pltpu.VMEM((UH, VR), F32),
            pltpu.VMEM((UH, VR), F32),
            pltpu.VMEM((5, UH, VR), F32),
            pltpu.VMEM((4, 2, UH, VR), F32),
            pltpu.VMEM((2, EDGE, VR), F32),
            pltpu.VMEM((UH, VR), F32),
            pltpu.VMEM((3, UH, VR), F32),
            pltpu.VMEM((GROUP, UH, VR), F32),
            pltpu.VMEM((4, 2, UH, VR), F32),
            pltpu.VMEM((EDGE, VR), F32),
            pltpu.VMEM((GROUP, DEPTH * ROWS, 2 * GRID), F32),
            pltpu.VMEM((GROUP, DEPTH * ROWS, VR), F32),
            pltpu.VMEM((2, 2 * SPAN, 2 * VR), BF),
            pltpu.VMEM((GROUP, ROWS, EDGE), F32),
            pltpu.VMEM((GROUP, LOCAL * ROWS, VR), BF),
            pltpu.VMEM((2, 2 * LOCAL * ROWS, GRID), F32),
            pltpu.VMEM((GROUP, LOCAL * ROWS, VR), F32),
            pltpu.VMEM((GROUP, LOCAL, ROWS, TP), F32),
            pltpu.VMEM((ROWS, TP), F32),
            pltpu.VMEM((ROWS, TP), F32),
            pltpu.VMEM((ROWS, TP), F32),
            dma((20,)),
            dma((6,)),
            dma((6,)),
            dma((3,)),
            dma((3,)),
            dma((4,)),
            dma((2,)),
            dma((5,)),
            dma((3,)),
            dma((4,)),
            dma,
        ],
        compiler_params=pltpu.CompilerParams(collective_id=0, has_side_effects=True, vmem_limit_bytes=32 * 1024 * 1024),
        name="window_gradient",
    )
    kernel_real, kernel_imag = (jnp.swapaxes(x, 1, 2) for x in (kernel_real, kernel_imag))
    arrays = (theta, target, kernel_real, kernel_imag, weights, thresholds, *(jnp.asarray(x) for x in constants))
    return call(*(pltpu.with_memory_space_constraint(x, pltpu.HBM) for x in arrays))


def solution(mesh):
    in_specs = (
        P(("tile", "cond"), None),
        P("tile", None),
        P("cond", None, None, None),
        P("cond", None, None, None),
        P(),
        P("cond"),
    )
    out_specs = P(("tile", "cond"), None)
    body = functools.partial(shards, mesh.shape["tile"])
    return jax.shard_map(body, mesh=mesh, in_specs=in_specs, out_specs=out_specs, check_vma=False)
```

```python
import functools
import math

import jax
import jax.numpy as jnp
import ml_dtypes
import numpy as np
from jax import lax
from jax.experimental import pallas as pl
from jax.experimental.pallas import tpu as pltpu
from jax.sharding import PartitionSpec as P

TP = 512
HALO = 32
KSUP = 65
HALF = KSUP // 2
CONDS = 8
KERNELS = 2
SIZE = TP + 2 * HALO
ROWS = 128
GROUP = 4
LOCAL = CONDS // GROUP
UH = 40
UR = 2 * UH
VR = 128
FLAT = 2 * HALF
DEPTH = LOCAL * KERNELS
USED = UH + HALF
EDGE = 2 * DEPTH
CHUNK = EDGE + DEPTH // 2 * USED
WIRE = EDGE + DEPTH * USED
SPAN = DEPTH * ROWS
GRID = 128
SPARE = HALF + 1

MASK_STEEP = 2.0
RESIST_STEEP = 4.0
BAND_WEIGHT = 1.0

BF = jnp.bfloat16
F32 = jnp.float32
MESH = pl.DeviceIdType.MESH


def split(x):
    hi = x.astype(BF)
    return hi, (x - hi.astype(F32)).astype(BF)


def np_split(x):
    hi = x.astype(ml_dtypes.bfloat16)
    return hi, (x - hi.astype(np.float64)).astype(ml_dtypes.bfloat16)


def waves(positions):
    phase = np.fmod(np.asarray(positions, np.float64)[:, None] * np.arange(HALF + 1)[None, :], SIZE)
    angles = phase * (2.0 * math.pi / SIZE)
    return np.cos(angles), np.sin(angles)


def row_basis(positions):
    cos, sin = waves(positions)
    out = np.zeros((len(positions), UR))
    out[:, :HALF] = cos[:, 1:]
    out[:, HALF] = 1.0
    out[:, UH:USED] = sin[:, 1:]
    return out


def column_basis(positions):
    cos, sin = waves(positions)
    out = np.zeros((len(positions), VR))
    out[:, :HALF] = cos[:, 1:]
    out[:, HALF:FLAT] = sin[:, 1:]
    out[:, FLAT] = 1.0
    return out


def parity_rows():
    out = np.zeros((UR, UR))
    out[HALF, HALF] = 1.0
    for j in range(1, HALF + 1):
        out[j - 1, HALF + j] = out[j - 1, HALF - j] = out[UH + j - 1, HALF + j] = 1.0
        out[UH + j - 1, HALF - j] = -1.0
    return out


def parity_columns():
    out = np.zeros((2 * VR, 2 * VR))
    for ri in range(2):
        out[ri * VR + HALF, VR + ri] = 1.0
        for j in range(1, HALF + 1):
            even = ri * FLAT + j - 1
            out[ri * VR + HALF + j, even] = out[ri * VR + HALF - j, even] = 1.0
            out[ri * VR + HALF + j, even + HALF] = 1.0
            out[ri * VR + HALF - j, even + HALF] = -1.0
    return out


def tables():
    bf = ml_dtypes.bfloat16
    cols = column_basis(np.arange(TP) + HALO)
    hi, lo = np_split(cols)
    by = np.concatenate([hi, lo], axis=1)
    bt = np.concatenate([hi.T, lo.T], axis=0)
    places = column_basis(np.arange(GRID) * (SIZE / GRID))
    hi, lo = np_split(places[:, :FLAT])
    sample = np.zeros((3 * VR, 2 * GRID), bf)
    gather = np.zeros((4 * GRID, 2 * VR), bf)
    for ri in range(2):
        for block, part in enumerate((hi, hi, lo)):
            at = block * VR + ri * FLAT
            sample[at : at + FLAT, ri * GRID : (ri + 1) * GRID] = part.T
        gather[ri * GRID : (ri + 1) * GRID, ri * FLAT : (ri + 1) * FLAT] = hi
        gather[ri * GRID : (ri + 1) * GRID, VR + ri * FLAT : VR + (ri + 1) * FLAT] = lo
        gather[(2 + ri) * GRID : (3 + ri) * GRID, ri * FLAT : (ri + 1) * FLAT] = hi
    phase = (np.arange(TP) + HALO) * (2.0 * math.pi / SIZE)
    place = np.arange(GRID) * (2.0 * math.pi / GRID)
    spread = np.ones((GRID, TP))
    for f in range(1, GRID // 2):
        spread += 2.0 * np.cos(f * (phase[None, :] - place[:, None]))
    spread += np.cos(GRID // 2 * place)[:, None] * np.cos(GRID // 2 * phase)[None, :]
    spread /= GRID
    last = np.sin(GRID // 2 * phase)
    hi, lo = np_split(spread)
    last_hi, last_lo = np_split(last)
    rest = np.zeros((VR, TP), bf)
    for at in (0, FLAT):
        rest[at + HALF - 2], rest[at + HALF - 1], rest[at + FLAT - 1] = last_hi, last_hi, last_lo
    fine = np.concatenate([hi, lo, rest], axis=0)
    coarse = np.concatenate([hi.T, lo.T], axis=1)
    half_last = np.broadcast_to(0.5 * last, (8, TP)).astype(np.float32)
    pack = []
    turned = []
    for c in range(GROUP):
        own = row_basis(np.arange(ROWS) + HALO + ROWS * c)
        near = np.zeros_like(own)
        if c == 0:
            near[:HALO] = row_basis(np.arange(HALO) + HALO + TP)
        if c == GROUP - 1:
            near[ROWS - HALO :] = row_basis(np.arange(HALO))
        row = []
        column = []
        for table in (own, near):
            thi, tlo = np_split(table)
            row += [thi, tlo, thi, np.zeros((ROWS, 256 - 3 * UR), bf)]
            column.append(np.concatenate([thi.T, thi.T], axis=1))
            column.append(np.concatenate([tlo.T, np.zeros((UR, ROWS), bf)], axis=1))
        pack.append(np.concatenate(row, axis=1))
        turned.append(np.concatenate(column, axis=0))
    pv = parity_columns().astype(bf)
    pu = parity_rows().astype(bf)
    pu = np.concatenate([pu, pu], axis=1)
    return by, bt, np.stack(pack), np.stack(turned), pv, pu, sample, gather, fine, coarse, half_last


def dot(a, b):
    return jnp.dot(a, b, preferred_element_type=F32)


def kernel(
    tiles,
    theta_h, target_h, kr_h, ki_h, weights_h, thresholds_h, by_h, bt_h, pack_h, turned_h, pv_h, pu_h,
    sample_h, gather_h, fine_h, coarse_h, half_last_h,
    out_v,
    weights_s, thresholds_s, theta_v, target_v, raw_v, by, bt, pack, turned, pv, pu,
    sample, gather, fine, coarse, half_last, stack, zbuf, coef, ecoef, passed, rpair, rown, rhalo, rin, rsum, erow, aown, ain, anear, jbuf, jflat, amps, crossed, rows_v, flat_v, edge_v, push_v, last_v, resists, band, wanted, factor,
    load_sem, zs_sem, zr_sem, rs_sem, rr_sem, hs_sem, hr_sem, as_sem, ar_sem, near_sem, pass_sem,
):
    t = lax.axis_index("tile")
    c = lax.axis_index("cond")
    first = c == 0
    final = c == GROUP - 1
    has_prev = t > 0
    has_next = t < tiles - 1

    loads = []

    def load(src, dst):
        copy = pltpu.make_async_copy(src, dst, load_sem.at[len(loads)])
        copy.start()
        loads.append(copy)
        return copy

    load_kr = load(kr_h, raw_v.at[0])
    load_ki = load(ki_h, raw_v.at[1])
    load_pv = [load(pv_h, pv.at[pl.ds(at, 2 * VR), :]) for at in (0, 2 * VR)]
    load_pu = load(pu_h, pu)
    load_thresholds = load(thresholds_h, thresholds_s)
    load_theta = load(theta_h, theta_v)
    load_by = load(by_h, by)
    load_turned = load(turned_h.at[c], turned)
    load_pack = load(pack_h.at[c], pack)
    load_sample = load(sample_h, sample)
    load_fine = [
        load(fine_h.at[pl.ds(0, GRID), :], fine.at[pl.ds(0, GRID), :]),
        load(fine_h, fine.at[pl.ds(GRID, 3 * GRID), :]),
    ]
    load_coarse = load(coarse_h, coarse)
    load_half = load(half_last_h, half_last)
    load_gather = load(gather_h, gather)
    load_bt = [
        load(bt_h.at[pl.ds(0, VR), :], bt.at[pl.ds(0, VR), :]),
        load(bt_h, bt.at[pl.ds(VR, 2 * VR), :]),
    ]
    load_weights = load(weights_h, weights_s)
    load_target = load(target_h.at[pl.ds(pl.multiple_of(c * ROWS, ROWS), ROWS), :], target_v)

    def partner(mask):
        return (t, c ^ mask)

    barrier = pltpu.get_barrier_semaphore()

    def greet(device):
        pl.semaphore_signal(barrier, inc=1, device_id=device, device_id_type=MESH)

    mirror = ((t + tiles // 2) % tiles, c ^ 2)
    for mask in range(1, GROUP):
        greet(partner(mask))
    greet(mirror)

    bend = tiles // 2 - 1
    between = bend - 12
    at_bend = t == bend
    after_bend = (t == bend + 1) & first
    relays = (t == between) & jnp.logical_not(first | final)

    @pl.when(has_next)
    def _():
        greet((jnp.where(at_bend, between, t + 1), jnp.where(at_bend, 1 + c // 2, 0)))

    @pl.when(has_prev)
    def _():
        greet((t - 1, GROUP - 1))

    @pl.when(relays)
    def _():
        greet((bend + 1, 0))

    lane = lax.broadcasted_iota(jnp.int32, (UH, VR), 1)
    row = lax.broadcasted_iota(jnp.int32, (UH, VR), 0)
    tall_lane = lax.broadcasted_iota(jnp.int32, (UR, VR), 1)
    diagonal = tall_lane == lax.broadcasted_iota(jnp.int32, (UR, VR), 0)
    odd = lane % FLAT >= HALF
    sign_v = jnp.where(odd, -1.0, 1.0).astype(F32)
    sign_i = jnp.where(lane >= FLAT, -1.0, 1.0).astype(F32)
    edge_lane = lane[: 2 * DEPTH]
    edge_row = row[: 2 * DEPTH]

    def swap(x):
        return jnp.where(odd, pltpu.roll(x, HALF, 1), pltpu.roll(x, VR - HALF, 1))

    def turned_edge(x):
        out = jnp.where(edge_lane < UH, pltpu.roll(x, VR - UH, 1), -pltpu.roll(x, UH, 1))
        return jnp.where(edge_lane < UR, out, 0.0)

    def stacked(x):
        near = x.astype(BF).astype(F32)
        return jnp.concatenate([near, x - near], axis=0).astype(BF)

    def packed(x):
        out = jnp.where(lane < FLAT, x[:UH], pltpu.roll(x[UH:], FLAT, 1))
        flat = jnp.sum(jnp.where(diagonal, x[:, FLAT : FLAT + 1], 0.0), axis=0, keepdims=True)
        return jnp.where(row == SPARE, flat, out)

    def unpacked(x):
        flat = jnp.sum(jnp.where(diagonal, x[SPARE : SPARE + 1], 0.0), axis=1, keepdims=True)
        keep = (lane < FLAT) & (row < SPARE)
        out = []
        for h, value in enumerate((x, pltpu.roll(x, FLAT, 1))):
            out.append(jnp.where(lane == FLAT, flat[h * UH : (h + 1) * UH], jnp.where(keep, value, 0.0)))
        return out

    def unpack_kernels(s):
        for n in range(DEPTH):
            at = EDGE + n * USED
            even = zbuf[s, at : at + UH, :]
            uneven = zbuf[s, at + UH : at + USED, :]
            odd_rows = odd[: USED - UH]
            coef[s, n, 0] = jnp.where(odd, pltpu.roll(even, HALF, 1), even)
            coef[s, n, 1] = jnp.where(odd, pltpu.roll(even, FLAT, 1), pltpu.roll(even, HALF, 1))
            coef[s, n, 2, : USED - UH] = jnp.where(
                odd_rows, pltpu.roll(uneven, VR - HALF, 1), pltpu.roll(uneven, FLAT, 1)
            )
            coef[s, n, 3, : USED - UH] = jnp.where(odd_rows, uneven, pltpu.roll(uneven, VR - HALF, 1))
        flat = jnp.where(edge_lane < USED, zbuf[s, :EDGE, :], 0.0)
        other = jnp.where(edge_row % 2 == 0, pltpu.roll(flat, EDGE - 1, 0), -pltpu.roll(flat, 1, 0))
        ecoef[s, 0] = jnp.where(edge_lane < UH, flat, jnp.where(edge_lane < UR, pltpu.roll(flat, UH, 1), 0.0))
        ecoef[s, 1] = jnp.where(
            edge_lane < UH, pltpu.roll(other, VR - UH, 1), jnp.where(edge_lane < UR, other, 0.0)
        )

    stack[...] = jnp.zeros_like(stack)
    load_kr.wait()
    load_ki.wait()
    for ri in range(2):
        for l in range(LOCAL):
            for k in range(KERNELS):
                at = (l * KERNELS + k) * UR
                stack[at : at + KSUP, ri * VR : ri * VR + KSUP] = raw_v[ri, l, :, k, :]
    for copy in load_pv:
        copy.wait()
    load_pu.wait()
    hi, lo = split(stack[...])
    folded = dot(jnp.concatenate([hi, lo], axis=1), pv[...])
    hi, lo = split(folded)
    coef[:, :, 2:, USED - UH :, :] = jnp.zeros((GROUP, DEPTH, 2, UR - USED, VR), F32)
    load_thresholds.wait()
    for n in range(DEPTH):
        rhs = jnp.concatenate([hi[n * UR : (n + 1) * UR], lo[n * UR : (n + 1) * UR]], axis=0)
        value = dot(pu[...], rhs)
        zbuf[0, EDGE + n * USED : EDGE + (n + 1) * USED, :] = value[:USED, :VR]
        for ri in range(2):
            flat = jnp.sum(jnp.where(diagonal, value[:, VR + ri : VR + ri + 1], 0.0), axis=0, keepdims=True)
            if 2 * n + ri < LOCAL:
                flat = jnp.where(lane[:1] == VR - 1, thresholds_s[2 * n + ri], flat)
            zbuf[0, 2 * n + ri : 2 * n + ri + 1, :] = flat

    load_theta.wait()
    load_by.wait()
    load_turned.wait()
    mask_rows = jnp.tanh(MASK_STEEP * theta_v[...])
    hi, lo = split(mask_rows)
    wide = dot(jnp.concatenate([hi, lo], axis=0), by[...])
    column = wide[:ROWS, :VR] + wide[:ROWS, VR:] + wide[ROWS:, :VR]
    hi, lo = split(column)
    both = dot(turned[...], jnp.concatenate([hi, lo], axis=0))
    rown[...] = packed(both[:UR] + both[UR : 2 * UR])
    rhalo[...] = packed(both[2 * UR : 3 * UR] + both[3 * UR :])

    edge_of = (has_next & final) | (has_prev & first)
    waited = jnp.where(edge_of, 2 * GROUP, GROUP)
    pl.semaphore_wait(barrier, jnp.where(after_bend | relays, GROUP + 2, waited))

    def remote(src, dst, send, recv, device):
        return pltpu.make_async_remote_copy(
            src_ref=src, dst_ref=dst, send_sem=send, recv_sem=recv, device_id=device, device_id_type=MESH
        )

    def halo_next(other):
        return remote(rhalo, rin.at[3], hs_sem.at[other], hr_sem.at[0], (t + 1, other))

    def halo_prev(other):
        return remote(rhalo, rin.at[4], hs_sem.at[other], hr_sem.at[1], (t - 1, other))

    def halo_via(side):
        return remote(rhalo, passed, hs_sem.at[side], pass_sem, (between, 1 + side))

    def halo_passed(core):
        return remote(passed, rin.at[4], hs_sem.at[core], hr_sem.at[1], (bend, 2 * (c - 1) + core))

    def part(mask):
        source = rown if mask == 1 else rpair
        return remote(source, rin.at[mask - 1], rs_sem.at[mask - 1], rr_sem.at[mask - 1], partner(mask))

    def kernels_to(mask, chunk):
        device = partner(1) if mask != 2 else mirror
        source = 2 if mask == 3 else 0
        rows = pl.ds(0, CHUNK) if chunk == 0 else pl.ds(CHUNK, WIRE - CHUNK)
        sem = 2 * (mask - 1) + chunk
        return remote(
            zbuf.at[source, rows, :], zbuf.at[mask, rows, :], zs_sem.at[sem], zr_sem.at[sem], device
        )

    @pl.when(has_next & final)
    def _():
        for other in range(GROUP):
            halo_next(other).start()

    @pl.when(has_prev & first & jnp.logical_not(after_bend))
    def _():
        for other in range(GROUP):
            halo_prev(other).start()

    @pl.when(after_bend)
    def _():
        for side in range(2):
            halo_via(side).start()

    part(1).start()
    kernels_to(2, 0).start()
    part(1).wait_recv()
    rpair[...] = rown[...] + rin[0]
    part(2).start()
    kernels_to(2, 1).start()
    for chunk in range(2):
        kernels_to(1, chunk).start()

    @pl.when(relays)
    def _():
        halo_via(0).wait_recv()
        for core in range(2):
            halo_passed(core).start()

    @pl.when(jnp.logical_not(has_prev))
    def _():
        rin[3] = jnp.zeros((UH, VR), F32)

    @pl.when(jnp.logical_not(has_next))
    def _():
        rin[4] = jnp.zeros((UH, VR), F32)

    unpack_kernels(0)
    for chunk in range(2):
        kernels_to(1, chunk).wait_recv()
    unpack_kernels(1)

    @pl.when(has_prev)
    def _():
        halo_next(0).wait_recv()

    @pl.when(has_next)
    def _():
        halo_prev(0).wait_recv()

    part(2).wait_recv()

    total = rpair[...] + rin[1] + rin[3] + rin[4]
    total = total * (1.0 / (SIZE * SIZE))
    keep = row < SPARE
    turn = pltpu.roll(total, FLAT, 1)
    halves = [
        jnp.where(keep, jnp.where(lane < FLAT, total, turn), 0.0),
        jnp.where(keep, jnp.where(lane < FLAT, turn, total), 0.0),
    ]
    for h in range(2):
        sign_u = 1.0 - 2.0 * h
        rsum[0, h] = halves[h]
        rsum[1, h] = sign_i * sign_v * swap(halves[h])
        rsum[2, h] = sign_u * sign_i * halves[1 - h]
        rsum[3, h] = (-sign_u) * sign_v * swap(halves[1 - h])
    flat = jnp.where(edge_lane < UR, total[SPARE : SPARE + 1], 0.0)
    erow[0] = flat
    erow[1] = turned_edge(flat)

    load_pack.wait()
    load_sample.wait()
    for copy in load_fine:
        copy.wait()
    block_lane = lax.broadcasted_iota(jnp.int32, (ROWS, VR), 1)

    def grids_and_rows(s):
        grids = []
        for n in range(DEPTH):
            grid = []
            for h in range(2):
                terms = [coef[s, n, m] * rsum[m, h] for m in range(4)]
                grid.append((terms[0] + terms[1]) + (terms[2] + terms[3]))
            grids.append(jnp.concatenate(grid, axis=0))
        cross = [None] * LOCAL
        for l in range(LOCAL):
            hi, lo = split(jnp.concatenate(grids[KERNELS * l : KERNELS * (l + 1)], axis=1))
            tall = dot(pack[:, : 3 * UR], jnp.concatenate([hi, hi, lo], axis=0))
            for k in range(KERNELS):
                part = tall[:, k * VR : (k + 1) * VR]
                at = (l * KERNELS + k) * ROWS
                other = jnp.where(block_lane % FLAT == HALF - 1, pltpu.roll(part, VR - HALF, 1), 0.0)
                other = jnp.where(block_lane % FLAT == FLAT - 1, pltpu.roll(part, HALF, 1), other)
                crossed[s, at : at + ROWS, :] = other
                other = part * other
                cross[l] = other if k == 0 else cross[l] + other
                hi, lo = split(part)
                rows_v[s // 2, s % 2 * SPAN + at : s % 2 * SPAN + at + ROWS, :VR] = hi
                rows_v[s // 2, s % 2 * SPAN + at : s % 2 * SPAN + at + ROWS, VR:] = lo
        for l in range(LOCAL):
            near = cross[l].astype(BF).astype(F32)
            far = pltpu.roll(cross[l] - near, VR - 1, 1)
            edge_v[s, l * ROWS : (l + 1) * ROWS, :] = jnp.where(block_lane % FLAT == HALF - 2, far, near).astype(BF)
        flat = stacked(ecoef[s, 0] * erow[0] + ecoef[s, 1] * erow[1])
        upper = dot(flat, turned[:VR, :ROWS])
        lower = dot(flat, turned[UR : UR + VR, :ROWS])
        flat_v[s] = (upper[:EDGE] + upper[EDGE:] + lower[:EDGE]).T

    def resist_of(slots):
        held = slots[0] // 2
        amp = dot(jnp.concatenate([rows_v[held], rows_v[held, :, :VR]], axis=1), sample[...])
        lhs = []
        for s in slots:
            for l in range(LOCAL):
                sampled = None
                for k in range(KERNELS):
                    n = l * KERNELS + k
                    at = s % 2 * SPAN + n * ROWS
                    for ri in range(2):
                        piece = amp[at : at + ROWS, ri * GRID : (ri + 1) * GRID]
                        piece = piece + flat_v[s, :, 2 * n + ri : 2 * n + ri + 1]
                        amps[s, n * ROWS : (n + 1) * ROWS, ri * GRID : (ri + 1) * GRID] = piece
                        sampled = piece * piece if k + ri == 0 else sampled + piece * piece
                hi, lo = split(sampled)
                lhs.append(jnp.concatenate([hi, lo, hi, edge_v[s, l * ROWS : (l + 1) * ROWS, :]], axis=1))
        intensities = dot(jnp.concatenate(lhs, axis=0), fine[...])
        total = None
        for s in slots:
            for l in range(LOCAL):
                at = (s % 2 * LOCAL + l) * ROWS
                level = zbuf[s, l : l + 1, VR - 1 : VR]
                resist = jax.nn.sigmoid(RESIST_STEEP * (intensities[at : at + ROWS] - level))
                resists[s, l] = resist
                total = resist if total is None else total + resist
        if slots[0] == 0:
            band[...] = total
        else:
            band[...] += total

    grids_and_rows(0)
    kernels_to(2, 0).wait_recv()
    kernels_to(3, 0).start()
    grids_and_rows(1)
    kernels_to(2, 1).wait_recv()
    kernels_to(3, 1).start()
    unpack_kernels(2)
    resist_of((0, 1))
    grids_and_rows(2)
    for chunk in range(2):
        kernels_to(3, chunk).wait_recv()
    unpack_kernels(3)
    grids_and_rows(3)
    resist_of((2, 3))

    load_target.wait()
    load_weights.wait()
    weight_sum = weights_s[0]
    for n in range(1, CONDS):
        weight_sum = weight_sum + weights_s[n]
    weight_sum = jnp.full((8, TP), weight_sum, jnp.int32).astype(F32)
    wanted[...] = target_v[...].astype(F32)
    band[...] = band[...] * (4.0 * RESIST_STEEP * BAND_WEIGHT / CONDS / CONDS)

    load_coarse.wait()
    load_half.wait()
    load_gather.wait()

    def push_of(slots):
        fields = []
        for s in slots:
            for l in range(LOCAL):
                weight = jnp.full((8, TP), weights_s[(c ^ s) * LOCAL + l], jnp.int32).astype(F32) / weight_sum
                pull = (4.0 * RESIST_STEEP) * weight[0:1]
                resist = resists[s, l]
                slope = (pull + 4.0 * RESIST_STEEP * BAND_WEIGHT / CONDS) * resist - (pull * wanted[...] + band[...])
                field = slope * (resist - resist * resist)
                last = jnp.sum(field * half_last[0:1, :], axis=1, keepdims=True)
                last_v[s, l * ROWS : (l + 1) * ROWS, :] = jnp.broadcast_to(last, (ROWS, VR))
                fields.append(field)
        hi, lo = split(jnp.concatenate(fields, axis=0))
        wide = dot(jnp.concatenate([hi, lo], axis=0), coarse[...])
        half = 2 * LOCAL * ROWS
        push_v[slots[0] // 2] = wide[:half, :GRID] + wide[:half, GRID:] + wide[half:, :GRID]

    def adjoint_of(slots):
        rows = []
        flats = []
        for s in slots:
            flat = []
            for n in range(DEPTH):
                at = (s % 2 * LOCAL + n // KERNELS) * ROWS
                push = push_v[slots[0] // 2, at : at + ROWS, :]
                drive = []
                for ri in range(2):
                    piece = push * amps[s, n * ROWS : (n + 1) * ROWS, ri * GRID : (ri + 1) * GRID]
                    flat.append(jnp.where(block_lane == 2 * n + ri, jnp.sum(piece, axis=1, keepdims=True), 0.0))
                    drive.append(piece)
                hi, lo = split(jnp.concatenate(drive, axis=1))
                rows.append(jnp.concatenate([hi, lo], axis=1))
            while len(flat) > 1:
                flat = [flat[i] + flat[i + 1] for i in range(0, len(flat), 2)]
            flats.append(flat[0])
        drive = dot(jnp.concatenate(rows, axis=0), gather[...])
        drive = drive[:, :VR] + drive[:, VR:]
        sums = [[None, None] for _ in range(4)]
        for s in slots:
            for l in range(LOCAL):
                pair = []
                for n in (KERNELS * l, KERNELS * l + 1):
                    at = s % 2 * SPAN + n * ROWS
                    last = last_v[s, l * ROWS : (l + 1) * ROWS, :]
                    pair.append(drive[at : at + ROWS] + last * crossed[s, n * ROWS : (n + 1) * ROWS, :])
                hi, lo = split(jnp.concatenate(pair, axis=1))
                back = dot(turned[: 2 * UR, :], jnp.concatenate([hi, lo], axis=0))
                back = back[:UR] + back[UR:]
                for k in range(KERNELS):
                    for h in range(2):
                        value = back[h * UH : (h + 1) * UH, k * VR : (k + 1) * VR]
                        for m in range(4):
                            term = coef[s, l * KERNELS + k, m] * value
                            sums[m][h] = term if sums[m][h] is None else sums[m][h] + term
        total = None
        for s, flat in zip(slots, flats):
            wide = dot(stacked(flat.T[:EDGE]), pack[:, : 2 * VR])
            here = wide[:EDGE, :VR] + wide[EDGE:, :VR]
            upper = pltpu.roll(wide[:EDGE, :VR], VR - UR, 1)
            lower = pltpu.roll(wide[:EDGE, VR:], VR - UR, 1)
            here = here + jnp.where(edge_lane < VR - UR, upper, lower)
            term = ecoef[s, 0] * here - ecoef[s, 1] * turned_edge(here)
            total = term if total is None else total + term
        for m in range(4):
            for h in range(2):
                if slots[0] == 0:
                    jbuf[m, h] = sums[m][h]
                else:
                    jbuf[m, h] += sums[m][h]
        if slots[0] == 0:
            jflat[...] = total
        else:
            jflat[...] += total

    push_of((0, 1))
    adjoint_of((0, 1))
    push_of((2, 3))
    adjoint_of((2, 3))

    def folded_part(m, h):
        sign = 1.0 if m in (0, 3) else -1.0
        return jbuf[m, h] + sign * pltpu.roll(jbuf[m, h], FLAT, 1)

    halves = []
    for h in range(2):
        sign_u = 1.0 - 2.0 * h
        halves.append(
            folded_part(0, h)
            + swap(sign_v * folded_part(1, h))
            - sign_u * folded_part(2, 1 - h)
            + swap(sign_u * sign_v * folded_part(3, 1 - h))
        )
    value = jnp.where(lane < FLAT, halves[0], pltpu.roll(halves[1], FLAT, 1))
    aown[...] = jnp.where(row == SPARE, jnp.sum(jflat[...], axis=0, keepdims=True), value)

    def adjoint_part(mask):
        return remote(aown, ain.at[mask - 1], as_sem.at[mask - 1], ar_sem.at[mask - 1], partner(mask))

    def adjoint_prev():
        return remote(aown, anear.at[c], as_sem.at[3], near_sem.at[c], (t - 1, GROUP - 1))

    def adjoint_next():
        return remote(aown, anear.at[c], as_sem.at[4], near_sem.at[c], (t + 1, 0))

    def adjoint_near(other):
        return remote(aown, anear.at[other], as_sem.at[3], near_sem.at[other], (t, c ^ 1))

    @pl.when(has_prev)
    def _():
        adjoint_prev().start()

    @pl.when(has_next)
    def _():
        adjoint_next().start()

    for mask in range(1, GROUP):
        adjoint_part(mask).start()

    near = (first & has_prev) | (final & has_next)

    factor[...] = (MASK_STEEP / (SIZE * SIZE)) * (1.0 - jnp.square(jnp.tanh(MASK_STEEP * theta_v[...])))
    for copy in load_bt:
        copy.wait()

    for mask in range(1, GROUP):
        adjoint_part(mask).wait_recv()

    def sensitivity(value, rows, columns):
        hi, lo = split(jnp.concatenate(unpacked(value), axis=0))
        value = jnp.concatenate([hi, hi, lo, jnp.zeros((256 - 3 * UR, VR), BF)], axis=0)
        hi, lo = split(dot(pack[rows, columns], value))
        return dot(jnp.concatenate([hi, lo, hi], axis=1), bt[...])

    out_v[...] = sensitivity(aown[...] + ain[0] + ain[1] + ain[2], slice(None), slice(0, 256)) * factor[...]

    @pl.when(near)
    def _():
        for other in range(GROUP):
            adjoint_near(other).wait_recv()
        edge = pl.ds(pl.multiple_of(jnp.where(first, 0, ROWS - HALO), HALO), HALO)
        value = anear[0] + anear[1] + anear[2] + anear[3]
        out_v[edge, :] += sensitivity(value, edge, slice(256, 512)) * factor[edge, :]

    @pl.when(has_next & final)
    def _():
        for other in range(GROUP):
            halo_next(other).wait_send()

    @pl.when(has_prev & first & jnp.logical_not(after_bend))
    def _():
        for other in range(GROUP):
            halo_prev(other).wait_send()

    @pl.when(after_bend)
    def _():
        for side in range(2):
            halo_via(side).wait_send()

    @pl.when(relays)
    def _():
        for core in range(2):
            halo_passed(core).wait_send()

    for mask in range(1, GROUP):
        if mask < GROUP - 1:
            part(mask).wait_send()
        for chunk in range(2):
            kernels_to(mask, chunk).wait_send()
        adjoint_part(mask).wait_send()

    @pl.when(has_prev)
    def _():
        adjoint_prev().wait_send()

    @pl.when(has_next)
    def _():
        adjoint_next().wait_send()


def shards(tiles, theta, target, kernel_real, kernel_imag, weights, thresholds):
    constants = tables()
    dma = pltpu.SemaphoreType.DMA
    by, bt, pack, turned, pv, pu, sample, gather, fine, coarse, half_last = constants
    call = pl.pallas_call(
        functools.partial(kernel, tiles),
        out_shape=jax.ShapeDtypeStruct((ROWS, TP), F32),
        in_specs=[pl.BlockSpec(memory_space=pltpu.HBM)] * 17,
        out_specs=pl.BlockSpec(memory_space=pltpu.VMEM),
        scratch_shapes=[
            pltpu.SMEM((CONDS,), jnp.int32),
            pltpu.SMEM((LOCAL,), F32),
            pltpu.VMEM((ROWS, TP), F32),
            pltpu.VMEM((ROWS, TP), jnp.int32),
            pltpu.VMEM((2, LOCAL, KSUP, KERNELS, KSUP), F32),
            pltpu.VMEM(by.shape, BF),
            pltpu.VMEM((3 * VR, TP), BF),
            pltpu.VMEM(pack.shape[1:], BF),
            pltpu.VMEM(turned.shape[1:], BF),
            pltpu.VMEM((4 * VR, 2 * VR), BF),
            pltpu.VMEM(pu.shape, BF),
            pltpu.VMEM(sample.shape, BF),
            pltpu.VMEM(gather.shape, BF),
            pltpu.VMEM((4 * GRID, TP), BF),
            pltpu.VMEM(coarse.shape, BF),
            pltpu.VMEM(half_last.shape, F32),
            pltpu.VMEM((DEPTH * UR, 2 * VR), F32),
            pltpu.VMEM((GROUP, WIRE, VR), F32),
            pltpu.VMEM((GROUP, DEPTH, 4, UH, VR), F32),
            pltpu.VMEM((GROUP, 2, EDGE, VR), F32),
            pltpu.VMEM((UH, VR), F32),
            pltpu.VMEM((UH, VR), F32),
            pltpu.VMEM((UH, VR), F32),
            pltpu.VMEM((UH, VR), F32),
            pltpu.VMEM((5, UH, VR), F32),
            pltpu.VMEM((4, 2, UH, VR), F32),
            pltpu.VMEM((2, EDGE, VR), F32),
            pltpu.VMEM((UH, VR), F32),
            pltpu.VMEM((3, UH, VR), F32),
            pltpu.VMEM((GROUP, UH, VR), F32),
            pltpu.VMEM((4, 2, UH, VR), F32),
            pltpu.VMEM((EDGE, VR), F32),
            pltpu.VMEM((GROUP, DEPTH * ROWS, 2 * GRID), F32),
            pltpu.VMEM((GROUP, DEPTH * ROWS, VR), F32),
            pltpu.VMEM((2, 2 * SPAN, 2 * VR), BF),
            pltpu.VMEM((GROUP, ROWS, EDGE), F32),
            pltpu.VMEM((GROUP, LOCAL * ROWS, VR), BF),
            pltpu.VMEM((2, 2 * LOCAL * ROWS, GRID), F32),
            pltpu.VMEM((GROUP, LOCAL * ROWS, VR), F32),
            pltpu.VMEM((GROUP, LOCAL, ROWS, TP), F32),
            pltpu.VMEM((ROWS, TP), F32),
            pltpu.VMEM((ROWS, TP), F32),
            pltpu.VMEM((ROWS, TP), F32),
            dma((20,)),
            dma((6,)),
            dma((6,)),
            dma((3,)),
            dma((3,)),
            dma((4,)),
            dma((2,)),
            dma((5,)),
            dma((3,)),
            dma((4,)),
            dma,
        ],
        compiler_params=pltpu.CompilerParams(collective_id=0, has_side_effects=True, vmem_limit_bytes=32 * 1024 * 1024),
        name="window_gradient",
    )
    kernel_real, kernel_imag = (jnp.swapaxes(x, 1, 2) for x in (kernel_real, kernel_imag))
    arrays = (theta, target, kernel_real, kernel_imag, weights, thresholds, *(jnp.asarray(x) for x in constants))
    return call(*(pltpu.with_memory_space_constraint(x, pltpu.HBM) for x in arrays))


def solution(mesh):
    in_specs = (
        P(("tile", "cond"), None),
        P("tile", None),
        P("cond", None, None, None),
        P("cond", None, None, None),
        P(),
        P("cond"),
    )
    out_specs = P(("tile", "cond"), None)
    body = functools.partial(shards, mesh.shape["tile"])
    return jax.shard_map(body, mesh=mesh, in_specs=in_specs, out_specs=out_specs, check_vma=False)
```

```python
import functools
import math

import jax
import jax.numpy as jnp
import ml_dtypes
import numpy as np
from jax import lax
from jax.experimental import pallas as pl
from jax.experimental.pallas import tpu as pltpu
from jax.sharding import PartitionSpec as P

TP = 512
HALO = 32
KSUP = 65
HALF = KSUP // 2
CONDS = 8
KERNELS = 2
SIZE = TP + 2 * HALO
ROWS = 128
GROUP = 4
LOCAL = CONDS // GROUP
UH = 40
UR = 2 * UH
VR = 128
FLAT = 2 * HALF
DEPTH = LOCAL * KERNELS
USED = UH + HALF
EDGE = 2 * DEPTH
CHUNK = EDGE + DEPTH // 2 * USED
WIRE = EDGE + DEPTH * USED
SPAN = DEPTH * ROWS
GRID = 128
SPARE = HALF + 1

MASK_STEEP = 2.0
RESIST_STEEP = 4.0
BAND_WEIGHT = 1.0

BF = jnp.bfloat16
F32 = jnp.float32
MESH = pl.DeviceIdType.MESH


def split(x):
    hi = x.astype(BF)
    return hi, (x - hi.astype(F32)).astype(BF)


def np_split(x):
    hi = x.astype(ml_dtypes.bfloat16)
    return hi, (x - hi.astype(np.float64)).astype(ml_dtypes.bfloat16)


def waves(positions):
    phase = np.fmod(np.asarray(positions, np.float64)[:, None] * np.arange(HALF + 1)[None, :], SIZE)
    angles = phase * (2.0 * math.pi / SIZE)
    return np.cos(angles), np.sin(angles)


def row_basis(positions):
    cos, sin = waves(positions)
    out = np.zeros((len(positions), UR))
    out[:, :HALF] = cos[:, 1:]
    out[:, HALF] = 1.0
    out[:, UH:USED] = sin[:, 1:]
    return out


def column_basis(positions):
    cos, sin = waves(positions)
    out = np.zeros((len(positions), VR))
    out[:, :HALF] = cos[:, 1:]
    out[:, HALF:FLAT] = sin[:, 1:]
    out[:, FLAT] = 1.0
    return out


def parity_rows():
    out = np.zeros((UR, UR))
    out[HALF, HALF] = 1.0
    for j in range(1, HALF + 1):
        out[j - 1, HALF + j] = out[j - 1, HALF - j] = out[UH + j - 1, HALF + j] = 1.0
        out[UH + j - 1, HALF - j] = -1.0
    return out


def parity_columns():
    out = np.zeros((2 * VR, 2 * VR))
    for ri in range(2):
        out[ri * VR + HALF, VR + ri] = 1.0
        for j in range(1, HALF + 1):
            even = ri * FLAT + j - 1
            out[ri * VR + HALF + j, even] = out[ri * VR + HALF - j, even] = 1.0
            out[ri * VR + HALF + j, even + HALF] = 1.0
            out[ri * VR + HALF - j, even + HALF] = -1.0
    return out


def tables():
    bf = ml_dtypes.bfloat16
    cols = column_basis(np.arange(TP) + HALO)
    hi, lo = np_split(cols)
    by = np.concatenate([hi, lo], axis=1)
    bt = np.concatenate([hi.T, lo.T], axis=0)
    places = column_basis(np.arange(GRID) * (SIZE / GRID))
    hi, lo = np_split(places[:, :FLAT])
    sample = np.zeros((3 * VR, 2 * GRID), bf)
    gather = np.zeros((4 * GRID, 2 * VR), bf)
    for ri in range(2):
        for block, part in enumerate((hi, hi, lo)):
            at = block * VR + ri * FLAT
            sample[at : at + FLAT, ri * GRID : (ri + 1) * GRID] = part.T
        gather[ri * GRID : (ri + 1) * GRID, ri * FLAT : (ri + 1) * FLAT] = hi
        gather[ri * GRID : (ri + 1) * GRID, VR + ri * FLAT : VR + (ri + 1) * FLAT] = lo
        gather[(2 + ri) * GRID : (3 + ri) * GRID, ri * FLAT : (ri + 1) * FLAT] = hi
    phase = (np.arange(TP) + HALO) * (2.0 * math.pi / SIZE)
    place = np.arange(GRID) * (2.0 * math.pi / GRID)
    spread = np.ones((GRID, TP))
    for f in range(1, GRID // 2):
        spread += 2.0 * np.cos(f * (phase[None, :] - place[:, None]))
    spread += np.cos(GRID // 2 * place)[:, None] * np.cos(GRID // 2 * phase)[None, :]
    spread /= GRID
    last = np.sin(GRID // 2 * phase)
    hi, lo = np_split(spread)
    last_hi, last_lo = np_split(last)
    rest = np.zeros((VR, TP), bf)
    for at in (0, FLAT):
        rest[at + HALF - 2], rest[at + HALF - 1], rest[at + FLAT - 1] = last_hi, last_hi, last_lo
    fine = np.concatenate([hi, lo, rest], axis=0)
    coarse = np.concatenate([hi.T, lo.T], axis=1)
    half_last = np.broadcast_to(0.5 * last, (8, TP)).astype(np.float32)
    pack = []
    turned = []
    for c in range(GROUP):
        own = row_basis(np.arange(ROWS) + HALO + ROWS * c)
        near = np.zeros_like(own)
        if c == 0:
            near[:HALO] = row_basis(np.arange(HALO) + HALO + TP)
        if c == GROUP - 1:
            near[ROWS - HALO :] = row_basis(np.arange(HALO))
        row = []
        column = []
        for table in (own, near):
            thi, tlo = np_split(table)
            row += [thi, tlo, thi, np.zeros((ROWS, 256 - 3 * UR), bf)]
            column.append(np.concatenate([thi.T, thi.T], axis=1))
            column.append(np.concatenate([tlo.T, np.zeros((UR, ROWS), bf)], axis=1))
        pack.append(np.concatenate(row, axis=1))
        turned.append(np.concatenate(column, axis=0))
    pv = parity_columns().astype(bf)
    pu = parity_rows().astype(bf)
    pu = np.concatenate([pu, pu], axis=1)
    return by, bt, np.stack(pack), np.stack(turned), pv, pu, sample, gather, fine, coarse, half_last


def dot(a, b):
    return jnp.dot(a, b, preferred_element_type=F32)


def kernel(
    tiles,
    theta_h, target_h, kr_h, ki_h, weights_h, thresholds_h, by_h, bt_h, pack_h, turned_h, pv_h, pu_h,
    sample_h, gather_h, fine_h, coarse_h, half_last_h,
    out_v,
    weights_s, thresholds_s, theta_v, target_v, raw_v, by, bt, pack, turned, pv, pu,
    sample, gather, fine, coarse, half_last, stack, zbuf, coef, ecoef, passed, rpair, apair, rown, rhalo, rin, rsum, erow, aown, ain, anear, jbuf, jflat, amps, crossed, rows_v, flat_v, edge_v, push_v, last_v, resists, band, wanted, factor,
    load_sem, zs_sem, zr_sem, rs_sem, rr_sem, hs_sem, hr_sem, as_sem, ar_sem, near_sem, pass_sem,
):
    t = lax.axis_index("tile")
    c = lax.axis_index("cond")
    first = c == 0
    final = c == GROUP - 1
    has_prev = t > 0
    has_next = t < tiles - 1

    loads = []

    def load(src, dst):
        copy = pltpu.make_async_copy(src, dst, load_sem.at[len(loads)])
        copy.start()
        loads.append(copy)
        return copy

    load_kr = load(kr_h, raw_v.at[0])
    load_ki = load(ki_h, raw_v.at[1])
    load_pv = [load(pv_h, pv.at[pl.ds(at, 2 * VR), :]) for at in (0, 2 * VR)]
    load_pu = load(pu_h, pu)
    load_thresholds = load(thresholds_h, thresholds_s)
    load_theta = load(theta_h, theta_v)
    load_by = load(by_h, by)
    load_turned = load(turned_h.at[c], turned)
    load_pack = load(pack_h.at[c], pack)
    load_sample = load(sample_h, sample)
    load_fine = [
        load(fine_h.at[pl.ds(0, GRID), :], fine.at[pl.ds(0, GRID), :]),
        load(fine_h, fine.at[pl.ds(GRID, 3 * GRID), :]),
    ]
    load_coarse = load(coarse_h, coarse)
    load_half = load(half_last_h, half_last)
    load_gather = load(gather_h, gather)
    load_bt = [
        load(bt_h.at[pl.ds(0, VR), :], bt.at[pl.ds(0, VR), :]),
        load(bt_h, bt.at[pl.ds(VR, 2 * VR), :]),
    ]
    load_weights = load(weights_h, weights_s)
    load_target = load(target_h.at[pl.ds(pl.multiple_of(c * ROWS, ROWS), ROWS), :], target_v)

    def partner(mask):
        return (t, c ^ mask)

    barrier = pltpu.get_barrier_semaphore()

    def greet(device):
        pl.semaphore_signal(barrier, inc=1, device_id=device, device_id_type=MESH)

    mirror = ((t + tiles // 2) % tiles, c ^ 2)
    for mask in range(1, GROUP):
        greet(partner(mask))
    greet(mirror)

    bend = tiles // 2 - 1
    between = bend - 12
    at_bend = t == bend
    after_bend = (t == bend + 1) & first
    relays = (t == between) & jnp.logical_not(first | final)

    @pl.when(has_next)
    def _():
        greet((jnp.where(at_bend, between, t + 1), jnp.where(at_bend, 1 + c // 2, 0)))

    @pl.when(has_prev)
    def _():
        greet((t - 1, GROUP - 1))

    @pl.when(relays)
    def _():
        greet((bend + 1, 0))

    lane = lax.broadcasted_iota(jnp.int32, (UH, VR), 1)
    row = lax.broadcasted_iota(jnp.int32, (UH, VR), 0)
    tall_lane = lax.broadcasted_iota(jnp.int32, (UR, VR), 1)
    diagonal = tall_lane == lax.broadcasted_iota(jnp.int32, (UR, VR), 0)
    odd = lane % FLAT >= HALF
    sign_v = jnp.where(odd, -1.0, 1.0).astype(F32)
    sign_i = jnp.where(lane >= FLAT, -1.0, 1.0).astype(F32)
    edge_lane = lane[: 2 * DEPTH]
    edge_row = row[: 2 * DEPTH]

    def swap(x):
        return jnp.where(odd, pltpu.roll(x, HALF, 1), pltpu.roll(x, VR - HALF, 1))

    def turned_edge(x):
        out = jnp.where(edge_lane < UH, pltpu.roll(x, VR - UH, 1), -pltpu.roll(x, UH, 1))
        return jnp.where(edge_lane < UR, out, 0.0)

    def stacked(x):
        near = x.astype(BF).astype(F32)
        return jnp.concatenate([near, x - near], axis=0).astype(BF)

    def packed(x):
        out = jnp.where(lane < FLAT, x[:UH], pltpu.roll(x[UH:], FLAT, 1))
        flat = jnp.sum(jnp.where(diagonal, x[:, FLAT : FLAT + 1], 0.0), axis=0, keepdims=True)
        return jnp.where(row == SPARE, flat, out)

    def unpacked(x):
        flat = jnp.sum(jnp.where(diagonal, x[SPARE : SPARE + 1], 0.0), axis=1, keepdims=True)
        keep = (lane < FLAT) & (row < SPARE)
        out = []
        for h, value in enumerate((x, pltpu.roll(x, FLAT, 1))):
            out.append(jnp.where(lane == FLAT, flat[h * UH : (h + 1) * UH], jnp.where(keep, value, 0.0)))
        return out

    def unpack_kernels(s):
        for n in range(DEPTH):
            at = EDGE + n * USED
            even = zbuf[s, at : at + UH, :]
            uneven = zbuf[s, at + UH : at + USED, :]
            odd_rows = odd[: USED - UH]
            coef[s, n, 0] = jnp.where(odd, pltpu.roll(even, HALF, 1), even)
            coef[s, n, 1] = jnp.where(odd, pltpu.roll(even, FLAT, 1), pltpu.roll(even, HALF, 1))
            coef[s, n, 2, : USED - UH] = jnp.where(
                odd_rows, pltpu.roll(uneven, VR - HALF, 1), pltpu.roll(uneven, FLAT, 1)
            )
            coef[s, n, 3, : USED - UH] = jnp.where(odd_rows, uneven, pltpu.roll(uneven, VR - HALF, 1))
        flat = jnp.where(edge_lane < USED, zbuf[s, :EDGE, :], 0.0)
        other = jnp.where(edge_row % 2 == 0, pltpu.roll(flat, EDGE - 1, 0), -pltpu.roll(flat, 1, 0))
        ecoef[s, 0] = jnp.where(edge_lane < UH, flat, jnp.where(edge_lane < UR, pltpu.roll(flat, UH, 1), 0.0))
        ecoef[s, 1] = jnp.where(
            edge_lane < UH, pltpu.roll(other, VR - UH, 1), jnp.where(edge_lane < UR, other, 0.0)
        )

    stack[...] = jnp.zeros_like(stack)
    load_kr.wait()
    load_ki.wait()
    for ri in range(2):
        for l in range(LOCAL):
            for k in range(KERNELS):
                at = (l * KERNELS + k) * UR
                stack[at : at + KSUP, ri * VR : ri * VR + KSUP] = raw_v[ri, l, :, k, :]
    for copy in load_pv:
        copy.wait()
    load_pu.wait()
    hi, lo = split(stack[...])
    folded = dot(jnp.concatenate([hi, lo], axis=1), pv[...])
    hi, lo = split(folded)
    coef[:, :, 2:, USED - UH :, :] = jnp.zeros((GROUP, DEPTH, 2, UR - USED, VR), F32)
    load_thresholds.wait()
    for n in range(DEPTH):
        rhs = jnp.concatenate([hi[n * UR : (n + 1) * UR], lo[n * UR : (n + 1) * UR]], axis=0)
        value = dot(pu[...], rhs)
        zbuf[0, EDGE + n * USED : EDGE + (n + 1) * USED, :] = value[:USED, :VR]
        for ri in range(2):
            flat = jnp.sum(jnp.where(diagonal, value[:, VR + ri : VR + ri + 1], 0.0), axis=0, keepdims=True)
            if 2 * n + ri < LOCAL:
                flat = jnp.where(lane[:1] == VR - 1, thresholds_s[2 * n + ri], flat)
            zbuf[0, 2 * n + ri : 2 * n + ri + 1, :] = flat

    load_theta.wait()
    load_by.wait()
    load_turned.wait()
    mask_rows = jnp.tanh(MASK_STEEP * theta_v[...])
    hi, lo = split(mask_rows)
    wide = dot(jnp.concatenate([hi, lo], axis=0), by[...])
    column = wide[:ROWS, :VR] + wide[:ROWS, VR:] + wide[ROWS:, :VR]
    hi, lo = split(column)
    both = dot(turned[...], jnp.concatenate([hi, lo], axis=0))
    rown[...] = packed(both[:UR] + both[UR : 2 * UR])
    rhalo[...] = packed(both[2 * UR : 3 * UR] + both[3 * UR :])

    edge_of = (has_next & final) | (has_prev & first)
    waited = jnp.where(edge_of, 2 * GROUP, GROUP)
    pl.semaphore_wait(barrier, jnp.where(after_bend | relays, GROUP + 2, waited))

    def remote(src, dst, send, recv, device):
        return pltpu.make_async_remote_copy(
            src_ref=src, dst_ref=dst, send_sem=send, recv_sem=recv, device_id=device, device_id_type=MESH
        )

    def halo_next(other):
        return remote(rhalo, rin.at[3], hs_sem.at[other], hr_sem.at[0], (t + 1, other))

    def halo_prev(other):
        return remote(rhalo, rin.at[4], hs_sem.at[other], hr_sem.at[1], (t - 1, other))

    def halo_via(side):
        return remote(rhalo, passed, hs_sem.at[side], pass_sem, (between, 1 + side))

    def halo_passed(core):
        return remote(passed, rin.at[4], hs_sem.at[core], hr_sem.at[1], (bend, 2 * (c - 1) + core))

    def part(mask):
        source = rown if mask == 1 else rpair
        return remote(source, rin.at[mask - 1], rs_sem.at[mask - 1], rr_sem.at[mask - 1], partner(mask))

    def kernels_to(mask, chunk):
        device = partner(1) if mask != 2 else mirror
        source = 2 if mask == 3 else 0
        rows = pl.ds(0, CHUNK) if chunk == 0 else pl.ds(CHUNK, WIRE - CHUNK)
        sem = 2 * (mask - 1) + chunk
        return remote(
            zbuf.at[source, rows, :], zbuf.at[mask, rows, :], zs_sem.at[sem], zr_sem.at[sem], device
        )

    @pl.when(has_next & final)
    def _():
        for other in range(GROUP):
            halo_next(other).start()

    @pl.when(has_prev & first & jnp.logical_not(after_bend))
    def _():
        for other in range(GROUP):
            halo_prev(other).start()

    @pl.when(after_bend)
    def _():
        for side in range(2):
            halo_via(side).start()

    part(1).start()
    kernels_to(2, 0).start()
    part(1).wait_recv()
    rpair[...] = rown[...] + rin[0]
    part(2).start()
    kernels_to(2, 1).start()
    for chunk in range(2):
        kernels_to(1, chunk).start()

    @pl.when(relays)
    def _():
        halo_via(0).wait_recv()
        for core in range(2):
            halo_passed(core).start()

    @pl.when(jnp.logical_not(has_prev))
    def _():
        rin[3] = jnp.zeros((UH, VR), F32)

    @pl.when(jnp.logical_not(has_next))
    def _():
        rin[4] = jnp.zeros((UH, VR), F32)

    unpack_kernels(0)
    for chunk in range(2):
        kernels_to(1, chunk).wait_recv()
    unpack_kernels(1)

    @pl.when(has_prev)
    def _():
        halo_next(0).wait_recv()

    @pl.when(has_next)
    def _():
        halo_prev(0).wait_recv()

    part(2).wait_recv()

    total = rpair[...] + rin[1] + rin[3] + rin[4]
    total = total * (1.0 / (SIZE * SIZE))
    keep = row < SPARE
    turn = pltpu.roll(total, FLAT, 1)
    halves = [
        jnp.where(keep, jnp.where(lane < FLAT, total, turn), 0.0),
        jnp.where(keep, jnp.where(lane < FLAT, turn, total), 0.0),
    ]
    for h in range(2):
        sign_u = 1.0 - 2.0 * h
        rsum[0, h] = halves[h]
        rsum[1, h] = sign_i * sign_v * swap(halves[h])
        rsum[2, h] = sign_u * sign_i * halves[1 - h]
        rsum[3, h] = (-sign_u) * sign_v * swap(halves[1 - h])
    flat = jnp.where(edge_lane < UR, total[SPARE : SPARE + 1], 0.0)
    erow[0] = flat
    erow[1] = turned_edge(flat)

    load_pack.wait()
    load_sample.wait()
    for copy in load_fine:
        copy.wait()
    block_lane = lax.broadcasted_iota(jnp.int32, (ROWS, VR), 1)

    def grids_and_rows(s):
        grids = []
        for n in range(DEPTH):
            grid = []
            for h in range(2):
                terms = [coef[s, n, m] * rsum[m, h] for m in range(4)]
                grid.append((terms[0] + terms[1]) + (terms[2] + terms[3]))
            grids.append(jnp.concatenate(grid, axis=0))
        cross = [None] * LOCAL
        for l in range(LOCAL):
            hi, lo = split(jnp.concatenate(grids[KERNELS * l : KERNELS * (l + 1)], axis=1))
            tall = dot(pack[:, : 3 * UR], jnp.concatenate([hi, hi, lo], axis=0))
            for k in range(KERNELS):
                part = tall[:, k * VR : (k + 1) * VR]
                at = (l * KERNELS + k) * ROWS
                other = jnp.where(block_lane % FLAT == HALF - 1, pltpu.roll(part, VR - HALF, 1), 0.0)
                other = jnp.where(block_lane % FLAT == FLAT - 1, pltpu.roll(part, HALF, 1), other)
                crossed[s, at : at + ROWS, :] = other
                other = part * other
                cross[l] = other if k == 0 else cross[l] + other
                hi, lo = split(part)
                rows_v[s // 2, s % 2 * SPAN + at : s % 2 * SPAN + at + ROWS, :VR] = hi
                rows_v[s // 2, s % 2 * SPAN + at : s % 2 * SPAN + at + ROWS, VR:] = lo
        for l in range(LOCAL):
            near = cross[l].astype(BF).astype(F32)
            far = pltpu.roll(cross[l] - near, VR - 1, 1)
            edge_v[s, l * ROWS : (l + 1) * ROWS, :] = jnp.where(block_lane % FLAT == HALF - 2, far, near).astype(BF)
        flat = stacked(ecoef[s, 0] * erow[0] + ecoef[s, 1] * erow[1])
        upper = dot(flat, turned[:VR, :ROWS])
        lower = dot(flat, turned[UR : UR + VR, :ROWS])
        flat_v[s] = (upper[:EDGE] + upper[EDGE:] + lower[:EDGE]).T

    def resist_of(slots):
        held = slots[0] // 2
        amp = dot(jnp.concatenate([rows_v[held], rows_v[held, :, :VR]], axis=1), sample[...])
        lhs = []
        for s in slots:
            for l in range(LOCAL):
                sampled = None
                for k in range(KERNELS):
                    n = l * KERNELS + k
                    at = s % 2 * SPAN + n * ROWS
                    for ri in range(2):
                        piece = amp[at : at + ROWS, ri * GRID : (ri + 1) * GRID]
                        piece = piece + flat_v[s, :, 2 * n + ri : 2 * n + ri + 1]
                        amps[s, n * ROWS : (n + 1) * ROWS, ri * GRID : (ri + 1) * GRID] = piece
                        sampled = piece * piece if k + ri == 0 else sampled + piece * piece
                hi, lo = split(sampled)
                lhs.append(jnp.concatenate([hi, lo, hi, edge_v[s, l * ROWS : (l + 1) * ROWS, :]], axis=1))
        intensities = dot(jnp.concatenate(lhs, axis=0), fine[...])
        total = None
        for s in slots:
            for l in range(LOCAL):
                at = (s % 2 * LOCAL + l) * ROWS
                level = zbuf[s, l : l + 1, VR - 1 : VR]
                resist = jax.nn.sigmoid(RESIST_STEEP * (intensities[at : at + ROWS] - level))
                resists[s, l] = resist
                total = resist if total is None else total + resist
        if slots[0] == 0:
            band[...] = total
        else:
            band[...] += total

    grids_and_rows(0)
    kernels_to(2, 0).wait_recv()
    kernels_to(3, 0).start()
    grids_and_rows(1)
    kernels_to(2, 1).wait_recv()
    kernels_to(3, 1).start()
    unpack_kernels(2)
    resist_of((0, 1))
    grids_and_rows(2)
    for chunk in range(2):
        kernels_to(3, chunk).wait_recv()
    unpack_kernels(3)
    grids_and_rows(3)
    resist_of((2, 3))

    load_target.wait()
    load_weights.wait()
    weight_sum = weights_s[0]
    for n in range(1, CONDS):
        weight_sum = weight_sum + weights_s[n]
    weight_sum = jnp.full((8, TP), weight_sum, jnp.int32).astype(F32)
    wanted[...] = target_v[...].astype(F32)
    band[...] = band[...] * (4.0 * RESIST_STEEP * BAND_WEIGHT / CONDS / CONDS)

    load_coarse.wait()
    load_half.wait()
    load_gather.wait()

    def push_of(slots):
        fields = []
        for s in slots:
            for l in range(LOCAL):
                weight = jnp.full((8, TP), weights_s[(c ^ s) * LOCAL + l], jnp.int32).astype(F32) / weight_sum
                pull = (4.0 * RESIST_STEEP) * weight[0:1]
                resist = resists[s, l]
                slope = (pull + 4.0 * RESIST_STEEP * BAND_WEIGHT / CONDS) * resist - (pull * wanted[...] + band[...])
                field = slope * (resist - resist * resist)
                last = jnp.sum(field * half_last[0:1, :], axis=1, keepdims=True)
                last_v[s, l * ROWS : (l + 1) * ROWS, :] = jnp.broadcast_to(last, (ROWS, VR))
                fields.append(field)
        hi, lo = split(jnp.concatenate(fields, axis=0))
        wide = dot(jnp.concatenate([hi, lo], axis=0), coarse[...])
        half = 2 * LOCAL * ROWS
        push_v[slots[0] // 2] = wide[:half, :GRID] + wide[:half, GRID:] + wide[half:, :GRID]

    def adjoint_of(slots):
        rows = []
        flats = []
        for s in slots:
            flat = []
            for n in range(DEPTH):
                at = (s % 2 * LOCAL + n // KERNELS) * ROWS
                push = push_v[slots[0] // 2, at : at + ROWS, :]
                drive = []
                for ri in range(2):
                    piece = push * amps[s, n * ROWS : (n + 1) * ROWS, ri * GRID : (ri + 1) * GRID]
                    flat.append(jnp.where(block_lane == 2 * n + ri, jnp.sum(piece, axis=1, keepdims=True), 0.0))
                    drive.append(piece)
                hi, lo = split(jnp.concatenate(drive, axis=1))
                rows.append(jnp.concatenate([hi, lo], axis=1))
            while len(flat) > 1:
                flat = [flat[i] + flat[i + 1] for i in range(0, len(flat), 2)]
            flats.append(flat[0])
        drive = dot(jnp.concatenate(rows, axis=0), gather[...])
        drive = drive[:, :VR] + drive[:, VR:]
        sums = [[None, None] for _ in range(4)]
        for s in slots:
            for l in range(LOCAL):
                pair = []
                for n in (KERNELS * l, KERNELS * l + 1):
                    at = s % 2 * SPAN + n * ROWS
                    last = last_v[s, l * ROWS : (l + 1) * ROWS, :]
                    pair.append(drive[at : at + ROWS] + last * crossed[s, n * ROWS : (n + 1) * ROWS, :])
                hi, lo = split(jnp.concatenate(pair, axis=1))
                back = dot(turned[: 2 * UR, :], jnp.concatenate([hi, lo], axis=0))
                back = back[:UR] + back[UR:]
                for k in range(KERNELS):
                    for h in range(2):
                        value = back[h * UH : (h + 1) * UH, k * VR : (k + 1) * VR]
                        for m in range(4):
                            term = coef[s, l * KERNELS + k, m] * value
                            sums[m][h] = term if sums[m][h] is None else sums[m][h] + term
        total = None
        for s, flat in zip(slots, flats):
            wide = dot(stacked(flat.T[:EDGE]), pack[:, : 2 * VR])
            here = wide[:EDGE, :VR] + wide[EDGE:, :VR]
            upper = pltpu.roll(wide[:EDGE, :VR], VR - UR, 1)
            lower = pltpu.roll(wide[:EDGE, VR:], VR - UR, 1)
            here = here + jnp.where(edge_lane < VR - UR, upper, lower)
            term = ecoef[s, 0] * here - ecoef[s, 1] * turned_edge(here)
            total = term if total is None else total + term
        for m in range(4):
            for h in range(2):
                if slots[0] == 0:
                    jbuf[m, h] = sums[m][h]
                else:
                    jbuf[m, h] += sums[m][h]
        if slots[0] == 0:
            jflat[...] = total
        else:
            jflat[...] += total

    push_of((0, 1))
    adjoint_of((0, 1))
    push_of((2, 3))
    adjoint_of((2, 3))

    def folded_part(m, h):
        sign = 1.0 if m in (0, 3) else -1.0
        return jbuf[m, h] + sign * pltpu.roll(jbuf[m, h], FLAT, 1)

    halves = []
    for h in range(2):
        sign_u = 1.0 - 2.0 * h
        halves.append(
            folded_part(0, h)
            + swap(sign_v * folded_part(1, h))
            - sign_u * folded_part(2, 1 - h)
            + swap(sign_u * sign_v * folded_part(3, 1 - h))
        )
    value = jnp.where(lane < FLAT, halves[0], pltpu.roll(halves[1], FLAT, 1))
    aown[...] = jnp.where(row == SPARE, jnp.sum(jflat[...], axis=0, keepdims=True), value)

    def adjoint_part(mask):
        source = aown if mask == 1 else apair
        return remote(source, ain.at[mask - 1], as_sem.at[mask - 1], ar_sem.at[mask - 1], partner(mask))

    def adjoint_prev():
        return remote(aown, anear.at[c], as_sem.at[3], near_sem.at[c], (t - 1, GROUP - 1))

    def adjoint_next():
        return remote(aown, anear.at[c], as_sem.at[4], near_sem.at[c], (t + 1, 0))

    def adjoint_near(other):
        return remote(aown, anear.at[other], as_sem.at[3], near_sem.at[other], (t, c ^ 1))

    @pl.when(has_prev)
    def _():
        adjoint_prev().start()

    @pl.when(has_next)
    def _():
        adjoint_next().start()

    adjoint_part(1).start()

    near = (first & has_prev) | (final & has_next)

    factor[...] = (MASK_STEEP / (SIZE * SIZE)) * (1.0 - jnp.square(jnp.tanh(MASK_STEEP * theta_v[...])))
    for copy in load_bt:
        copy.wait()

    adjoint_part(1).wait_recv()
    apair[...] = aown[...] + ain[0]
    adjoint_part(2).start()
    adjoint_part(2).wait_recv()

    def sensitivity(value, rows, columns):
        hi, lo = split(jnp.concatenate(unpacked(value), axis=0))
        value = jnp.concatenate([hi, hi, lo, jnp.zeros((256 - 3 * UR, VR), BF)], axis=0)
        hi, lo = split(dot(pack[rows, columns], value))
        return dot(jnp.concatenate([hi, lo, hi], axis=1), bt[...])

    out_v[...] = sensitivity(apair[...] + ain[1], slice(None), slice(0, 256)) * factor[...]

    @pl.when(near)
    def _():
        for other in range(GROUP):
            adjoint_near(other).wait_recv()
        edge = pl.ds(pl.multiple_of(jnp.where(first, 0, ROWS - HALO), HALO), HALO)
        value = anear[0] + anear[1] + anear[2] + anear[3]
        out_v[edge, :] += sensitivity(value, edge, slice(256, 512)) * factor[edge, :]

    @pl.when(has_next & final)
    def _():
        for other in range(GROUP):
            halo_next(other).wait_send()

    @pl.when(has_prev & first & jnp.logical_not(after_bend))
    def _():
        for other in range(GROUP):
            halo_prev(other).wait_send()

    @pl.when(after_bend)
    def _():
        for side in range(2):
            halo_via(side).wait_send()

    @pl.when(relays)
    def _():
        for core in range(2):
            halo_passed(core).wait_send()

    for mask in range(1, GROUP):
        if mask < GROUP - 1:
            part(mask).wait_send()
            adjoint_part(mask).wait_send()
        for chunk in range(2):
            kernels_to(mask, chunk).wait_send()

    @pl.when(has_prev)
    def _():
        adjoint_prev().wait_send()

    @pl.when(has_next)
    def _():
        adjoint_next().wait_send()


def shards(tiles, theta, target, kernel_real, kernel_imag, weights, thresholds):
    constants = tables()
    dma = pltpu.SemaphoreType.DMA
    by, bt, pack, turned, pv, pu, sample, gather, fine, coarse, half_last = constants
    call = pl.pallas_call(
        functools.partial(kernel, tiles),
        out_shape=jax.ShapeDtypeStruct((ROWS, TP), F32),
        in_specs=[pl.BlockSpec(memory_space=pltpu.HBM)] * 17,
        out_specs=pl.BlockSpec(memory_space=pltpu.VMEM),
        scratch_shapes=[
            pltpu.SMEM((CONDS,), jnp.int32),
            pltpu.SMEM((LOCAL,), F32),
            pltpu.VMEM((ROWS, TP), F32),
            pltpu.VMEM((ROWS, TP), jnp.int32),
            pltpu.VMEM((2, LOCAL, KSUP, KERNELS, KSUP), F32),
            pltpu.VMEM(by.shape, BF),
            pltpu.VMEM((3 * VR, TP), BF),
            pltpu.VMEM(pack.shape[1:], BF),
            pltpu.VMEM(turned.shape[1:], BF),
            pltpu.VMEM((4 * VR, 2 * VR), BF),
            pltpu.VMEM(pu.shape, BF),
            pltpu.VMEM(sample.shape, BF),
            pltpu.VMEM(gather.shape, BF),
            pltpu.VMEM((4 * GRID, TP), BF),
            pltpu.VMEM(coarse.shape, BF),
            pltpu.VMEM(half_last.shape, F32),
            pltpu.VMEM((DEPTH * UR, 2 * VR), F32),
            pltpu.VMEM((GROUP, WIRE, VR), F32),
            pltpu.VMEM((GROUP, DEPTH, 4, UH, VR), F32),
            pltpu.VMEM((GROUP, 2, EDGE, VR), F32),
            pltpu.VMEM((UH, VR), F32),
            pltpu.VMEM((UH, VR), F32),
            pltpu.VMEM((UH, VR), F32),
            pltpu.VMEM((UH, VR), F32),
            pltpu.VMEM((UH, VR), F32),
            pltpu.VMEM((5, UH, VR), F32),
            pltpu.VMEM((4, 2, UH, VR), F32),
            pltpu.VMEM((2, EDGE, VR), F32),
            pltpu.VMEM((UH, VR), F32),
            pltpu.VMEM((3, UH, VR), F32),
            pltpu.VMEM((GROUP, UH, VR), F32),
            pltpu.VMEM((4, 2, UH, VR), F32),
            pltpu.VMEM((EDGE, VR), F32),
            pltpu.VMEM((GROUP, DEPTH * ROWS, 2 * GRID), F32),
            pltpu.VMEM((GROUP, DEPTH * ROWS, VR), F32),
            pltpu.VMEM((2, 2 * SPAN, 2 * VR), BF),
            pltpu.VMEM((GROUP, ROWS, EDGE), F32),
            pltpu.VMEM((GROUP, LOCAL * ROWS, VR), BF),
            pltpu.VMEM((2, 2 * LOCAL * ROWS, GRID), F32),
            pltpu.VMEM((GROUP, LOCAL * ROWS, VR), F32),
            pltpu.VMEM((GROUP, LOCAL, ROWS, TP), F32),
            pltpu.VMEM((ROWS, TP), F32),
            pltpu.VMEM((ROWS, TP), F32),
            pltpu.VMEM((ROWS, TP), F32),
            dma((20,)),
            dma((6,)),
            dma((6,)),
            dma((3,)),
            dma((3,)),
            dma((4,)),
            dma((2,)),
            dma((5,)),
            dma((3,)),
            dma((4,)),
            dma,
        ],
        compiler_params=pltpu.CompilerParams(collective_id=0, has_side_effects=True, vmem_limit_bytes=32 * 1024 * 1024),
        name="window_gradient",
    )
    kernel_real, kernel_imag = (jnp.swapaxes(x, 1, 2) for x in (kernel_real, kernel_imag))
    arrays = (theta, target, kernel_real, kernel_imag, weights, thresholds, *(jnp.asarray(x) for x in constants))
    return call(*(pltpu.with_memory_space_constraint(x, pltpu.HBM) for x in arrays))


def solution(mesh):
    in_specs = (
        P(("tile", "cond"), None),
        P("tile", None),
        P("cond", None, None, None),
        P("cond", None, None, None),
        P(),
        P("cond"),
    )
    out_specs = P(("tile", "cond"), None)
    body = functools.partial(shards, mesh.shape["tile"])
    return jax.shard_map(body, mesh=mesh, in_specs=in_specs, out_specs=out_specs, check_vma=False)
```

```python
import functools
import math

import jax
import jax.numpy as jnp
import ml_dtypes
import numpy as np
from jax import lax
from jax.experimental import pallas as pl
from jax.experimental.pallas import tpu as pltpu
from jax.sharding import PartitionSpec as P

TP = 512
HALO = 32
KSUP = 65
HALF = KSUP // 2
CONDS = 8
KERNELS = 2
SIZE = TP + 2 * HALO
ROWS = 128
GROUP = 4
LOCAL = CONDS // GROUP
UH = 40
UR = 2 * UH
VR = 128
FLAT = 2 * HALF
DEPTH = LOCAL * KERNELS
USED = UH + HALF
EDGE = 2 * DEPTH
CHUNK = EDGE + DEPTH // 2 * USED
WIRE = EDGE + DEPTH * USED
SPAN = DEPTH * ROWS
GRID = 128
SPARE = HALF + 1

MASK_STEEP = 2.0
RESIST_STEEP = 4.0
BAND_WEIGHT = 1.0

BF = jnp.bfloat16
F32 = jnp.float32
MESH = pl.DeviceIdType.MESH


def split(x):
    hi = x.astype(BF)
    return hi, (x - hi.astype(F32)).astype(BF)


def np_split(x):
    hi = x.astype(ml_dtypes.bfloat16)
    return hi, (x - hi.astype(np.float64)).astype(ml_dtypes.bfloat16)


def waves(positions):
    phase = np.fmod(np.asarray(positions, np.float64)[:, None] * np.arange(HALF + 1)[None, :], SIZE)
    angles = phase * (2.0 * math.pi / SIZE)
    return np.cos(angles), np.sin(angles)


def row_basis(positions):
    cos, sin = waves(positions)
    out = np.zeros((len(positions), UR))
    out[:, :HALF] = cos[:, 1:]
    out[:, HALF] = 1.0
    out[:, UH:USED] = sin[:, 1:]
    return out


def column_basis(positions):
    cos, sin = waves(positions)
    out = np.zeros((len(positions), VR))
    out[:, :HALF] = cos[:, 1:]
    out[:, HALF:FLAT] = sin[:, 1:]
    out[:, FLAT] = 1.0
    return out


def parity_rows():
    out = np.zeros((UR, UR))
    out[HALF, HALF] = 1.0
    for j in range(1, HALF + 1):
        out[j - 1, HALF + j] = out[j - 1, HALF - j] = out[UH + j - 1, HALF + j] = 1.0
        out[UH + j - 1, HALF - j] = -1.0
    return out


def parity_columns():
    out = np.zeros((2 * VR, 2 * VR))
    for ri in range(2):
        out[ri * VR + HALF, VR + ri] = 1.0
        for j in range(1, HALF + 1):
            even = ri * FLAT + j - 1
            out[ri * VR + HALF + j, even] = out[ri * VR + HALF - j, even] = 1.0
            out[ri * VR + HALF + j, even + HALF] = 1.0
            out[ri * VR + HALF - j, even + HALF] = -1.0
    return out


def tables():
    bf = ml_dtypes.bfloat16
    cols = column_basis(np.arange(TP) + HALO)
    hi, lo = np_split(cols)
    by = np.concatenate([hi, lo], axis=1)
    bt = np.concatenate([hi.T, lo.T], axis=0)
    places = column_basis(np.arange(GRID) * (SIZE / GRID))
    hi, lo = np_split(places[:, :FLAT])
    sample = np.zeros((3 * VR, 2 * GRID), bf)
    gather = np.zeros((4 * GRID, 2 * VR), bf)
    for ri in range(2):
        for block, part in enumerate((hi, hi, lo)):
            at = block * VR + ri * FLAT
            sample[at : at + FLAT, ri * GRID : (ri + 1) * GRID] = part.T
        gather[ri * GRID : (ri + 1) * GRID, ri * FLAT : (ri + 1) * FLAT] = hi
        gather[ri * GRID : (ri + 1) * GRID, VR + ri * FLAT : VR + (ri + 1) * FLAT] = lo
        gather[(2 + ri) * GRID : (3 + ri) * GRID, ri * FLAT : (ri + 1) * FLAT] = hi
    phase = (np.arange(TP) + HALO) * (2.0 * math.pi / SIZE)
    place = np.arange(GRID) * (2.0 * math.pi / GRID)
    spread = np.ones((GRID, TP))
    for f in range(1, GRID // 2):
        spread += 2.0 * np.cos(f * (phase[None, :] - place[:, None]))
    spread += np.cos(GRID // 2 * place)[:, None] * np.cos(GRID // 2 * phase)[None, :]
    spread /= GRID
    last = np.sin(GRID // 2 * phase)
    hi, lo = np_split(spread)
    last_hi, last_lo = np_split(last)
    rest = np.zeros((VR, TP), bf)
    for at in (0, FLAT):
        rest[at + HALF - 2], rest[at + HALF - 1], rest[at + FLAT - 1] = last_hi, last_hi, last_lo
    fine = np.concatenate([hi, lo, rest], axis=0)
    coarse = np.concatenate([hi.T, lo.T], axis=1)
    half_last = np.broadcast_to(0.5 * last, (8, TP)).astype(np.float32)
    pack = []
    turned = []
    for c in range(GROUP):
        own = row_basis(np.arange(ROWS) + HALO + ROWS * c)
        near = np.zeros_like(own)
        if c == 0:
            near[:HALO] = row_basis(np.arange(HALO) + HALO + TP)
        if c == GROUP - 1:
            near[ROWS - HALO :] = row_basis(np.arange(HALO))
        row = []
        column = []
        for table in (own, near):
            thi, tlo = np_split(table)
            row += [thi, tlo, thi, np.zeros((ROWS, 256 - 3 * UR), bf)]
            column.append(np.concatenate([thi.T, thi.T], axis=1))
            column.append(np.concatenate([tlo.T, np.zeros((UR, ROWS), bf)], axis=1))
        pack.append(np.concatenate(row, axis=1))
        turned.append(np.concatenate(column, axis=0))
    pv = parity_columns().astype(bf)
    pu = parity_rows().astype(bf)
    pu = np.concatenate([pu, pu], axis=1)
    return by, bt, np.stack(pack), np.stack(turned), pv, pu, sample, gather, fine, coarse, half_last


def dot(a, b):
    return jnp.dot(a, b, preferred_element_type=F32)


def kernel(
    tiles,
    theta_h, target_h, kr_h, ki_h, weights_h, thresholds_h, by_h, bt_h, pack_h, turned_h, pv_h, pu_h,
    sample_h, gather_h, fine_h, coarse_h, half_last_h,
    out_v,
    weights_s, thresholds_s, theta_v, target_v, raw_v, by, bt, pack, turned, pv, pu,
    sample, gather, fine, coarse, half_last, stack, zbuf, coef, ecoef, passed, rpair, rown, rhalo, rin, rsum, erow, aown, ain, anear, jbuf, jflat, amps, crossed, rows_v, flat_v, edge_v, push_v, last_v, resists, band, wanted, factor,
    load_sem, zs_sem, zr_sem, rs_sem, rr_sem, hs_sem, hr_sem, as_sem, ar_sem, near_sem, pass_sem,
):
    t = lax.axis_index("tile")
    c = lax.axis_index("cond")
    first = c == 0
    final = c == GROUP - 1
    has_prev = t > 0
    has_next = t < tiles - 1

    loads = []

    def load(src, dst):
        copy = pltpu.make_async_copy(src, dst, load_sem.at[len(loads)])
        copy.start()
        loads.append(copy)
        return copy

    load_kr = load(kr_h, raw_v.at[0])
    load_ki = load(ki_h, raw_v.at[1])
    load_pv = [load(pv_h, pv.at[pl.ds(at, 2 * VR), :]) for at in (0, 2 * VR)]
    load_pu = load(pu_h, pu)
    load_thresholds = load(thresholds_h, thresholds_s)
    load_theta = load(theta_h, theta_v)
    load_by = load(by_h, by)
    load_turned = load(turned_h.at[c], turned)
    load_pack = load(pack_h.at[c], pack)
    load_sample = load(sample_h, sample)
    load_fine = [
        load(fine_h.at[pl.ds(0, GRID), :], fine.at[pl.ds(0, GRID), :]),
        load(fine_h, fine.at[pl.ds(GRID, 3 * GRID), :]),
    ]
    load_coarse = load(coarse_h, coarse)
    load_half = load(half_last_h, half_last)
    load_gather = load(gather_h, gather)
    load_bt = [
        load(bt_h.at[pl.ds(0, VR), :], bt.at[pl.ds(0, VR), :]),
        load(bt_h, bt.at[pl.ds(VR, 2 * VR), :]),
    ]
    load_weights = load(weights_h, weights_s)
    load_target = load(target_h.at[pl.ds(pl.multiple_of(c * ROWS, ROWS), ROWS), :], target_v)

    def partner(mask):
        return (t, c ^ mask)

    barrier = pltpu.get_barrier_semaphore()

    def greet(device):
        pl.semaphore_signal(barrier, inc=1, device_id=device, device_id_type=MESH)

    mirror = ((t + tiles // 2) % tiles, c ^ 2)
    for mask in range(1, GROUP):
        greet(partner(mask))
    greet(mirror)

    bend = tiles // 2 - 1
    between = bend - 12
    at_bend = t == bend
    after_bend = (t == bend + 1) & first
    relays = (t == between) & jnp.logical_not(first | final)

    @pl.when(has_next)
    def _():
        greet((jnp.where(at_bend, between, t + 1), jnp.where(at_bend, 1 + c // 2, 0)))

    @pl.when(has_prev)
    def _():
        greet((t - 1, GROUP - 1))

    @pl.when(relays)
    def _():
        greet((bend + 1, 0))

    lane = lax.broadcasted_iota(jnp.int32, (UH, VR), 1)
    row = lax.broadcasted_iota(jnp.int32, (UH, VR), 0)
    tall_lane = lax.broadcasted_iota(jnp.int32, (UR, VR), 1)
    diagonal = tall_lane == lax.broadcasted_iota(jnp.int32, (UR, VR), 0)
    odd = lane % FLAT >= HALF
    sign_v = jnp.where(odd, -1.0, 1.0).astype(F32)
    sign_i = jnp.where(lane >= FLAT, -1.0, 1.0).astype(F32)
    edge_lane = lane[: 2 * DEPTH]
    edge_row = row[: 2 * DEPTH]

    def swap(x):
        return jnp.where(odd, pltpu.roll(x, HALF, 1), pltpu.roll(x, VR - HALF, 1))

    def turned_edge(x):
        out = jnp.where(edge_lane < UH, pltpu.roll(x, VR - UH, 1), -pltpu.roll(x, UH, 1))
        return jnp.where(edge_lane < UR, out, 0.0)

    def stacked(x):
        near = x.astype(BF).astype(F32)
        return jnp.concatenate([near, x - near], axis=0).astype(BF)

    def packed(x):
        out = jnp.where(lane < FLAT, x[:UH], pltpu.roll(x[UH:], FLAT, 1))
        flat = jnp.sum(jnp.where(diagonal, x[:, FLAT : FLAT + 1], 0.0), axis=0, keepdims=True)
        return jnp.where(row == SPARE, flat, out)

    def unpacked(x):
        flat = jnp.sum(jnp.where(diagonal, x[SPARE : SPARE + 1], 0.0), axis=1, keepdims=True)
        keep = (lane < FLAT) & (row < SPARE)
        out = []
        for h, value in enumerate((x, pltpu.roll(x, FLAT, 1))):
            out.append(jnp.where(lane == FLAT, flat[h * UH : (h + 1) * UH], jnp.where(keep, value, 0.0)))
        return out

    def unpack_kernels(s):
        for n in range(DEPTH):
            at = EDGE + n * USED
            even = zbuf[s, at : at + UH, :]
            uneven = zbuf[s, at + UH : at + USED, :]
            odd_rows = odd[: USED - UH]
            coef[s, n, 0] = jnp.where(odd, pltpu.roll(even, HALF, 1), even)
            coef[s, n, 1] = jnp.where(odd, pltpu.roll(even, FLAT, 1), pltpu.roll(even, HALF, 1))
            coef[s, n, 2, : USED - UH] = jnp.where(
                odd_rows, pltpu.roll(uneven, VR - HALF, 1), pltpu.roll(uneven, FLAT, 1)
            )
            coef[s, n, 3, : USED - UH] = jnp.where(odd_rows, uneven, pltpu.roll(uneven, VR - HALF, 1))
        flat = jnp.where(edge_lane < USED, zbuf[s, :EDGE, :], 0.0)
        other = jnp.where(edge_row % 2 == 0, pltpu.roll(flat, EDGE - 1, 0), -pltpu.roll(flat, 1, 0))
        ecoef[s, 0] = jnp.where(edge_lane < UH, flat, jnp.where(edge_lane < UR, pltpu.roll(flat, UH, 1), 0.0))
        ecoef[s, 1] = jnp.where(
            edge_lane < UH, pltpu.roll(other, VR - UH, 1), jnp.where(edge_lane < UR, other, 0.0)
        )

    stack[...] = jnp.zeros_like(stack)
    load_kr.wait()
    load_ki.wait()
    for ri in range(2):
        for l in range(LOCAL):
            for k in range(KERNELS):
                at = (l * KERNELS + k) * UR
                stack[at : at + KSUP, ri * VR : ri * VR + KSUP] = raw_v[ri, l, :, k, :]
    for copy in load_pv:
        copy.wait()
    load_pu.wait()
    hi, lo = split(stack[...])
    folded = dot(jnp.concatenate([hi, lo], axis=1), pv[...])
    hi, lo = split(folded)
    coef[:, :, 2:, USED - UH :, :] = jnp.zeros((GROUP, DEPTH, 2, UR - USED, VR), F32)
    load_thresholds.wait()
    for n in range(DEPTH):
        rhs = jnp.concatenate([hi[n * UR : (n + 1) * UR], lo[n * UR : (n + 1) * UR]], axis=0)
        value = dot(pu[...], rhs)
        zbuf[0, EDGE + n * USED : EDGE + (n + 1) * USED, :] = value[:USED, :VR]
        for ri in range(2):
            flat = jnp.sum(jnp.where(diagonal, value[:, VR + ri : VR + ri + 1], 0.0), axis=0, keepdims=True)
            if 2 * n + ri < LOCAL:
                flat = jnp.where(lane[:1] == VR - 1, thresholds_s[2 * n + ri], flat)
            zbuf[0, 2 * n + ri : 2 * n + ri + 1, :] = flat

    load_theta.wait()
    load_by.wait()
    load_turned.wait()
    mask_rows = jnp.tanh(MASK_STEEP * theta_v[...])
    hi, lo = split(mask_rows)
    wide = dot(jnp.concatenate([hi, lo], axis=0), by[...])
    column = wide[:ROWS, :VR] + wide[:ROWS, VR:] + wide[ROWS:, :VR]
    hi, lo = split(column)
    both = dot(turned[...], jnp.concatenate([hi, lo], axis=0))
    rown[...] = packed(both[:UR] + both[UR : 2 * UR])
    rhalo[...] = packed(both[2 * UR : 3 * UR] + both[3 * UR :])

    edge_of = (has_next & final) | (has_prev & first)
    waited = jnp.where(edge_of, 2 * GROUP, GROUP)
    pl.semaphore_wait(barrier, jnp.where(after_bend | relays, GROUP + 2, waited))

    def remote(src, dst, send, recv, device):
        return pltpu.make_async_remote_copy(
            src_ref=src, dst_ref=dst, send_sem=send, recv_sem=recv, device_id=device, device_id_type=MESH
        )

    def halo_next(other):
        return remote(rhalo, rin.at[3], hs_sem.at[other], hr_sem.at[0], (t + 1, other))

    def halo_prev(other):
        return remote(rhalo, rin.at[4], hs_sem.at[other], hr_sem.at[1], (t - 1, other))

    def halo_via(side):
        return remote(rhalo, passed, hs_sem.at[side], pass_sem, (between, 1 + side))

    def halo_passed(core):
        return remote(passed, rin.at[4], hs_sem.at[core], hr_sem.at[1], (bend, 2 * (c - 1) + core))

    def part(mask):
        source = rown if mask == 1 else rpair
        return remote(source, rin.at[mask - 1], rs_sem.at[mask - 1], rr_sem.at[mask - 1], partner(mask))

    def kernels_to(mask, chunk):
        device = partner(1) if mask != 2 else mirror
        source = 2 if mask == 3 else 0
        rows = pl.ds(0, CHUNK) if chunk == 0 else pl.ds(CHUNK, WIRE - CHUNK)
        sem = 2 * (mask - 1) + chunk
        return remote(
            zbuf.at[source, rows, :], zbuf.at[mask, rows, :], zs_sem.at[sem], zr_sem.at[sem], device
        )

    @pl.when(has_next & final)
    def _():
        for other in range(GROUP):
            halo_next(other).start()

    @pl.when(has_prev & first & jnp.logical_not(after_bend))
    def _():
        for other in range(GROUP):
            halo_prev(other).start()

    @pl.when(after_bend)
    def _():
        for side in range(2):
            halo_via(side).start()

    part(1).start()
    kernels_to(2, 0).start()
    kernels_to(2, 1).start()
    part(1).wait_recv()
    rpair[...] = rown[...] + rin[0]
    part(2).start()
    for chunk in range(2):
        kernels_to(1, chunk).start()

    @pl.when(relays)
    def _():
        halo_via(0).wait_recv()
        for core in range(2):
            halo_passed(core).start()

    @pl.when(jnp.logical_not(has_prev))
    def _():
        rin[3] = jnp.zeros((UH, VR), F32)

    @pl.when(jnp.logical_not(has_next))
    def _():
        rin[4] = jnp.zeros((UH, VR), F32)

    unpack_kernels(0)
    for chunk in range(2):
        kernels_to(1, chunk).wait_recv()
    unpack_kernels(1)

    @pl.when(has_prev)
    def _():
        halo_next(0).wait_recv()

    @pl.when(has_next)
    def _():
        halo_prev(0).wait_recv()

    part(2).wait_recv()

    total = rpair[...] + rin[1] + rin[3] + rin[4]
    total = total * (1.0 / (SIZE * SIZE))
    keep = row < SPARE
    turn = pltpu.roll(total, FLAT, 1)
    halves = [
        jnp.where(keep, jnp.where(lane < FLAT, total, turn), 0.0),
        jnp.where(keep, jnp.where(lane < FLAT, turn, total), 0.0),
    ]
    for h in range(2):
        sign_u = 1.0 - 2.0 * h
        rsum[0, h] = halves[h]
        rsum[1, h] = sign_i * sign_v * swap(halves[h])
        rsum[2, h] = sign_u * sign_i * halves[1 - h]
        rsum[3, h] = (-sign_u) * sign_v * swap(halves[1 - h])
    flat = jnp.where(edge_lane < UR, total[SPARE : SPARE + 1], 0.0)
    erow[0] = flat
    erow[1] = turned_edge(flat)

    load_pack.wait()
    load_sample.wait()
    for copy in load_fine:
        copy.wait()
    block_lane = lax.broadcasted_iota(jnp.int32, (ROWS, VR), 1)

    def grids_and_rows(s):
        grids = []
        for n in range(DEPTH):
            grid = []
            for h in range(2):
                terms = [coef[s, n, m] * rsum[m, h] for m in range(4)]
                grid.append((terms[0] + terms[1]) + (terms[2] + terms[3]))
            grids.append(jnp.concatenate(grid, axis=0))
        cross = [None] * LOCAL
        for l in range(LOCAL):
            hi, lo = split(jnp.concatenate(grids[KERNELS * l : KERNELS * (l + 1)], axis=1))
            tall = dot(pack[:, : 3 * UR], jnp.concatenate([hi, hi, lo], axis=0))
            for k in range(KERNELS):
                part = tall[:, k * VR : (k + 1) * VR]
                at = (l * KERNELS + k) * ROWS
                other = jnp.where(block_lane % FLAT == HALF - 1, pltpu.roll(part, VR - HALF, 1), 0.0)
                other = jnp.where(block_lane % FLAT == FLAT - 1, pltpu.roll(part, HALF, 1), other)
                crossed[s, at : at + ROWS, :] = other
                other = part * other
                cross[l] = other if k == 0 else cross[l] + other
                hi, lo = split(part)
                rows_v[s // 2, s % 2 * SPAN + at : s % 2 * SPAN + at + ROWS, :VR] = hi
                rows_v[s // 2, s % 2 * SPAN + at : s % 2 * SPAN + at + ROWS, VR:] = lo
        for l in range(LOCAL):
            near = cross[l].astype(BF).astype(F32)
            far = pltpu.roll(cross[l] - near, VR - 1, 1)
            edge_v[s, l * ROWS : (l + 1) * ROWS, :] = jnp.where(block_lane % FLAT == HALF - 2, far, near).astype(BF)
        flat = stacked(ecoef[s, 0] * erow[0] + ecoef[s, 1] * erow[1])
        upper = dot(flat, turned[:VR, :ROWS])
        lower = dot(flat, turned[UR : UR + VR, :ROWS])
        flat_v[s] = (upper[:EDGE] + upper[EDGE:] + lower[:EDGE]).T

    def resist_of(slots):
        held = slots[0] // 2
        amp = dot(jnp.concatenate([rows_v[held], rows_v[held, :, :VR]], axis=1), sample[...])
        lhs = []
        for s in slots:
            for l in range(LOCAL):
                sampled = None
                for k in range(KERNELS):
                    n = l * KERNELS + k
                    at = s % 2 * SPAN + n * ROWS
                    for ri in range(2):
                        piece = amp[at : at + ROWS, ri * GRID : (ri + 1) * GRID]
                        piece = piece + flat_v[s, :, 2 * n + ri : 2 * n + ri + 1]
                        amps[s, n * ROWS : (n + 1) * ROWS, ri * GRID : (ri + 1) * GRID] = piece
                        sampled = piece * piece if k + ri == 0 else sampled + piece * piece
                hi, lo = split(sampled)
                lhs.append(jnp.concatenate([hi, lo, hi, edge_v[s, l * ROWS : (l + 1) * ROWS, :]], axis=1))
        intensities = dot(jnp.concatenate(lhs, axis=0), fine[...])
        total = None
        for s in slots:
            for l in range(LOCAL):
                at = (s % 2 * LOCAL + l) * ROWS
                level = zbuf[s, l : l + 1, VR - 1 : VR]
                resist = jax.nn.sigmoid(RESIST_STEEP * (intensities[at : at + ROWS] - level))
                resists[s, l] = resist
                total = resist if total is None else total + resist
        if slots[0] == 0:
            band[...] = total
        else:
            band[...] += total

    grids_and_rows(0)
    kernels_to(2, 0).wait_recv()
    kernels_to(3, 0).start()
    grids_and_rows(1)
    kernels_to(2, 1).wait_recv()
    kernels_to(3, 1).start()
    unpack_kernels(2)
    resist_of((0, 1))
    grids_and_rows(2)
    for chunk in range(2):
        kernels_to(3, chunk).wait_recv()
    unpack_kernels(3)
    grids_and_rows(3)
    resist_of((2, 3))

    load_target.wait()
    load_weights.wait()
    weight_sum = weights_s[0]
    for n in range(1, CONDS):
        weight_sum = weight_sum + weights_s[n]
    weight_sum = jnp.full((8, TP), weight_sum, jnp.int32).astype(F32)
    wanted[...] = target_v[...].astype(F32)
    band[...] = band[...] * (4.0 * RESIST_STEEP * BAND_WEIGHT / CONDS / CONDS)

    load_coarse.wait()
    load_half.wait()
    load_gather.wait()

    def push_of(slots):
        fields = []
        for s in slots:
            for l in range(LOCAL):
                weight = jnp.full((8, TP), weights_s[(c ^ s) * LOCAL + l], jnp.int32).astype(F32) / weight_sum
                pull = (4.0 * RESIST_STEEP) * weight[0:1]
                resist = resists[s, l]
                slope = (pull + 4.0 * RESIST_STEEP * BAND_WEIGHT / CONDS) * resist - (pull * wanted[...] + band[...])
                field = slope * (resist - resist * resist)
                last = jnp.sum(field * half_last[0:1, :], axis=1, keepdims=True)
                last_v[s, l * ROWS : (l + 1) * ROWS, :] = jnp.broadcast_to(last, (ROWS, VR))
                fields.append(field)
        hi, lo = split(jnp.concatenate(fields, axis=0))
        wide = dot(jnp.concatenate([hi, lo], axis=0), coarse[...])
        half = 2 * LOCAL * ROWS
        push_v[slots[0] // 2] = wide[:half, :GRID] + wide[:half, GRID:] + wide[half:, :GRID]

    def adjoint_of(slots):
        rows = []
        flats = []
        for s in slots:
            flat = []
            for n in range(DEPTH):
                at = (s % 2 * LOCAL + n // KERNELS) * ROWS
                push = push_v[slots[0] // 2, at : at + ROWS, :]
                drive = []
                for ri in range(2):
                    piece = push * amps[s, n * ROWS : (n + 1) * ROWS, ri * GRID : (ri + 1) * GRID]
                    flat.append(jnp.where(block_lane == 2 * n + ri, jnp.sum(piece, axis=1, keepdims=True), 0.0))
                    drive.append(piece)
                hi, lo = split(jnp.concatenate(drive, axis=1))
                rows.append(jnp.concatenate([hi, lo], axis=1))
            while len(flat) > 1:
                flat = [flat[i] + flat[i + 1] for i in range(0, len(flat), 2)]
            flats.append(flat[0])
        drive = dot(jnp.concatenate(rows, axis=0), gather[...])
        drive = drive[:, :VR] + drive[:, VR:]
        sums = [[None, None] for _ in range(4)]
        for s in slots:
            for l in range(LOCAL):
                pair = []
                for n in (KERNELS * l, KERNELS * l + 1):
                    at = s % 2 * SPAN + n * ROWS
                    last = last_v[s, l * ROWS : (l + 1) * ROWS, :]
                    pair.append(drive[at : at + ROWS] + last * crossed[s, n * ROWS : (n + 1) * ROWS, :])
                hi, lo = split(jnp.concatenate(pair, axis=1))
                back = dot(turned[: 2 * UR, :], jnp.concatenate([hi, lo], axis=0))
                back = back[:UR] + back[UR:]
                for k in range(KERNELS):
                    for h in range(2):
                        value = back[h * UH : (h + 1) * UH, k * VR : (k + 1) * VR]
                        for m in range(4):
                            term = coef[s, l * KERNELS + k, m] * value
                            sums[m][h] = term if sums[m][h] is None else sums[m][h] + term
        total = None
        for s, flat in zip(slots, flats):
            wide = dot(stacked(flat.T[:EDGE]), pack[:, : 2 * VR])
            here = wide[:EDGE, :VR] + wide[EDGE:, :VR]
            upper = pltpu.roll(wide[:EDGE, :VR], VR - UR, 1)
            lower = pltpu.roll(wide[:EDGE, VR:], VR - UR, 1)
            here = here + jnp.where(edge_lane < VR - UR, upper, lower)
            term = ecoef[s, 0] * here - ecoef[s, 1] * turned_edge(here)
            total = term if total is None else total + term
        for m in range(4):
            for h in range(2):
                if slots[0] == 0:
                    jbuf[m, h] = sums[m][h]
                else:
                    jbuf[m, h] += sums[m][h]
        if slots[0] == 0:
            jflat[...] = total
        else:
            jflat[...] += total

    push_of((0, 1))
    adjoint_of((0, 1))
    push_of((2, 3))
    adjoint_of((2, 3))

    def folded_part(m, h):
        sign = 1.0 if m in (0, 3) else -1.0
        return jbuf[m, h] + sign * pltpu.roll(jbuf[m, h], FLAT, 1)

    halves = []
    for h in range(2):
        sign_u = 1.0 - 2.0 * h
        halves.append(
            folded_part(0, h)
            + swap(sign_v * folded_part(1, h))
            - sign_u * folded_part(2, 1 - h)
            + swap(sign_u * sign_v * folded_part(3, 1 - h))
        )
    value = jnp.where(lane < FLAT, halves[0], pltpu.roll(halves[1], FLAT, 1))
    aown[...] = jnp.where(row == SPARE, jnp.sum(jflat[...], axis=0, keepdims=True), value)

    def adjoint_part(mask):
        return remote(aown, ain.at[mask - 1], as_sem.at[mask - 1], ar_sem.at[mask - 1], partner(mask))

    def adjoint_prev():
        return remote(aown, anear.at[c], as_sem.at[3], near_sem.at[c], (t - 1, GROUP - 1))

    def adjoint_next():
        return remote(aown, anear.at[c], as_sem.at[4], near_sem.at[c], (t + 1, 0))

    def adjoint_near(other):
        return remote(aown, anear.at[other], as_sem.at[3], near_sem.at[other], (t, c ^ 1))

    @pl.when(has_prev)
    def _():
        adjoint_prev().start()

    @pl.when(has_next)
    def _():
        adjoint_next().start()

    for mask in range(1, GROUP):
        adjoint_part(mask).start()

    near = (first & has_prev) | (final & has_next)

    factor[...] = (MASK_STEEP / (SIZE * SIZE)) * (1.0 - jnp.square(jnp.tanh(MASK_STEEP * theta_v[...])))
    for copy in load_bt:
        copy.wait()

    for mask in range(1, GROUP):
        adjoint_part(mask).wait_recv()

    def sensitivity(value, rows, columns):
        hi, lo = split(jnp.concatenate(unpacked(value), axis=0))
        value = jnp.concatenate([hi, hi, lo, jnp.zeros((256 - 3 * UR, VR), BF)], axis=0)
        hi, lo = split(dot(pack[rows, columns], value))
        return dot(jnp.concatenate([hi, lo, hi], axis=1), bt[...])

    out_v[...] = sensitivity(aown[...] + ain[0] + ain[1] + ain[2], slice(None), slice(0, 256)) * factor[...]

    @pl.when(near)
    def _():
        for other in range(GROUP):
            adjoint_near(other).wait_recv()
        edge = pl.ds(pl.multiple_of(jnp.where(first, 0, ROWS - HALO), HALO), HALO)
        value = anear[0] + anear[1] + anear[2] + anear[3]
        out_v[edge, :] += sensitivity(value, edge, slice(256, 512)) * factor[edge, :]

    @pl.when(has_next & final)
    def _():
        for other in range(GROUP):
            halo_next(other).wait_send()

    @pl.when(has_prev & first & jnp.logical_not(after_bend))
    def _():
        for other in range(GROUP):
            halo_prev(other).wait_send()

    @pl.when(after_bend)
    def _():
        for side in range(2):
            halo_via(side).wait_send()

    @pl.when(relays)
    def _():
        for core in range(2):
            halo_passed(core).wait_send()

    for mask in range(1, GROUP):
        if mask < GROUP - 1:
            part(mask).wait_send()
        for chunk in range(2):
            kernels_to(mask, chunk).wait_send()
        adjoint_part(mask).wait_send()

    @pl.when(has_prev)
    def _():
        adjoint_prev().wait_send()

    @pl.when(has_next)
    def _():
        adjoint_next().wait_send()


def shards(tiles, theta, target, kernel_real, kernel_imag, weights, thresholds):
    constants = tables()
    dma = pltpu.SemaphoreType.DMA
    by, bt, pack, turned, pv, pu, sample, gather, fine, coarse, half_last = constants
    call = pl.pallas_call(
        functools.partial(kernel, tiles),
        out_shape=jax.ShapeDtypeStruct((ROWS, TP), F32),
        in_specs=[pl.BlockSpec(memory_space=pltpu.HBM)] * 17,
        out_specs=pl.BlockSpec(memory_space=pltpu.VMEM),
        scratch_shapes=[
            pltpu.SMEM((CONDS,), jnp.int32),
            pltpu.SMEM((LOCAL,), F32),
            pltpu.VMEM((ROWS, TP), F32),
            pltpu.VMEM((ROWS, TP), jnp.int32),
            pltpu.VMEM((2, LOCAL, KSUP, KERNELS, KSUP), F32),
            pltpu.VMEM(by.shape, BF),
            pltpu.VMEM((3 * VR, TP), BF),
            pltpu.VMEM(pack.shape[1:], BF),
            pltpu.VMEM(turned.shape[1:], BF),
            pltpu.VMEM((4 * VR, 2 * VR), BF),
            pltpu.VMEM(pu.shape, BF),
            pltpu.VMEM(sample.shape, BF),
            pltpu.VMEM(gather.shape, BF),
            pltpu.VMEM((4 * GRID, TP), BF),
            pltpu.VMEM(coarse.shape, BF),
            pltpu.VMEM(half_last.shape, F32),
            pltpu.VMEM((DEPTH * UR, 2 * VR), F32),
            pltpu.VMEM((GROUP, WIRE, VR), F32),
            pltpu.VMEM((GROUP, DEPTH, 4, UH, VR), F32),
            pltpu.VMEM((GROUP, 2, EDGE, VR), F32),
            pltpu.VMEM((UH, VR), F32),
            pltpu.VMEM((UH, VR), F32),
            pltpu.VMEM((UH, VR), F32),
            pltpu.VMEM((UH, VR), F32),
            pltpu.VMEM((5, UH, VR), F32),
            pltpu.VMEM((4, 2, UH, VR), F32),
            pltpu.VMEM((2, EDGE, VR), F32),
            pltpu.VMEM((UH, VR), F32),
            pltpu.VMEM((3, UH, VR), F32),
            pltpu.VMEM((GROUP, UH, VR), F32),
            pltpu.VMEM((4, 2, UH, VR), F32),
            pltpu.VMEM((EDGE, VR), F32),
            pltpu.VMEM((GROUP, DEPTH * ROWS, 2 * GRID), F32),
            pltpu.VMEM((GROUP, DEPTH * ROWS, VR), F32),
            pltpu.VMEM((2, 2 * SPAN, 2 * VR), BF),
            pltpu.VMEM((GROUP, ROWS, EDGE), F32),
            pltpu.VMEM((GROUP, LOCAL * ROWS, VR), BF),
            pltpu.VMEM((2, 2 * LOCAL * ROWS, GRID), F32),
            pltpu.VMEM((GROUP, LOCAL * ROWS, VR), F32),
            pltpu.VMEM((GROUP, LOCAL, ROWS, TP), F32),
            pltpu.VMEM((ROWS, TP), F32),
            pltpu.VMEM((ROWS, TP), F32),
            pltpu.VMEM((ROWS, TP), F32),
            dma((20,)),
            dma((6,)),
            dma((6,)),
            dma((3,)),
            dma((3,)),
            dma((4,)),
            dma((2,)),
            dma((5,)),
            dma((3,)),
            dma((4,)),
            dma,
        ],
        compiler_params=pltpu.CompilerParams(collective_id=0, has_side_effects=True, vmem_limit_bytes=32 * 1024 * 1024),
        name="window_gradient",
    )
    kernel_real, kernel_imag = (jnp.swapaxes(x, 1, 2) for x in (kernel_real, kernel_imag))
    arrays = (theta, target, kernel_real, kernel_imag, weights, thresholds, *(jnp.asarray(x) for x in constants))
    return call(*(pltpu.with_memory_space_constraint(x, pltpu.HBM) for x in arrays))


def solution(mesh):
    in_specs = (
        P(("tile", "cond"), None),
        P("tile", None),
        P("cond", None, None, None),
        P("cond", None, None, None),
        P(),
        P("cond"),
    )
    out_specs = P(("tile", "cond"), None)
    body = functools.partial(shards, mesh.shape["tile"])
    return jax.shard_map(body, mesh=mesh, in_specs=in_specs, out_specs=out_specs, check_vma=False)
```
